32 devices in a mesh: dp: 32 (over z, y, x, core).
Axes of the slice: x: 2, y: 2, z: 4, core: 2. Of those that a mesh axis runs over, the one named last changes fastest.
Arguments:
- tokens: bfloat16 [32768, 1024], P('dp'), may hold values from -6 to 6
- lengths: int32 [32], P('dp'), may hold values from 256 to 1024, as said below
- expert_ids: int32 [32768, 2], P('dp'), may hold values from 0 to 15, all different within a row
- slot_order: int32 [32, 1024], P('dp'), may hold values from 0 to 1023, each once within a row
- gain_attn: float32 [1024], replicated, may hold values from 0.1 to 1.9
- w_qkv: bfloat16 [1024, 3072], replicated, may hold values from -0.1875 to 0.1875
- w_out: bfloat16 [1024, 1024], replicated, may hold values from -1.5 to 1.5
- gain_moe: float32 [1024], replicated, may hold values from 0.1 to 1.9
- w_router: bfloat16 [1024, 16], replicated, may hold values from -0.09375 to 0.09375
- w_gate: bfloat16 [32, 1024, 1408], P('dp'), may hold values from -0.1875 to 0.1875
- w_up: bfloat16 [32, 1024, 1408], P('dp'), may hold values from -0.1875 to 0.1875
- w_down: bfloat16 [32, 1408, 1024], P('dp'), may hold values from -0.21875 to 0.21875
- out_grad: bfloat16 [32768, 1024], P('dp'), may hold values from -6 to 6
Outputs:
- block_out: bfloat16 [32768, 1024], P('dp')
- tokens_grad: float32 [32768, 1024], P('dp')
- gain_attn_grad: float32 [1024], P('dp')
- w_qkv_grad: float32 [1024, 3072], P('dp')
- w_out_grad: float32 [1024, 1024], P('dp')
- gain_moe_grad: float32 [1024], P('dp')
- w_router_grad: float32 [1024, 16], P('dp')
- w_gate_grad: float32 [32, 1024, 1408], P('dp')
- w_up_grad: float32 [32, 1024, 1408], P('dp')
- w_down_grad: float32 [32, 1408, 1024], P('dp')
The draws below stay inside these ranges and needn't reach their ends.
Inputs may be any that keep to these rules, and one draw needn't show every extreme that they name: `lengths`: valid tokens of each sequence, counted from its start; some sequence has 1024. `expert_ids`: a token's two experts differ. `slot_order`: each row is a permutation of the ranks 0 to 1023 of one group's tokens.
All inputs are finite; a program needn't handle non-finite values.
Results may differ from the reference program's by a relative error of at most 0.015.
Values may be sent and summed in bfloat16 or wider, within the bound.
A program may use at most 576 MiB of HBM per device.

```python
import math
import jax
import jax.numpy as jnp
from jax import lax

D = 1024
HEADS = 16
HEAD_DIM = 64
FF = 2816
EXPERTS = 16
SPLIT = 2
FF_PART = 1408
LEN = 1024
SEQS = 32
TOK_DEV = 1024
TOKENS = 32768
CAPACITY = 80
N_DP = 32


def draw_lengths(key, part):
    lower_key, upper_key = jax.random.split(key)
    spread = 3 * LEN // 4
    lower_draw = jax.random.randint(lower_key, (SEQS,), 0, spread + 1, dtype=jnp.int32)
    upper_draw = jax.random.randint(upper_key, (SEQS,), 0, spread + 1, dtype=jnp.int32)
    lengths_drawn = LEN // 4 + jnp.minimum(lower_draw, upper_draw)
    return lengths_drawn.at[0].set(LEN).astype(jnp.int32)


def raised(array, rng, source, target, blocks, factor):
    def block_of(dim):
        return (jnp.arange(array.shape[dim]) // (array.shape[dim] // blocks)).reshape((-1,) + (1,) * (array.ndim - 1 - dim))

    first = jax.random.permutation(rng, blocks)[block_of(target)]
    second = (block_of(target) + blocks // 2) % blocks
    return jnp.where((block_of(source) == first) | (block_of(source) == second), factor * array, array)


def block_levels(own_key, dims, pieces, least, high):
    factor_of = 1.0
    for axis_at, parts in pieces:
        heights = jax.random.uniform(jax.random.fold_in(jax.random.fold_in(own_key, 6), axis_at), (parts,), jnp.float32, least / len(pieces), high / len(pieces))
        factor_of = factor_of * jnp.repeat(jnp.exp(heights), dims[axis_at] // parts).reshape((-1,) + (1,) * (len(dims) - 1 - axis_at))
    return factor_of


def distinct(stream_key, rows, number_of, top, lift):
    ranking = jax.random.permutation(jax.random.fold_in(stream_key, 1), number_of)
    favour = ranking
    for power in range(3):
        favour = favour * favour // number_of
    favour = favour * lift // number_of
    lots = jax.random.randint(jax.random.fold_in(stream_key, 2), (rows, number_of), 0, 4096) + favour
    sure = jax.random.permutation(jax.random.fold_in(stream_key, 3), rows)[jnp.arange(number_of) % rows]
    lots = jnp.where(jnp.arange(rows)[:, None] == sure[None, :], 1 << 14, lots)
    merit = lots * number_of + jnp.arange(number_of)
    return lax.top_k(merit.astype(jnp.int32), top)[1].astype(jnp.int32)


def gaussian(stream_key, extent, deviation, most, pieces=(), kind=jnp.bfloat16):
    entries = deviation * jax.random.normal(stream_key, extent, jnp.float32)
    if pieces:
        entries = entries * block_levels(stream_key, extent, pieces, -0.22, 0.18)
    return jnp.clip(entries, -most, most).astype(kind)


def bell_draw_with(rng, shape, scale, limit, cuts, heavy, kind=jnp.bfloat16):
    result = scale * jax.random.normal(rng, shape, jnp.float32)
    if cuts:
        result = result * block_levels(rng, shape, cuts, -0.22, 0.18)
    return jnp.clip(raised(result, jax.random.fold_in(rng, 3), *heavy), -limit, limit).astype(kind)


def setup_inputs(seed: int = 0) -> dict:
    keys = jax.random.split(jax.random.key(seed), 14)
    return {
        "tokens": bell_draw_with(keys[0], (TOKENS, D), 1.0, 6.0, ((0, 32),), (0, 1, 32, 2.75)),
        "lengths": draw_lengths(jax.random.fold_in(keys[13], 71), 0),
        "expert_ids": distinct(keys[2], TOKENS, EXPERTS, 2, 1024),
        "slot_order": jax.vmap(lambda own: jax.random.permutation(own, TOK_DEV))(jax.random.split(keys[3], N_DP)).reshape((N_DP, TOK_DEV)).astype(jnp.int32),
        "gain_attn": jnp.clip(1.0 + 0.18 * jax.random.normal(keys[4], (D,), jnp.float32), 0.1, 1.9),
        "w_qkv": gaussian(keys[5], (D, 3 * D), D ** -0.5, 0.1875),
        "w_out": gaussian(keys[6], (D, D), (D // 64) ** -0.5, 1.5),
        "gain_moe": jnp.clip(1.0 + 0.18 * jax.random.normal(keys[7], (D,), jnp.float32), 0.1, 1.9),
        "w_router": gaussian(keys[8], (D, EXPERTS), (4 * D) ** -0.5, 0.09375),
        "w_gate": gaussian(keys[9], (EXPERTS * SPLIT, D, FF_PART), D ** -0.5, 0.1875, ((0, 32),)),
        "w_up": gaussian(keys[10], (EXPERTS * SPLIT, D, FF_PART), D ** -0.5, 0.1875, ((0, 32),)),
        "w_down": gaussian(keys[11], (EXPERTS * SPLIT, FF_PART, D), (FF // 4) ** -0.5, 0.21875, ((0, 32),)),
        "out_grad": gaussian(keys[12], (TOKENS, D), 1.0, 6.0, ((0, 32),)),
    }


@jax.custom_vjp
def low(v):
    return lax.optimization_barrier(v.astype(jnp.bfloat16)).astype(jnp.float32)

@jax.custom_vjp
def low_back(v):
    return v

def low_keep(v):
    return (low(v), None)

def low_pass(kept, grad):
    return (grad,)

def back_keep(v):
    return (v, None)

def back_low(kept, grad):
    return (low(grad),)
low.defvjp(low_keep, low_pass)
low_back.defvjp(back_keep, back_low)
epsilon = 1e-06
mask_fill = -1e+30

def rms_scale(values, gain_vec):
    return values * lax.rsqrt(lax.optimization_barrier(jnp.mean(values * values, axis=-1, keepdims=True)) + epsilon) * gain_vec

def high_dot(left, right):
    return jnp.dot(left, right, precision=lax.Precision.HIGHEST)

def routing_slots(expert_ids, valid, ranks, experts, capacity):
    count = ranks.shape[0]
    order = jnp.zeros((count,), jnp.int32).at[ranks].set(jnp.arange(count, dtype=jnp.int32))
    choices_hot = (expert_ids[:, :, None] == jnp.arange(experts, dtype=jnp.int32)[None, None, :]).astype(jnp.int32)
    choices_hot = choices_hot * valid[:, None, None].astype(jnp.int32)
    ordered = choices_hot[order]
    first_hot = ordered[:, 0, :]
    second_hot = ordered[:, 1, :]
    first_before = jnp.cumsum(first_hot, axis=0, dtype=jnp.int32) - first_hot
    second_before = jnp.cumsum(second_hot, axis=0, dtype=jnp.int32) - second_hot
    second_before = second_before + lax.optimization_barrier(jnp.sum(first_hot, axis=0, dtype=jnp.int32))[None, :]
    ranked_slots = jnp.stack([lax.optimization_barrier(jnp.sum(first_before * first_hot, axis=1, dtype=jnp.int32)), lax.optimization_barrier(jnp.sum(second_before * second_hot, axis=1, dtype=jnp.int32))], axis=1)
    slots = ranked_slots[ranks]
    kept = valid[:, None] & (slots < capacity)
    return (slots, kept)

def attend_group(weights, inputs):
    gain_attn, w_qkv, w_out = weights
    token_rows, length_rows = inputs
    count = length_rows.shape[0]
    normed = low(rms_scale(token_rows, gain_attn))
    projected = low(low_back(high_dot(normed, w_qkv)))
    shaped = projected.reshape(count, LEN, 3, HEADS, HEAD_DIM)
    queries = shaped[:, :, 0]
    key_rows = shaped[:, :, 1]
    value_rows = shaped[:, :, 2]
    scores = jnp.einsum('gqhd,gkhd->ghqk', queries, key_rows, precision=lax.Precision.HIGHEST) * (1.0 / math.sqrt(HEAD_DIM))
    scores = low_back(scores)
    places = jnp.arange(LEN, dtype=jnp.int32)
    allowed = (places[None, None, :] <= places[None, :, None]) & (places[None, None, :] < length_rows[:, None, None])
    scores = jnp.where(allowed[:, None], scores, mask_fill)
    weights_low = low(jax.nn.softmax(scores, axis=-1))
    mixed = jnp.einsum('ghqk,gkhd->gqhd', weights_low, value_rows, precision=lax.Precision.HIGHEST)
    mixed = low(low_back(mixed.reshape(count * LEN, HEADS * HEAD_DIM)))
    attn_out = low_back(high_dot(mixed, w_out))
    valid_rows = (places[None, :] < length_rows[:, None]).reshape(-1, 1).astype(token_rows.dtype)
    return token_rows + valid_rows * attn_out

def expert_block(inputs):
    rows_in, gate_parts, up_parts, down_parts = inputs
    total_in = low_back(rows_in)
    summed = jnp.zeros((rows_in.shape[0], D), jnp.float32)
    for part_index in range(SPLIT):
        rows_part = low_back(total_in)
        gate_pre = low_back(high_dot(rows_part, gate_parts[part_index]))
        up_pre = low_back(high_dot(rows_part, up_parts[part_index]))
        hidden_act = low(jax.nn.gelu(gate_pre) * up_pre)
        summed = summed + low(high_dot(hidden_act, down_parts[part_index]))
    return low(low_back(summed))

def reference(tokens, lengths, expert_ids, slot_order, gain_attn, w_qkv, w_out, gain_moe, w_router, w_gate, w_up, w_down, out_grad):
    places = jnp.arange(TOKENS, dtype=jnp.int32)
    valid = places % LEN < lengths[places // LEN]

    def group_slots(group_ids, group_valid, group_ranks):
        return routing_slots(group_ids, group_valid, group_ranks, EXPERTS, CAPACITY)
    slots, kept = jax.vmap(group_slots)(expert_ids.reshape(N_DP, TOK_DEV, 2), valid.reshape(N_DP, TOK_DEV), slot_order)
    slots = slots.reshape(TOKENS, 2)
    kept = kept.reshape(TOKENS, 2)
    group_of = (places // TOK_DEV)[:, None]
    buffer_rows = EXPERTS * N_DP * CAPACITY
    flat = jnp.where(kept, (expert_ids * N_DP + group_of) * CAPACITY + slots, buffer_rows).astype(jnp.int32)
    filler = jnp.full((buffer_rows + 1,), TOKENS, jnp.int32).at[flat.reshape(-1)].set(jnp.repeat(places, 2))[:buffer_rows]
    group_size = math.gcd(SEQS, max(1, 4096 // LEN))

    def forward(token_vals, gain_attn_f, w_qkv_f, w_out_f, gain_moe_f, w_router_f, w_gate_f, w_up_f, w_down_f):
        valid_f = valid.astype(token_vals.dtype)[:, None]

        def group_step(carry, inputs):
            return (carry, jax.checkpoint(attend_group)((gain_attn_f, w_qkv_f, w_out_f), inputs))
        unused_carry, hidden_groups = lax.scan(group_step, jnp.zeros((), jnp.float32), (token_vals.reshape(SEQS // group_size, group_size * LEN, D), lengths.reshape(SEQS // group_size, group_size)))
        hidden_state = hidden_groups.reshape(TOKENS, D)
        normed_moe = low(rms_scale(hidden_state, gain_moe_f))
        logits = low_back(high_dot(normed_moe, w_router_f))
        chosen = jnp.take_along_axis(logits, expert_ids, axis=1)
        gates = jax.nn.softmax(chosen, axis=1)
        padded = jnp.concatenate([normed_moe, jnp.zeros((1, D), normed_moe.dtype)], axis=0)
        expert_in = padded[filler]
        expert_out = lax.map(jax.checkpoint(expert_block), (expert_in.reshape(EXPERTS, N_DP * CAPACITY, D), w_gate_f.reshape(EXPERTS, SPLIT, D, FF_PART), w_up_f.reshape(EXPERTS, SPLIT, D, FF_PART), w_down_f.reshape(EXPERTS, SPLIT, FF_PART, D)))
        out_ext = jnp.concatenate([expert_out.reshape(buffer_rows, D), jnp.zeros((1, D), expert_out.dtype)], axis=0)
        picked = out_ext[flat]
        mixture = gates[:, 0:1] * picked[:, 0] + gates[:, 1:2] * picked[:, 1]
        return hidden_state + valid_f * mixture
    float_args = (tokens.astype(jnp.float32), gain_attn.astype(jnp.float32), w_qkv.astype(jnp.float32), w_out.astype(jnp.float32), gain_moe.astype(jnp.float32), w_router.astype(jnp.float32), w_gate.astype(jnp.float32), w_up.astype(jnp.float32), w_down.astype(jnp.float32))
    block_out, pull_back = jax.vjp(forward, *float_args)
    grads = pull_back(out_grad.astype(jnp.float32))
    return (block_out.astype(jnp.bfloat16), grads[0], grads[1], grads[2], grads[3], grads[4], grads[5], grads[6], grads[7], grads[8])
```

```python
import functools
import math

import jax
import jax.numpy as jnp
from jax import lax
from jax.experimental import pallas as pl
from jax.experimental.pallas import tpu as pltpu
from jax.sharding import PartitionSpec as P

HEADS = 16
HEAD_DIM = 64
LEN = 1024
LANES = 128
MIB = 1 << 20

epsilon = 1e-06
mask_fill = -1e30
f32 = jnp.float32
bf16 = jnp.bfloat16


def dot_nn(left, right, **kw):
    return lax.dot_general(left, right, (((1,), (0,)), ((), ())), preferred_element_type=f32, **kw)


def dot_nt(left, right, **kw):
    return lax.dot_general(left, right, (((1,), (1,)), ((), ())), preferred_element_type=f32, **kw)


def dot_tn(left, right, **kw):
    return lax.dot_general(left, right, (((0,), (0,)), ((), ())), preferred_element_type=f32, **kw)


def iota(shape, dim):
    return lax.broadcasted_iota(jnp.int32, shape, dim)


def params(mib, **kw):
    return pltpu.CompilerParams(vmem_limit_bytes=mib * MIB, **kw)


def cost(flops, nbytes, trans=0):
    return pl.CostEstimate(flops=int(flops), bytes_accessed=int(nbytes), transcendentals=int(trans))


def slot_kernel(capacity, experts, len_ref, ids_ref, rank_col_ref, rank_row_ref, col_ref, row_ref):
    count = ids_ref.shape[0]
    length = len_ref[0]
    ids = ids_ref[...]
    first, second = ids[:, 0:1], ids[:, 1:2]
    lane = iota((count, LANES), 1)
    place = iota((count, LANES), 0)
    hot0 = (lane == first) & (lane < experts)
    hot1 = (lane == second + experts) & (lane >= experts) & (lane < 2 * experts)
    valid = place < length
    hot = jnp.where((hot0 | hot1) & valid, 1.0, 0.0).astype(bf16)
    before = (rank_row_ref[...] < rank_col_ref[...]).astype(f32).astype(bf16)
    counts = dot_nn(before, hot)
    shifted = (lane == first + experts) & (lane >= experts) & (lane < 2 * experts) & valid
    totals = jnp.sum(jnp.where(shifted, 1.0, 0.0), axis=0, keepdims=True)
    slot0 = jnp.sum(jnp.where(hot0, counts, 0.0), axis=1, keepdims=True).astype(jnp.int32)
    slot1 = jnp.sum(jnp.where(hot1, counts + totals, 0.0), axis=1, keepdims=True).astype(jnp.int32)
    sentinel = experts * capacity
    ok = valid[:, 0:1]
    flat0 = jnp.where(ok & (slot0 < capacity), first * capacity + slot0, sentinel)
    flat1 = jnp.where(ok & (slot1 < capacity), second * capacity + slot1, sentinel)
    col = jnp.where(lane == 0, flat0, 0) + jnp.where(lane == 1, flat1, 0)
    col = col + jnp.where(lane == 2, first, 0) + jnp.where(lane == 3, second, 0)
    col = col + jnp.where(lane == 4, ok.astype(jnp.int32), 0)
    col_ref[...] = col
    row_ref[...] = jnp.transpose(col.astype(f32))[0:8, :].astype(jnp.int32)


def make_slots(lengths, expert_ids, slot_order, experts, capacity):
    count = expert_ids.shape[0]
    return pl.pallas_call(
        functools.partial(slot_kernel, capacity, experts),
        out_shape=(
            jax.ShapeDtypeStruct((count, LANES), jnp.int32),
            jax.ShapeDtypeStruct((8, count), jnp.int32),
        ),
        in_specs=[
            pl.BlockSpec(memory_space=pltpu.SMEM),
            pl.BlockSpec(memory_space=pltpu.VMEM),
            pl.BlockSpec(memory_space=pltpu.VMEM),
            pl.BlockSpec(memory_space=pltpu.VMEM),
        ],
        out_specs=(pl.BlockSpec(memory_space=pltpu.VMEM), pl.BlockSpec(memory_space=pltpu.VMEM)),
        compiler_params=params(40),
        cost_estimate=cost(2 * count * count * LANES, 4 * count * LANES),
        name="slots",
    )(lengths, expert_ids, slot_order.reshape(count, 1), slot_order)


def dispatch_kernel(rows, row_ref, data_ref, out_ref):
    count = data_ref.shape[0]
    slot = pl.program_id(0) * rows + iota((rows, count), 0)
    hot = (slot == row_ref[0:1, :]) | (slot == row_ref[1:2, :])
    out_ref[...] = dot_nn(jnp.where(hot, 1.0, 0.0).astype(bf16), data_ref[...]).astype(bf16)


def dispatch(row, data, slots):
    count, width = data.shape
    rows = 256
    return pl.pallas_call(
        functools.partial(dispatch_kernel, rows),
        out_shape=jax.ShapeDtypeStruct((slots, width), bf16),
        grid=(slots // rows,),
        in_specs=[
            pl.BlockSpec((8, count), lambda i: (0, 0)),
            pl.BlockSpec((count, width), lambda i: (0, 0)),
        ],
        out_specs=pl.BlockSpec((rows, width), lambda i: (i, 0)),
        compiler_params=params(40),
        cost_estimate=cost(2 * slots * count * width, 2 * (slots + count) * width),
        name="dispatch",
    )(row, data)


def dispatch_grad_kernel(rows, row_ref, data_ref, out_ref):
    count, width = data_ref.shape
    slot = pl.program_id(0) * rows + iota((rows, count), 0)
    hot0 = slot == row_ref[0:1, :]
    hot1 = slot == row_ref[1:2, :]
    both = jnp.where(hot0 | hot1, 1.0, 0.0).astype(bf16)
    out_ref[:, 0:width] = dot_nn(both, data_ref[...]).astype(bf16)
    other = jnp.where(hot0, row_ref[3:4, :], 0) + jnp.where(hot1, row_ref[2:3, :], 0)
    other = jnp.sum(other.astype(f32), axis=1, keepdims=True)
    out_ref[:, width:] = jnp.broadcast_to(other, (rows, LANES)).astype(bf16)


def dispatch_grad(row, data, slots):
    count, width = data.shape
    rows = 256
    return pl.pallas_call(
        functools.partial(dispatch_grad_kernel, rows),
        out_shape=jax.ShapeDtypeStruct((slots, width + LANES), bf16),
        grid=(slots // rows,),
        in_specs=[
            pl.BlockSpec((8, count), lambda i: (0, 0)),
            pl.BlockSpec((count, width), lambda i: (0, 0)),
        ],
        out_specs=pl.BlockSpec((rows, width + LANES), lambda i: (i, 0)),
        compiler_params=params(40),
        cost_estimate=cost(2 * slots * count * width, 2 * (slots + count) * width),
        name="dispatch_grad",
    )(row, data)


SCALE2 = math.log2(math.e) / math.sqrt(HEAD_DIM)
QB = 256


def attend_kernel(q_ref, k_ref, v_ref, mixed_ref, lse_ref):
    lane = iota((QB, LANES), 1)
    wide = jnp.concatenate([v_ref[...], jnp.ones_like(v_ref)], axis=1)
    causal = iota((QB, QB), 1) <= iota((QB, QB), 0)
    for block in range(LEN // QB):
        start, stop = block * QB, (block + 1) * QB
        query = q_ref[start:stop, :]
        halves, norms = [], []
        for head in range(2):
            mine = (lane // HEAD_DIM) == head
            scores = dot_nt(jnp.where(mine, query, jnp.zeros_like(query)), k_ref[0:stop, :])
            tail = jnp.where(causal, scores[:, start:stop], mask_fill)
            scores = tail if block == 0 else jnp.concatenate([scores[:, 0:start], tail], axis=1)
            highest = jnp.max(scores, axis=1, keepdims=True) * SCALE2
            raised = jnp.exp2(scores * SCALE2 - highest)
            out = dot_nn(raised.astype(bf16), wide[0:stop, :])
            summed = out[:, LANES:]
            halves.append(out[:, 0:LANES] / summed)
            norms.append(highest + jnp.log2(summed))
        mixed_ref[start:stop, :] = jnp.where(lane < HEAD_DIM, halves[0], halves[1]).astype(bf16)
        norm = jnp.where(lane == 0, norms[0], norms[1])
        lse_ref[0, :, start:stop] = jnp.transpose(norm)[0:8, :]


def attend(qkv):
    count, width3 = qkv.shape
    width = width3 // 3
    pairs = width // LANES
    return pl.pallas_call(
        attend_kernel,
        out_shape=(
            jax.ShapeDtypeStruct((count, width), bf16),
            jax.ShapeDtypeStruct((pairs, 8, count), f32),
        ),
        grid=(pairs,),
        in_specs=[
            pl.BlockSpec((count, LANES), lambda i: (0, i)),
            pl.BlockSpec((count, LANES), lambda i: (0, i + pairs)),
            pl.BlockSpec((count, LANES), lambda i: (0, i + 2 * pairs)),
        ],
        out_specs=(
            pl.BlockSpec((count, LANES), lambda i: (0, i)),
            pl.BlockSpec((1, 8, count), lambda i: (i, 0, 0)),
        ),
        compiler_params=params(40),
        cost_estimate=cost(2 * 4 * count * count * width, 8 * count * width, 8 * count * count),
        name="attend",
    )(qkv, qkv, qkv)


def attend_back_kernel(q_ref, k_ref, v_ref, o_ref, do_ref, lse_ref, out_ref, dk_sc, dv_sc):
    lane = iota((QB, LANES), 1)
    keep = iota((QB, QB), 0) <= iota((QB, QB), 1)
    dk_sc[...] = jnp.zeros_like(dk_sc)
    dv_sc[...] = jnp.zeros_like(dv_sc)
    sub = iota((8, LANES), 0)
    picks = jnp.where(iota((8, LANES), 1) // HEAD_DIM == sub, 1.0, 0.0)
    low = (iota((LEN, LANES), 1) // HEAD_DIM) == 0
    key = k_ref[...]
    none = jnp.zeros_like(key)
    keys = (jnp.where(low, key, none), jnp.where(low, none, key))
    for block in range(LEN // QB):
        start, stop = block * QB, (block + 1) * QB
        query = q_ref[start:stop, :]
        d_out = do_ref[start:stop, :]
        product = d_out.astype(f32) * o_ref[start:stop, :].astype(f32)
        delta = dot_nt(picks, product, precision=lax.Precision.HIGHEST)
        d_query = jnp.zeros((QB, LANES), f32)
        for head in range(2):
            mine = (lane // HEAD_DIM) == head
            query_one = jnp.where(mine, query, jnp.zeros_like(query))
            d_one = jnp.where(mine, d_out, jnp.zeros_like(d_out))
            scores = dot_nt(k_ref[0:stop, :], query_one)
            tail = jnp.where(keep, scores[start:stop, :], mask_fill)
            scores = tail if block == 0 else jnp.concatenate([scores[0:start, :], tail], axis=0)
            probs = jnp.exp2(scores * SCALE2 - lse_ref[0, head : head + 1, start:stop])
            d_probs = dot_nt(v_ref[0:stop, :], d_one)
            d_scores = (probs * (d_probs - delta[head : head + 1, :])).astype(bf16)
            dv_sc[0:stop, :] += dot_nn(probs.astype(bf16), d_one)
            dk_sc[0:stop, :] += dot_nn(d_scores, query_one)
            d_query = d_query + dot_tn(d_scores, keys[head][0:stop, :])
        out_ref[0, start:stop, :] = (d_query * (1.0 / math.sqrt(HEAD_DIM))).astype(bf16)
    out_ref[1, :, :] = (dk_sc[...] * (1.0 / math.sqrt(HEAD_DIM))).astype(bf16)
    out_ref[2, :, :] = dv_sc[...].astype(bf16)


def attend_back(qkv, mixed, d_mixed, lse):
    count, width = mixed.shape
    pairs = width // LANES
    return pl.pallas_call(
        attend_back_kernel,
        out_shape=jax.ShapeDtypeStruct((3, count, width), bf16),
        grid=(pairs,),
        in_specs=[
            pl.BlockSpec((count, LANES), lambda i: (0, i)),
            pl.BlockSpec((count, LANES), lambda i: (0, i + pairs)),
            pl.BlockSpec((count, LANES), lambda i: (0, i + 2 * pairs)),
            pl.BlockSpec((count, LANES), lambda i: (0, i)),
            pl.BlockSpec((count, LANES), lambda i: (0, i)),
            pl.BlockSpec((1, 8, count), lambda i: (i, 0, 0)),
        ],
        out_specs=pl.BlockSpec((3, count, LANES), lambda i: (0, 0, i)),
        scratch_shapes=[pltpu.VMEM((count, LANES), f32), pltpu.VMEM((count, LANES), f32)],
        compiler_params=params(40),
        cost_estimate=cost(5 * 4 * count * count * width, 16 * count * width, 8 * count * count),
        name="attend_back",
    )(qkv, qkv, qkv, mixed, d_mixed, lse)


def middle_kernel(experts, mixed_ref, w_out_ref, tok_ref, gain_ref, wr_ref, col_ref, h_ref, low_ref, gate_ref):
    rows = mixed_ref.shape[0]
    col = col_ref[...]
    first, second, valid = col[:, 2:3], col[:, 3:4], col[:, 4:5].astype(f32)
    attn = dot_nn(mixed_ref[...], w_out_ref[...])
    hidden = tok_ref[...].astype(f32) + valid * attn
    h_ref[...] = hidden
    inverse = lax.rsqrt(jnp.mean(hidden * hidden, axis=1, keepdims=True) + epsilon)
    low = (hidden * inverse * gain_ref[...]).astype(bf16)
    low_ref[...] = low
    logits = dot_nn(low, wr_ref[...])
    lane = iota((rows, LANES), 1)
    own = jnp.sum(jnp.where(lane == first, logits, 0.0), axis=1, keepdims=True)
    alt = jnp.sum(jnp.where(lane == second, logits, 0.0), axis=1, keepdims=True)
    gate0 = 1.0 / (1.0 + jnp.exp(alt - own))
    gate1 = 1.0 / (1.0 + jnp.exp(own - alt))
    gate_ref[...] = jnp.where(lane == 0, gate0, 0.0) + jnp.where(lane == 1, gate1, 0.0)


def middle(mixed, w_out, tokens, gain, wr, col, experts):
    count, width = mixed.shape
    rows = 256
    whole = lambda i: (0, 0)
    part = lambda i: (i, 0)
    return pl.pallas_call(
        functools.partial(middle_kernel, experts),
        out_shape=(
            jax.ShapeDtypeStruct((count, width), f32),
            jax.ShapeDtypeStruct((count, width), bf16),
            jax.ShapeDtypeStruct((count, LANES), f32),
        ),
        grid=(count // rows,),
        in_specs=[
            pl.BlockSpec((rows, width), part),
            pl.BlockSpec((width, width), whole),
            pl.BlockSpec((rows, width), part),
            pl.BlockSpec((1, width), whole),
            pl.BlockSpec((width, LANES), whole),
            pl.BlockSpec((rows, LANES), part),
        ],
        out_specs=(
            pl.BlockSpec((rows, width), part),
            pl.BlockSpec((rows, width), part),
            pl.BlockSpec((rows, LANES), part),
        ),
        compiler_params=params(40),
        cost_estimate=cost(2 * count * width * width, 12 * count * width),
        name="middle",
    )(mixed, w_out, tokens, gain.reshape(1, width), wr, col)


GELU_C = math.sqrt(2.0 / math.pi)


def expert_kernel(
    split, x_ref, g_ref, wg_ref, wu_ref, wd_ref, wr_ref, act_ref, dgp_ref, dup_ref, de_ref, part_ref, din_ref
):
    rows, width = x_ref.shape
    me = lax.axis_index("dp")
    expert, part = me // split, lax.rem(me, split)
    x = x_ref[...]
    lane = iota((rows, LANES), 1)
    logits = dot_nn(x, wr_ref[...])
    own = jnp.sum(jnp.where(lane == expert, logits, 0.0), axis=1, keepdims=True)
    other = g_ref[:, width:].astype(f32).astype(jnp.int32)
    alt = jnp.sum(jnp.where(lane == other, logits, 0.0), axis=1, keepdims=True)
    gate = 1.0 / (1.0 + jnp.exp(alt - own))
    d_rows = (g_ref[:, 0:width].astype(f32) * gate).astype(bf16)
    de_ref[...] = d_rows
    pre = dot_nn(x, wg_ref[...])
    up = dot_nn(x, wu_ref[...])
    d_hidden = dot_nt(d_rows, wd_ref[...])
    square = pre * pre
    bent = jnp.tanh(GELU_C * pre * (1.0 + 0.044715 * square))
    half = 0.5 * (1.0 + bent)
    gelu = pre * half
    slope = half + 0.5 * pre * (1.0 - bent * bent) * (GELU_C * (1.0 + 3 * 0.044715 * square))
    act = (gelu * up).astype(bf16)
    act_ref[...] = act
    dgp = (d_hidden * up * slope).astype(bf16)
    dup = (d_hidden * gelu).astype(bf16)
    dgp_ref[...] = dgp
    dup_ref[...] = dup
    pull = jnp.sum(act.astype(f32) * d_hidden, axis=1, keepdims=True)
    pull_high = pull.astype(bf16)
    pull_low = (pull - pull_high.astype(f32)).astype(bf16)
    part_ref[...] = dot_nn(act, wd_ref[...]).astype(bf16)
    din_ref[:, 0:width] = (dot_nt(dgp, wg_ref[...]) + dot_nt(dup, wu_ref[...])).astype(bf16)
    extra = jnp.where(lane == 2 * part, pull_high.astype(f32), 0.0)
    extra = extra + jnp.where(lane == 2 * part + 1, pull_low.astype(f32), 0.0)
    din_ref[:, width:] = extra.astype(bf16)


def expert_pass(x, g, wg, wu, wd, wr, split):
    count, width = x.shape
    ff = wg.shape[1]
    rows = 256
    whole = lambda i: (0, 0)
    part = lambda i: (i, 0)
    once = dict(pipeline_mode=pl.Buffered(1))
    return pl.pallas_call(
        functools.partial(expert_kernel, split),
        out_shape=(
            jax.ShapeDtypeStruct((count, ff), bf16),
            jax.ShapeDtypeStruct((count, ff), bf16),
            jax.ShapeDtypeStruct((count, ff), bf16),
            jax.ShapeDtypeStruct((count, width), bf16),
            jax.ShapeDtypeStruct((count, width), bf16),
            jax.ShapeDtypeStruct((count, width + LANES), bf16),
        ),
        grid=(count // rows,),
        in_specs=[
            pl.BlockSpec((rows, width), part),
            pl.BlockSpec((rows, width + LANES), part),
            pl.BlockSpec((width, ff), whole, **once),
            pl.BlockSpec((width, ff), whole, **once),
            pl.BlockSpec((ff, width), whole, **once),
            pl.BlockSpec((width, LANES), whole),
        ],
        out_specs=(
            pl.BlockSpec((rows, ff), part),
            pl.BlockSpec((rows, ff), part),
            pl.BlockSpec((rows, ff), part),
            pl.BlockSpec((rows, width), part),
            pl.BlockSpec((rows, width), part),
            pl.BlockSpec((rows, width + LANES), part),
        ),
        compiler_params=params(56),
        cost_estimate=cost(12 * count * width * ff, 2 * count * (3 * ff + 5 * width), count * ff),
        name="experts",
    )(x, g, wg, wu, wd, wr)


def hot_rows(col, k, rows, slots):
    return jnp.where(iota((rows, slots), 1) == col[:, k : k + 1], 1.0, 0.0).astype(bf16)


def state_kernel(
    col_ref, gate_ref, din_ref, h_ref, og_ref, gain_ref, wr_ref, dstate_ref, dattn_ref, dlog_ref, gterm_ref
):
    rows, width = h_ref.shape
    slots = din_ref.shape[0]
    col = col_ref[...]
    valid = col[:, 4:5].astype(f32)
    hot0, hot1 = hot_rows(col, 0, rows, slots), hot_rows(col, 1, rows, slots)
    pulls = din_ref[:, width:]
    pull0 = jnp.sum(dot_nn(hot0, pulls), axis=1, keepdims=True)
    pull1 = jnp.sum(dot_nn(hot1, pulls), axis=1, keepdims=True)
    gathered = dot_nn(hot0 + hot1, din_ref[:, 0:width])
    gate0, gate1 = gate_ref[:, 0:1], gate_ref[:, 1:2]
    total = pull0 + pull1
    lane = iota((rows, LANES), 1)
    d_log = jnp.where(lane == col[:, 2:3], pull0 - gate0 * total, 0.0)
    d_log = d_log + jnp.where(lane == col[:, 3:4], pull1 - gate1 * total, 0.0)
    d_log = d_log.astype(bf16)
    dlog_ref[...] = d_log
    d_moe = gathered + dot_nt(d_log, wr_ref[...])
    hidden = h_ref[...]
    inverse = lax.rsqrt(jnp.mean(hidden * hidden, axis=1, keepdims=True) + epsilon)
    normal = hidden * inverse
    scaled = gain_ref[...] * d_moe
    share = jnp.mean(normal * scaled, axis=1, keepdims=True)
    d_state = og_ref[...].astype(f32) + inverse * (scaled - normal * share)
    dstate_ref[...] = d_state
    dattn_ref[...] = (valid * d_state).astype(bf16)
    term = jnp.sum((normal * d_moe).reshape(rows // 8, 8, width), axis=0)

    @pl.when(pl.program_id(0) == 0)
    def _():
        gterm_ref[...] = jnp.zeros_like(gterm_ref)

    gterm_ref[...] += term


def state_back(col, gates, din, hidden, out_grad, gain, wr):
    count, width = hidden.shape
    slots = din.shape[0]
    rows = 256
    whole = lambda i: (0, 0)
    part = lambda i: (i, 0)
    return pl.pallas_call(
        state_kernel,
        out_shape=(
            jax.ShapeDtypeStruct((count, width), f32),
            jax.ShapeDtypeStruct((count, width), bf16),
            jax.ShapeDtypeStruct((count, LANES), bf16),
            jax.ShapeDtypeStruct((8, width), f32),
        ),
        grid=(count // rows,),
        in_specs=[
            pl.BlockSpec((rows, LANES), part),
            pl.BlockSpec((rows, LANES), part),
            pl.BlockSpec((slots, width + LANES), whole),
            pl.BlockSpec((rows, width), part),
            pl.BlockSpec((rows, width), part),
            pl.BlockSpec((1, width), whole),
            pl.BlockSpec((width, LANES), whole),
        ],
        out_specs=(
            pl.BlockSpec((rows, width), part),
            pl.BlockSpec((rows, width), part),
            pl.BlockSpec((rows, LANES), part),
            pl.BlockSpec((8, width), whole),
        ),
        compiler_params=params(48),
        cost_estimate=cost(2 * slots * count * width, 14 * count * width),
        name="state_back",
    )(col, gates, din, hidden, out_grad, gain.reshape(1, width), wr)


def block_out_kernel(col_ref, gate_ref, rows_ref, h_ref, out_ref):
    rows, width = h_ref.shape
    slots = rows_ref.shape[0]
    col = col_ref[...]
    pick0 = dot_nn(hot_rows(col, 0, rows, slots), rows_ref[...])
    pick1 = dot_nn(hot_rows(col, 1, rows, slots), rows_ref[...])
    out_ref[...] = (h_ref[...] + gate_ref[:, 0:1] * pick0 + gate_ref[:, 1:2] * pick1).astype(bf16)


def make_block_out(col, gates, slot_rows, hidden):
    count, width = hidden.shape
    slots = slot_rows.shape[0]
    rows = 256
    whole = lambda i: (0, 0)
    part = lambda i: (i, 0)
    return pl.pallas_call(
        block_out_kernel,
        out_shape=jax.ShapeDtypeStruct((count, width), bf16),
        grid=(count // rows,),
        in_specs=[
            pl.BlockSpec((rows, LANES), part),
            pl.BlockSpec((rows, LANES), part),
            pl.BlockSpec((slots, width), whole),
            pl.BlockSpec((rows, width), part),
        ],
        out_specs=pl.BlockSpec((rows, width), part),
        compiler_params=params(40),
        cost_estimate=cost(4 * slots * count * width, 9 * count * width),
        name="block_out",
    )(col, gates, slot_rows, hidden)


def input_kernel(d_ref, w_ref, tok_ref, gain_ref, dstate_ref, grad_ref, gterm_ref):
    rows, width = tok_ref.shape
    d_normed = dot_nt(d_ref[0], w_ref[:, 0:width])
    for i in range(1, 3):
        d_normed = d_normed + dot_nt(d_ref[i], w_ref[:, i * width : (i + 1) * width])
    values = tok_ref[...].astype(f32)
    inverse = lax.rsqrt(jnp.mean(values * values, axis=1, keepdims=True) + epsilon)
    normal = values * inverse
    scaled = gain_ref[...] * d_normed
    share = jnp.mean(normal * scaled, axis=1, keepdims=True)
    grad_ref[...] = dstate_ref[...] + inverse * (scaled - normal * share)
    term = jnp.sum((normal * d_normed).reshape(rows // 8, 8, width), axis=0)

    @pl.when(pl.program_id(0) == 0)
    def _():
        gterm_ref[...] = jnp.zeros_like(gterm_ref)

    gterm_ref[...] += term


def input_back(d_qkv, w_qkv, tokens, gain, d_state):
    count, width = tokens.shape
    rows = 256
    whole = lambda i: (0, 0)
    part = lambda i: (i, 0)
    return pl.pallas_call(
        input_kernel,
        out_shape=(
            jax.ShapeDtypeStruct((count, width), f32),
            jax.ShapeDtypeStruct((8, width), f32),
        ),
        grid=(count // rows,),
        in_specs=[
            pl.BlockSpec((3, rows, width), lambda i: (0, i, 0)),
            pl.BlockSpec((width, 3 * width), whole),
            pl.BlockSpec((rows, width), part),
            pl.BlockSpec((1, width), whole),
            pl.BlockSpec((rows, width), part),
        ],
        out_specs=(pl.BlockSpec((rows, width), part), pl.BlockSpec((8, width), whole)),
        compiler_params=params(48),
        cost_estimate=cost(6 * count * width * width, 22 * count * width),
        name="input_back",
    )(d_qkv, w_qkv, tokens, gain.reshape(1, width), d_state)


def shards(
    tokens,
    lengths,
    expert_ids,
    slot_order,
    gain_attn,
    w_qkv,
    w_out,
    gain_moe,
    w_router,
    w_gate,
    w_up,
    w_down,
    out_grad,
):
    tok_dev, width = tokens.shape
    n_dev = lax.axis_size("dp")
    experts = w_router.shape[1]
    split = n_dev // experts
    capacity = split * (5 * tok_dev // (4 * n_dev))
    slots = experts * capacity
    me = lax.axis_index("dp")
    part = lax.rem(me, split)
    same_part = [[e * split + p for e in range(experts)] for p in range(split)]
    same_expert = [[e * split + p for p in range(split)] for e in range(experts)]
    swap = [(d, d ^ 1) for d in range(n_dev)]

    def across(blocks):
        return lax.all_to_all(blocks, "dp", 0, 0, axis_index_groups=same_part, tiled=True)

    def share(rows):
        if split == 2:
            return jnp.concatenate([rows, lax.ppermute(rows, "dp", swap)], axis=0)
        return lax.all_gather(rows, "dp", axis_index_groups=same_expert, tiled=True)

    def settle(pieces):
        if split == 2:
            theirs = lax.ppermute(pieces[1], "dp", swap)
            return (pieces[0].astype(f32) + theirs.astype(f32)).astype(bf16)
        got = lax.all_to_all(pieces, "dp", 0, 0, axis_index_groups=same_expert, tiled=True)
        return jnp.sum(got.astype(f32), axis=0).astype(bf16)

    def send_in(rows):
        return share(across(rows.reshape(experts, capacity, -1)).reshape(slots, -1))

    def send_back(rows):
        summed = settle(rows.reshape(split, slots, -1))
        return across(summed.reshape(experts, capacity, -1)).reshape(slots, -1)

    def reduce_rows(term):
        pieces = term.reshape(experts, split, -1, term.shape[-1])
        if split == 2:
            mine = lax.dynamic_index_in_dim(pieces, part, 1, keepdims=False)
            theirs = lax.dynamic_index_in_dim(pieces, 1 - part, 1, keepdims=False)
            theirs = lax.ppermute(theirs.astype(bf16), "dp", swap)
            summed = (mine + theirs.astype(f32)).astype(bf16)
        else:
            pieces = jnp.moveaxis(pieces, 1, 0).astype(bf16)
            got = lax.all_to_all(pieces, "dp", 0, 0, axis_index_groups=same_expert, tiled=True)
            summed = jnp.sum(got.astype(f32), axis=0).astype(bf16)
        return jnp.sum(across(summed).astype(f32), axis=0)

    wr = jnp.pad(w_router, ((0, 0), (0, LANES - experts)))
    col, row = make_slots(lengths, expert_ids, slot_order, experts, capacity)
    grad_in = send_in(dispatch_grad(row, out_grad, slots))

    token_vals = tokens.astype(f32)
    inverse_attn = lax.rsqrt(jnp.mean(token_vals * token_vals, axis=-1, keepdims=True) + epsilon)
    normed_low = (token_vals * inverse_attn * gain_attn).astype(bf16)
    qkv = jnp.dot(normed_low, w_qkv, preferred_element_type=f32).astype(bf16)
    mixed, lse = attend(qkv)
    hidden, moe_low, gates = middle(mixed, w_out, tokens, gain_moe, wr, col, experts)

    rows_in = send_in(dispatch(row, moe_low, slots))
    act, d_pre, d_up, d_rows, partial_out, d_in = expert_pass(
        rows_in, grad_in, w_gate[0], w_up[0], w_down[0], wr, split
    )
    d_in_back = send_back(d_in)
    slot_out = send_back(partial_out)

    d_state, d_attn, d_log, gain_moe_rows = state_back(
        col, gates, d_in_back, hidden, out_grad, gain_moe, wr
    )
    out_term = dot_tn(mixed, d_attn)
    router_term = dot_tn(moe_low, d_log)
    gain_moe_term = jnp.sum(gain_moe_rows, axis=0)
    d_mixed = dot_nt(d_attn, w_out).astype(bf16)
    d_qkv = attend_back(qkv, mixed, d_mixed, lse)
    tokens_grad, gain_attn_rows = input_back(d_qkv, w_qkv, tokens, gain_attn, d_state)
    qkv_term = jnp.concatenate([dot_tn(normed_low, d_qkv[i]) for i in range(3)], axis=1)
    gain_attn_term = jnp.sum(gain_attn_rows, axis=0)

    lane = jnp.arange(LANES, dtype=jnp.int32)[None, :]
    extra = jnp.where(lane == experts, gain_moe_term[:, None], router_term)
    early = reduce_rows(jnp.concatenate([out_term, extra], axis=1))
    late_extra = jnp.where(lane == 0, gain_attn_term[:, None], 0.0)
    late = reduce_rows(jnp.concatenate([qkv_term, late_extra], axis=1))

    down_grad = dot_tn(act, d_rows)
    gate_grad = dot_tn(rows_in, d_pre)
    up_grad = dot_tn(rows_in, d_up)
    block_out = make_block_out(col, gates, slot_out, hidden)
    return (
        block_out,
        tokens_grad,
        late[:, 3 * width],
        late[:, 0 : 3 * width],
        early[:, 0:width],
        early[:, width + experts],
        early[:, width : width + experts],
        gate_grad[None],
        up_grad[None],
        down_grad[None],
    )


def solution(mesh):
    rows, one = P("dp", None), P("dp")
    cube = P("dp", None, None)
    return jax.shard_map(
        shards,
        mesh=mesh,
        in_specs=(rows, one, rows, rows, P(), P(), P(), P(), P(), cube, cube, cube, rows),
        out_specs=(rows, rows, one, rows, rows, one, rows, cube, cube, cube),
        check_vma=False,
    )
```

```python
import functools
import math

import jax
import jax.numpy as jnp
from jax import lax
from jax.experimental import pallas as pl
from jax.experimental.pallas import tpu as pltpu
from jax.sharding import PartitionSpec as P

HEADS = 16
HEAD_DIM = 64
LEN = 1024
LANES = 128
MIB = 1 << 20

epsilon = 1e-06
mask_fill = -1e30
f32 = jnp.float32
bf16 = jnp.bfloat16


def dot_nn(left, right, **kw):
    return lax.dot_general(left, right, (((1,), (0,)), ((), ())), preferred_element_type=f32, **kw)


def dot_nt(left, right, **kw):
    return lax.dot_general(left, right, (((1,), (1,)), ((), ())), preferred_element_type=f32, **kw)


def dot_tn(left, right, **kw):
    return lax.dot_general(left, right, (((0,), (0,)), ((), ())), preferred_element_type=f32, **kw)


def iota(shape, dim):
    return lax.broadcasted_iota(jnp.int32, shape, dim)


def params(mib, **kw):
    return pltpu.CompilerParams(vmem_limit_bytes=mib * MIB, **kw)


def cost(flops, nbytes, trans=0):
    return pl.CostEstimate(flops=int(flops), bytes_accessed=int(nbytes), transcendentals=int(trans))


def slot_kernel(capacity, experts, len_ref, ids_ref, rank_col_ref, rank_row_ref, col_ref, row_ref):
    count = ids_ref.shape[0]
    length = len_ref[0]
    ids = ids_ref[...]
    first, second = ids[:, 0:1], ids[:, 1:2]
    lane = iota((count, LANES), 1)
    place = iota((count, LANES), 0)
    hot0 = (lane == first) & (lane < experts)
    hot1 = (lane == second + experts) & (lane >= experts) & (lane < 2 * experts)
    valid = place < length
    hot = jnp.where((hot0 | hot1) & valid, 1.0, 0.0).astype(bf16)
    before = (rank_row_ref[...] < rank_col_ref[...]).astype(f32).astype(bf16)
    counts = dot_nn(before, hot)
    shifted = (lane == first + experts) & (lane >= experts) & (lane < 2 * experts) & valid
    totals = jnp.sum(jnp.where(shifted, 1.0, 0.0), axis=0, keepdims=True)
    slot0 = jnp.sum(jnp.where(hot0, counts, 0.0), axis=1, keepdims=True).astype(jnp.int32)
    slot1 = jnp.sum(jnp.where(hot1, counts + totals, 0.0), axis=1, keepdims=True).astype(jnp.int32)
    sentinel = experts * capacity
    ok = valid[:, 0:1]
    flat0 = jnp.where(ok & (slot0 < capacity), first * capacity + slot0, sentinel)
    flat1 = jnp.where(ok & (slot1 < capacity), second * capacity + slot1, sentinel)
    col = jnp.where(lane == 0, flat0, 0) + jnp.where(lane == 1, flat1, 0)
    col = col + jnp.where(lane == 2, first, 0) + jnp.where(lane == 3, second, 0)
    col = col + jnp.where(lane == 4, ok.astype(jnp.int32), 0)
    col_ref[...] = col
    row_ref[...] = jnp.transpose(col.astype(f32))[0:8, :].astype(jnp.int32)


def make_slots(lengths, expert_ids, slot_order, experts, capacity):
    count = expert_ids.shape[0]
    return pl.pallas_call(
        functools.partial(slot_kernel, capacity, experts),
        out_shape=(
            jax.ShapeDtypeStruct((count, LANES), jnp.int32),
            jax.ShapeDtypeStruct((8, count), jnp.int32),
        ),
        in_specs=[
            pl.BlockSpec(memory_space=pltpu.SMEM),
            pl.BlockSpec(memory_space=pltpu.VMEM),
            pl.BlockSpec(memory_space=pltpu.VMEM),
            pl.BlockSpec(memory_space=pltpu.VMEM),
        ],
        out_specs=(pl.BlockSpec(memory_space=pltpu.VMEM), pl.BlockSpec(memory_space=pltpu.VMEM)),
        compiler_params=params(40),
        cost_estimate=cost(2 * count * count * LANES, 4 * count * LANES),
        name="slots",
    )(lengths, expert_ids, slot_order.reshape(count, 1), slot_order)


def dispatch_kernel(rows, row_ref, data_ref, out_ref):
    count = data_ref.shape[0]
    slot = pl.program_id(0) * rows + iota((rows, count), 0)
    hot = (slot == row_ref[0:1, :]) | (slot == row_ref[1:2, :])
    out_ref[...] = dot_nn(jnp.where(hot, 1.0, 0.0).astype(bf16), data_ref[...]).astype(bf16)


def dispatch(row, data, slots):
    count, width = data.shape
    rows = 256
    return pl.pallas_call(
        functools.partial(dispatch_kernel, rows),
        out_shape=jax.ShapeDtypeStruct((slots, width), bf16),
        grid=(slots // rows,),
        in_specs=[
            pl.BlockSpec((8, count), lambda i: (0, 0)),
            pl.BlockSpec((count, width), lambda i: (0, 0)),
        ],
        out_specs=pl.BlockSpec((rows, width), lambda i: (i, 0)),
        compiler_params=params(40),
        cost_estimate=cost(2 * slots * count * width, 2 * (slots + count) * width),
        name="dispatch",
    )(row, data)


def dispatch_grad_kernel(rows, row_ref, data_ref, out_ref):
    count, width = data_ref.shape
    slot = pl.program_id(0) * rows + iota((rows, count), 0)
    hot0 = slot == row_ref[0:1, :]
    hot1 = slot == row_ref[1:2, :]
    both = jnp.where(hot0 | hot1, 1.0, 0.0).astype(bf16)
    out_ref[:, 0:width] = dot_nn(both, data_ref[...]).astype(bf16)
    other = jnp.where(hot0, row_ref[3:4, :], 0) + jnp.where(hot1, row_ref[2:3, :], 0)
    other = jnp.sum(other.astype(f32), axis=1, keepdims=True)
    out_ref[:, width:] = jnp.broadcast_to(other, (rows, LANES)).astype(bf16)


def dispatch_grad(row, data, slots):
    count, width = data.shape
    rows = 256
    return pl.pallas_call(
        functools.partial(dispatch_grad_kernel, rows),
        out_shape=jax.ShapeDtypeStruct((slots, width + LANES), bf16),
        grid=(slots // rows,),
        in_specs=[
            pl.BlockSpec((8, count), lambda i: (0, 0)),
            pl.BlockSpec((count, width), lambda i: (0, 0)),
        ],
        out_specs=pl.BlockSpec((rows, width + LANES), lambda i: (i, 0)),
        compiler_params=params(40),
        cost_estimate=cost(2 * slots * count * width, 2 * (slots + count) * width),
        name="dispatch_grad",
    )(row, data)


MESH = pl.DeviceIdType.MESH


def flip(chip, bits, experts):
    out, b = chip, 1
    while b < experts:
        if isinstance(bits, int):
            out = out + (bits // b % 2) * (b - 2 * b * lax.rem(lax.div(chip, b), 2))
        else:
            mine, theirs = lax.rem(lax.div(chip, b), 2), lax.rem(lax.div(bits, b), 2)
            out = out + b * theirs * (1 - 2 * mine)
        b *= 2
    return out


def greet(peers):
    barrier = pltpu.get_barrier_semaphore()
    for peer in peers:
        pl.semaphore_signal(barrier, inc=1, device_id=(peer,), device_id_type=MESH)
    pl.semaphore_wait(barrier, len(peers))


def exchange_copies(src, dst, send_sem, recv_sem, local_sem):
    experts = src.shape[0]
    me = lax.axis_index("dp")
    chip, core = lax.div(me, 2), lax.rem(me, 2)
    copies = [pltpu.make_async_copy(src.at[chip], dst.at[chip], local_sem)]
    peers = []
    half = experts // 2
    for place in range(1, experts):
        step = half + place // 2 if place % 2 else place // 2
        peer = flip(chip, step, experts)
        peers.append(2 * peer + core)
        copies.append(
            pltpu.make_async_remote_copy(
                src_ref=src.at[peer],
                dst_ref=dst.at[chip],
                send_sem=send_sem.at[step],
                recv_sem=recv_sem.at[step],
                device_id=(2 * peer + core,),
                device_id_type=MESH,
            )
        )
    return peers, copies


def exchange_sems(experts):
    return [
        pltpu.SemaphoreType.DMA((experts,)),
        pltpu.SemaphoreType.DMA((experts,)),
        pltpu.SemaphoreType.DMA,
    ]


def riding(body, n_in, n_out):
    def kernel(*refs):
        ins, src = refs[:n_in], refs[n_in]
        outs, dst = refs[n_in + 1 : n_in + 1 + n_out], refs[n_in + 1 + n_out]
        rest, sems = refs[n_in + n_out + 2 : -3], refs[-3:]
        peers, copies = exchange_copies(src, dst, *sems)

        @pl.when(pl.program_id(0) == 0)
        def _():
            greet(peers)
            for copy in copies:
                copy.start()

        body(*ins, *outs, *rest)

        @pl.when(pl.program_id(0) == pl.num_programs(0) - 1)
        def _():
            for copy in copies:
                copy.wait()

    return kernel


SCALE2 = math.log2(math.e) / math.sqrt(HEAD_DIM)
QB = 256


def attend_kernel(q_ref, k_ref, v_ref, mixed_ref, lse_ref):
    lane = iota((QB, LANES), 1)
    wide = jnp.concatenate([v_ref[...], jnp.ones_like(v_ref)], axis=1)
    causal = iota((QB, QB), 1) <= iota((QB, QB), 0)
    for block in range(LEN // QB):
        start, stop = block * QB, (block + 1) * QB
        query = q_ref[start:stop, :]
        halves, norms = [], []
        for head in range(2):
            mine = (lane // HEAD_DIM) == head
            scores = dot_nt(jnp.where(mine, query, jnp.zeros_like(query)), k_ref[0:stop, :])
            tail = jnp.where(causal, scores[:, start:stop], mask_fill)
            scores = tail if block == 0 else jnp.concatenate([scores[:, 0:start], tail], axis=1)
            highest = jnp.max(scores, axis=1, keepdims=True) * SCALE2
            raised = jnp.exp2(scores * SCALE2 - highest)
            out = dot_nn(raised.astype(bf16), wide[0:stop, :])
            summed = out[:, LANES:]
            halves.append(out[:, 0:LANES] / summed)
            norms.append(highest + jnp.log2(summed))
        mixed_ref[start:stop, :] = jnp.where(lane < HEAD_DIM, halves[0], halves[1]).astype(bf16)
        norm = jnp.where(lane == 0, norms[0], norms[1])
        lse_ref[0, :, start:stop] = jnp.transpose(norm)[0:8, :]


def attend(qkv, blocks=None):
    count, width3 = qkv.shape
    width = width3 // 3
    pairs = width // LANES
    in_specs = [
        pl.BlockSpec((count, LANES), lambda i: (0, i)),
        pl.BlockSpec((count, LANES), lambda i: (0, i + pairs)),
        pl.BlockSpec((count, LANES), lambda i: (0, i + 2 * pairs)),
    ]
    out_specs = [
        pl.BlockSpec((count, LANES), lambda i: (0, i)),
        pl.BlockSpec((1, 8, count), lambda i: (i, 0, 0)),
    ]
    out_shape = [
        jax.ShapeDtypeStruct((count, width), bf16),
        jax.ShapeDtypeStruct((pairs, 8, count), f32),
    ]
    body, args, scratch, extra = attend_kernel, [qkv, qkv, qkv], [], {}
    if blocks is not None:
        body = riding(attend_kernel, len(in_specs), len(out_specs))
        in_specs.append(pl.BlockSpec(memory_space=pl.ANY))
        out_specs.append(pl.BlockSpec(memory_space=pl.ANY))
        out_shape.append(jax.ShapeDtypeStruct(blocks.shape, blocks.dtype))
        args.append(blocks)
        scratch = exchange_sems(blocks.shape[0])
        extra = dict(collective_id=0, has_side_effects=True)
    return pl.pallas_call(
        body,
        out_shape=out_shape,
        grid=(pairs,),
        in_specs=in_specs,
        out_specs=out_specs,
        scratch_shapes=scratch,
        compiler_params=params(40, **extra),
        cost_estimate=cost(2 * 4 * count * count * width, 8 * count * width, 8 * count * count),
        name="attend",
    )(*args)


def attend_back_kernel(q_ref, k_ref, v_ref, o_ref, do_ref, lse_ref, out_ref, dk_sc, dv_sc):
    lane = iota((QB, LANES), 1)
    keep = iota((QB, QB), 0) <= iota((QB, QB), 1)
    dk_sc[...] = jnp.zeros_like(dk_sc)
    dv_sc[...] = jnp.zeros_like(dv_sc)
    sub = iota((8, LANES), 0)
    picks = jnp.where(iota((8, LANES), 1) // HEAD_DIM == sub, 1.0, 0.0)
    low = (iota((LEN, LANES), 1) // HEAD_DIM) == 0
    key = k_ref[...]
    none = jnp.zeros_like(key)
    keys = (jnp.where(low, key, none), jnp.where(low, none, key))
    for block in range(LEN // QB):
        start, stop = block * QB, (block + 1) * QB
        query = q_ref[start:stop, :]
        d_out = do_ref[start:stop, :]
        product = d_out.astype(f32) * o_ref[start:stop, :].astype(f32)
        delta = dot_nt(picks, product, precision=lax.Precision.HIGHEST)
        d_query = jnp.zeros((QB, LANES), f32)
        for head in range(2):
            mine = (lane // HEAD_DIM) == head
            query_one = jnp.where(mine, query, jnp.zeros_like(query))
            d_one = jnp.where(mine, d_out, jnp.zeros_like(d_out))
            scores = dot_nt(k_ref[0:stop, :], query_one)
            tail = jnp.where(keep, scores[start:stop, :], mask_fill)
            scores = tail if block == 0 else jnp.concatenate([scores[0:start, :], tail], axis=0)
            probs = jnp.exp2(scores * SCALE2 - lse_ref[0, head : head + 1, start:stop])
            d_probs = dot_nt(v_ref[0:stop, :], d_one)
            d_scores = (probs * (d_probs - delta[head : head + 1, :])).astype(bf16)
            dv_sc[0:stop, :] += dot_nn(probs.astype(bf16), d_one)
            dk_sc[0:stop, :] += dot_nn(d_scores, query_one)
            d_query = d_query + dot_tn(d_scores, keys[head][0:stop, :])
        out_ref[0, start:stop, :] = (d_query * (1.0 / math.sqrt(HEAD_DIM))).astype(bf16)
    out_ref[1, :, :] = (dk_sc[...] * (1.0 / math.sqrt(HEAD_DIM))).astype(bf16)
    out_ref[2, :, :] = dv_sc[...].astype(bf16)


def attend_back(qkv, mixed, d_mixed, lse, blocks=None):
    count, width = mixed.shape
    pairs = width // LANES
    in_specs = [
        pl.BlockSpec((count, LANES), lambda i: (0, i)),
        pl.BlockSpec((count, LANES), lambda i: (0, i + pairs)),
        pl.BlockSpec((count, LANES), lambda i: (0, i + 2 * pairs)),
        pl.BlockSpec((count, LANES), lambda i: (0, i)),
        pl.BlockSpec((count, LANES), lambda i: (0, i)),
        pl.BlockSpec((1, 8, count), lambda i: (i, 0, 0)),
    ]
    out_specs = [pl.BlockSpec((3, count, LANES), lambda i: (0, 0, i))]
    out_shape = [jax.ShapeDtypeStruct((3, count, width), bf16)]
    body, args, extra = attend_back_kernel, [qkv, qkv, qkv, mixed, d_mixed, lse], {}
    scratch = [pltpu.VMEM((count, LANES), f32), pltpu.VMEM((count, LANES), f32)]
    if blocks is not None:
        body = riding(attend_back_kernel, len(in_specs), len(out_specs))
        in_specs.append(pl.BlockSpec(memory_space=pl.ANY))
        out_specs.append(pl.BlockSpec(memory_space=pl.ANY))
        out_shape.append(jax.ShapeDtypeStruct(blocks.shape, blocks.dtype))
        args.append(blocks)
        scratch = scratch + exchange_sems(blocks.shape[0])
        extra = dict(collective_id=1, has_side_effects=True)
    return pl.pallas_call(
        body,
        out_shape=out_shape,
        grid=(pairs,),
        in_specs=in_specs,
        out_specs=out_specs,
        scratch_shapes=scratch,
        compiler_params=params(40, **extra),
        cost_estimate=cost(5 * 4 * count * count * width, 16 * count * width, 8 * count * count),
        name="attend_back",
    )(*args)


def middle_kernel(experts, mixed_ref, w_out_ref, tok_ref, gain_ref, wr_ref, col_ref, h_ref, low_ref, gate_ref):
    rows = mixed_ref.shape[0]
    col = col_ref[...]
    first, second, valid = col[:, 2:3], col[:, 3:4], col[:, 4:5].astype(f32)
    attn = dot_nn(mixed_ref[...], w_out_ref[...])
    hidden = tok_ref[...].astype(f32) + valid * attn
    h_ref[...] = hidden
    inverse = lax.rsqrt(jnp.mean(hidden * hidden, axis=1, keepdims=True) + epsilon)
    low = (hidden * inverse * gain_ref[...]).astype(bf16)
    low_ref[...] = low
    logits = dot_nn(low, wr_ref[...])
    lane = iota((rows, LANES), 1)
    own = jnp.sum(jnp.where(lane == first, logits, 0.0), axis=1, keepdims=True)
    alt = jnp.sum(jnp.where(lane == second, logits, 0.0), axis=1, keepdims=True)
    gate0 = 1.0 / (1.0 + jnp.exp(alt - own))
    gate1 = 1.0 / (1.0 + jnp.exp(own - alt))
    gate_ref[...] = jnp.where(lane == 0, gate0, 0.0) + jnp.where(lane == 1, gate1, 0.0)


def middle(mixed, w_out, tokens, gain, wr, col, experts):
    count, width = mixed.shape
    rows = 256
    whole = lambda i: (0, 0)
    part = lambda i: (i, 0)
    return pl.pallas_call(
        functools.partial(middle_kernel, experts),
        out_shape=(
            jax.ShapeDtypeStruct((count, width), f32),
            jax.ShapeDtypeStruct((count, width), bf16),
            jax.ShapeDtypeStruct((count, LANES), f32),
        ),
        grid=(count // rows,),
        in_specs=[
            pl.BlockSpec((rows, width), part),
            pl.BlockSpec((width, width), whole),
            pl.BlockSpec((rows, width), part),
            pl.BlockSpec((1, width), whole),
            pl.BlockSpec((width, LANES), whole),
            pl.BlockSpec((rows, LANES), part),
        ],
        out_specs=(
            pl.BlockSpec((rows, width), part),
            pl.BlockSpec((rows, width), part),
            pl.BlockSpec((rows, LANES), part),
        ),
        compiler_params=params(40),
        cost_estimate=cost(2 * count * width * width, 12 * count * width),
        name="middle",
    )(mixed, w_out, tokens, gain.reshape(1, width), wr, col)


GELU_C = math.sqrt(2.0 / math.pi)


def expert_kernel(
    split, x_ref, g_ref, wg_ref, wu_ref, wd_ref, wr_ref, act_ref, dgp_ref, dup_ref, de_ref, part_ref, din_ref
):
    rows, width = x_ref.shape
    me = lax.axis_index("dp")
    expert, part = me // split, lax.rem(me, split)
    x = x_ref[...]
    lane = iota((rows, LANES), 1)
    logits = dot_nn(x, wr_ref[...])
    own = jnp.sum(jnp.where(lane == expert, logits, 0.0), axis=1, keepdims=True)
    other = g_ref[:, width:].astype(f32).astype(jnp.int32)
    alt = jnp.sum(jnp.where(lane == other, logits, 0.0), axis=1, keepdims=True)
    gate = 1.0 / (1.0 + jnp.exp(alt - own))
    d_rows = (g_ref[:, 0:width].astype(f32) * gate).astype(bf16)
    de_ref[...] = d_rows
    pre = dot_nn(x, wg_ref[...])
    up = dot_nn(x, wu_ref[...])
    d_hidden = dot_nt(d_rows, wd_ref[...])
    square = pre * pre
    bent = jnp.tanh(GELU_C * pre * (1.0 + 0.044715 * square))
    half = 0.5 * (1.0 + bent)
    gelu = pre * half
    slope = half + 0.5 * pre * (1.0 - bent * bent) * (GELU_C * (1.0 + 3 * 0.044715 * square))
    act = (gelu * up).astype(bf16)
    act_ref[...] = act
    dgp = (d_hidden * up * slope).astype(bf16)
    dup = (d_hidden * gelu).astype(bf16)
    dgp_ref[...] = dgp
    dup_ref[...] = dup
    pull = jnp.sum(act.astype(f32) * d_hidden, axis=1, keepdims=True)
    pull_high = pull.astype(bf16)
    pull_low = (pull - pull_high.astype(f32)).astype(bf16)
    part_ref[...] = dot_nn(act, wd_ref[...]).astype(bf16)
    din_ref[:, 0:width] = (dot_nt(dgp, wg_ref[...]) + dot_nt(dup, wu_ref[...])).astype(bf16)
    extra = jnp.where(lane == 2 * part, pull_high.astype(f32), 0.0)
    extra = extra + jnp.where(lane == 2 * part + 1, pull_low.astype(f32), 0.0)
    din_ref[:, width:] = extra.astype(bf16)


def expert_pass(x, g, wg, wu, wd, wr, split):
    count, width = x.shape
    ff = wg.shape[1]
    rows = 256
    whole = lambda i: (0, 0)
    part = lambda i: (i, 0)
    once = dict(pipeline_mode=pl.Buffered(1))
    return pl.pallas_call(
        functools.partial(expert_kernel, split),
        out_shape=(
            jax.ShapeDtypeStruct((count, ff), bf16),
            jax.ShapeDtypeStruct((count, ff), bf16),
            jax.ShapeDtypeStruct((count, ff), bf16),
            jax.ShapeDtypeStruct((count, width), bf16),
            jax.ShapeDtypeStruct((count, width), bf16),
            jax.ShapeDtypeStruct((count, width + LANES), bf16),
        ),
        grid=(count // rows,),
        in_specs=[
            pl.BlockSpec((rows, width), part),
            pl.BlockSpec((rows, width + LANES), part),
            pl.BlockSpec((width, ff), whole, **once),
            pl.BlockSpec((width, ff), whole, **once),
            pl.BlockSpec((ff, width), whole, **once),
            pl.BlockSpec((width, LANES), whole),
        ],
        out_specs=(
            pl.BlockSpec((rows, ff), part),
            pl.BlockSpec((rows, ff), part),
            pl.BlockSpec((rows, ff), part),
            pl.BlockSpec((rows, width), part),
            pl.BlockSpec((rows, width), part),
            pl.BlockSpec((rows, width + LANES), part),
        ),
        compiler_params=params(56),
        cost_estimate=cost(12 * count * width * ff, 2 * count * (3 * ff + 5 * width), count * ff),
        name="experts",
    )(x, g, wg, wu, wd, wr)


def expert_exchange_kernel(
    group, x_ref, g_ref, wg_hbm, wu_hbm, wd_hbm, wr_ref,
    act_ref, dgp_ref, dup_ref, de_ref, xs_ref, slot_ref, back_ref,
    xb, gb, ds, rd, pd, sp, rp, pp, st_act, st_dgp, st_dup, st_de, wg_ref, wu_ref, wd_ref,
    w_sem, x_send, x_recv, f_send, f_recv, g_own, g_send, g_recv,
    d_send, d_recv, p_send, p_recv, b_send, b_recv, o_sem, s_sem, l_sem,
):
    experts, capacity, width = x_ref.shape
    steps = experts // group
    pair = 2 * capacity
    half = experts // 2
    me = lax.axis_index("dp")
    chip, core = lax.div(me, 2), lax.rem(me, 2)
    mate = 2 * chip + 1 - core

    def bits(place):
        if isinstance(place, int):
            return half + place // 2 if place % 2 else place // 2
        odd = lax.rem(place, 2)
        return odd * half + lax.div(place, 2)

    def chip_at(place):
        return flip(chip, bits(place), experts)

    def remote(src, dst, send, recv, device):
        return pltpu.make_async_remote_copy(
            src_ref=src, dst_ref=dst, send_sem=send, recv_sem=recv, device_id=(device,), device_id_type=MESH
        )

    def own(buf, q, g):
        return buf.at[q, g * pair : g * pair + capacity]

    def theirs(buf, q, g):
        return buf.at[q, g * pair + capacity : (g + 1) * pair]

    def x_copy(place):
        q, g = place // group, place % group
        peer = chip_at(place)
        return remote(x_ref.at[peer], own(xb, q, g), x_send.at[place], x_recv.at[place], 2 * peer + core)

    def x_arrival(q, g):
        place = q * group + g
        return remote(x_ref.at[chip], own(xb, q, g), x_send.at[place], x_recv.at[place], mate)

    def forward(q, g):
        place = q * group + g
        return remote(own(xb, q, g), theirs(xb, q, g), f_send.at[place], f_recv.at[place], mate)

    def g_mine(q, g):
        place = q * group + g
        return pltpu.make_async_copy(g_ref.at[chip_at(place)], own(gb, q, g), g_own.at[place])

    def g_mate(q, g):
        place = q * group + g
        return remote(g_ref.at[chip_at(place)], theirs(gb, q, g), g_send.at[place], g_recv.at[place], mate)

    def d_copy(q, g):
        place = q * group + g
        return remote(pd.at[lax.rem(q, 2), g], rd.at[place], d_send.at[place], d_recv.at[place], mate)

    def p_copy(q, g):
        place = q * group + g
        return remote(pp.at[lax.rem(q, 2), g], rp.at[place], p_send.at[place], p_recv.at[place], mate)

    def back_copy(q, g):
        place = q * group + g
        return remote(ds.at[place], back_ref.at[chip], b_send.at[place], b_recv.at[place], 2 * chip_at(place) + core)

    def slot_copy(q, g):
        place = q * group + g
        return pltpu.make_async_copy(sp.at[place], slot_ref.at[chip_at(place)], s_sem.at[place])

    def stage_copies(q):
        slot = lax.rem(q, 2)
        return (
            pltpu.make_async_copy(st_act.at[slot], act_ref.at[q], o_sem.at[slot, 0]),
            pltpu.make_async_copy(st_dgp.at[slot], dgp_ref.at[q], o_sem.at[slot, 1]),
            pltpu.make_async_copy(st_dup.at[slot], dup_ref.at[q], o_sem.at[slot, 2]),
            pltpu.make_async_copy(st_de.at[slot], de_ref.at[q], o_sem.at[slot, 3]),
        )

    def xs_copy(q):
        return pltpu.make_async_copy(xb.at[q], xs_ref.at[q], l_sem.at[1 + q])

    weights = [
        pltpu.make_async_copy(src, dst, w_sem.at[i])
        for i, (src, dst) in enumerate(((wg_hbm, wg_ref), (wu_hbm, wu_ref), (wd_hbm, wd_ref)))
    ]
    self_x = pltpu.make_async_copy(x_ref.at[chip], own(xb, 0, 0), l_sem.at[0])
    self_back = pltpu.make_async_copy(ds.at[0], back_ref.at[chip], l_sem.at[1 + steps])

    for copy in weights:
        copy.start()
    self_x.start()
    greet([2 * chip_at(place) + core for place in range(1, experts)] + [mate])
    for place in range(1, group):
        x_copy(place).start()
    for q in range(steps):
        for g in range(group):
            g_mine(q, g).start()
            g_mate(q, g).start()
        for g in range(group):
            place = (q + 1) * group + g
            if place < experts:
                x_copy(place).start()
    self_x.wait()
    forward(0, 0).start()
    for g in range(1, group):
        x_arrival(0, g).wait_recv()
        forward(0, g).start()
    for copy in weights:
        copy.wait()

    def finish(q):
        for g in range(group):
            place = q * group + g
            d_copy(q, g).wait_recv()
            ds[place] = (ds[place].astype(f32) + rd[place].astype(f32)).astype(bf16)
            if g == 0:

                @pl.when(q == 0)
                def _():
                    self_back.start()

                @pl.when(q > 0)
                def _():
                    back_copy(q, g).start()

            else:
                back_copy(q, g).start()
        for g in range(group):
            place = q * group + g
            p_copy(q, g).wait_recv()
            sp[place] = (sp[place].astype(f32) + rp[place].astype(f32)).astype(bf16)
            slot_copy(q, g).start()

    def step(q, carry):
        for g in range(group):
            g_mine(q, g).wait()
            g_mate(q, g).wait_recv()
            forward(q, g).wait_recv()
        xs_copy(q).start()
        x = xb[q]
        rows = group * pair
        lane = iota((rows, LANES), 1)
        logits = dot_nn(x, wr_ref[...])
        mine = jnp.sum(jnp.where(lane == chip, logits, 0.0), axis=1, keepdims=True)
        other = gb[q, :, width:].astype(f32).astype(jnp.int32)
        alt = jnp.sum(jnp.where(lane == other, logits, 0.0), axis=1, keepdims=True)
        gate = 1.0 / (1.0 + jnp.exp(alt - mine))
        d_rows = (gb[q, :, 0:width].astype(f32) * gate).astype(bf16)
        pre = dot_nn(x, wg_ref[...])
        up = dot_nn(x, wu_ref[...])
        d_hidden = dot_nt(d_rows, wd_ref[...])
        square = pre * pre
        bent = jnp.tanh(GELU_C * pre * (1.0 + 0.044715 * square))
        hill = 0.5 * (1.0 + bent)
        gelu = pre * hill
        slope = hill + 0.5 * pre * (1.0 - bent * bent) * (GELU_C * (1.0 + 3 * 0.044715 * square))
        act = (gelu * up).astype(bf16)
        dgp = (d_hidden * up * slope).astype(bf16)
        dup = (d_hidden * gelu).astype(bf16)
        pull = jnp.sum(act.astype(f32) * d_hidden, axis=1, keepdims=True)

        @pl.when(q >= 2)
        def _():
            for copy in stage_copies(q - 2):
                copy.wait()
            for g in range(group):
                d_copy(q - 2, g).wait_send()
                p_copy(q - 2, g).wait_send()

        slot = lax.rem(q, 2)
        st_act[slot] = act
        st_dgp[slot] = dgp
        st_dup[slot] = dup
        st_de[slot] = d_rows
        for copy in stage_copies(q):
            copy.start()

        @pl.when(q + 1 < steps)
        def _():
            for g in range(group):
                x_arrival(q + 1, g).wait_recv()
                forward(q + 1, g).start()

        @pl.when(q >= 1)
        def _():
            finish(q - 1)

        d_in = (dot_nt(dgp, wg_ref[...]) + dot_nt(dup, wu_ref[...])).astype(bf16)
        pull_high = pull.astype(bf16).astype(f32)
        extra = jnp.where(lane == 2 * core, pull_high, 0.0)
        extra = (extra + jnp.where(lane == 2 * core + 1, pull - pull_high, 0.0)).astype(bf16)
        for g in range(group):
            place = q * group + g
            low, mid, high = g * pair, g * pair + capacity, (g + 1) * pair
            ds[place, :, 0:width] = d_in[low:mid]
            ds[place, :, width:] = extra[low:mid]
            pd[slot, g, :, 0:width] = d_in[mid:high]
            pd[slot, g, :, width:] = extra[mid:high]
            d_copy(q, g).start()
        partial = dot_nn(act, wd_ref[...]).astype(bf16)
        for g in range(group):
            place = q * group + g
            low, mid, high = g * pair, g * pair + capacity, (g + 1) * pair
            sp[place] = partial[low:mid]
            pp[slot, g] = partial[mid:high]
            p_copy(q, g).start()
        return carry

    lax.fori_loop(0, steps, step, 0)
    finish(steps - 1)
    for q in (steps - 2, steps - 1):
        for copy in stage_copies(q):
            copy.wait()
        for g in range(group):
            d_copy(q, g).wait_send()
            p_copy(q, g).wait_send()
    self_back.wait()
    for q in range(steps):
        xs_copy(q).wait()
        for g in range(group):
            place = q * group + g
            slot_copy(q, g).wait()
            forward(q, g).wait_send()
            g_mate(q, g).wait_send()
            if place:
                x_copy(place).wait_send()
                back_copy(q, g).wait()


def expert_exchange(x, g, wg, wu, wd, wr):
    experts, capacity, width = x.shape
    ff = wg.shape[1]
    group = 2
    steps = experts // group
    rows = 2 * capacity * group
    wide = width + LANES
    anywhere = pl.BlockSpec(memory_space=pl.ANY)
    vmem, dma = pltpu.VMEM, pltpu.SemaphoreType.DMA
    each = dma((experts,))
    count = rows * steps
    outs = pl.pallas_call(
        functools.partial(expert_exchange_kernel, group),
        out_shape=(
            jax.ShapeDtypeStruct((steps, rows, ff), bf16),
            jax.ShapeDtypeStruct((steps, rows, ff), bf16),
            jax.ShapeDtypeStruct((steps, rows, ff), bf16),
            jax.ShapeDtypeStruct((steps, rows, width), bf16),
            jax.ShapeDtypeStruct((steps, rows, width), bf16),
            jax.ShapeDtypeStruct((experts, capacity, width), bf16),
            jax.ShapeDtypeStruct((experts, capacity, wide), bf16),
        ),
        in_specs=[anywhere] * 5 + [pl.BlockSpec(memory_space=vmem)],
        out_specs=(anywhere,) * 7,
        scratch_shapes=[
            vmem((steps, rows, width), bf16),
            vmem((steps, rows, wide), bf16),
            vmem((experts, capacity, wide), bf16),
            vmem((experts, capacity, wide), bf16),
            vmem((2, group, capacity, wide), bf16),
            vmem((experts, capacity, width), bf16),
            vmem((experts, capacity, width), bf16),
            vmem((2, group, capacity, width), bf16),
            vmem((2, rows, ff), bf16),
            vmem((2, rows, ff), bf16),
            vmem((2, rows, ff), bf16),
            vmem((2, rows, width), bf16),
            vmem((width, ff), bf16),
            vmem((width, ff), bf16),
            vmem((ff, width), bf16),
            dma((3,)),
            each, each, each, each, each, each, each,
            each, each, each, each, each, each,
            dma((2, 4)),
            each,
            dma((2 + steps,)),
        ],
        compiler_params=params(60, collective_id=2, has_side_effects=True),
        cost_estimate=cost(12 * count * width * ff, 2 * count * (3 * ff + 5 * width), count * ff),
        name="experts",
    )(x, g, wg, wu, wd, wr)
    act, d_pre, d_up, d_rows, rows_in = (a.reshape(count, a.shape[-1]) for a in outs[:5])
    return act, d_pre, d_up, d_rows, rows_in, outs[5], outs[6]


def hot_rows(col, k, rows, slots):
    return jnp.where(iota((rows, slots), 1) == col[:, k : k + 1], 1.0, 0.0).astype(bf16)


def state_kernel(
    col_ref, gate_ref, din_ref, h_ref, og_ref, gain_ref, wr_ref, dstate_ref, dattn_ref, dlog_ref, gterm_ref
):
    rows, width = h_ref.shape
    slots = din_ref.shape[0]
    col = col_ref[...]
    valid = col[:, 4:5].astype(f32)
    hot0, hot1 = hot_rows(col, 0, rows, slots), hot_rows(col, 1, rows, slots)
    pulls = din_ref[:, width:]
    pull0 = jnp.sum(dot_nn(hot0, pulls), axis=1, keepdims=True)
    pull1 = jnp.sum(dot_nn(hot1, pulls), axis=1, keepdims=True)
    gathered = dot_nn(hot0 + hot1, din_ref[:, 0:width])
    gate0, gate1 = gate_ref[:, 0:1], gate_ref[:, 1:2]
    total = pull0 + pull1
    lane = iota((rows, LANES), 1)
    d_log = jnp.where(lane == col[:, 2:3], pull0 - gate0 * total, 0.0)
    d_log = d_log + jnp.where(lane == col[:, 3:4], pull1 - gate1 * total, 0.0)
    d_log = d_log.astype(bf16)
    dlog_ref[...] = d_log
    d_moe = gathered + dot_nt(d_log, wr_ref[...])
    hidden = h_ref[...]
    inverse = lax.rsqrt(jnp.mean(hidden * hidden, axis=1, keepdims=True) + epsilon)
    normal = hidden * inverse
    scaled = gain_ref[...] * d_moe
    share = jnp.mean(normal * scaled, axis=1, keepdims=True)
    d_state = og_ref[...].astype(f32) + inverse * (scaled - normal * share)
    dstate_ref[...] = d_state
    dattn_ref[...] = (valid * d_state).astype(bf16)
    term = jnp.sum((normal * d_moe).reshape(rows // 8, 8, width), axis=0)

    @pl.when(pl.program_id(0) == 0)
    def _():
        gterm_ref[...] = jnp.zeros_like(gterm_ref)

    gterm_ref[...] += term


def state_back(col, gates, din, hidden, out_grad, gain, wr):
    count, width = hidden.shape
    slots = din.shape[0]
    rows = 256
    whole = lambda i: (0, 0)
    part = lambda i: (i, 0)
    return pl.pallas_call(
        state_kernel,
        out_shape=(
            jax.ShapeDtypeStruct((count, width), f32),
            jax.ShapeDtypeStruct((count, width), bf16),
            jax.ShapeDtypeStruct((count, LANES), bf16),
            jax.ShapeDtypeStruct((8, width), f32),
        ),
        grid=(count // rows,),
        in_specs=[
            pl.BlockSpec((rows, LANES), part),
            pl.BlockSpec((rows, LANES), part),
            pl.BlockSpec((slots, width + LANES), whole),
            pl.BlockSpec((rows, width), part),
            pl.BlockSpec((rows, width), part),
            pl.BlockSpec((1, width), whole),
            pl.BlockSpec((width, LANES), whole),
        ],
        out_specs=(
            pl.BlockSpec((rows, width), part),
            pl.BlockSpec((rows, width), part),
            pl.BlockSpec((rows, LANES), part),
            pl.BlockSpec((8, width), whole),
        ),
        compiler_params=params(48),
        cost_estimate=cost(2 * slots * count * width, 14 * count * width),
        name="state_back",
    )(col, gates, din, hidden, out_grad, gain.reshape(1, width), wr)


def block_out_kernel(col_ref, gate_ref, rows_ref, h_ref, out_ref):
    rows, width = h_ref.shape
    slots = rows_ref.shape[0]
    col = col_ref[...]
    pick0 = dot_nn(hot_rows(col, 0, rows, slots), rows_ref[...])
    pick1 = dot_nn(hot_rows(col, 1, rows, slots), rows_ref[...])
    out_ref[...] = (h_ref[...] + gate_ref[:, 0:1] * pick0 + gate_ref[:, 1:2] * pick1).astype(bf16)


def make_block_out(col, gates, slot_rows, hidden):
    count, width = hidden.shape
    slots = slot_rows.shape[0]
    rows = 256
    whole = lambda i: (0, 0)
    part = lambda i: (i, 0)
    return pl.pallas_call(
        block_out_kernel,
        out_shape=jax.ShapeDtypeStruct((count, width), bf16),
        grid=(count // rows,),
        in_specs=[
            pl.BlockSpec((rows, LANES), part),
            pl.BlockSpec((rows, LANES), part),
            pl.BlockSpec((slots, width), whole),
            pl.BlockSpec((rows, width), part),
        ],
        out_specs=pl.BlockSpec((rows, width), part),
        compiler_params=params(40),
        cost_estimate=cost(4 * slots * count * width, 9 * count * width),
        name="block_out",
    )(col, gates, slot_rows, hidden)


def input_kernel(d_ref, w_ref, tok_ref, gain_ref, dstate_ref, grad_ref, gterm_ref):
    rows, width = tok_ref.shape
    d_normed = dot_nt(d_ref[0], w_ref[:, 0:width])
    for i in range(1, 3):
        d_normed = d_normed + dot_nt(d_ref[i], w_ref[:, i * width : (i + 1) * width])
    values = tok_ref[...].astype(f32)
    inverse = lax.rsqrt(jnp.mean(values * values, axis=1, keepdims=True) + epsilon)
    normal = values * inverse
    scaled = gain_ref[...] * d_normed
    share = jnp.mean(normal * scaled, axis=1, keepdims=True)
    grad_ref[...] = dstate_ref[...] + inverse * (scaled - normal * share)
    term = jnp.sum((normal * d_normed).reshape(rows // 8, 8, width), axis=0)

    @pl.when(pl.program_id(0) == 0)
    def _():
        gterm_ref[...] = jnp.zeros_like(gterm_ref)

    gterm_ref[...] += term


def input_back(d_qkv, w_qkv, tokens, gain, d_state):
    count, width = tokens.shape
    rows = 256
    whole = lambda i: (0, 0)
    part = lambda i: (i, 0)
    return pl.pallas_call(
        input_kernel,
        out_shape=(
            jax.ShapeDtypeStruct((count, width), f32),
            jax.ShapeDtypeStruct((8, width), f32),
        ),
        grid=(count // rows,),
        in_specs=[
            pl.BlockSpec((3, rows, width), lambda i: (0, i, 0)),
            pl.BlockSpec((width, 3 * width), whole),
            pl.BlockSpec((rows, width), part),
            pl.BlockSpec((1, width), whole),
            pl.BlockSpec((rows, width), part),
        ],
        out_specs=(pl.BlockSpec((rows, width), part), pl.BlockSpec((8, width), whole)),
        compiler_params=params(48),
        cost_estimate=cost(6 * count * width * width, 22 * count * width),
        name="input_back",
    )(d_qkv, w_qkv, tokens, gain.reshape(1, width), d_state)


def shards(
    tokens,
    lengths,
    expert_ids,
    slot_order,
    gain_attn,
    w_qkv,
    w_out,
    gain_moe,
    w_router,
    w_gate,
    w_up,
    w_down,
    out_grad,
):
    tok_dev, width = tokens.shape
    n_dev = lax.axis_size("dp")
    experts = w_router.shape[1]
    split = n_dev // experts
    capacity = split * (5 * tok_dev // (4 * n_dev))
    slots = experts * capacity
    me = lax.axis_index("dp")
    part = lax.rem(me, split)
    same_part = [[e * split + p for e in range(experts)] for p in range(split)]
    same_expert = [[e * split + p for p in range(split)] for e in range(experts)]
    swap = [(d, d ^ 1) for d in range(n_dev)]

    def across(blocks):
        return lax.all_to_all(blocks, "dp", 0, 0, axis_index_groups=same_part, tiled=True)

    def share(rows):
        if split == 2:
            return jnp.concatenate([rows, lax.ppermute(rows, "dp", swap)], axis=0)
        return lax.all_gather(rows, "dp", axis_index_groups=same_expert, tiled=True)

    def settle(pieces):
        if split == 2:
            theirs = lax.ppermute(pieces[1], "dp", swap)
            return (pieces[0].astype(f32) + theirs.astype(f32)).astype(bf16)
        got = lax.all_to_all(pieces, "dp", 0, 0, axis_index_groups=same_expert, tiled=True)
        return jnp.sum(got.astype(f32), axis=0).astype(bf16)

    def send_in(rows):
        return share(across(rows.reshape(experts, capacity, -1)).reshape(slots, -1))

    def send_back(rows):
        summed = settle(rows.reshape(split, slots, -1))
        return across(summed.reshape(experts, capacity, -1)).reshape(slots, -1)

    def reduce_rows(term):
        pieces = term.reshape(experts, split, -1, term.shape[-1])
        if split == 2:
            mine = lax.dynamic_index_in_dim(pieces, part, 1, keepdims=False)
            theirs = lax.dynamic_index_in_dim(pieces, 1 - part, 1, keepdims=False)
            theirs = lax.ppermute(theirs.astype(bf16), "dp", swap)
            summed = (mine + theirs.astype(f32)).astype(bf16)
        else:
            pieces = jnp.moveaxis(pieces, 1, 0).astype(bf16)
            got = lax.all_to_all(pieces, "dp", 0, 0, axis_index_groups=same_expert, tiled=True)
            summed = jnp.sum(got.astype(f32), axis=0).astype(bf16)
        return jnp.sum(across(summed).astype(f32), axis=0)

    wr = jnp.pad(w_router, ((0, 0), (0, LANES - experts)))
    col, row = make_slots(lengths, expert_ids, slot_order, experts, capacity)
    direct = split == 2 and experts & (experts - 1) == 0 and experts >= 4
    grad_out = dispatch_grad(row, out_grad, slots)

    token_vals = tokens.astype(f32)
    inverse_attn = lax.rsqrt(jnp.mean(token_vals * token_vals, axis=-1, keepdims=True) + epsilon)
    normed_low = (token_vals * inverse_attn * gain_attn).astype(bf16)
    qkv = jnp.dot(normed_low, w_qkv, preferred_element_type=f32).astype(bf16)
    if direct:
        mixed, lse, grad_in = attend(qkv, grad_out.reshape(experts, capacity, -1))
    else:
        mixed, lse = attend(qkv)
        grad_in = send_in(grad_out)
    hidden, moe_low, gates = middle(mixed, w_out, tokens, gain_moe, wr, col, experts)

    rows_out = dispatch(row, moe_low, slots)
    if direct:
        act, d_pre, d_up, d_rows, rows_in, slot_part, d_in_back = expert_exchange(
            rows_out.reshape(experts, capacity, -1), grad_in, w_gate[0], w_up[0], w_down[0], wr
        )
        d_in_back = d_in_back.reshape(slots, -1)
    else:
        rows_in = send_in(rows_out)
        act, d_pre, d_up, d_rows, partial_out, d_in = expert_pass(
            rows_in, grad_in, w_gate[0], w_up[0], w_down[0], wr, split
        )
        d_in_back = send_back(d_in)
        slot_out = send_back(partial_out)

    d_state, d_attn, d_log, gain_moe_rows = state_back(
        col, gates, d_in_back, hidden, out_grad, gain_moe, wr
    )
    out_term = dot_tn(mixed, d_attn)
    router_term = dot_tn(moe_low, d_log)
    gain_moe_term = jnp.sum(gain_moe_rows, axis=0)
    d_mixed = dot_nt(d_attn, w_out).astype(bf16)
    if direct:
        d_qkv, slot_out = attend_back(qkv, mixed, d_mixed, lse, slot_part)
        slot_out = slot_out.reshape(slots, -1)
    else:
        (d_qkv,) = attend_back(qkv, mixed, d_mixed, lse)
    tokens_grad, gain_attn_rows = input_back(d_qkv, w_qkv, tokens, gain_attn, d_state)
    qkv_term = jnp.concatenate([dot_tn(normed_low, d_qkv[i]) for i in range(3)], axis=1)
    gain_attn_term = jnp.sum(gain_attn_rows, axis=0)

    lane = jnp.arange(LANES, dtype=jnp.int32)[None, :]
    extra = jnp.where(lane == experts, gain_moe_term[:, None], router_term)
    early = reduce_rows(jnp.concatenate([out_term, extra], axis=1))
    late_extra = jnp.where(lane == 0, gain_attn_term[:, None], 0.0)
    late = reduce_rows(jnp.concatenate([qkv_term, late_extra], axis=1))

    down_grad = dot_tn(act, d_rows)
    gate_grad = dot_tn(rows_in, d_pre)
    up_grad = dot_tn(rows_in, d_up)
    block_out = make_block_out(col, gates, slot_out, hidden)
    return (
        block_out,
        tokens_grad,
        late[:, 3 * width],
        late[:, 0 : 3 * width],
        early[:, 0:width],
        early[:, width + experts],
        early[:, width : width + experts],
        gate_grad[None],
        up_grad[None],
        down_grad[None],
    )


def solution(mesh):
    rows, one = P("dp", None), P("dp")
    cube = P("dp", None, None)
    return jax.shard_map(
        shards,
        mesh=mesh,
        in_specs=(rows, one, rows, rows, P(), P(), P(), P(), P(), cube, cube, cube, rows),
        out_specs=(rows, rows, one, rows, rows, one, rows, cube, cube, cube),
        check_vma=False,
    )
```

```python
import functools
import math

import jax
import jax.numpy as jnp
from jax import lax
from jax.experimental import pallas as pl
from jax.experimental.pallas import tpu as pltpu
from jax.sharding import PartitionSpec as P

HEADS = 16
HEAD_DIM = 64
LEN = 1024
LANES = 128
MIB = 1 << 20

epsilon = 1e-06
mask_fill = -1e30
f32 = jnp.float32
bf16 = jnp.bfloat16


def dot_nn(left, right, **kw):
    return lax.dot_general(left, right, (((1,), (0,)), ((), ())), preferred_element_type=f32, **kw)


def dot_nt(left, right, **kw):
    return lax.dot_general(left, right, (((1,), (1,)), ((), ())), preferred_element_type=f32, **kw)


def dot_tn(left, right, **kw):
    return lax.dot_general(left, right, (((0,), (0,)), ((), ())), preferred_element_type=f32, **kw)


def iota(shape, dim):
    return lax.broadcasted_iota(jnp.int32, shape, dim)


def params(mib, **kw):
    return pltpu.CompilerParams(vmem_limit_bytes=mib * MIB, **kw)


def cost(flops, nbytes, trans=0):
    return pl.CostEstimate(flops=int(flops), bytes_accessed=int(nbytes), transcendentals=int(trans))


def slot_kernel(capacity, experts, len_ref, ids_ref, rank_col_ref, rank_row_ref, col_ref, row_ref):
    count = ids_ref.shape[0]
    length = len_ref[0]
    ids = ids_ref[...]
    first, second = ids[:, 0:1], ids[:, 1:2]
    lane = iota((count, LANES), 1)
    place = iota((count, LANES), 0)
    hot0 = (lane == first) & (lane < experts)
    hot1 = (lane == second + experts) & (lane >= experts) & (lane < 2 * experts)
    valid = place < length
    hot = jnp.where((hot0 | hot1) & valid, 1.0, 0.0).astype(bf16)
    before = (rank_row_ref[...] < rank_col_ref[...]).astype(f32).astype(bf16)
    counts = dot_nn(before, hot)
    shifted = (lane == first + experts) & (lane >= experts) & (lane < 2 * experts) & valid
    totals = jnp.sum(jnp.where(shifted, 1.0, 0.0), axis=0, keepdims=True)
    slot0 = jnp.sum(jnp.where(hot0, counts, 0.0), axis=1, keepdims=True).astype(jnp.int32)
    slot1 = jnp.sum(jnp.where(hot1, counts + totals, 0.0), axis=1, keepdims=True).astype(jnp.int32)
    sentinel = experts * capacity
    ok = valid[:, 0:1]
    flat0 = jnp.where(ok & (slot0 < capacity), first * capacity + slot0, sentinel)
    flat1 = jnp.where(ok & (slot1 < capacity), second * capacity + slot1, sentinel)
    col = jnp.where(lane == 0, flat0, 0) + jnp.where(lane == 1, flat1, 0)
    col = col + jnp.where(lane == 2, first, 0) + jnp.where(lane == 3, second, 0)
    col = col + jnp.where(lane == 4, ok.astype(jnp.int32), 0)
    col_ref[...] = col
    row_ref[...] = jnp.transpose(col.astype(f32))[0:8, :].astype(jnp.int32)


def make_slots(lengths, expert_ids, slot_order, experts, capacity):
    count = expert_ids.shape[0]
    return pl.pallas_call(
        functools.partial(slot_kernel, capacity, experts),
        out_shape=(
            jax.ShapeDtypeStruct((count, LANES), jnp.int32),
            jax.ShapeDtypeStruct((8, count), jnp.int32),
        ),
        in_specs=[
            pl.BlockSpec(memory_space=pltpu.SMEM),
            pl.BlockSpec(memory_space=pltpu.VMEM),
            pl.BlockSpec(memory_space=pltpu.VMEM),
            pl.BlockSpec(memory_space=pltpu.VMEM),
        ],
        out_specs=(pl.BlockSpec(memory_space=pltpu.VMEM), pl.BlockSpec(memory_space=pltpu.VMEM)),
        compiler_params=params(40),
        cost_estimate=cost(2 * count * count * LANES, 4 * count * LANES),
        name="slots",
    )(lengths, expert_ids, slot_order.reshape(count, 1), slot_order)


def dispatch_kernel(rows, row_ref, data_ref, out_ref):
    count = data_ref.shape[0]
    slot = pl.program_id(0) * rows + iota((rows, count), 0)
    hot = (slot == row_ref[0:1, :]) | (slot == row_ref[1:2, :])
    out_ref[...] = dot_nn(jnp.where(hot, 1.0, 0.0).astype(bf16), data_ref[...]).astype(bf16)


def dispatch(row, data, slots):
    count, width = data.shape
    rows = 256
    return pl.pallas_call(
        functools.partial(dispatch_kernel, rows),
        out_shape=jax.ShapeDtypeStruct((slots, width), bf16),
        grid=(slots // rows,),
        in_specs=[
            pl.BlockSpec((8, count), lambda i: (0, 0)),
            pl.BlockSpec((count, width), lambda i: (0, 0)),
        ],
        out_specs=pl.BlockSpec((rows, width), lambda i: (i, 0)),
        compiler_params=params(40),
        cost_estimate=cost(2 * slots * count * width, 2 * (slots + count) * width),
        name="dispatch",
    )(row, data)


def dispatch_grad_kernel(rows, row_ref, data_ref, out_ref):
    count, width = data_ref.shape
    slot = pl.program_id(0) * rows + iota((rows, count), 0)
    hot0 = slot == row_ref[0:1, :]
    hot1 = slot == row_ref[1:2, :]
    both = jnp.where(hot0 | hot1, 1.0, 0.0).astype(bf16)
    out_ref[:, 0:width] = dot_nn(both, data_ref[...]).astype(bf16)
    other = jnp.where(hot0, row_ref[3:4, :], 0) + jnp.where(hot1, row_ref[2:3, :], 0)
    other = jnp.sum(other.astype(f32), axis=1, keepdims=True)
    out_ref[:, width:] = jnp.broadcast_to(other, (rows, LANES)).astype(bf16)


def dispatch_grad(row, data, slots):
    count, width = data.shape
    rows = 256
    return pl.pallas_call(
        functools.partial(dispatch_grad_kernel, rows),
        out_shape=jax.ShapeDtypeStruct((slots, width + LANES), bf16),
        grid=(slots // rows,),
        in_specs=[
            pl.BlockSpec((8, count), lambda i: (0, 0)),
            pl.BlockSpec((count, width), lambda i: (0, 0)),
        ],
        out_specs=pl.BlockSpec((rows, width + LANES), lambda i: (i, 0)),
        compiler_params=params(40),
        cost_estimate=cost(2 * slots * count * width, 2 * (slots + count) * width),
        name="dispatch_grad",
    )(row, data)


MESH = pl.DeviceIdType.MESH


def flip(chip, bits, experts):
    out, b = chip, 1
    while b < experts:
        if isinstance(bits, int):
            out = out + (bits // b % 2) * (b - 2 * b * lax.rem(lax.div(chip, b), 2))
        else:
            mine, theirs = lax.rem(lax.div(chip, b), 2), lax.rem(lax.div(bits, b), 2)
            out = out + b * theirs * (1 - 2 * mine)
        b *= 2
    return out


def greet(peers):
    barrier = pltpu.get_barrier_semaphore()
    for peer in peers:
        pl.semaphore_signal(barrier, inc=1, device_id=(peer,), device_id_type=MESH)
    pl.semaphore_wait(barrier, len(peers))


def exchange_copies(src, dst, send_sem, recv_sem, local_sem):
    experts = src.shape[0]
    me = lax.axis_index("dp")
    chip, core = lax.div(me, 2), lax.rem(me, 2)
    copies = [pltpu.make_async_copy(src.at[chip], dst.at[chip], local_sem)]
    peers = []
    half = experts // 2
    for place in range(1, experts):
        step = half + place // 2 if place % 2 else place // 2
        peer = flip(chip, step, experts)
        peers.append(2 * peer + core)
        copies.append(
            pltpu.make_async_remote_copy(
                src_ref=src.at[peer],
                dst_ref=dst.at[chip],
                send_sem=send_sem.at[step],
                recv_sem=recv_sem.at[step],
                device_id=(2 * peer + core,),
                device_id_type=MESH,
            )
        )
    return peers, copies


def exchange_sems(experts):
    return [
        pltpu.SemaphoreType.DMA((experts,)),
        pltpu.SemaphoreType.DMA((experts,)),
        pltpu.SemaphoreType.DMA,
    ]


def riding(body, n_in, n_out):
    def kernel(*refs):
        ins, src = refs[:n_in], refs[n_in]
        outs, dst = refs[n_in + 1 : n_in + 1 + n_out], refs[n_in + 1 + n_out]
        rest, sems = refs[n_in + n_out + 2 : -3], refs[-3:]
        peers, copies = exchange_copies(src, dst, *sems)

        @pl.when(pl.program_id(0) == 0)
        def _():
            greet(peers)
            for copy in copies:
                copy.start()

        body(*ins, *outs, *rest)

        @pl.when(pl.program_id(0) == pl.num_programs(0) - 1)
        def _():
            for copy in copies:
                copy.wait()

    return kernel


SCALE2 = math.log2(math.e) / math.sqrt(HEAD_DIM)
QB = 256


def attend_kernel(q_ref, k_ref, v_ref, mixed_ref, lse_ref):
    lane = iota((QB, LANES), 1)
    wide = jnp.concatenate([v_ref[...], jnp.ones_like(v_ref)], axis=1)
    causal = iota((QB, QB), 1) <= iota((QB, QB), 0)
    for block in range(LEN // QB):
        start, stop = block * QB, (block + 1) * QB
        query = q_ref[start:stop, :]
        halves, norms = [], []
        for head in range(2):
            mine = (lane // HEAD_DIM) == head
            scores = dot_nt(jnp.where(mine, query, jnp.zeros_like(query)), k_ref[0:stop, :])
            tail = jnp.where(causal, scores[:, start:stop], mask_fill)
            scores = tail if block == 0 else jnp.concatenate([scores[:, 0:start], tail], axis=1)
            highest = jnp.max(scores, axis=1, keepdims=True) * SCALE2
            raised = jnp.exp2(scores * SCALE2 - highest)
            out = dot_nn(raised.astype(bf16), wide[0:stop, :])
            summed = out[:, LANES:]
            halves.append(out[:, 0:LANES] / summed)
            norms.append(highest + jnp.log2(summed))
        mixed_ref[start:stop, :] = jnp.where(lane < HEAD_DIM, halves[0], halves[1]).astype(bf16)
        norm = jnp.where(lane == 0, norms[0], norms[1])
        lse_ref[0, :, start:stop] = jnp.transpose(norm)[0:8, :]


def attend(qkv, blocks=None):
    count, width3 = qkv.shape
    width = width3 // 3
    pairs = width // LANES
    in_specs = [
        pl.BlockSpec((count, LANES), lambda i: (0, i)),
        pl.BlockSpec((count, LANES), lambda i: (0, i + pairs)),
        pl.BlockSpec((count, LANES), lambda i: (0, i + 2 * pairs)),
    ]
    out_specs = [
        pl.BlockSpec((count, LANES), lambda i: (0, i)),
        pl.BlockSpec((1, 8, count), lambda i: (i, 0, 0)),
    ]
    out_shape = [
        jax.ShapeDtypeStruct((count, width), bf16),
        jax.ShapeDtypeStruct((pairs, 8, count), f32),
    ]
    body, args, scratch, extra = attend_kernel, [qkv, qkv, qkv], [], {}
    if blocks is not None:
        body = riding(attend_kernel, len(in_specs), len(out_specs))
        in_specs.append(pl.BlockSpec(memory_space=pl.ANY))
        out_specs.append(pl.BlockSpec(memory_space=pl.ANY))
        out_shape.append(jax.ShapeDtypeStruct(blocks.shape, blocks.dtype))
        args.append(blocks)
        scratch = exchange_sems(blocks.shape[0])
        extra = dict(collective_id=0, has_side_effects=True)
    return pl.pallas_call(
        body,
        out_shape=out_shape,
        grid=(pairs,),
        in_specs=in_specs,
        out_specs=out_specs,
        scratch_shapes=scratch,
        compiler_params=params(40, **extra),
        cost_estimate=cost(2 * 4 * count * count * width, 8 * count * width, 8 * count * count),
        name="attend",
    )(*args)


def attend_back_kernel(q_ref, k_ref, v_ref, o_ref, do_ref, lse_ref, out_ref, dk_sc, dv_sc):
    lane = iota((QB, LANES), 1)
    keep = iota((QB, QB), 0) <= iota((QB, QB), 1)
    dk_sc[...] = jnp.zeros_like(dk_sc)
    dv_sc[...] = jnp.zeros_like(dv_sc)
    sub = iota((8, LANES), 0)
    picks = jnp.where(iota((8, LANES), 1) // HEAD_DIM == sub, 1.0, 0.0)
    low = (iota((LEN, LANES), 1) // HEAD_DIM) == 0
    key = k_ref[...]
    none = jnp.zeros_like(key)
    keys = (jnp.where(low, key, none), jnp.where(low, none, key))
    for block in range(LEN // QB):
        start, stop = block * QB, (block + 1) * QB
        query = q_ref[start:stop, :]
        d_out = do_ref[start:stop, :]
        product = d_out.astype(f32) * o_ref[start:stop, :].astype(f32)
        delta = dot_nt(picks, product, precision=lax.Precision.HIGHEST)
        d_query = jnp.zeros((QB, LANES), f32)
        for head in range(2):
            mine = (lane // HEAD_DIM) == head
            query_one = jnp.where(mine, query, jnp.zeros_like(query))
            d_one = jnp.where(mine, d_out, jnp.zeros_like(d_out))
            scores = dot_nt(k_ref[0:stop, :], query_one)
            tail = jnp.where(keep, scores[start:stop, :], mask_fill)
            scores = tail if block == 0 else jnp.concatenate([scores[0:start, :], tail], axis=0)
            probs = jnp.exp2(scores * SCALE2 - lse_ref[0, head : head + 1, start:stop])
            d_probs = dot_nt(v_ref[0:stop, :], d_one)
            d_scores = (probs * (d_probs - delta[head : head + 1, :])).astype(bf16)
            dv_sc[0:stop, :] += dot_nn(probs.astype(bf16), d_one)
            dk_sc[0:stop, :] += dot_nn(d_scores, query_one)
            d_query = d_query + dot_tn(d_scores, keys[head][0:stop, :])
        out_ref[0, start:stop, :] = (d_query * (1.0 / math.sqrt(HEAD_DIM))).astype(bf16)
    out_ref[1, :, :] = (dk_sc[...] * (1.0 / math.sqrt(HEAD_DIM))).astype(bf16)
    out_ref[2, :, :] = dv_sc[...].astype(bf16)


def attend_back(qkv, mixed, d_mixed, lse):
    count, width = mixed.shape
    pairs = width // LANES
    return pl.pallas_call(
        attend_back_kernel,
        out_shape=jax.ShapeDtypeStruct((3, count, width), bf16),
        grid=(pairs,),
        in_specs=[
            pl.BlockSpec((count, LANES), lambda i: (0, i)),
            pl.BlockSpec((count, LANES), lambda i: (0, i + pairs)),
            pl.BlockSpec((count, LANES), lambda i: (0, i + 2 * pairs)),
            pl.BlockSpec((count, LANES), lambda i: (0, i)),
            pl.BlockSpec((count, LANES), lambda i: (0, i)),
            pl.BlockSpec((1, 8, count), lambda i: (i, 0, 0)),
        ],
        out_specs=pl.BlockSpec((3, count, LANES), lambda i: (0, 0, i)),
        scratch_shapes=[pltpu.VMEM((count, LANES), f32), pltpu.VMEM((count, LANES), f32)],
        compiler_params=params(40),
        cost_estimate=cost(5 * 4 * count * count * width, 16 * count * width, 8 * count * count),
        name="attend_back",
    )(qkv, qkv, qkv, mixed, d_mixed, lse)


def back_reduce_kernel(
    chips,
    q_ref, k_ref, v_ref, o_ref, do_ref, lse_ref, datt_ref, norm_ref, mix_ref, moe_ref, dlog_ref, gm_ref, slot_ref,
    out_ref, sum_ref, extra_ref, back_ref,
    dk_sc, dv_sc, norm_t, mix_t, right, terms, firsts, sums, half0, half1, half2, half3, s_send, s_recv,
    *ride_sems,
):
    halves = (half0, half1, half2, half3)
    levels = chips.bit_length() - 1
    count = k_ref.shape[0]
    width = norm_ref.shape[1]
    rows = terms.shape[3]
    turn = pl.program_id(0)
    pairs = sum_ref.shape[0]
    me = lax.axis_index("dp")
    chip, core = lax.div(me, 2), lax.rem(me, 2)
    mate = 2 * chip + 1 - core
    order0 = [1 << b for b in range(levels)]
    order1 = list(order0)
    order1[0], order1[1] = order0[1], order0[0]
    order0[2:] = order0[2:][::-1]

    def bit(mask):
        return lax.rem(lax.div(chip, mask), 2)

    own, peers = [], []
    for level in range(levels):
        b0, b1 = bit(order0[level]), bit(order1[level])
        own.append(b0 + core * (b1 - b0))
        p0 = order0[level] * (1 - 2 * b0)
        p1 = order1[level] * (1 - 2 * b1)
        peers.append(2 * (chip + p0 + core * (p1 - p0)) + core)
    bases = [0]
    for level in range(levels):
        bases.append(bases[-1] + own[level] * (chips >> (level + 1)))

    def remote(src, dst, c, level, device):
        return pltpu.make_async_remote_copy(
            src_ref=src, dst_ref=dst, send_sem=s_send.at[c, level], recv_sem=s_recv.at[c, level],
            device_id=(device,), device_id_type=MESH,
        )

    def cols(c):
        return pl.ds(0, LANES) if isinstance(c, int) else slice(None)

    def swap(c):
        return remote(
            terms.at[c, :, 1 - core, :, cols(c)], firsts.at[c, :, :, cols(c)], c, levels, mate
        )

    def send(c, level):
        span = chips >> (level + 1)
        start = bases[level] + (1 - own[level]) * span
        return remote(
            sums.at[c, pl.ds(start, span), :, cols(c)], halves[level].at[c, :, :, cols(c)], c, level, peers[level]
        )

    def fold_swap(c):
        swap(c).wait_recv()
        for b in range(chips):
            places = []
            for order in (order0, order1):
                place = 0
                for level in range(levels):
                    place += (b // order[level] % 2) * (chips >> (level + 1))
                places.append(place)
            at = places[0] + core * (places[1] - places[0])
            total = terms[c, b, core, :, cols(c)].astype(f32) + firsts[c, b, :, cols(c)].astype(f32)
            sums[c, at, :, cols(c)] = total.astype(bf16)

    def fold(c, level):
        send(c, level).wait()
        for t in range(chips >> (level + 1)):
            at = bases[level + 1] + t
            total = sums[c, at, :, cols(c)].astype(f32) + halves[level][c, t, :, cols(c)].astype(f32)
            if level < levels - 1:
                sums[c, at, :, cols(c)] = total.astype(bf16)
            elif isinstance(c, int):
                extra_ref[...] = total
            else:
                sum_ref[c] = total

    def stage(c, s):
        if s == 1:
            fold_swap(c)
        else:
            fold(c, s - 2)
        if s - 1 < levels:
            send(c, s - 1).start()

    riders, ride = exchange_copies(slot_ref, back_ref, *ride_sems)
    span = 256
    per = span // (2 * rows)

    @pl.when(turn == 0)
    def _():
        greet([mate] + riders)
        for copy in ride:
            copy.start()
        norm_t[...] = jnp.transpose(norm_ref[...])
        mix_t[...] = jnp.transpose(mix_ref[...])
        for row in range(0, width, span):
            extra = dot_tn(moe_ref[:, row : row + span], dlog_ref[...])
            gain = jnp.transpose(jnp.sum(gm_ref[:, row : row + span], axis=0, keepdims=True))
            extra = extra + jnp.where(iota(extra.shape, 1) == 64, gain, 0.0)
            at = row // (2 * rows)
            terms[pairs, at : at + per, :, :, 0:LANES] = extra.astype(bf16).reshape(per, 2, rows, LANES)
        swap(pairs).start()

    for s in range(levels + 1, 0, -1):
        c = turn - s

        @pl.when((c >= 0) & (c < pairs))
        def _():
            stage(c, s)

        @pl.when(c == 0)
        def _():
            stage(pairs, s)

    @pl.when(turn < pairs)
    def _():
        attend_back_kernel(q_ref, k_ref, v_ref, o_ref, do_ref, lse_ref, out_ref, dk_sc, dv_sc)
        for i in range(3):
            right[:, i * LANES : (i + 1) * LANES] = out_ref[i]
        for row in range(0, width, span):
            qkv_rows = dot_nn(norm_t[row : row + span, :], right[...])
            out_rows = dot_nn(mix_t[row : row + span, :], datt_ref[...])
            at = row // (2 * rows)
            terms[turn, at : at + per, :, :, 0 : 3 * LANES] = (
                qkv_rows.astype(bf16).reshape(per, 2, rows, 3 * LANES)
            )
            terms[turn, at : at + per, :, :, 3 * LANES :] = out_rows.astype(bf16).reshape(per, 2, rows, LANES)
        swap(turn).start()

    @pl.when(turn == pl.num_programs(0) - 1)
    def _():
        for c in range(pairs):
            swap(jnp.int32(c)).wait_send()
        swap(pairs).wait_send()
        for copy in ride:
            copy.wait()


def attend_back_reduce(qkv, mixed, d_mixed, lse, d_attn, normed, moe_low, d_log, gain_rows, slot_rows, n_dev):
    count, width = mixed.shape
    pairs = width // LANES
    chips = n_dev // 2
    levels = chips.bit_length() - 1
    rows = width // n_dev
    wide = 4 * LANES
    vmem, dma = pltpu.VMEM, pltpu.SemaphoreType.DMA
    anywhere = pl.BlockSpec(memory_space=pl.ANY)

    def column(offset=0):
        return pl.BlockSpec((count, LANES), lambda i: (0, jnp.minimum(i, pairs - 1) + offset))

    def whole(array):
        return pl.BlockSpec(array.shape, lambda i: (0, 0), pipeline_mode=pl.Buffered(1))

    d_qkv, sums, extra, back = pl.pallas_call(
        functools.partial(back_reduce_kernel, chips),
        out_shape=(
            jax.ShapeDtypeStruct((3, count, width), bf16),
            jax.ShapeDtypeStruct((pairs, rows, wide), f32),
            jax.ShapeDtypeStruct((rows, LANES), f32),
            jax.ShapeDtypeStruct(slot_rows.shape, bf16),
        ),
        grid=(pairs + levels + 1,),
        in_specs=[
            column(),
            column(pairs),
            column(2 * pairs),
            column(),
            column(),
            pl.BlockSpec((1, 8, count), lambda i: (jnp.minimum(i, pairs - 1), 0, 0)),
            column(),
            whole(normed),
            whole(mixed),
            whole(moe_low),
            whole(d_log),
            whole(gain_rows),
            anywhere,
        ],
        out_specs=(
            pl.BlockSpec((3, count, LANES), lambda i: (0, 0, jnp.minimum(i, pairs - 1))),
            pl.BlockSpec((pairs, rows, wide), lambda i: (0, 0, 0)),
            pl.BlockSpec((rows, LANES), lambda i: (0, 0)),
            anywhere,
        ),
        scratch_shapes=[
            vmem((count, LANES), f32),
            vmem((count, LANES), f32),
            vmem((width, count), bf16),
            vmem((width, count), bf16),
            vmem((count, 3 * LANES), bf16),
            vmem((pairs + 1, chips, 2, rows, wide), bf16),
            vmem((pairs + 1, chips, rows, wide), bf16),
            vmem((pairs + 1, chips, rows, wide), bf16),
        ]
        + [vmem((pairs + 1, chips >> (level + 1), rows, wide), bf16) for level in range(levels)]
        + [dma((pairs + 1, levels + 1)), dma((pairs + 1, levels + 1))]
        + exchange_sems(chips),
        compiler_params=params(58, collective_id=1, has_side_effects=True),
        cost_estimate=cost(5 * 4 * count * count * width, 40 * count * width, 8 * count * count),
        name="attend_back_reduce",
    )(qkv, qkv, qkv, mixed, d_mixed, lse, d_attn, normed, mixed, moe_low, d_log, gain_rows, slot_rows)
    parts = sums.reshape(pairs, rows, 4, LANES)
    parts = jnp.transpose(parts, (1, 2, 0, 3)).reshape(rows, 4 * width)
    return d_qkv, parts[:, 0 : 3 * width], parts[:, 3 * width :], extra, back


def middle_kernel(experts, mixed_ref, w_out_ref, tok_ref, gain_ref, wr_ref, col_ref, h_ref, low_ref, gate_ref):
    rows = mixed_ref.shape[0]
    col = col_ref[...]
    first, second, valid = col[:, 2:3], col[:, 3:4], col[:, 4:5].astype(f32)
    attn = dot_nn(mixed_ref[...], w_out_ref[...])
    hidden = tok_ref[...].astype(f32) + valid * attn
    h_ref[...] = hidden
    inverse = lax.rsqrt(jnp.mean(hidden * hidden, axis=1, keepdims=True) + epsilon)
    low = (hidden * inverse * gain_ref[...]).astype(bf16)
    low_ref[...] = low
    logits = dot_nn(low, wr_ref[...])
    lane = iota((rows, LANES), 1)
    own = jnp.sum(jnp.where(lane == first, logits, 0.0), axis=1, keepdims=True)
    alt = jnp.sum(jnp.where(lane == second, logits, 0.0), axis=1, keepdims=True)
    gate0 = 1.0 / (1.0 + jnp.exp(alt - own))
    gate1 = 1.0 / (1.0 + jnp.exp(own - alt))
    gate_ref[...] = jnp.where(lane == 0, gate0, 0.0) + jnp.where(lane == 1, gate1, 0.0)


def middle(mixed, w_out, tokens, gain, wr, col, experts):
    count, width = mixed.shape
    rows = 256
    whole = lambda i: (0, 0)
    part = lambda i: (i, 0)
    return pl.pallas_call(
        functools.partial(middle_kernel, experts),
        out_shape=(
            jax.ShapeDtypeStruct((count, width), f32),
            jax.ShapeDtypeStruct((count, width), bf16),
            jax.ShapeDtypeStruct((count, LANES), f32),
        ),
        grid=(count // rows,),
        in_specs=[
            pl.BlockSpec((rows, width), part),
            pl.BlockSpec((width, width), whole),
            pl.BlockSpec((rows, width), part),
            pl.BlockSpec((1, width), whole),
            pl.BlockSpec((width, LANES), whole),
            pl.BlockSpec((rows, LANES), part),
        ],
        out_specs=(
            pl.BlockSpec((rows, width), part),
            pl.BlockSpec((rows, width), part),
            pl.BlockSpec((rows, LANES), part),
        ),
        compiler_params=params(40),
        cost_estimate=cost(2 * count * width * width, 12 * count * width),
        name="middle",
    )(mixed, w_out, tokens, gain.reshape(1, width), wr, col)


GELU_C = math.sqrt(2.0 / math.pi)


def expert_kernel(
    split, x_ref, g_ref, wg_ref, wu_ref, wd_ref, wr_ref, act_ref, dgp_ref, dup_ref, de_ref, part_ref, din_ref
):
    rows, width = x_ref.shape
    me = lax.axis_index("dp")
    expert, part = me // split, lax.rem(me, split)
    x = x_ref[...]
    lane = iota((rows, LANES), 1)
    logits = dot_nn(x, wr_ref[...])
    own = jnp.sum(jnp.where(lane == expert, logits, 0.0), axis=1, keepdims=True)
    other = g_ref[:, width:].astype(f32).astype(jnp.int32)
    alt = jnp.sum(jnp.where(lane == other, logits, 0.0), axis=1, keepdims=True)
    gate = 1.0 / (1.0 + jnp.exp(alt - own))
    d_rows = (g_ref[:, 0:width].astype(f32) * gate).astype(bf16)
    de_ref[...] = d_rows
    pre = dot_nn(x, wg_ref[...])
    up = dot_nn(x, wu_ref[...])
    d_hidden = dot_nt(d_rows, wd_ref[...])
    square = pre * pre
    bent = jnp.tanh(GELU_C * pre * (1.0 + 0.044715 * square))
    half = 0.5 * (1.0 + bent)
    gelu = pre * half
    slope = half + 0.5 * pre * (1.0 - bent * bent) * (GELU_C * (1.0 + 3 * 0.044715 * square))
    act = (gelu * up).astype(bf16)
    act_ref[...] = act
    dgp = (d_hidden * up * slope).astype(bf16)
    dup = (d_hidden * gelu).astype(bf16)
    dgp_ref[...] = dgp
    dup_ref[...] = dup
    pull = jnp.sum(act.astype(f32) * d_hidden, axis=1, keepdims=True)
    pull_high = pull.astype(bf16)
    pull_low = (pull - pull_high.astype(f32)).astype(bf16)
    part_ref[...] = dot_nn(act, wd_ref[...]).astype(bf16)
    din_ref[:, 0:width] = (dot_nt(dgp, wg_ref[...]) + dot_nt(dup, wu_ref[...])).astype(bf16)
    extra = jnp.where(lane == 2 * part, pull_high.astype(f32), 0.0)
    extra = extra + jnp.where(lane == 2 * part + 1, pull_low.astype(f32), 0.0)
    din_ref[:, width:] = extra.astype(bf16)


def expert_pass(x, g, wg, wu, wd, wr, split):
    count, width = x.shape
    ff = wg.shape[1]
    rows = 256
    whole = lambda i: (0, 0)
    part = lambda i: (i, 0)
    once = dict(pipeline_mode=pl.Buffered(1))
    return pl.pallas_call(
        functools.partial(expert_kernel, split),
        out_shape=(
            jax.ShapeDtypeStruct((count, ff), bf16),
            jax.ShapeDtypeStruct((count, ff), bf16),
            jax.ShapeDtypeStruct((count, ff), bf16),
            jax.ShapeDtypeStruct((count, width), bf16),
            jax.ShapeDtypeStruct((count, width), bf16),
            jax.ShapeDtypeStruct((count, width + LANES), bf16),
        ),
        grid=(count // rows,),
        in_specs=[
            pl.BlockSpec((rows, width), part),
            pl.BlockSpec((rows, width + LANES), part),
            pl.BlockSpec((width, ff), whole, **once),
            pl.BlockSpec((width, ff), whole, **once),
            pl.BlockSpec((ff, width), whole, **once),
            pl.BlockSpec((width, LANES), whole),
        ],
        out_specs=(
            pl.BlockSpec((rows, ff), part),
            pl.BlockSpec((rows, ff), part),
            pl.BlockSpec((rows, ff), part),
            pl.BlockSpec((rows, width), part),
            pl.BlockSpec((rows, width), part),
            pl.BlockSpec((rows, width + LANES), part),
        ),
        compiler_params=params(56),
        cost_estimate=cost(12 * count * width * ff, 2 * count * (3 * ff + 5 * width), count * ff),
        name="experts",
    )(x, g, wg, wu, wd, wr)


def expert_exchange_kernel(
    group, window, x_ref, g_ref, wg_hbm, wu_hbm, wd_hbm, wr_ref,
    act_ref, dgp_ref, dup_ref, de_ref, xs_ref, slot_ref, back_ref,
    xb, gb, ds, rd, pd, sp, rp, pp, st_act, st_dgp, st_dup, st_de, wg_ref, wu_ref, wd_ref,
    w_sem, x_send, x_recv, f_send, f_recv, g_own, g_send, g_recv,
    d_send, d_recv, p_send, p_recv, b_send, b_recv, o_sem, s_sem, l_sem,
):
    experts, capacity, width = x_ref.shape
    steps = experts // group
    pair = 2 * capacity
    half = experts // 2
    me = lax.axis_index("dp")
    chip, core = lax.div(me, 2), lax.rem(me, 2)
    mate = 2 * chip + 1 - core

    def bits(place):
        if isinstance(place, int):
            return half + place // 2 if place % 2 else place // 2
        odd = lax.rem(place, 2)
        return odd * half + lax.div(place, 2)

    def chip_at(place):
        return flip(chip, bits(place), experts)

    def remote(src, dst, send, recv, device):
        return pltpu.make_async_remote_copy(
            src_ref=src, dst_ref=dst, send_sem=send, recv_sem=recv, device_id=(device,), device_id_type=MESH
        )

    def own(buf, q, g):
        if isinstance(g, int):
            return buf.at[q, g * pair : g * pair + capacity]
        return buf.at[q, pl.ds(pl.multiple_of(g * pair, 16), capacity)]

    def theirs(buf, q, g):
        return buf.at[q, g * pair + capacity : (g + 1) * pair]

    def x_copy(place):
        if isinstance(place, int):
            q, g = place // group, place % group
        else:
            q, g = lax.div(place, group), lax.rem(place, group)
        peer = chip_at(place)
        return remote(x_ref.at[peer], own(xb, q, g), x_send.at[place], x_recv.at[place], 2 * peer + core)

    def x_arrival(q, g):
        place = q * group + g
        return remote(x_ref.at[chip], own(xb, q, g), x_send.at[place], x_recv.at[place], mate)

    def forward(q, g):
        place = q * group + g
        return remote(own(xb, q, g), theirs(xb, q, g), f_send.at[place], f_recv.at[place], mate)

    def g_mine(q, g):
        place = q * group + g
        return pltpu.make_async_copy(g_ref.at[chip_at(place)], own(gb, q, g), g_own.at[place])

    def g_mate(q, g):
        place = q * group + g
        return remote(g_ref.at[chip_at(place)], theirs(gb, q, g), g_send.at[place], g_recv.at[place], mate)

    def d_copy(q, g):
        place = q * group + g
        return remote(pd.at[lax.rem(q, 2), g], rd.at[place], d_send.at[place], d_recv.at[place], mate)

    def p_copy(q, g):
        place = q * group + g
        return remote(pp.at[lax.rem(q, 2), g], rp.at[place], p_send.at[place], p_recv.at[place], mate)

    def back_copy(q, g):
        place = q * group + g
        return remote(ds.at[place], back_ref.at[chip], b_send.at[place], b_recv.at[place], 2 * chip_at(place) + core)

    def slot_copy(q, g):
        place = q * group + g
        return pltpu.make_async_copy(sp.at[place], slot_ref.at[chip_at(place)], s_sem.at[place])

    def stage_copies(q):
        slot = lax.rem(q, 2)
        return (
            pltpu.make_async_copy(st_act.at[slot], act_ref.at[q], o_sem.at[slot, 0]),
            pltpu.make_async_copy(st_dgp.at[slot], dgp_ref.at[q], o_sem.at[slot, 1]),
            pltpu.make_async_copy(st_dup.at[slot], dup_ref.at[q], o_sem.at[slot, 2]),
            pltpu.make_async_copy(st_de.at[slot], de_ref.at[q], o_sem.at[slot, 3]),
        )

    def xs_copy(q):
        return pltpu.make_async_copy(xb.at[q], xs_ref.at[q], l_sem.at[1 + q])

    weights = [
        pltpu.make_async_copy(src, dst, w_sem.at[i])
        for i, (src, dst) in enumerate(((wg_hbm, wg_ref), (wu_hbm, wu_ref), (wd_hbm, wd_ref)))
    ]
    self_x = pltpu.make_async_copy(x_ref.at[chip], own(xb, 0, 0), l_sem.at[0])
    self_back = pltpu.make_async_copy(ds.at[0], back_ref.at[chip], l_sem.at[1 + steps])

    for copy in weights:
        copy.start()
    self_x.start()
    greet([2 * chip_at(place) + core for place in range(1, experts)] + [mate])
    for place in range(1, min(group + window, experts)):
        x_copy(place).start()
    for q in range(steps):
        for g in range(group):
            g_mine(q, g).start()
            g_mate(q, g).start()
    self_x.wait()
    forward(0, 0).start()
    for g in range(1, group):
        x_arrival(0, g).wait_recv()
        forward(0, g).start()
    for copy in weights:
        copy.wait()

    def finish(q):
        for g in range(group):
            place = q * group + g
            d_copy(q, g).wait_recv()
            ds[place] = (ds[place].astype(f32) + rd[place].astype(f32)).astype(bf16)
            if g == 0:

                @pl.when(q == 0)
                def _():
                    self_back.start()

                @pl.when(q > 0)
                def _():
                    back_copy(q, g).start()

            else:
                back_copy(q, g).start()
        for g in range(group):
            place = q * group + g
            p_copy(q, g).wait_recv()
            sp[place] = (sp[place].astype(f32) + rp[place].astype(f32)).astype(bf16)
            slot_copy(q, g).start()

    def step(q, carry):
        for g in range(group):
            g_mine(q, g).wait()
            g_mate(q, g).wait_recv()
            forward(q, g).wait_recv()
        xs_copy(q).start()
        x = xb[q]
        rows = group * pair
        lane = iota((rows, LANES), 1)
        logits = dot_nn(x, wr_ref[...])
        mine = jnp.sum(jnp.where(lane == chip, logits, 0.0), axis=1, keepdims=True)
        other = gb[q, :, width:].astype(f32).astype(jnp.int32)
        alt = jnp.sum(jnp.where(lane == other, logits, 0.0), axis=1, keepdims=True)
        gate = 1.0 / (1.0 + jnp.exp(alt - mine))
        d_rows = (gb[q, :, 0:width].astype(f32) * gate).astype(bf16)
        pre = dot_nn(x, wg_ref[...])
        up = dot_nn(x, wu_ref[...])
        d_hidden = dot_nt(d_rows, wd_ref[...])
        square = pre * pre
        bent = jnp.tanh(GELU_C * pre * (1.0 + 0.044715 * square))
        hill = 0.5 * (1.0 + bent)
        gelu = pre * hill
        slope = hill + 0.5 * pre * (1.0 - bent * bent) * (GELU_C * (1.0 + 3 * 0.044715 * square))
        act = (gelu * up).astype(bf16)
        dgp = (d_hidden * up * slope).astype(bf16)
        dup = (d_hidden * gelu).astype(bf16)
        pull = jnp.sum(act.astype(f32) * d_hidden, axis=1, keepdims=True)

        @pl.when(q >= 2)
        def _():
            for copy in stage_copies(q - 2):
                copy.wait()
            for g in range(group):
                d_copy(q - 2, g).wait_send()
                p_copy(q - 2, g).wait_send()

        slot = lax.rem(q, 2)
        st_act[slot] = act
        st_dgp[slot] = dgp
        st_dup[slot] = dup
        st_de[slot] = d_rows
        for copy in stage_copies(q):
            copy.start()

        @pl.when(q + 1 < steps)
        def _():
            for g in range(group):
                x_arrival(q + 1, g).wait_recv()
                forward(q + 1, g).start()
            for g in range(group):
                place = (q + 1) * group + window + g

                @pl.when(place < experts)
                def _():
                    x_copy(place).start()

        @pl.when(q >= 1)
        def _():
            finish(q - 1)

        d_in = (dot_nt(dgp, wg_ref[...]) + dot_nt(dup, wu_ref[...])).astype(bf16)
        pull_high = pull.astype(bf16).astype(f32)
        extra = jnp.where(lane == 2 * core, pull_high, 0.0)
        extra = (extra + jnp.where(lane == 2 * core + 1, pull - pull_high, 0.0)).astype(bf16)
        for g in range(group):
            place = q * group + g
            low, mid, high = g * pair, g * pair + capacity, (g + 1) * pair
            ds[place, :, 0:width] = d_in[low:mid]
            ds[place, :, width:] = extra[low:mid]
            pd[slot, g, :, 0:width] = d_in[mid:high]
            pd[slot, g, :, width:] = extra[mid:high]
            d_copy(q, g).start()
        partial = dot_nn(act, wd_ref[...]).astype(bf16)
        for g in range(group):
            place = q * group + g
            low, mid, high = g * pair, g * pair + capacity, (g + 1) * pair
            sp[place] = partial[low:mid]
            pp[slot, g] = partial[mid:high]
            p_copy(q, g).start()
        return carry

    lax.fori_loop(0, steps, step, 0)
    finish(steps - 1)
    for q in (steps - 2, steps - 1):
        for copy in stage_copies(q):
            copy.wait()
        for g in range(group):
            d_copy(q, g).wait_send()
            p_copy(q, g).wait_send()
    self_back.wait()
    for q in range(steps):
        xs_copy(q).wait()
        for g in range(group):
            place = q * group + g
            slot_copy(q, g).wait()
            forward(q, g).wait_send()
            g_mate(q, g).wait_send()
            if place:
                x_copy(place).wait_send()
                back_copy(q, g).wait()


def expert_exchange(x, g, wg, wu, wd, wr, group=2, window=4):
    experts, capacity, width = x.shape
    ff = wg.shape[1]
    steps = experts // group
    rows = 2 * capacity * group
    wide = width + LANES
    anywhere = pl.BlockSpec(memory_space=pl.ANY)
    vmem, dma = pltpu.VMEM, pltpu.SemaphoreType.DMA
    each = dma((experts,))
    count = rows * steps
    outs = pl.pallas_call(
        functools.partial(expert_exchange_kernel, group, window),
        out_shape=(
            jax.ShapeDtypeStruct((steps, rows, ff), bf16),
            jax.ShapeDtypeStruct((steps, rows, ff), bf16),
            jax.ShapeDtypeStruct((steps, rows, ff), bf16),
            jax.ShapeDtypeStruct((steps, rows, width), bf16),
            jax.ShapeDtypeStruct((steps, rows, width), bf16),
            jax.ShapeDtypeStruct((experts, capacity, width), bf16),
            jax.ShapeDtypeStruct((experts, capacity, wide), bf16),
        ),
        in_specs=[anywhere] * 5 + [pl.BlockSpec(memory_space=vmem)],
        out_specs=(anywhere,) * 7,
        scratch_shapes=[
            vmem((steps, rows, width), bf16),
            vmem((steps, rows, wide), bf16),
            vmem((experts, capacity, wide), bf16),
            vmem((experts, capacity, wide), bf16),
            vmem((2, group, capacity, wide), bf16),
            vmem((experts, capacity, width), bf16),
            vmem((experts, capacity, width), bf16),
            vmem((2, group, capacity, width), bf16),
            vmem((2, rows, ff), bf16),
            vmem((2, rows, ff), bf16),
            vmem((2, rows, ff), bf16),
            vmem((2, rows, width), bf16),
            vmem((width, ff), bf16),
            vmem((width, ff), bf16),
            vmem((ff, width), bf16),
            dma((3,)),
            each, each, each, each, each, each, each,
            each, each, each, each, each, each,
            dma((2, 4)),
            each,
            dma((2 + steps,)),
        ],
        compiler_params=params(60, collective_id=2, has_side_effects=True),
        cost_estimate=cost(12 * count * width * ff, 2 * count * (3 * ff + 5 * width), count * ff),
        name="experts",
    )(x, g, wg, wu, wd, wr)
    act, d_pre, d_up, d_rows, rows_in = (a.reshape(count, a.shape[-1]) for a in outs[:5])
    return act, d_pre, d_up, d_rows, rows_in, outs[5], outs[6]


def hot_rows(col, k, rows, slots):
    return jnp.where(iota((rows, slots), 1) == col[:, k : k + 1], 1.0, 0.0).astype(bf16)


def state_kernel(
    col_ref, gate_ref, din_ref, h_ref, og_ref, gain_ref, wr_ref, dstate_ref, dattn_ref, dlog_ref, gterm_ref
):
    rows, width = h_ref.shape
    slots = din_ref.shape[0]
    col = col_ref[...]
    valid = col[:, 4:5].astype(f32)
    hot0, hot1 = hot_rows(col, 0, rows, slots), hot_rows(col, 1, rows, slots)
    pulls = din_ref[:, width:]
    pull0 = jnp.sum(dot_nn(hot0, pulls), axis=1, keepdims=True)
    pull1 = jnp.sum(dot_nn(hot1, pulls), axis=1, keepdims=True)
    gathered = dot_nn(hot0 + hot1, din_ref[:, 0:width])
    gate0, gate1 = gate_ref[:, 0:1], gate_ref[:, 1:2]
    total = pull0 + pull1
    lane = iota((rows, LANES), 1)
    d_log = jnp.where(lane == col[:, 2:3], pull0 - gate0 * total, 0.0)
    d_log = d_log + jnp.where(lane == col[:, 3:4], pull1 - gate1 * total, 0.0)
    d_log = d_log.astype(bf16)
    dlog_ref[...] = d_log
    d_moe = gathered + dot_nt(d_log, wr_ref[...])
    hidden = h_ref[...]
    inverse = lax.rsqrt(jnp.mean(hidden * hidden, axis=1, keepdims=True) + epsilon)
    normal = hidden * inverse
    scaled = gain_ref[...] * d_moe
    share = jnp.mean(normal * scaled, axis=1, keepdims=True)
    d_state = og_ref[...].astype(f32) + inverse * (scaled - normal * share)
    dstate_ref[...] = d_state
    dattn_ref[...] = (valid * d_state).astype(bf16)
    term = jnp.sum((normal * d_moe).reshape(rows // 8, 8, width), axis=0)

    @pl.when(pl.program_id(0) == 0)
    def _():
        gterm_ref[...] = jnp.zeros_like(gterm_ref)

    gterm_ref[...] += term


def state_back(col, gates, din, hidden, out_grad, gain, wr):
    count, width = hidden.shape
    slots = din.shape[0]
    rows = 256
    whole = lambda i: (0, 0)
    part = lambda i: (i, 0)
    return pl.pallas_call(
        state_kernel,
        out_shape=(
            jax.ShapeDtypeStruct((count, width), f32),
            jax.ShapeDtypeStruct((count, width), bf16),
            jax.ShapeDtypeStruct((count, LANES), bf16),
            jax.ShapeDtypeStruct((8, width), f32),
        ),
        grid=(count // rows,),
        in_specs=[
            pl.BlockSpec((rows, LANES), part),
            pl.BlockSpec((rows, LANES), part),
            pl.BlockSpec((slots, width + LANES), whole),
            pl.BlockSpec((rows, width), part),
            pl.BlockSpec((rows, width), part),
            pl.BlockSpec((1, width), whole),
            pl.BlockSpec((width, LANES), whole),
        ],
        out_specs=(
            pl.BlockSpec((rows, width), part),
            pl.BlockSpec((rows, width), part),
            pl.BlockSpec((rows, LANES), part),
            pl.BlockSpec((8, width), whole),
        ),
        compiler_params=params(48),
        cost_estimate=cost(2 * slots * count * width, 14 * count * width),
        name="state_back",
    )(col, gates, din, hidden, out_grad, gain.reshape(1, width), wr)


def block_out_kernel(col_ref, gate_ref, rows_ref, h_ref, out_ref):
    rows, width = h_ref.shape
    slots = rows_ref.shape[0]
    col = col_ref[...]
    pick0 = dot_nn(hot_rows(col, 0, rows, slots), rows_ref[...])
    pick1 = dot_nn(hot_rows(col, 1, rows, slots), rows_ref[...])
    out_ref[...] = (h_ref[...] + gate_ref[:, 0:1] * pick0 + gate_ref[:, 1:2] * pick1).astype(bf16)


def make_block_out(col, gates, slot_rows, hidden):
    count, width = hidden.shape
    slots = slot_rows.shape[0]
    rows = 256
    whole = lambda i: (0, 0)
    part = lambda i: (i, 0)
    return pl.pallas_call(
        block_out_kernel,
        out_shape=jax.ShapeDtypeStruct((count, width), bf16),
        grid=(count // rows,),
        in_specs=[
            pl.BlockSpec((rows, LANES), part),
            pl.BlockSpec((rows, LANES), part),
            pl.BlockSpec((slots, width), whole),
            pl.BlockSpec((rows, width), part),
        ],
        out_specs=pl.BlockSpec((rows, width), part),
        compiler_params=params(40),
        cost_estimate=cost(4 * slots * count * width, 9 * count * width),
        name="block_out",
    )(col, gates, slot_rows, hidden)


def input_kernel(d_ref, w_ref, tok_ref, gain_ref, dstate_ref, grad_ref):
    rows, width = tok_ref.shape
    d_normed = dot_nt(d_ref[0], w_ref[:, 0:width])
    for i in range(1, 3):
        d_normed = d_normed + dot_nt(d_ref[i], w_ref[:, i * width : (i + 1) * width])
    values = tok_ref[...].astype(f32)
    inverse = lax.rsqrt(jnp.mean(values * values, axis=1, keepdims=True) + epsilon)
    normal = values * inverse
    scaled = gain_ref[...] * d_normed
    share = jnp.mean(normal * scaled, axis=1, keepdims=True)
    grad_ref[...] = dstate_ref[...] + inverse * (scaled - normal * share)


def input_back(d_qkv, w_qkv, tokens, gain, d_state):
    count, width = tokens.shape
    rows = 256
    whole = lambda i: (0, 0)
    part = lambda i: (i, 0)
    return pl.pallas_call(
        input_kernel,
        out_shape=jax.ShapeDtypeStruct((count, width), f32),
        grid=(count // rows,),
        in_specs=[
            pl.BlockSpec((3, rows, width), lambda i: (0, i, 0)),
            pl.BlockSpec((width, 3 * width), whole),
            pl.BlockSpec((rows, width), part),
            pl.BlockSpec((1, width), whole),
            pl.BlockSpec((rows, width), part),
        ],
        out_specs=pl.BlockSpec((rows, width), part),
        compiler_params=params(48),
        cost_estimate=cost(6 * count * width * width, 22 * count * width),
        name="input_back",
    )(d_qkv, w_qkv, tokens, gain.reshape(1, width), d_state)


def shards(
    tokens,
    lengths,
    expert_ids,
    slot_order,
    gain_attn,
    w_qkv,
    w_out,
    gain_moe,
    w_router,
    w_gate,
    w_up,
    w_down,
    out_grad,
):
    tok_dev, width = tokens.shape
    n_dev = lax.axis_size("dp")
    experts = w_router.shape[1]
    split = n_dev // experts
    capacity = split * (5 * tok_dev // (4 * n_dev))
    slots = experts * capacity
    me = lax.axis_index("dp")
    part = lax.rem(me, split)
    same_part = [[e * split + p for e in range(experts)] for p in range(split)]
    same_expert = [[e * split + p for p in range(split)] for e in range(experts)]
    swap = [(d, d ^ 1) for d in range(n_dev)]

    def across(blocks):
        return lax.all_to_all(blocks, "dp", 0, 0, axis_index_groups=same_part, tiled=True)

    def share(rows):
        if split == 2:
            return jnp.concatenate([rows, lax.ppermute(rows, "dp", swap)], axis=0)
        return lax.all_gather(rows, "dp", axis_index_groups=same_expert, tiled=True)

    def settle(pieces):
        if split == 2:
            theirs = lax.ppermute(pieces[1], "dp", swap)
            return (pieces[0].astype(f32) + theirs.astype(f32)).astype(bf16)
        got = lax.all_to_all(pieces, "dp", 0, 0, axis_index_groups=same_expert, tiled=True)
        return jnp.sum(got.astype(f32), axis=0).astype(bf16)

    def send_in(rows):
        return share(across(rows.reshape(experts, capacity, -1)).reshape(slots, -1))

    def send_back(rows):
        summed = settle(rows.reshape(split, slots, -1))
        return across(summed.reshape(experts, capacity, -1)).reshape(slots, -1)

    def reduce_rows(term):
        pieces = term.reshape(experts, split, -1, term.shape[-1])
        if split == 2:
            mine = lax.dynamic_index_in_dim(pieces, part, 1, keepdims=False)
            theirs = lax.dynamic_index_in_dim(pieces, 1 - part, 1, keepdims=False)
            theirs = lax.ppermute(theirs.astype(bf16), "dp", swap)
            summed = (mine + theirs.astype(f32)).astype(bf16)
        else:
            pieces = jnp.moveaxis(pieces, 1, 0).astype(bf16)
            got = lax.all_to_all(pieces, "dp", 0, 0, axis_index_groups=same_expert, tiled=True)
            summed = jnp.sum(got.astype(f32), axis=0).astype(bf16)
        return jnp.sum(across(summed).astype(f32), axis=0)

    wr = jnp.pad(w_router, ((0, 0), (0, LANES - experts)))
    col, row = make_slots(lengths, expert_ids, slot_order, experts, capacity)
    direct = split == 2 and experts & (experts - 1) == 0 and experts >= 4
    grad_out = dispatch_grad(row, out_grad, slots)

    token_vals = tokens.astype(f32)
    inverse_attn = lax.rsqrt(jnp.mean(token_vals * token_vals, axis=-1, keepdims=True) + epsilon)
    normed_low = (token_vals * inverse_attn * gain_attn).astype(bf16)
    qkv = jnp.dot(normed_low, w_qkv, preferred_element_type=f32).astype(bf16)
    if direct:
        mixed, lse, grad_in = attend(qkv, grad_out.reshape(experts, capacity, -1))
    else:
        mixed, lse = attend(qkv)
        grad_in = send_in(grad_out)
    hidden, moe_low, gates = middle(mixed, w_out, tokens, gain_moe, wr, col, experts)

    rows_out = dispatch(row, moe_low, slots)
    if direct:
        act, d_pre, d_up, d_rows, rows_in, slot_part, d_in_back = expert_exchange(
            rows_out.reshape(experts, capacity, -1), grad_in, w_gate[0], w_up[0], w_down[0], wr
        )
        d_in_back = d_in_back.reshape(slots, -1)
    else:
        rows_in = send_in(rows_out)
        act, d_pre, d_up, d_rows, partial_out, d_in = expert_pass(
            rows_in, grad_in, w_gate[0], w_up[0], w_down[0], wr, split
        )
        d_in_back = send_back(d_in)
        slot_out = send_back(partial_out)

    d_state, d_attn, d_log, gain_moe_rows = state_back(
        col, gates, d_in_back, hidden, out_grad, gain_moe, wr
    )
    d_mixed = dot_nt(d_attn, w_out).astype(bf16)
    if direct:
        d_qkv, qkv_sum, out_rows, extra, slot_out = attend_back_reduce(
            qkv, mixed, d_mixed, lse, d_attn, normed_low, moe_low, d_log, gain_moe_rows, slot_part, n_dev
        )
        slot_out = slot_out.reshape(slots, -1)
        router_sum, gain_moe_sum = extra[:, 0:experts], extra[:, 64]
    else:
        d_qkv = attend_back(qkv, mixed, d_mixed, lse)
        lane = jnp.arange(LANES, dtype=jnp.int32)[None, :]
        gain_moe_term = jnp.sum(gain_moe_rows, axis=0)
        extra = jnp.where(lane == experts, gain_moe_term[:, None], dot_tn(moe_low, d_log))
        early = reduce_rows(jnp.concatenate([dot_tn(mixed, d_attn), extra], axis=1))
        out_rows, router_sum, gain_moe_sum = (
            early[:, 0:width], early[:, width : width + experts], early[:, width + experts]
        )
        qkv_sum = reduce_rows(jnp.concatenate([dot_tn(normed_low, d_qkv[i]) for i in range(3)], axis=1))
    tokens_grad = input_back(d_qkv, w_qkv, tokens, gain_attn, d_state)
    my_rows = width // n_dev
    weight_rows = lax.dynamic_slice_in_dim(w_qkv, me * my_rows, my_rows, 0).astype(f32)
    gain_attn_sum = jnp.sum(weight_rows * qkv_sum, axis=1) / lax.dynamic_slice_in_dim(gain_attn, me * my_rows, my_rows, 0)

    down_grad = dot_tn(act, d_rows)
    gate_grad = dot_tn(rows_in, d_pre)
    up_grad = dot_tn(rows_in, d_up)
    block_out = make_block_out(col, gates, slot_out, hidden)
    return (
        block_out,
        tokens_grad,
        gain_attn_sum,
        qkv_sum,
        out_rows,
        gain_moe_sum,
        router_sum,
        gate_grad[None],
        up_grad[None],
        down_grad[None],
    )


def solution(mesh):
    rows, one = P("dp", None), P("dp")
    cube = P("dp", None, None)
    return jax.shard_map(
        shards,
        mesh=mesh,
        in_specs=(rows, one, rows, rows, P(), P(), P(), P(), P(), cube, cube, cube, rows),
        out_specs=(rows, rows, one, rows, rows, one, rows, cube, cube, cube),
        check_vma=False,
    )
```

```python
import functools
import math

import jax
import jax.numpy as jnp
from jax import lax
from jax.experimental import pallas as pl
from jax.experimental.pallas import tpu as pltpu
from jax.sharding import PartitionSpec as P

HEADS = 16
HEAD_DIM = 64
LEN = 1024
LANES = 128
MIB = 1 << 20

epsilon = 1e-06
mask_fill = -1e30
f32 = jnp.float32
bf16 = jnp.bfloat16


def dot_nn(left, right, **kw):
    return lax.dot_general(left, right, (((1,), (0,)), ((), ())), preferred_element_type=f32, **kw)


def dot_nt(left, right, **kw):
    return lax.dot_general(left, right, (((1,), (1,)), ((), ())), preferred_element_type=f32, **kw)


def dot_tn(left, right, **kw):
    return lax.dot_general(left, right, (((0,), (0,)), ((), ())), preferred_element_type=f32, **kw)


def iota(shape, dim):
    return lax.broadcasted_iota(jnp.int32, shape, dim)


def params(mib, **kw):
    return pltpu.CompilerParams(vmem_limit_bytes=mib * MIB, **kw)


def cost(flops, nbytes, trans=0):
    return pl.CostEstimate(flops=int(flops), bytes_accessed=int(nbytes), transcendentals=int(trans))


def slot_kernel(capacity, experts, len_ref, ids_ref, rank_col_ref, rank_row_ref, col_ref, row_ref):
    count = ids_ref.shape[0]
    length = len_ref[0]
    ids = ids_ref[...]
    first, second = ids[:, 0:1], ids[:, 1:2]
    lane = iota((count, LANES), 1)
    place = iota((count, LANES), 0)
    hot0 = (lane == first) & (lane < experts)
    hot1 = (lane == second + experts) & (lane >= experts) & (lane < 2 * experts)
    valid = place < length
    hot = jnp.where((hot0 | hot1) & valid, 1.0, 0.0).astype(bf16)
    before = (rank_row_ref[...] < rank_col_ref[...]).astype(f32).astype(bf16)
    counts = dot_nn(before, hot)
    shifted = (lane == first + experts) & (lane >= experts) & (lane < 2 * experts) & valid
    totals = jnp.sum(jnp.where(shifted, 1.0, 0.0), axis=0, keepdims=True)
    slot0 = jnp.sum(jnp.where(hot0, counts, 0.0), axis=1, keepdims=True).astype(jnp.int32)
    slot1 = jnp.sum(jnp.where(hot1, counts + totals, 0.0), axis=1, keepdims=True).astype(jnp.int32)
    sentinel = experts * capacity
    ok = valid[:, 0:1]
    flat0 = jnp.where(ok & (slot0 < capacity), first * capacity + slot0, sentinel)
    flat1 = jnp.where(ok & (slot1 < capacity), second * capacity + slot1, sentinel)
    col = jnp.where(lane == 0, flat0, 0) + jnp.where(lane == 1, flat1, 0)
    col = col + jnp.where(lane == 2, first, 0) + jnp.where(lane == 3, second, 0)
    col = col + jnp.where(lane == 4, ok.astype(jnp.int32), 0)
    col_ref[...] = col
    row_ref[...] = jnp.transpose(col.astype(f32))[0:8, :].astype(jnp.int32)


def make_slots(lengths, expert_ids, slot_order, experts, capacity):
    count = expert_ids.shape[0]
    return pl.pallas_call(
        functools.partial(slot_kernel, capacity, experts),
        out_shape=(
            jax.ShapeDtypeStruct((count, LANES), jnp.int32),
            jax.ShapeDtypeStruct((8, count), jnp.int32),
        ),
        in_specs=[
            pl.BlockSpec(memory_space=pltpu.SMEM),
            pl.BlockSpec(memory_space=pltpu.VMEM),
            pl.BlockSpec(memory_space=pltpu.VMEM),
            pl.BlockSpec(memory_space=pltpu.VMEM),
        ],
        out_specs=(pl.BlockSpec(memory_space=pltpu.VMEM), pl.BlockSpec(memory_space=pltpu.VMEM)),
        compiler_params=params(40),
        cost_estimate=cost(2 * count * count * LANES, 4 * count * LANES),
        name="slots",
    )(lengths, expert_ids, slot_order.reshape(count, 1), slot_order)


def dispatch_kernel(rows, row_ref, data_ref, out_ref):
    count = data_ref.shape[0]
    slot = pl.program_id(0) * rows + iota((rows, count), 0)
    hot = (slot == row_ref[0:1, :]) | (slot == row_ref[1:2, :])
    out_ref[...] = dot_nn(jnp.where(hot, 1.0, 0.0).astype(bf16), data_ref[...]).astype(bf16)


def dispatch(row, data, slots):
    count, width = data.shape
    rows = 256
    return pl.pallas_call(
        functools.partial(dispatch_kernel, rows),
        out_shape=jax.ShapeDtypeStruct((slots, width), bf16),
        grid=(slots // rows,),
        in_specs=[
            pl.BlockSpec((8, count), lambda i: (0, 0)),
            pl.BlockSpec((count, width), lambda i: (0, 0)),
        ],
        out_specs=pl.BlockSpec((rows, width), lambda i: (i, 0)),
        compiler_params=params(40),
        cost_estimate=cost(2 * slots * count * width, 2 * (slots + count) * width),
        name="dispatch",
    )(row, data)


def dispatch_grad_kernel(rows, row_ref, data_ref, out_ref):
    count, width = data_ref.shape
    slot = pl.program_id(0) * rows + iota((rows, count), 0)
    hot0 = slot == row_ref[0:1, :]
    hot1 = slot == row_ref[1:2, :]
    both = jnp.where(hot0 | hot1, 1.0, 0.0).astype(bf16)
    out_ref[:, 0:width] = dot_nn(both, data_ref[...]).astype(bf16)
    other = jnp.where(hot0, row_ref[3:4, :], 0) + jnp.where(hot1, row_ref[2:3, :], 0)
    other = jnp.sum(other.astype(f32), axis=1, keepdims=True)
    out_ref[:, width:] = jnp.broadcast_to(other, (rows, LANES)).astype(bf16)


def dispatch_grad(row, data, slots):
    count, width = data.shape
    rows = 256
    return pl.pallas_call(
        functools.partial(dispatch_grad_kernel, rows),
        out_shape=jax.ShapeDtypeStruct((slots, width + LANES), bf16),
        grid=(slots // rows,),
        in_specs=[
            pl.BlockSpec((8, count), lambda i: (0, 0)),
            pl.BlockSpec((count, width), lambda i: (0, 0)),
        ],
        out_specs=pl.BlockSpec((rows, width + LANES), lambda i: (i, 0)),
        compiler_params=params(40),
        cost_estimate=cost(2 * slots * count * width, 2 * (slots + count) * width),
        name="dispatch_grad",
    )(row, data)


def dispatch_pair_kernel(capacity, row_ref, data_ref, out_ref, other_ref):
    count = data_ref.shape[0]
    rows = out_ref.shape[0]
    slot = pl.program_id(0) * rows + iota((rows, count), 0)
    hot0 = jnp.where(slot == row_ref[0:1, :], 1.0, 0.0).astype(bf16)
    hot1 = jnp.where(slot == row_ref[1:2, :], 1.0, 0.0).astype(bf16)
    out_ref[...] = dot_nn(hot0 + hot1, data_ref[...]).astype(bf16)
    ids = row_ref[...].astype(f32).astype(bf16)
    other = dot_nt(ids, hot0)[3:4] + dot_nt(ids, hot1)[2:3]
    other_ref[...] = jnp.zeros_like(other_ref)
    for i in range(other_ref.shape[0]):
        mine = other[:, i * capacity : (i + 1) * capacity]
        other_ref[i, :, 0:capacity] = jnp.broadcast_to(mine, (8, capacity))


def dispatch_pair(row, data, experts, capacity):
    count, width = data.shape
    each = 2
    return pl.pallas_call(
        functools.partial(dispatch_pair_kernel, capacity),
        out_shape=(
            jax.ShapeDtypeStruct((experts * capacity, width), bf16),
            jax.ShapeDtypeStruct((experts, 8, LANES), f32),
        ),
        grid=(experts // each,),
        in_specs=[
            pl.BlockSpec((8, count), lambda i: (0, 0)),
            pl.BlockSpec((count, width), lambda i: (0, 0)),
        ],
        out_specs=(
            pl.BlockSpec((each * capacity, width), lambda i: (i, 0)),
            pl.BlockSpec((each, 8, LANES), lambda i: (i, 0, 0)),
        ),
        compiler_params=params(40),
        cost_estimate=cost(2 * experts * capacity * count * width, 2 * (experts * capacity + count) * width),
        name="dispatch_pair",
    )(row, data)


MESH = pl.DeviceIdType.MESH


def flip(chip, bits, experts):
    out, b = chip, 1
    while b < experts:
        if isinstance(bits, int):
            out = out + (bits // b % 2) * (b - 2 * b * lax.rem(lax.div(chip, b), 2))
        else:
            mine, theirs = lax.rem(lax.div(chip, b), 2), lax.rem(lax.div(bits, b), 2)
            out = out + b * theirs * (1 - 2 * mine)
        b *= 2
    return out


def greet(peers):
    barrier = pltpu.get_barrier_semaphore()
    for peer in peers:
        pl.semaphore_signal(barrier, inc=1, device_id=(peer,), device_id_type=MESH)
    pl.semaphore_wait(barrier, len(peers))


def exchange_copies(src, dst, send_sem, recv_sem, local_sem):
    experts = src.shape[0]
    me = lax.axis_index("dp")
    chip, core = lax.div(me, 2), lax.rem(me, 2)
    copies = [pltpu.make_async_copy(src.at[chip], dst.at[chip], local_sem)]
    peers = []
    half = experts // 2
    for place in range(1, experts):
        step = half + place // 2 if place % 2 else place // 2
        peer = flip(chip, step, experts)
        peers.append(2 * peer + core)
        copies.append(
            pltpu.make_async_remote_copy(
                src_ref=src.at[peer],
                dst_ref=dst.at[chip],
                send_sem=send_sem.at[step],
                recv_sem=recv_sem.at[step],
                device_id=(2 * peer + core,),
                device_id_type=MESH,
            )
        )
    return peers, copies


def exchange_sems(experts):
    return [
        pltpu.SemaphoreType.DMA((experts,)),
        pltpu.SemaphoreType.DMA((experts,)),
        pltpu.SemaphoreType.DMA,
    ]


def riding(body, n_in, n_out, n_ride):
    def kernel(*refs):
        ins, srcs = refs[:n_in], refs[n_in : n_in + n_ride]
        outs = refs[n_in + n_ride : n_in + n_ride + n_out]
        dsts = refs[n_in + n_ride + n_out : n_in + 2 * n_ride + n_out]
        rest, sems = refs[n_in + 2 * n_ride + n_out : -3 * n_ride], refs[-3 * n_ride :]
        copies = []
        for r in range(n_ride):
            peers, more = exchange_copies(srcs[r], dsts[r], *sems[3 * r : 3 * r + 3])
            copies += more

        @pl.when(pl.program_id(0) == 0)
        def _():
            greet(peers)
            for copy in copies:
                copy.start()

        body(*ins, *outs, *rest)

        @pl.when(pl.program_id(0) == pl.num_programs(0) - 1)
        def _():
            for copy in copies:
                copy.wait()

    return kernel


SCALE2 = math.log2(math.e) / math.sqrt(HEAD_DIM)
QB = 256


def attend_kernel(q_ref, k_ref, v_ref, mixed_ref, lse_ref):
    lane = iota((QB, LANES), 1)
    wide = jnp.concatenate([v_ref[...], jnp.ones_like(v_ref)], axis=1)
    causal = iota((QB, QB), 1) <= iota((QB, QB), 0)
    for block in range(LEN // QB):
        start, stop = block * QB, (block + 1) * QB
        query = q_ref[start:stop, :]
        halves, norms = [], []
        for head in range(2):
            mine = (lane // HEAD_DIM) == head
            scores = dot_nt(jnp.where(mine, query, jnp.zeros_like(query)), k_ref[0:stop, :])
            tail = jnp.where(causal, scores[:, start:stop], mask_fill)
            scores = tail if block == 0 else jnp.concatenate([scores[:, 0:start], tail], axis=1)
            highest = jnp.max(scores, axis=1, keepdims=True) * SCALE2
            raised = jnp.exp2(scores * SCALE2 - highest)
            out = dot_nn(raised.astype(bf16), wide[0:stop, :])
            summed = out[:, LANES:]
            halves.append(out[:, 0:LANES] / summed)
            norms.append(highest + jnp.log2(summed))
        mixed_ref[start:stop, :] = jnp.where(lane < HEAD_DIM, halves[0], halves[1]).astype(bf16)
        norm = jnp.where(lane == 0, norms[0], norms[1])
        lse_ref[0, :, start:stop] = jnp.transpose(norm)[0:8, :]


def attend(qkv, blocks=()):
    count, width3 = qkv.shape
    width = width3 // 3
    pairs = width // LANES
    in_specs = [
        pl.BlockSpec((count, LANES), lambda i: (0, i)),
        pl.BlockSpec((count, LANES), lambda i: (0, i + pairs)),
        pl.BlockSpec((count, LANES), lambda i: (0, i + 2 * pairs)),
    ]
    out_specs = [
        pl.BlockSpec((count, LANES), lambda i: (0, i)),
        pl.BlockSpec((1, 8, count), lambda i: (i, 0, 0)),
    ]
    out_shape = [
        jax.ShapeDtypeStruct((count, width), bf16),
        jax.ShapeDtypeStruct((pairs, 8, count), f32),
    ]
    body, args, scratch, extra = attend_kernel, [qkv, qkv, qkv], [], {}
    if blocks:
        body = riding(attend_kernel, len(in_specs), len(out_specs), len(blocks))
        for array in blocks:
            in_specs.append(pl.BlockSpec(memory_space=pl.ANY))
            out_specs.append(pl.BlockSpec(memory_space=pl.ANY))
            out_shape.append(jax.ShapeDtypeStruct(array.shape, array.dtype))
            args.append(array)
            scratch = scratch + exchange_sems(array.shape[0])
        extra = dict(collective_id=0, has_side_effects=True)
    return pl.pallas_call(
        body,
        out_shape=out_shape,
        grid=(pairs,),
        in_specs=in_specs,
        out_specs=out_specs,
        scratch_shapes=scratch,
        compiler_params=params(40, **extra),
        cost_estimate=cost(2 * 4 * count * count * width, 8 * count * width, 8 * count * count),
        name="attend",
    )(*args)


def attend_back_kernel(q_ref, k_ref, v_ref, o_ref, do_ref, lse_ref, out_ref, dk_sc, dv_sc):
    lane = iota((QB, LANES), 1)
    keep = iota((QB, QB), 0) <= iota((QB, QB), 1)
    dk_sc[...] = jnp.zeros_like(dk_sc)
    dv_sc[...] = jnp.zeros_like(dv_sc)
    sub = iota((8, LANES), 0)
    picks = jnp.where(iota((8, LANES), 1) // HEAD_DIM == sub, 1.0, 0.0)
    low = (iota((LEN, LANES), 1) // HEAD_DIM) == 0
    key = k_ref[...]
    none = jnp.zeros_like(key)
    keys = (jnp.where(low, key, none), jnp.where(low, none, key))
    for block in range(LEN // QB):
        start, stop = block * QB, (block + 1) * QB
        query = q_ref[start:stop, :]
        d_out = do_ref[start:stop, :]
        product = d_out.astype(f32) * o_ref[start:stop, :].astype(f32)
        delta = dot_nt(picks, product, precision=lax.Precision.HIGHEST)
        d_query = jnp.zeros((QB, LANES), f32)
        for head in range(2):
            mine = (lane // HEAD_DIM) == head
            query_one = jnp.where(mine, query, jnp.zeros_like(query))
            d_one = jnp.where(mine, d_out, jnp.zeros_like(d_out))
            scores = dot_nt(k_ref[0:stop, :], query_one)
            tail = jnp.where(keep, scores[start:stop, :], mask_fill)
            scores = tail if block == 0 else jnp.concatenate([scores[0:start, :], tail], axis=0)
            probs = jnp.exp2(scores * SCALE2 - lse_ref[0, head : head + 1, start:stop])
            d_probs = dot_nt(v_ref[0:stop, :], d_one)
            d_scores = (probs * (d_probs - delta[head : head + 1, :])).astype(bf16)
            dv_sc[0:stop, :] += dot_nn(probs.astype(bf16), d_one)
            dk_sc[0:stop, :] += dot_nn(d_scores, query_one)
            d_query = d_query + dot_tn(d_scores, keys[head][0:stop, :])
        out_ref[0, start:stop, :] = (d_query * (1.0 / math.sqrt(HEAD_DIM))).astype(bf16)
    out_ref[1, :, :] = (dk_sc[...] * (1.0 / math.sqrt(HEAD_DIM))).astype(bf16)
    out_ref[2, :, :] = dv_sc[...].astype(bf16)


def attend_back(qkv, mixed, d_mixed, lse):
    count, width = mixed.shape
    pairs = width // LANES
    return pl.pallas_call(
        attend_back_kernel,
        out_shape=jax.ShapeDtypeStruct((3, count, width), bf16),
        grid=(pairs,),
        in_specs=[
            pl.BlockSpec((count, LANES), lambda i: (0, i)),
            pl.BlockSpec((count, LANES), lambda i: (0, i + pairs)),
            pl.BlockSpec((count, LANES), lambda i: (0, i + 2 * pairs)),
            pl.BlockSpec((count, LANES), lambda i: (0, i)),
            pl.BlockSpec((count, LANES), lambda i: (0, i)),
            pl.BlockSpec((1, 8, count), lambda i: (i, 0, 0)),
        ],
        out_specs=pl.BlockSpec((3, count, LANES), lambda i: (0, 0, i)),
        scratch_shapes=[pltpu.VMEM((count, LANES), f32), pltpu.VMEM((count, LANES), f32)],
        compiler_params=params(40),
        cost_estimate=cost(5 * 4 * count * count * width, 16 * count * width, 8 * count * count),
        name="attend_back",
    )(qkv, qkv, qkv, mixed, d_mixed, lse)


RIDE_PER_TURN = 2


def back_reduce_kernel(
    chips,
    q_ref, k_ref, v_ref, o_ref, do_ref, lse_ref, datt_ref, norm_ref, mix_ref, moe_ref, dlog_ref, gm_ref, slot_ref,
    out_ref, sum_ref, extra_ref, back_ref,
    dk_sc, dv_sc, norm_t, mix_t, right, terms, firsts, sums, half0, half1, half2, half3, s_send, s_recv,
    *ride_sems,
):
    halves = (half0, half1, half2, half3)
    levels = chips.bit_length() - 1
    count = k_ref.shape[0]
    width = norm_ref.shape[1]
    rows = terms.shape[3]
    turn = pl.program_id(0)
    pairs = sum_ref.shape[0]
    me = lax.axis_index("dp")
    chip, core = lax.div(me, 2), lax.rem(me, 2)
    mate = 2 * chip + 1 - core
    order0 = [1 << b for b in range(levels)]
    order1 = list(order0)
    order1[0], order1[1] = order0[1], order0[0]
    order0[2:] = order0[2:][::-1]

    def bit(mask):
        return lax.rem(lax.div(chip, mask), 2)

    own, peers = [], []
    for level in range(levels):
        b0, b1 = bit(order0[level]), bit(order1[level])
        own.append(b0 + core * (b1 - b0))
        p0 = order0[level] * (1 - 2 * b0)
        p1 = order1[level] * (1 - 2 * b1)
        peers.append(2 * (chip + p0 + core * (p1 - p0)) + core)
    bases = [0]
    for level in range(levels):
        bases.append(bases[-1] + own[level] * (chips >> (level + 1)))

    def remote(src, dst, c, level, device):
        return pltpu.make_async_remote_copy(
            src_ref=src, dst_ref=dst, send_sem=s_send.at[c, level], recv_sem=s_recv.at[c, level],
            device_id=(device,), device_id_type=MESH,
        )

    def cols(c):
        return pl.ds(0, LANES) if isinstance(c, int) else slice(None)

    def swap(c):
        return remote(
            terms.at[c, :, 1 - core, :, cols(c)], firsts.at[c, :, :, cols(c)], c, levels, mate
        )

    def send(c, level):
        span = chips >> (level + 1)
        start = bases[level] + (1 - own[level]) * span
        return remote(
            sums.at[c, pl.ds(start, span), :, cols(c)], halves[level].at[c, :, :, cols(c)], c, level, peers[level]
        )

    def fold_swap(c):
        swap(c).wait_recv()
        for b in range(chips):
            places = []
            for order in (order0, order1):
                place = 0
                for level in range(levels):
                    place += (b // order[level] % 2) * (chips >> (level + 1))
                places.append(place)
            at = places[0] + core * (places[1] - places[0])
            total = terms[c, b, core, :, cols(c)].astype(f32) + firsts[c, b, :, cols(c)].astype(f32)
            sums[c, at, :, cols(c)] = total.astype(bf16)

    def fold(c, level):
        send(c, level).wait()
        for t in range(chips >> (level + 1)):
            at = bases[level + 1] + t
            total = sums[c, at, :, cols(c)].astype(f32) + halves[level][c, t, :, cols(c)].astype(f32)
            if level < levels - 1:
                sums[c, at, :, cols(c)] = total.astype(bf16)
            elif isinstance(c, int):
                extra_ref[...] = total
            else:
                sum_ref[c] = total

    def stage(c, s):
        if s == 1:
            fold_swap(c)
        else:
            fold(c, s - 2)
        if s - 1 < levels:
            send(c, s - 1).start()

    riders, ride = exchange_copies(slot_ref, back_ref, *ride_sems)
    span = 256
    per = span // (2 * rows)

    @pl.when(turn == 0)
    def _():
        greet([mate] + riders)
        norm_t[...] = jnp.transpose(norm_ref[...])
        mix_t[...] = jnp.transpose(mix_ref[...])
        for row in range(0, width, span):
            extra = dot_tn(moe_ref[:, row : row + span], dlog_ref[...])
            gain = jnp.transpose(jnp.sum(gm_ref[:, row : row + span], axis=0, keepdims=True))
            extra = extra + jnp.where(iota(extra.shape, 1) == 64, gain, 0.0)
            at = row // (2 * rows)
            terms[pairs, at : at + per, :, :, 0:LANES] = extra.astype(bf16).reshape(per, 2, rows, LANES)
        swap(pairs).start()

    for s in range(levels + 1, 0, -1):
        c = turn - s

        @pl.when((c >= 0) & (c < pairs))
        def _():
            stage(c, s)

        @pl.when(c == 0)
        def _():
            stage(pairs, s)

    @pl.when(turn < pairs)
    def _():
        attend_back_kernel(q_ref, k_ref, v_ref, o_ref, do_ref, lse_ref, out_ref, dk_sc, dv_sc)
        for i in range(3):
            right[:, i * LANES : (i + 1) * LANES] = out_ref[i]
        for row in range(0, width, span):
            qkv_rows = dot_nn(norm_t[row : row + span, :], right[...])
            out_rows = dot_nn(mix_t[row : row + span, :], datt_ref[...])
            at = row // (2 * rows)
            terms[turn, at : at + per, :, :, 0 : 3 * LANES] = (
                qkv_rows.astype(bf16).reshape(per, 2, rows, 3 * LANES)
            )
            terms[turn, at : at + per, :, :, 3 * LANES :] = out_rows.astype(bf16).reshape(per, 2, rows, LANES)
        swap(turn).start()

    for first in range(0, len(ride), RIDE_PER_TURN):

        @pl.when(turn == first // RIDE_PER_TURN)
        def _():
            for copy in ride[first : first + RIDE_PER_TURN]:
                copy.start()

    @pl.when(turn == pl.num_programs(0) - 1)
    def _():
        for c in range(pairs):
            swap(jnp.int32(c)).wait_send()
        swap(pairs).wait_send()
        for copy in ride:
            copy.wait()


def attend_back_reduce(qkv, mixed, d_mixed, lse, d_attn, normed, moe_low, d_log, gain_rows, slot_rows, n_dev):
    count, width = mixed.shape
    pairs = width // LANES
    chips = n_dev // 2
    levels = chips.bit_length() - 1
    rows = width // n_dev
    wide = 4 * LANES
    vmem, dma = pltpu.VMEM, pltpu.SemaphoreType.DMA
    anywhere = pl.BlockSpec(memory_space=pl.ANY)

    def column(offset=0):
        return pl.BlockSpec((count, LANES), lambda i: (0, jnp.minimum(i, pairs - 1) + offset))

    def whole(array):
        return pl.BlockSpec(array.shape, lambda i: (0, 0), pipeline_mode=pl.Buffered(1))

    d_qkv, sums, extra, back = pl.pallas_call(
        functools.partial(back_reduce_kernel, chips),
        out_shape=(
            jax.ShapeDtypeStruct((3, count, width), bf16),
            jax.ShapeDtypeStruct((pairs, rows, wide), f32),
            jax.ShapeDtypeStruct((rows, LANES), f32),
            jax.ShapeDtypeStruct(slot_rows.shape, bf16),
        ),
        grid=(pairs + levels + 1,),
        in_specs=[
            column(),
            column(pairs),
            column(2 * pairs),
            column(),
            column(),
            pl.BlockSpec((1, 8, count), lambda i: (jnp.minimum(i, pairs - 1), 0, 0)),
            column(),
            whole(normed),
            whole(mixed),
            whole(moe_low),
            whole(d_log),
            whole(gain_rows),
            anywhere,
        ],
        out_specs=(
            pl.BlockSpec((3, count, LANES), lambda i: (0, 0, jnp.minimum(i, pairs - 1))),
            pl.BlockSpec((pairs, rows, wide), lambda i: (0, 0, 0)),
            pl.BlockSpec((rows, LANES), lambda i: (0, 0)),
            anywhere,
        ),
        scratch_shapes=[
            vmem((count, LANES), f32),
            vmem((count, LANES), f32),
            vmem((width, count), bf16),
            vmem((width, count), bf16),
            vmem((count, 3 * LANES), bf16),
            vmem((pairs + 1, chips, 2, rows, wide), bf16),
            vmem((pairs + 1, chips, rows, wide), bf16),
            vmem((pairs + 1, chips, rows, wide), bf16),
        ]
        + [vmem((pairs + 1, chips >> (level + 1), rows, wide), bf16) for level in range(levels)]
        + [dma((pairs + 1, levels + 1)), dma((pairs + 1, levels + 1))]
        + exchange_sems(chips),
        compiler_params=params(58, collective_id=1, has_side_effects=True),
        cost_estimate=cost(5 * 4 * count * count * width, 40 * count * width, 8 * count * count),
        name="attend_back_reduce",
    )(qkv, qkv, qkv, mixed, d_mixed, lse, d_attn, normed, mixed, moe_low, d_log, gain_rows, slot_rows)
    parts = sums.reshape(pairs, rows, 4, LANES)
    parts = jnp.transpose(parts, (1, 2, 0, 3)).reshape(rows, 4 * width)
    return d_qkv, parts[:, 0 : 3 * width], parts[:, 3 * width :], extra, back


def middle_kernel(experts, mixed_ref, w_out_ref, tok_ref, gain_ref, wr_ref, col_ref, h_ref, low_ref, gate_ref):
    rows = mixed_ref.shape[0]
    col = col_ref[...]
    first, second, valid = col[:, 2:3], col[:, 3:4], col[:, 4:5].astype(f32)
    attn = dot_nn(mixed_ref[...], w_out_ref[...])
    hidden = tok_ref[...].astype(f32) + valid * attn
    h_ref[...] = hidden
    inverse = lax.rsqrt(jnp.mean(hidden * hidden, axis=1, keepdims=True) + epsilon)
    low = (hidden * inverse * gain_ref[...]).astype(bf16)
    low_ref[...] = low
    logits = dot_nn(low, wr_ref[...])
    lane = iota((rows, LANES), 1)
    own = jnp.sum(jnp.where(lane == first, logits, 0.0), axis=1, keepdims=True)
    alt = jnp.sum(jnp.where(lane == second, logits, 0.0), axis=1, keepdims=True)
    gate0 = 1.0 / (1.0 + jnp.exp(alt - own))
    gate1 = 1.0 / (1.0 + jnp.exp(own - alt))
    gate_ref[...] = jnp.where(lane == 0, gate0, 0.0) + jnp.where(lane == 1, gate1, 0.0)


def middle(mixed, w_out, tokens, gain, wr, col, experts):
    count, width = mixed.shape
    rows = 256
    whole = lambda i: (0, 0)
    part = lambda i: (i, 0)
    return pl.pallas_call(
        functools.partial(middle_kernel, experts),
        out_shape=(
            jax.ShapeDtypeStruct((count, width), f32),
            jax.ShapeDtypeStruct((count, width), bf16),
            jax.ShapeDtypeStruct((count, LANES), f32),
        ),
        grid=(count // rows,),
        in_specs=[
            pl.BlockSpec((rows, width), part),
            pl.BlockSpec((width, width), whole),
            pl.BlockSpec((rows, width), part),
            pl.BlockSpec((1, width), whole),
            pl.BlockSpec((width, LANES), whole),
            pl.BlockSpec((rows, LANES), part),
        ],
        out_specs=(
            pl.BlockSpec((rows, width), part),
            pl.BlockSpec((rows, width), part),
            pl.BlockSpec((rows, LANES), part),
        ),
        compiler_params=params(40),
        cost_estimate=cost(2 * count * width * width, 12 * count * width),
        name="middle",
    )(mixed, w_out, tokens, gain.reshape(1, width), wr, col)


GELU_C = math.sqrt(2.0 / math.pi)


def expert_kernel(
    split, x_ref, g_ref, wg_ref, wu_ref, wd_ref, wr_ref, act_ref, dgp_ref, dup_ref, de_ref, part_ref, din_ref
):
    rows, width = x_ref.shape
    me = lax.axis_index("dp")
    expert, part = me // split, lax.rem(me, split)
    x = x_ref[...]
    lane = iota((rows, LANES), 1)
    logits = dot_nn(x, wr_ref[...])
    own = jnp.sum(jnp.where(lane == expert, logits, 0.0), axis=1, keepdims=True)
    other = g_ref[:, width:].astype(f32).astype(jnp.int32)
    alt = jnp.sum(jnp.where(lane == other, logits, 0.0), axis=1, keepdims=True)
    gate = 1.0 / (1.0 + jnp.exp(alt - own))
    d_rows = (g_ref[:, 0:width].astype(f32) * gate).astype(bf16)
    de_ref[...] = d_rows
    pre = dot_nn(x, wg_ref[...])
    up = dot_nn(x, wu_ref[...])
    d_hidden = dot_nt(d_rows, wd_ref[...])
    square = pre * pre
    bent = jnp.tanh(GELU_C * pre * (1.0 + 0.044715 * square))
    half = 0.5 * (1.0 + bent)
    gelu = pre * half
    slope = half + 0.5 * pre * (1.0 - bent * bent) * (GELU_C * (1.0 + 3 * 0.044715 * square))
    act = (gelu * up).astype(bf16)
    act_ref[...] = act
    dgp = (d_hidden * up * slope).astype(bf16)
    dup = (d_hidden * gelu).astype(bf16)
    dgp_ref[...] = dgp
    dup_ref[...] = dup
    pull = jnp.sum(act.astype(f32) * d_hidden, axis=1, keepdims=True)
    pull_high = pull.astype(bf16)
    pull_low = (pull - pull_high.astype(f32)).astype(bf16)
    part_ref[...] = dot_nn(act, wd_ref[...]).astype(bf16)
    din_ref[:, 0:width] = (dot_nt(dgp, wg_ref[...]) + dot_nt(dup, wu_ref[...])).astype(bf16)
    extra = jnp.where(lane == 2 * part, pull_high.astype(f32), 0.0)
    extra = extra + jnp.where(lane == 2 * part + 1, pull_low.astype(f32), 0.0)
    din_ref[:, width:] = extra.astype(bf16)


def expert_pass(x, g, wg, wu, wd, wr, split):
    count, width = x.shape
    ff = wg.shape[1]
    rows = 256
    whole = lambda i: (0, 0)
    part = lambda i: (i, 0)
    once = dict(pipeline_mode=pl.Buffered(1))
    return pl.pallas_call(
        functools.partial(expert_kernel, split),
        out_shape=(
            jax.ShapeDtypeStruct((count, ff), bf16),
            jax.ShapeDtypeStruct((count, ff), bf16),
            jax.ShapeDtypeStruct((count, ff), bf16),
            jax.ShapeDtypeStruct((count, width), bf16),
            jax.ShapeDtypeStruct((count, width), bf16),
            jax.ShapeDtypeStruct((count, width + LANES), bf16),
        ),
        grid=(count // rows,),
        in_specs=[
            pl.BlockSpec((rows, width), part),
            pl.BlockSpec((rows, width + LANES), part),
            pl.BlockSpec((width, ff), whole, **once),
            pl.BlockSpec((width, ff), whole, **once),
            pl.BlockSpec((ff, width), whole, **once),
            pl.BlockSpec((width, LANES), whole),
        ],
        out_specs=(
            pl.BlockSpec((rows, ff), part),
            pl.BlockSpec((rows, ff), part),
            pl.BlockSpec((rows, ff), part),
            pl.BlockSpec((rows, width), part),
            pl.BlockSpec((rows, width), part),
            pl.BlockSpec((rows, width + LANES), part),
        ),
        compiler_params=params(56),
        cost_estimate=cost(12 * count * width * ff, 2 * count * (3 * ff + 5 * width), count * ff),
        name="experts",
    )(x, g, wg, wu, wd, wr)


def expert_exchange_kernel(
    group, x_ref, g_ref, oth_ref, wg_hbm, wu_hbm, wd_hbm, wr_ref,
    gg_ref, ug_ref, dg_ref, slot_ref, back_ref, pulls_ref, gm_ref,
    xb, gb, oth, oth_mate, ds, rd, pd, sp, rp, pp, pt, pq, rq, act, dgp, dup, de, xt, acc_g, acc_u, acc_d,
    wg_ref, wu_ref, wd_ref,
    w_sem, x_send, x_recv, f_send, f_recv, g_load, g_send, g_recv,
    d_send, d_recv, p_send, p_recv, q_send, q_recv, b_send, b_recv, t_send, t_recv, s_sem, l_sem, o_sem,
):
    experts, capacity, width = x_ref.shape
    ff = wg_ref.shape[1]
    steps = experts // group
    pair = 2 * capacity
    rows = group * pair
    half = experts // 2
    me = lax.axis_index("dp")
    chip, core = lax.div(me, 2), lax.rem(me, 2)
    mate = 2 * chip + 1 - core

    def bits(place):
        if isinstance(place, int):
            return half + place // 2 if place % 2 else place // 2
        return lax.rem(place, 2) * half + lax.div(place, 2)

    def chip_at(place):
        return flip(chip, bits(place), experts)

    def remote(src, dst, send, recv, device):
        return pltpu.make_async_remote_copy(
            src_ref=src, dst_ref=dst, send_sem=send, recv_sem=recv, device_id=(device,), device_id_type=MESH
        )

    def block(q, g, second):
        start = q * rows + g * pair + second * capacity
        return xb.at[pl.ds(start if isinstance(start, int) else pl.multiple_of(start, 16), capacity)]

    def x_copy(place):
        peer = chip_at(place)
        own = block(place // group, place % group, 0)
        return remote(x_ref.at[peer], own, x_send.at[place], x_recv.at[place], 2 * peer + core)

    def x_arrival(q, g):
        place = q * group + g
        return remote(x_ref.at[chip], block(q, g, 0), x_send.at[place], x_recv.at[place], mate)

    def forward(q, g):
        place = q * group + g
        return remote(block(q, g, 0), block(q, g, 1), f_send.at[place], f_recv.at[place], mate)

    def g_mate(q, g):
        place = q * group + g
        at = chip_at(place)
        return remote(g_ref.at[at], gm_ref.at[at], g_send.at[place], g_recv.at[place], mate)

    def g_loads(q, g):
        slot, at = lax.rem(q, 2), chip_at(q * group + g)
        first, second = g * pair, g * pair + capacity
        return (
            pltpu.make_async_copy(g_ref.at[at], gb.at[slot, first:second], g_load.at[slot, 2 * g]),
            pltpu.make_async_copy(gm_ref.at[at], gb.at[slot, second : second + capacity], g_load.at[slot, 2 * g + 1]),
        )

    def load_g(q):
        for g in range(group):
            g_mate(q, g).wait_recv()
            for copy in g_loads(q, g):
                copy.start()

    def d_copy(q, g):
        place, slot = q * group + g, lax.rem(q, 2)
        return remote(pd.at[slot, g], rd.at[slot, g], d_send.at[place], d_recv.at[place], mate)

    def p_copy(q, g):
        place, slot = q * group + g, lax.rem(q, 2)
        return remote(pp.at[slot, g], rp.at[slot, g], p_send.at[place], p_recv.at[place], mate)

    def q_copy(q, g):
        place, slot = q * group + g, lax.rem(q, 2)
        return remote(pq.at[slot, g], rq.at[slot, g], q_send.at[place], q_recv.at[place], mate)

    def back_copies(q, g):
        place = q * group + g
        device = 2 * chip_at(place) + core
        return (
            remote(pt.at[place], pulls_ref.at[chip], t_send.at[place], t_recv.at[place], device),
            remote(ds.at[place], back_ref.at[chip], b_send.at[place], b_recv.at[place], device),
        )

    def slot_copy(q, g):
        place = q * group + g
        return pltpu.make_async_copy(sp.at[place], slot_ref.at[chip_at(place)], s_sem.at[place])

    weights = [
        pltpu.make_async_copy(src, dst, w_sem.at[i])
        for i, (src, dst) in enumerate(((wg_hbm, wg_ref), (wu_hbm, wu_ref), (wd_hbm, wd_ref)))
    ]
    grads = [
        pltpu.make_async_copy(src, dst, o_sem.at[i])
        for i, (src, dst) in enumerate(((acc_g, gg_ref), (acc_u, ug_ref), (acc_d, dg_ref)))
    ]
    self_x = pltpu.make_async_copy(x_ref.at[chip], block(0, 0, 0), l_sem.at[0])
    self_pull = pltpu.make_async_copy(pt.at[0], pulls_ref.at[chip], l_sem.at[1])
    self_back = pltpu.make_async_copy(ds.at[0], back_ref.at[chip], l_sem.at[2])
    oth_own = pltpu.make_async_copy(oth_ref, oth, l_sem.at[3])
    oth_copy = remote(oth_ref, oth_mate, l_sem.at[4], l_sem.at[5], mate)

    for copy in weights:
        copy.start()
    self_x.start()
    oth_own.start()
    greet([2 * chip_at(place) + core for place in range(1, experts)] + [mate])
    oth_copy.start()
    for place in range(1, group):
        x_copy(place).start()
    for q in range(steps):
        for g in range(group):
            g_mate(q, g).start()
        for g in range(group):
            if (q + 1) * group + g < experts:
                x_copy((q + 1) * group + g).start()
    for acc in (acc_g, acc_u, acc_d):
        acc[...] = jnp.zeros_like(acc)
    pt[...] = jnp.zeros_like(pt)
    pq[...] = jnp.zeros_like(pq)
    self_x.wait()
    forward(0, 0).start()
    oth_own.wait()
    oth_copy.wait()
    load_g(jnp.int32(0))
    for g in range(1, group):
        x_arrival(0, g).wait_recv()
        forward(0, g).start()
    for copy in weights:
        copy.wait()

    def finish(q):
        slot = lax.rem(q, 2)
        for g in range(group):
            place = q * group + g
            q_copy(q, g).wait_recv()
            d_copy(q, g).wait_recv()
            pt[place] = pt[place] + rq[slot, g]
            ds[place] = (ds[place].astype(f32) + rd[slot, g].astype(f32)).astype(bf16)
            if g == 0:

                @pl.when(q == 0)
                def _():
                    self_pull.start()
                    self_back.start()

                @pl.when(q > 0)
                def _():
                    for copy in back_copies(q, g):
                        copy.start()

            else:
                for copy in back_copies(q, g):
                    copy.start()
        for g in range(group):
            place = q * group + g
            p_copy(q, g).wait_recv()
            sp[place] = (sp[place].astype(f32) + rp[slot, g].astype(f32)).astype(bf16)
            slot_copy(q, g).start()

    def weight_grads(q):
        xt[...] = jnp.transpose(xb[pl.ds(pl.multiple_of((q - 2) * rows, 16), 2 * rows), :])
        span = 256
        for row in range(0, width, span):
            acc_g[row : row + span, :] += dot_nn(xt[row : row + span, :], dgp[...])
            acc_u[row : row + span, :] += dot_nn(xt[row : row + span, :], dup[...])
        for row in range(0, ff, LANES):
            acc_d[row : row + LANES, :] += dot_tn(act[:, row : row + LANES], de[...])

    def main(q):
        slot = lax.rem(q, 2)
        here = pl.ds(pl.multiple_of(slot * rows, 16), rows)
        for g in range(group):
            for copy in g_loads(q, g):
                copy.wait()
            forward(q, g).wait_recv()

        @pl.when(q + 1 < steps)
        def _():
            load_g(q + 1)

        x = xb[pl.ds(pl.multiple_of(q * rows, 16), rows), :]
        lane = iota((rows, LANES), 1)
        logits = dot_nn(x, wr_ref[...])
        mine = jnp.sum(jnp.where(lane == chip, logits, 0.0), axis=1, keepdims=True)
        ids = []
        for g in range(group):
            at = chip_at(q * group + g)
            for table in (oth, oth_mate):
                ids.append(jnp.transpose(table[at])[0:capacity, 0:1])
        other = jnp.concatenate(ids, axis=0).astype(jnp.int32)
        alt = jnp.sum(jnp.where(lane == other, logits, 0.0), axis=1, keepdims=True)
        gate = 1.0 / (1.0 + jnp.exp(alt - mine))
        d_rows = (gb[slot].astype(f32) * gate).astype(bf16)
        de[here, :] = d_rows
        pre = dot_nn(x, wg_ref[...])
        up = dot_nn(x, wu_ref[...])
        d_hidden = dot_nt(d_rows, wd_ref[...])
        square = pre * pre
        bent = jnp.tanh(GELU_C * pre * (1.0 + 0.044715 * square))
        hill = 0.5 * (1.0 + bent)
        gelu = pre * hill
        slope = hill + 0.5 * pre * (1.0 - bent * bent) * (GELU_C * (1.0 + 3 * 0.044715 * square))
        now = (gelu * up).astype(bf16)
        act[here, :] = now
        dgp[here, :] = (d_hidden * up * slope).astype(bf16)
        dup[here, :] = (d_hidden * gelu).astype(bf16)
        pull = jnp.sum(now.astype(f32) * d_hidden, axis=1, keepdims=True)

        @pl.when(q + 1 < steps)
        def _():
            for g in range(group):
                x_arrival(q + 1, g).wait_recv()
                forward(q + 1, g).start()

        @pl.when(q >= 1)
        def _():
            finish(q - 1)

        @pl.when(q >= 2)
        def _():
            for g in range(group):
                q_copy(q - 2, g).wait_send()
                d_copy(q - 2, g).wait_send()
                p_copy(q - 2, g).wait_send()

        d_in = (dot_nt(dgp[here, :], wg_ref[...]) + dot_nt(dup[here, :], wu_ref[...])).astype(bf16)
        pull = jnp.broadcast_to(pull, (rows, LANES))
        for g in range(group):
            place = q * group + g
            low, mid, high = g * pair, g * pair + capacity, (g + 1) * pair
            pt[place, :, 0:capacity] = jnp.transpose(pull[low:mid])[0:8, :]
            pq[slot, g, :, 0:capacity] = jnp.transpose(pull[mid:high])[0:8, :]
            ds[place] = d_in[low:mid]
            pd[slot, g] = d_in[mid:high]
            q_copy(q, g).start()
            d_copy(q, g).start()
        partial = dot_nn(act[here, :], wd_ref[...]).astype(bf16)
        for g in range(group):
            place = q * group + g
            low, mid, high = g * pair, g * pair + capacity, (g + 1) * pair
            sp[place] = partial[low:mid]
            pp[slot, g] = partial[mid:high]
            p_copy(q, g).start()

    def step(q, carry):
        @pl.when(q == steps)
        def _():
            finish(q - 1)

        @pl.when((q >= 2) & (lax.rem(q, 2) == 0))
        def _():
            weight_grads(q)

        @pl.when(q < steps)
        def _():
            main(q)

        return carry

    lax.fori_loop(0, steps + 1, step, 0)
    for copy in grads:
        copy.start()
    for q in (steps - 2, steps - 1):
        for g in range(group):
            q_copy(q, g).wait_send()
            d_copy(q, g).wait_send()
            p_copy(q, g).wait_send()
    self_pull.wait()
    self_back.wait()
    for q in range(steps):
        for g in range(group):
            place = q * group + g
            slot_copy(q, g).wait()
            forward(q, g).wait_send()
            g_mate(q, g).wait_send()
            if place:
                x_copy(place).wait_send()
                for copy in back_copies(q, g):
                    copy.wait()
    for copy in grads:
        copy.wait()


def expert_exchange(x, g, others, wg, wu, wd, wr, group=2):
    experts, capacity, width = x.shape
    ff = wg.shape[1]
    steps = experts // group
    rows = 2 * capacity * group
    anywhere = pl.BlockSpec(memory_space=pl.ANY)
    vmem, dma = pltpu.VMEM, pltpu.SemaphoreType.DMA
    each = dma((experts,))
    count = rows * steps
    outs = pl.pallas_call(
        functools.partial(expert_exchange_kernel, group),
        out_shape=(
            jax.ShapeDtypeStruct((width, ff), f32),
            jax.ShapeDtypeStruct((width, ff), f32),
            jax.ShapeDtypeStruct((ff, width), f32),
            jax.ShapeDtypeStruct((experts, capacity, width), bf16),
            jax.ShapeDtypeStruct((experts, capacity, width), bf16),
            jax.ShapeDtypeStruct((experts, 8, LANES), f32),
            jax.ShapeDtypeStruct((experts, capacity, width), bf16),
        ),
        in_specs=[anywhere] * 6 + [pl.BlockSpec(memory_space=vmem)],
        out_specs=(anywhere,) * 7,
        scratch_shapes=[
            vmem((steps * rows, width), bf16),
            vmem((2, rows, width), bf16),
            vmem((experts, 8, LANES), f32),
            vmem((experts, 8, LANES), f32),
            vmem((experts, capacity, width), bf16),
            vmem((2, group, capacity, width), bf16),
            vmem((2, group, capacity, width), bf16),
            vmem((experts, capacity, width), bf16),
            vmem((2, group, capacity, width), bf16),
            vmem((2, group, capacity, width), bf16),
            vmem((experts, 8, LANES), f32),
            vmem((2, group, 8, LANES), f32),
            vmem((2, group, 8, LANES), f32),
            vmem((2 * rows, ff), bf16),
            vmem((2 * rows, ff), bf16),
            vmem((2 * rows, ff), bf16),
            vmem((2 * rows, width), bf16),
            vmem((width, 2 * rows), bf16),
            vmem((width, ff), f32),
            vmem((width, ff), f32),
            vmem((ff, width), f32),
            vmem((width, ff), bf16),
            vmem((width, ff), bf16),
            vmem((ff, width), bf16),
            dma((3,)),
            each, each, each, each,
            dma((2, 2 * group)),
            each, each,
            each, each, each, each, each, each, each, each, each, each, each,
            dma((6,)),
            dma((3,)),
        ],
        compiler_params=params(62, collective_id=2, has_side_effects=True),
        cost_estimate=cost(18 * count * width * ff, 2 * count * 4 * width + 18 * width * ff, count * ff),
        name="experts",
    )(x, g, others, wg, wu, wd, wr)
    return outs[:6]


def hot_rows(col, k, rows, slots):
    return jnp.where(iota((rows, slots), 1) == col[:, k : k + 1], 1.0, 0.0).astype(bf16)


def state_kernel(
    n_pull, col_ref, gate_ref, din_ref, h_ref, og_ref, gain_ref, wr_ref, *refs
):
    dstate_ref, dattn_ref, dlog_ref, gterm_ref = refs[n_pull:]
    rows, width = h_ref.shape
    slots = din_ref.shape[0]
    col = col_ref[...]
    valid = col[:, 4:5].astype(f32)
    hot0, hot1 = hot_rows(col, 0, rows, slots), hot_rows(col, 1, rows, slots)
    if n_pull:
        table = refs[0][:, 0, :]
        experts = table.shape[0]
        capacity = slots // experts

        def pull_of(k):
            chosen = jnp.where(iota((rows, experts), 1) == col[:, 2 + k : 3 + k], 1.0, 0.0)
            values = dot_nn(chosen, table, precision=lax.Precision.HIGHEST)
            slot = col[:, k : k + 1] - capacity * col[:, 2 + k : 3 + k]
            here = (iota((rows, LANES), 1) == slot) & (col[:, k : k + 1] < slots)
            return jnp.sum(jnp.where(here, values, 0.0), axis=1, keepdims=True)

        pull0, pull1 = pull_of(0), pull_of(1)
    else:
        pulls = din_ref[:, width:]
        pull0 = jnp.sum(dot_nn(hot0, pulls), axis=1, keepdims=True)
        pull1 = jnp.sum(dot_nn(hot1, pulls), axis=1, keepdims=True)
    gathered = dot_nn(hot0 + hot1, din_ref[:, 0:width])
    gate0, gate1 = gate_ref[:, 0:1], gate_ref[:, 1:2]
    total = pull0 + pull1
    lane = iota((rows, LANES), 1)
    d_log = jnp.where(lane == col[:, 2:3], pull0 - gate0 * total, 0.0)
    d_log = d_log + jnp.where(lane == col[:, 3:4], pull1 - gate1 * total, 0.0)
    d_log = d_log.astype(bf16)
    dlog_ref[...] = d_log
    d_moe = gathered + dot_nt(d_log, wr_ref[...])
    hidden = h_ref[...]
    inverse = lax.rsqrt(jnp.mean(hidden * hidden, axis=1, keepdims=True) + epsilon)
    normal = hidden * inverse
    scaled = gain_ref[...] * d_moe
    share = jnp.mean(normal * scaled, axis=1, keepdims=True)
    d_state = og_ref[...].astype(f32) + inverse * (scaled - normal * share)
    dstate_ref[...] = d_state
    dattn_ref[...] = (valid * d_state).astype(bf16)
    term = jnp.sum((normal * d_moe).reshape(rows // 8, 8, width), axis=0)

    @pl.when(pl.program_id(0) == 0)
    def _():
        gterm_ref[...] = jnp.zeros_like(gterm_ref)

    gterm_ref[...] += term


def state_back(col, gates, din, hidden, out_grad, gain, wr, pulls=()):
    count, width = hidden.shape
    slots = din.shape[0]
    rows = 256
    whole = lambda i: (0, 0)
    part = lambda i: (i, 0)
    return pl.pallas_call(
        functools.partial(state_kernel, len(pulls)),
        out_shape=(
            jax.ShapeDtypeStruct((count, width), f32),
            jax.ShapeDtypeStruct((count, width), bf16),
            jax.ShapeDtypeStruct((count, LANES), bf16),
            jax.ShapeDtypeStruct((8, width), f32),
        ),
        grid=(count // rows,),
        in_specs=[
            pl.BlockSpec((rows, LANES), part),
            pl.BlockSpec((rows, LANES), part),
            pl.BlockSpec(din.shape, whole),
            pl.BlockSpec((rows, width), part),
            pl.BlockSpec((rows, width), part),
            pl.BlockSpec((1, width), whole),
            pl.BlockSpec((width, LANES), whole),
        ]
        + [pl.BlockSpec(p.shape, lambda i: (0, 0, 0)) for p in pulls],
        out_specs=(
            pl.BlockSpec((rows, width), part),
            pl.BlockSpec((rows, width), part),
            pl.BlockSpec((rows, LANES), part),
            pl.BlockSpec((8, width), whole),
        ),
        compiler_params=params(48),
        cost_estimate=cost(2 * slots * count * width, 14 * count * width),
        name="state_back",
    )(col, gates, din, hidden, out_grad, gain.reshape(1, width), wr, *pulls)


def block_out_kernel(col_ref, gate_ref, rows_ref, h_ref, out_ref):
    rows, width = h_ref.shape
    slots = rows_ref.shape[0]
    col = col_ref[...]
    pick0 = dot_nn(hot_rows(col, 0, rows, slots), rows_ref[...])
    pick1 = dot_nn(hot_rows(col, 1, rows, slots), rows_ref[...])
    out_ref[...] = (h_ref[...] + gate_ref[:, 0:1] * pick0 + gate_ref[:, 1:2] * pick1).astype(bf16)


def make_block_out(col, gates, slot_rows, hidden):
    count, width = hidden.shape
    slots = slot_rows.shape[0]
    rows = 256
    whole = lambda i: (0, 0)
    part = lambda i: (i, 0)
    return pl.pallas_call(
        block_out_kernel,
        out_shape=jax.ShapeDtypeStruct((count, width), bf16),
        grid=(count // rows,),
        in_specs=[
            pl.BlockSpec((rows, LANES), part),
            pl.BlockSpec((rows, LANES), part),
            pl.BlockSpec((slots, width), whole),
            pl.BlockSpec((rows, width), part),
        ],
        out_specs=pl.BlockSpec((rows, width), part),
        compiler_params=params(40),
        cost_estimate=cost(4 * slots * count * width, 9 * count * width),
        name="block_out",
    )(col, gates, slot_rows, hidden)


def input_kernel(n_ride, d_ref, w_ref, tok_ref, gain_ref, dstate_ref, *refs):
    srcs, grad_ref, dsts = refs[:n_ride], refs[n_ride], refs[n_ride + 1 :]
    for src, dst in zip(srcs, dsts):
        dst[...] = src[...]
    rows, width = tok_ref.shape
    d_normed = dot_nt(d_ref[0], w_ref[:, 0:width])
    for i in range(1, 3):
        d_normed = d_normed + dot_nt(d_ref[i], w_ref[:, i * width : (i + 1) * width])
    values = tok_ref[...].astype(f32)
    inverse = lax.rsqrt(jnp.mean(values * values, axis=1, keepdims=True) + epsilon)
    normal = values * inverse
    scaled = gain_ref[...] * d_normed
    share = jnp.mean(normal * scaled, axis=1, keepdims=True)
    grad_ref[...] = dstate_ref[...] + inverse * (scaled - normal * share)


def input_back(d_qkv, w_qkv, tokens, gain, d_state, riders=()):
    count, width = tokens.shape
    rows = 256
    steps = count // rows
    whole = lambda i: (0, 0)
    part = lambda i: (i, 0)
    passed = [pl.BlockSpec((array.shape[0] // steps, array.shape[1]), part) for array in riders]
    return pl.pallas_call(
        functools.partial(input_kernel, len(riders)),
        out_shape=[jax.ShapeDtypeStruct((count, width), f32)]
        + [jax.ShapeDtypeStruct(array.shape, array.dtype) for array in riders],
        grid=(steps,),
        in_specs=[
            pl.BlockSpec((3, rows, width), lambda i: (0, i, 0)),
            pl.BlockSpec((width, 3 * width), whole),
            pl.BlockSpec((rows, width), part),
            pl.BlockSpec((1, width), whole),
            pl.BlockSpec((rows, width), part),
        ]
        + passed,
        out_specs=[pl.BlockSpec((rows, width), part)] + passed,
        compiler_params=params(56),
        cost_estimate=cost(6 * count * width * width, 22 * count * width),
        name="input_back",
    )(d_qkv, w_qkv, tokens, gain.reshape(1, width), d_state, *riders)


def shards(
    tokens,
    lengths,
    expert_ids,
    slot_order,
    gain_attn,
    w_qkv,
    w_out,
    gain_moe,
    w_router,
    w_gate,
    w_up,
    w_down,
    out_grad,
):
    tok_dev, width = tokens.shape
    n_dev = lax.axis_size("dp")
    experts = w_router.shape[1]
    split = n_dev // experts
    capacity = split * (5 * tok_dev // (4 * n_dev))
    slots = experts * capacity
    me = lax.axis_index("dp")
    part = lax.rem(me, split)
    same_part = [[e * split + p for e in range(experts)] for p in range(split)]
    same_expert = [[e * split + p for p in range(split)] for e in range(experts)]
    swap = [(d, d ^ 1) for d in range(n_dev)]

    def across(blocks):
        return lax.all_to_all(blocks, "dp", 0, 0, axis_index_groups=same_part, tiled=True)

    def share(rows):
        if split == 2:
            return jnp.concatenate([rows, lax.ppermute(rows, "dp", swap)], axis=0)
        return lax.all_gather(rows, "dp", axis_index_groups=same_expert, tiled=True)

    def settle(pieces):
        if split == 2:
            theirs = lax.ppermute(pieces[1], "dp", swap)
            return (pieces[0].astype(f32) + theirs.astype(f32)).astype(bf16)
        got = lax.all_to_all(pieces, "dp", 0, 0, axis_index_groups=same_expert, tiled=True)
        return jnp.sum(got.astype(f32), axis=0).astype(bf16)

    def send_in(rows):
        return share(across(rows.reshape(experts, capacity, -1)).reshape(slots, -1))

    def send_back(rows):
        summed = settle(rows.reshape(split, slots, -1))
        return across(summed.reshape(experts, capacity, -1)).reshape(slots, -1)

    def reduce_rows(term):
        pieces = term.reshape(experts, split, -1, term.shape[-1])
        if split == 2:
            mine = lax.dynamic_index_in_dim(pieces, part, 1, keepdims=False)
            theirs = lax.dynamic_index_in_dim(pieces, 1 - part, 1, keepdims=False)
            theirs = lax.ppermute(theirs.astype(bf16), "dp", swap)
            summed = (mine + theirs.astype(f32)).astype(bf16)
        else:
            pieces = jnp.moveaxis(pieces, 1, 0).astype(bf16)
            got = lax.all_to_all(pieces, "dp", 0, 0, axis_index_groups=same_expert, tiled=True)
            summed = jnp.sum(got.astype(f32), axis=0).astype(bf16)
        return jnp.sum(across(summed).astype(f32), axis=0)

    wr = jnp.pad(w_router, ((0, 0), (0, LANES - experts)))
    col, row = make_slots(lengths, expert_ids, slot_order, experts, capacity)
    direct = split == 2 and experts & (experts - 1) == 0 and experts >= 4

    token_vals = tokens.astype(f32)
    inverse_attn = lax.rsqrt(jnp.mean(token_vals * token_vals, axis=-1, keepdims=True) + epsilon)
    normed_low = (token_vals * inverse_attn * gain_attn).astype(bf16)
    qkv = jnp.dot(normed_low, w_qkv, preferred_element_type=f32).astype(bf16)
    if direct:
        grad_out, others = dispatch_pair(row, out_grad, experts, capacity)
        mixed, lse, grad_in, others = attend(qkv, (grad_out.reshape(experts, capacity, -1), others))
    else:
        mixed, lse = attend(qkv)
        grad_in = send_in(dispatch_grad(row, out_grad, slots))
    hidden, moe_low, gates = middle(mixed, w_out, tokens, gain_moe, wr, col, experts)

    rows_out = dispatch(row, moe_low, slots)
    if direct:
        gate_grad, up_grad, down_grad, slot_part, d_in_back, pulls = expert_exchange(
            rows_out.reshape(experts, capacity, -1), grad_in, others, w_gate[0], w_up[0], w_down[0], wr
        )
        d_in_back = d_in_back.reshape(slots, -1)
        pulls = (pulls,)
    else:
        rows_in = send_in(rows_out)
        act, d_pre, d_up, d_rows, partial_out, d_in = expert_pass(
            rows_in, grad_in, w_gate[0], w_up[0], w_down[0], wr, split
        )
        d_in_back = send_back(d_in)
        slot_out = send_back(partial_out)
        pulls = ()
        down_grad = dot_tn(act, d_rows)
        gate_grad = dot_tn(rows_in, d_pre)
        up_grad = dot_tn(rows_in, d_up)

    d_state, d_attn, d_log, gain_moe_rows = state_back(
        col, gates, d_in_back, hidden, out_grad, gain_moe, wr, pulls
    )
    d_mixed = dot_nt(d_attn, w_out).astype(bf16)
    if direct:
        d_qkv, qkv_sum, out_rows, extra, slot_out = attend_back_reduce(
            qkv, mixed, d_mixed, lse, d_attn, normed_low, moe_low, d_log, gain_moe_rows, slot_part, n_dev
        )
        slot_out = slot_out.reshape(slots, -1)
        router_sum, gain_moe_sum = extra[:, 0:experts], extra[:, 64]
    else:
        d_qkv = attend_back(qkv, mixed, d_mixed, lse)
        lane = jnp.arange(LANES, dtype=jnp.int32)[None, :]
        gain_moe_term = jnp.sum(gain_moe_rows, axis=0)
        extra = jnp.where(lane == experts, gain_moe_term[:, None], dot_tn(moe_low, d_log))
        early = reduce_rows(jnp.concatenate([dot_tn(mixed, d_attn), extra], axis=1))
        out_rows, router_sum, gain_moe_sum = (
            early[:, 0:width], early[:, width : width + experts], early[:, width + experts]
        )
        qkv_sum = reduce_rows(jnp.concatenate([dot_tn(normed_low, d_qkv[i]) for i in range(3)], axis=1))
    if direct:
        tokens_grad, gate_grad, up_grad, down_grad = input_back(
            d_qkv, w_qkv, tokens, gain_attn, d_state, (gate_grad, up_grad, down_grad)
        )
    else:
        (tokens_grad,) = input_back(d_qkv, w_qkv, tokens, gain_attn, d_state)
    my_rows = width // n_dev
    weight_rows = lax.dynamic_slice_in_dim(w_qkv, me * my_rows, my_rows, 0).astype(f32)
    gain_attn_sum = jnp.sum(weight_rows * qkv_sum, axis=1) / lax.dynamic_slice_in_dim(gain_attn, me * my_rows, my_rows, 0)

    block_out = make_block_out(col, gates, slot_out, hidden)
    return (
        block_out,
        tokens_grad,
        gain_attn_sum,
        qkv_sum,
        out_rows,
        gain_moe_sum,
        router_sum,
        gate_grad[None],
        up_grad[None],
        down_grad[None],
    )


def solution(mesh):
    rows, one = P("dp", None), P("dp")
    cube = P("dp", None, None)
    return jax.shard_map(
        shards,
        mesh=mesh,
        in_specs=(rows, one, rows, rows, P(), P(), P(), P(), P(), cube, cube, cube, rows),
        out_specs=(rows, rows, one, rows, rows, one, rows, cube, cube, cube),
        check_vma=False,
    )
```

```python
import functools
import math

import jax
import jax.numpy as jnp
from jax import lax
from jax.experimental import pallas as pl
from jax.experimental.pallas import tpu as pltpu
from jax.sharding import PartitionSpec as P

HEADS = 16
HEAD_DIM = 64
LEN = 1024
LANES = 128
MIB = 1 << 20

epsilon = 1e-06
mask_fill = -1e30
f32 = jnp.float32
bf16 = jnp.bfloat16


def dot_nn(left, right, **kw):
    return lax.dot_general(left, right, (((1,), (0,)), ((), ())), preferred_element_type=f32, **kw)


def dot_nt(left, right, **kw):
    return lax.dot_general(left, right, (((1,), (1,)), ((), ())), preferred_element_type=f32, **kw)


def dot_tn(left, right, **kw):
    return lax.dot_general(left, right, (((0,), (0,)), ((), ())), preferred_element_type=f32, **kw)


def iota(shape, dim):
    return lax.broadcasted_iota(jnp.int32, shape, dim)


def params(mib, **kw):
    return pltpu.CompilerParams(vmem_limit_bytes=mib * MIB, **kw)


def cost(flops, nbytes, trans=0):
    return pl.CostEstimate(flops=int(flops), bytes_accessed=int(nbytes), transcendentals=int(trans))


def slot_kernel(capacity, experts, len_ref, ids_ref, rank_col_ref, rank_row_ref, col_ref, row_ref):
    count = ids_ref.shape[0]
    length = len_ref[0]
    ids = ids_ref[...]
    first, second = ids[:, 0:1], ids[:, 1:2]
    lane = iota((count, LANES), 1)
    place = iota((count, LANES), 0)
    hot0 = (lane == first) & (lane < experts)
    hot1 = (lane == second + experts) & (lane >= experts) & (lane < 2 * experts)
    valid = place < length
    hot = jnp.where((hot0 | hot1) & valid, 1.0, 0.0).astype(bf16)
    before = (rank_row_ref[...] < rank_col_ref[...]).astype(f32).astype(bf16)
    counts = dot_nn(before, hot)
    shifted = (lane == first + experts) & (lane >= experts) & (lane < 2 * experts) & valid
    totals = jnp.sum(jnp.where(shifted, 1.0, 0.0), axis=0, keepdims=True)
    slot0 = jnp.sum(jnp.where(hot0, counts, 0.0), axis=1, keepdims=True).astype(jnp.int32)
    slot1 = jnp.sum(jnp.where(hot1, counts + totals, 0.0), axis=1, keepdims=True).astype(jnp.int32)
    sentinel = experts * capacity
    ok = valid[:, 0:1]
    flat0 = jnp.where(ok & (slot0 < capacity), first * capacity + slot0, sentinel)
    flat1 = jnp.where(ok & (slot1 < capacity), second * capacity + slot1, sentinel)
    col = jnp.where(lane == 0, flat0, 0) + jnp.where(lane == 1, flat1, 0)
    col = col + jnp.where(lane == 2, first, 0) + jnp.where(lane == 3, second, 0)
    col = col + jnp.where(lane == 4, ok.astype(jnp.int32), 0)
    col_ref[...] = col
    row_ref[...] = jnp.transpose(col.astype(f32))[0:8, :].astype(jnp.int32)


def make_slots(lengths, expert_ids, slot_order, experts, capacity):
    count = expert_ids.shape[0]
    return pl.pallas_call(
        functools.partial(slot_kernel, capacity, experts),
        out_shape=(
            jax.ShapeDtypeStruct((count, LANES), jnp.int32),
            jax.ShapeDtypeStruct((8, count), jnp.int32),
        ),
        in_specs=[
            pl.BlockSpec(memory_space=pltpu.SMEM),
            pl.BlockSpec(memory_space=pltpu.VMEM),
            pl.BlockSpec(memory_space=pltpu.VMEM),
            pl.BlockSpec(memory_space=pltpu.VMEM),
        ],
        out_specs=(pl.BlockSpec(memory_space=pltpu.VMEM), pl.BlockSpec(memory_space=pltpu.VMEM)),
        compiler_params=params(40),
        cost_estimate=cost(2 * count * count * LANES, 4 * count * LANES),
        name="slots",
    )(lengths, expert_ids, slot_order.reshape(count, 1), slot_order)


def dispatch_kernel(rows, row_ref, data_ref, out_ref):
    count = data_ref.shape[0]
    slot = pl.program_id(0) * rows + iota((rows, count), 0)
    hot = (slot == row_ref[0:1, :]) | (slot == row_ref[1:2, :])
    out_ref[...] = dot_nn(jnp.where(hot, 1.0, 0.0).astype(bf16), data_ref[...]).astype(bf16)


def dispatch(row, data, slots):
    count, width = data.shape
    rows = 256
    return pl.pallas_call(
        functools.partial(dispatch_kernel, rows),
        out_shape=jax.ShapeDtypeStruct((slots, width), bf16),
        grid=(slots // rows,),
        in_specs=[
            pl.BlockSpec((8, count), lambda i: (0, 0)),
            pl.BlockSpec((count, width), lambda i: (0, 0)),
        ],
        out_specs=pl.BlockSpec((rows, width), lambda i: (i, 0)),
        compiler_params=params(40),
        cost_estimate=cost(2 * slots * count * width, 2 * (slots + count) * width),
        name="dispatch",
    )(row, data)


def dispatch_grad_kernel(rows, row_ref, data_ref, out_ref):
    count, width = data_ref.shape
    slot = pl.program_id(0) * rows + iota((rows, count), 0)
    hot0 = slot == row_ref[0:1, :]
    hot1 = slot == row_ref[1:2, :]
    both = jnp.where(hot0 | hot1, 1.0, 0.0).astype(bf16)
    out_ref[:, 0:width] = dot_nn(both, data_ref[...]).astype(bf16)
    other = jnp.where(hot0, row_ref[3:4, :], 0) + jnp.where(hot1, row_ref[2:3, :], 0)
    other = jnp.sum(other.astype(f32), axis=1, keepdims=True)
    out_ref[:, width:] = jnp.broadcast_to(other, (rows, LANES)).astype(bf16)


def dispatch_grad(row, data, slots):
    count, width = data.shape
    rows = 256
    return pl.pallas_call(
        functools.partial(dispatch_grad_kernel, rows),
        out_shape=jax.ShapeDtypeStruct((slots, width + LANES), bf16),
        grid=(slots // rows,),
        in_specs=[
            pl.BlockSpec((8, count), lambda i: (0, 0)),
            pl.BlockSpec((count, width), lambda i: (0, 0)),
        ],
        out_specs=pl.BlockSpec((rows, width + LANES), lambda i: (i, 0)),
        compiler_params=params(40),
        cost_estimate=cost(2 * slots * count * width, 2 * (slots + count) * width),
        name="dispatch_grad",
    )(row, data)


def dispatch_pair_kernel(capacity, row_ref, data_ref, out_ref, other_ref):
    count = data_ref.shape[0]
    rows = out_ref.shape[0]
    slot = pl.program_id(0) * rows + iota((rows, count), 0)
    hot0 = jnp.where(slot == row_ref[0:1, :], 1.0, 0.0).astype(bf16)
    hot1 = jnp.where(slot == row_ref[1:2, :], 1.0, 0.0).astype(bf16)
    out_ref[...] = dot_nn(hot0 + hot1, data_ref[...]).astype(bf16)
    ids = row_ref[...].astype(f32).astype(bf16)
    other = dot_nt(ids, hot0)[3:4] + dot_nt(ids, hot1)[2:3]
    other_ref[...] = jnp.zeros_like(other_ref)
    for i in range(other_ref.shape[0]):
        mine = other[:, i * capacity : (i + 1) * capacity]
        other_ref[i, :, 0:capacity] = jnp.broadcast_to(mine, (8, capacity))


def dispatch_pair(row, data, experts, capacity):
    count, width = data.shape
    each = 2
    return pl.pallas_call(
        functools.partial(dispatch_pair_kernel, capacity),
        out_shape=(
            jax.ShapeDtypeStruct((experts * capacity, width), bf16),
            jax.ShapeDtypeStruct((experts, 8, LANES), f32),
        ),
        grid=(experts // each,),
        in_specs=[
            pl.BlockSpec((8, count), lambda i: (0, 0)),
            pl.BlockSpec((count, width), lambda i: (0, 0)),
        ],
        out_specs=(
            pl.BlockSpec((each * capacity, width), lambda i: (i, 0)),
            pl.BlockSpec((each, 8, LANES), lambda i: (i, 0, 0)),
        ),
        compiler_params=params(40),
        cost_estimate=cost(2 * experts * capacity * count * width, 2 * (experts * capacity + count) * width),
        name="dispatch_pair",
    )(row, data)


MESH = pl.DeviceIdType.MESH


def flip(chip, bits, experts):
    out, b = chip, 1
    while b < experts:
        if isinstance(bits, int):
            out = out + (bits // b % 2) * (b - 2 * b * lax.rem(lax.div(chip, b), 2))
        else:
            mine, theirs = lax.rem(lax.div(chip, b), 2), lax.rem(lax.div(bits, b), 2)
            out = out + b * theirs * (1 - 2 * mine)
        b *= 2
    return out


def greet(peers):
    barrier = pltpu.get_barrier_semaphore()
    for peer in peers:
        pl.semaphore_signal(barrier, inc=1, device_id=(peer,), device_id_type=MESH)
    pl.semaphore_wait(barrier, len(peers))


def exchange_copies(src, dst, send_sem, recv_sem, local_sem):
    experts = src.shape[0]
    me = lax.axis_index("dp")
    chip, core = lax.div(me, 2), lax.rem(me, 2)
    copies = [pltpu.make_async_copy(src.at[chip], dst.at[chip], local_sem)]
    peers = []
    half = experts // 2
    for place in range(1, experts):
        step = half + place // 2 if place % 2 else place // 2
        peer = flip(chip, step, experts)
        peers.append(2 * peer + core)
        copies.append(
            pltpu.make_async_remote_copy(
                src_ref=src.at[peer],
                dst_ref=dst.at[chip],
                send_sem=send_sem.at[step],
                recv_sem=recv_sem.at[step],
                device_id=(2 * peer + core,),
                device_id_type=MESH,
            )
        )
    return peers, copies


def exchange_sems(experts):
    return [
        pltpu.SemaphoreType.DMA((experts,)),
        pltpu.SemaphoreType.DMA((experts,)),
        pltpu.SemaphoreType.DMA,
    ]


def riding(body, n_in, n_out, n_ride):
    def kernel(*refs):
        ins, srcs = refs[:n_in], refs[n_in : n_in + n_ride]
        outs = refs[n_in + n_ride : n_in + n_ride + n_out]
        dsts = refs[n_in + n_ride + n_out : n_in + 2 * n_ride + n_out]
        rest, sems = refs[n_in + 2 * n_ride + n_out : -3 * n_ride], refs[-3 * n_ride :]
        copies = []
        for r in range(n_ride):
            peers, more = exchange_copies(srcs[r], dsts[r], *sems[3 * r : 3 * r + 3])
            copies += more

        @pl.when(pl.program_id(0) == 0)
        def _():
            greet(peers)
            for copy in copies:
                copy.start()

        body(*ins, *outs, *rest)

        @pl.when(pl.program_id(0) == pl.num_programs(0) - 1)
        def _():
            for copy in copies:
                copy.wait()

    return kernel


SCALE2 = math.log2(math.e) / math.sqrt(HEAD_DIM)
QB = 256


def attend_kernel(q_ref, k_ref, v_ref, mixed_ref, lse_ref):
    lane = iota((QB, LANES), 1)
    wide = jnp.concatenate([v_ref[...], jnp.ones(v_ref.shape, bf16)], axis=1)
    causal = iota((QB, QB), 1) <= iota((QB, QB), 0)
    for block in range(LEN // QB):
        start, stop = block * QB, (block + 1) * QB
        query = q_ref[start:stop, :]
        halves, norms = [], []
        for head in range(2):
            mine = (lane // HEAD_DIM) == head
            scores = dot_nt(jnp.where(mine, query, jnp.zeros_like(query)), k_ref[0:stop, :])
            tail = jnp.where(causal, scores[:, start:stop], mask_fill)
            scores = tail if block == 0 else jnp.concatenate([scores[:, 0:start], tail], axis=1)
            highest = jnp.max(scores, axis=1, keepdims=True) * SCALE2
            raised = jnp.exp2(scores * SCALE2 - highest)
            out = dot_nn(raised.astype(bf16), wide[0:stop, :])
            summed = out[:, LANES:]
            halves.append(out[:, 0:LANES] / summed)
            norms.append(highest + jnp.log2(summed))
        mixed_ref[start:stop, :] = jnp.where(lane < HEAD_DIM, halves[0], halves[1]).astype(bf16)
        norm = jnp.where(lane == 0, norms[0], norms[1])
        lse_ref[0, :, start:stop] = jnp.transpose(norm)[0:8, :]


def attend(qkv):
    count, width3 = qkv.shape
    width = width3 // 3
    pairs = width // LANES
    return pl.pallas_call(
        attend_kernel,
        out_shape=(
            jax.ShapeDtypeStruct((count, width), bf16),
            jax.ShapeDtypeStruct((pairs, 8, count), f32),
        ),
        grid=(pairs,),
        in_specs=[
            pl.BlockSpec((count, LANES), lambda i: (0, i)),
            pl.BlockSpec((count, LANES), lambda i: (0, i + pairs)),
            pl.BlockSpec((count, LANES), lambda i: (0, i + 2 * pairs)),
        ],
        out_specs=(
            pl.BlockSpec((count, LANES), lambda i: (0, i)),
            pl.BlockSpec((1, 8, count), lambda i: (i, 0, 0)),
        ),
        compiler_params=params(40),
        cost_estimate=cost(2 * 4 * count * count * width, 8 * count * width, 8 * count * count),
        name="attend",
    )(qkv, qkv, qkv)


def front_kernel(
    pairs, blocks,
    tok_ref, gain_ref, wq_ref, wk_ref, wv_ref, w_out_ref, gain_moe_ref, wr_ref, col_ref, row_ref,
    norm_ref, qkv_ref, mixed_ref, lse_ref, h_ref, low_ref, gate_ref, rows_ref,
    mixed_sc,
):
    turn = pl.program_id(0)

    @pl.when(turn == 0)
    def _():
        values = tok_ref[...].astype(f32)
        inverse = lax.rsqrt(jnp.mean(values * values, axis=1, keepdims=True) + epsilon)
        norm_ref[...] = (values * inverse * gain_ref[...]).astype(bf16)

    @pl.when(turn < pairs)
    def _():
        weights = jnp.concatenate([wq_ref[...], wk_ref[...], wv_ref[...]], axis=1)
        for row in range(0, LEN, QB):
            part = dot_nn(norm_ref[row : row + QB, :], weights).astype(bf16)
            for i in range(3):
                qkv_ref[i, row : row + QB, :] = part[:, i * LANES : (i + 1) * LANES]
        attend_kernel(qkv_ref.at[0], qkv_ref.at[1], qkv_ref.at[2], mixed_ref, lse_ref)
        mixed_sc[:, pl.ds(pl.multiple_of(turn * LANES, LANES), LANES)] = mixed_ref[...]

    span = h_ref.shape[0]

    @pl.when((turn >= pairs) & (turn < pairs + blocks))
    def _():
        here = pl.ds(pl.multiple_of((turn - pairs) * span, span), span)
        h_ref[...], low, gate_ref[...] = middle_rows(
            mixed_sc[here, :], w_out_ref[...], tok_ref[here, :], gain_moe_ref[...], wr_ref[...], col_ref[...]
        )
        low_ref[here, :] = low

    @pl.when(turn >= pairs + blocks)
    def _():
        rows, count = rows_ref.shape[0], low_ref.shape[0]
        slot = (turn - pairs - blocks) * rows + iota((rows, count), 0)
        hot = (slot == row_ref[0:1, :]) | (slot == row_ref[1:2, :])
        rows_ref[...] = dot_nn(jnp.where(hot, 1.0, 0.0).astype(bf16), low_ref[...]).astype(bf16)


def front(tokens, gain, w_qkv, w_out, gain_moe, wr, col, row, slots, rides):
    count, width = tokens.shape
    pairs = width // LANES
    span = 256
    blocks, turns = count // span, slots // span
    anywhere = pl.BlockSpec(memory_space=pl.ANY)

    def pair_at(i):
        return jnp.minimum(i, pairs - 1)

    def block_at(i):
        return jnp.clip(i - pairs, 0, blocks - 1)

    def fixed(array):
        return pl.BlockSpec(array.shape, lambda i: (0, 0), pipeline_mode=pl.Buffered(1))

    gain, gain_moe = gain.reshape(1, width), gain_moe.reshape(1, width)
    in_specs = [
        fixed(tokens),
        fixed(gain),
        pl.BlockSpec((width, LANES), lambda i: (0, pair_at(i))),
        pl.BlockSpec((width, LANES), lambda i: (0, pair_at(i) + pairs)),
        pl.BlockSpec((width, LANES), lambda i: (0, pair_at(i) + 2 * pairs)),
        fixed(w_out),
        fixed(gain_moe),
        fixed(wr),
        pl.BlockSpec((span, LANES), lambda i: (block_at(i), 0)),
        fixed(row),
    ]
    out_specs = [
        pl.BlockSpec((count, width), lambda i: (0, 0)),
        pl.BlockSpec((3, count, LANES), lambda i: (0, 0, pair_at(i))),
        pl.BlockSpec((count, LANES), lambda i: (0, pair_at(i))),
        pl.BlockSpec((1, 8, count), lambda i: (pair_at(i), 0, 0)),
        pl.BlockSpec((span, width), lambda i: (block_at(i), 0)),
        pl.BlockSpec((count, width), lambda i: (0, 0)),
        pl.BlockSpec((span, LANES), lambda i: (block_at(i), 0)),
        pl.BlockSpec((span, width), lambda i: (jnp.clip(i - pairs - blocks, 0, turns - 1), 0)),
    ]
    out_shape = [
        jax.ShapeDtypeStruct((count, width), bf16),
        jax.ShapeDtypeStruct((3, count, width), bf16),
        jax.ShapeDtypeStruct((count, width), bf16),
        jax.ShapeDtypeStruct((pairs, 8, count), f32),
        jax.ShapeDtypeStruct((count, width), f32),
        jax.ShapeDtypeStruct((count, width), bf16),
        jax.ShapeDtypeStruct((count, LANES), f32),
        jax.ShapeDtypeStruct((slots, width), bf16),
    ]
    scratch = [pltpu.VMEM((count, width), bf16)]
    for array in rides:
        scratch += exchange_sems(array.shape[0])
    return pl.pallas_call(
        riding(functools.partial(front_kernel, pairs, blocks), len(in_specs), len(out_specs), len(rides)),
        out_shape=out_shape + [jax.ShapeDtypeStruct(array.shape, array.dtype) for array in rides],
        grid=(pairs + blocks + turns,),
        in_specs=in_specs + [anywhere] * len(rides),
        out_specs=out_specs + [anywhere] * len(rides),
        scratch_shapes=scratch,
        compiler_params=params(52, collective_id=0, has_side_effects=True),
        cost_estimate=cost(18 * count * count * width, 24 * count * width, 8 * count * count),
        name="front",
    )(tokens, gain, w_qkv, w_qkv, w_qkv, w_out, gain_moe, wr, col, row, *rides)


def attend_back_kernel(q_ref, k_ref, v_ref, o_ref, do_ref, lse_ref, out_ref, dk_sc, dv_sc):
    lane = iota((QB, LANES), 1)
    keep = iota((QB, QB), 0) <= iota((QB, QB), 1)
    dk_sc[...] = jnp.zeros_like(dk_sc)
    dv_sc[...] = jnp.zeros_like(dv_sc)
    sub = iota((8, LANES), 0)
    picks = jnp.where(iota((8, LANES), 1) // HEAD_DIM == sub, 1.0, 0.0)
    low = (iota((LEN, LANES), 1) // HEAD_DIM) == 0
    key = k_ref[...]
    none = jnp.zeros_like(key)
    keys = (jnp.where(low, key, none), jnp.where(low, none, key))
    for block in range(LEN // QB):
        start, stop = block * QB, (block + 1) * QB
        query = q_ref[start:stop, :]
        d_out = do_ref[start:stop, :]
        product = d_out.astype(f32) * o_ref[start:stop, :].astype(f32)
        delta = dot_nt(picks, product, precision=lax.Precision.HIGHEST)
        d_query = jnp.zeros((QB, LANES), f32)
        for head in range(2):
            mine = (lane // HEAD_DIM) == head
            query_one = jnp.where(mine, query, jnp.zeros_like(query))
            d_one = jnp.where(mine, d_out, jnp.zeros_like(d_out))
            scores = dot_nt(k_ref[0:stop, :], query_one)
            tail = jnp.where(keep, scores[start:stop, :], mask_fill)
            scores = tail if block == 0 else jnp.concatenate([scores[0:start, :], tail], axis=0)
            probs = jnp.exp2(scores * SCALE2 - lse_ref[0, head : head + 1, start:stop])
            d_probs = dot_nt(v_ref[0:stop, :], d_one)
            d_scores = (probs * (d_probs - delta[head : head + 1, :])).astype(bf16)
            dv_sc[0:stop, :] += dot_nn(probs.astype(bf16), d_one)
            dk_sc[0:stop, :] += dot_nn(d_scores, query_one)
            d_query = d_query + dot_tn(d_scores, keys[head][0:stop, :])
        out_ref[0, start:stop, :] = (d_query * (1.0 / math.sqrt(HEAD_DIM))).astype(bf16)
    out_ref[1, :, :] = (dk_sc[...] * (1.0 / math.sqrt(HEAD_DIM))).astype(bf16)
    out_ref[2, :, :] = dv_sc[...].astype(bf16)


def attend_back(qkv, mixed, d_mixed, lse):
    count, width = mixed.shape
    pairs = width // LANES
    return pl.pallas_call(
        attend_back_kernel,
        out_shape=jax.ShapeDtypeStruct((3, count, width), bf16),
        grid=(pairs,),
        in_specs=[
            pl.BlockSpec((count, LANES), lambda i: (0, i)),
            pl.BlockSpec((count, LANES), lambda i: (0, i + pairs)),
            pl.BlockSpec((count, LANES), lambda i: (0, i + 2 * pairs)),
            pl.BlockSpec((count, LANES), lambda i: (0, i)),
            pl.BlockSpec((count, LANES), lambda i: (0, i)),
            pl.BlockSpec((1, 8, count), lambda i: (i, 0, 0)),
        ],
        out_specs=pl.BlockSpec((3, count, LANES), lambda i: (0, 0, i)),
        scratch_shapes=[pltpu.VMEM((count, LANES), f32), pltpu.VMEM((count, LANES), f32)],
        compiler_params=params(40),
        cost_estimate=cost(5 * 4 * count * count * width, 16 * count * width, 8 * count * count),
        name="attend_back",
    )(qkv, qkv, qkv, mixed, d_mixed, lse)


RIDE_PER_TURN = 2
LAG = 2


def back_reduce_kernel(
    chips,
    q_ref, k_ref, v_ref, o_ref, lse_ref, norm_ref, mix_ref, moe_ref,
    col_ref, gate_ref, din_ref, h_ref, og_ref, gain_ref, wr_ref, pull_ref, w_out_ref, slot_ref,
    dstate_ref, out_ref, sum_ref, extra_ref, back_ref,
    datt_ref, dmix_ref, dlog_ref, gm_ref,
    dk_sc, dv_sc, norm_t, mix_t, right, terms, firsts, sums, half0, half1, half2, half3, s_send, s_recv,
    *ride_sems,
):
    halves = (half0, half1, half2, half3)
    levels = chips.bit_length() - 1
    count = k_ref.shape[0]
    width = norm_ref.shape[1]
    rows = terms.shape[3]
    span = 256
    blocks = count // span
    turn = pl.program_id(0) - blocks
    pairs = sum_ref.shape[0]
    me = lax.axis_index("dp")
    chip, core = lax.div(me, 2), lax.rem(me, 2)
    mate = 2 * chip + 1 - core
    order0 = [1 << b for b in range(levels)]
    order1 = list(order0)
    order1[0], order1[1] = order0[1], order0[0]
    order0[2:] = order0[2:][::-1]

    def bit(mask):
        return lax.rem(lax.div(chip, mask), 2)

    own, peers = [], []
    for level in range(levels):
        b0, b1 = bit(order0[level]), bit(order1[level])
        own.append(b0 + core * (b1 - b0))
        p0 = order0[level] * (1 - 2 * b0)
        p1 = order1[level] * (1 - 2 * b1)
        peers.append(2 * (chip + p0 + core * (p1 - p0)) + core)
    bases = [0]
    for level in range(levels):
        bases.append(bases[-1] + own[level] * (chips >> (level + 1)))

    def remote(src, dst, c, level, device):
        return pltpu.make_async_remote_copy(
            src_ref=src, dst_ref=dst, send_sem=s_send.at[c, level], recv_sem=s_recv.at[c, level],
            device_id=(device,), device_id_type=MESH,
        )

    def cols(c):
        return pl.ds(0, LANES) if isinstance(c, int) else slice(None)

    def place(c):
        return LAG + 1 if isinstance(c, int) else lax.rem(c, LAG + 1)

    def swap(c):
        return remote(
            terms.at[place(c), :, 1 - core, :, cols(c)], firsts.at[c, :, :, cols(c)], c, levels, mate
        )

    def send(c, level):
        span = chips >> (level + 1)
        start = bases[level] + (1 - own[level]) * span
        return remote(
            sums.at[c, pl.ds(start, span), :, cols(c)], halves[level].at[c, :, :, cols(c)], c, level, peers[level]
        )

    def fold_swap(c):
        swap(c).wait()
        for b in range(chips):
            places = []
            for order in (order0, order1):
                spot = 0
                for level in range(levels):
                    spot += (b // order[level] % 2) * (chips >> (level + 1))
                places.append(spot)
            at = places[0] + core * (places[1] - places[0])
            total = terms[place(c), b, core, :, cols(c)].astype(f32) + firsts[c, b, :, cols(c)].astype(f32)
            sums[c, at, :, cols(c)] = total.astype(bf16)

    def fold(c, level):
        send(c, level).wait()
        for t in range(chips >> (level + 1)):
            at = bases[level + 1] + t
            total = sums[c, at, :, cols(c)].astype(f32) + halves[level][c, t, :, cols(c)].astype(f32)
            if level < levels - 1:
                sums[c, at, :, cols(c)] = total.astype(bf16)
            elif isinstance(c, int):
                extra_ref[...] = total
            else:
                sum_ref[c] = total

    def stage(c, s):
        if s == 1:
            fold_swap(c)
        else:
            fold(c, s - 2)
        if s - 1 < levels:
            send(c, s - 1).start()

    riders, ride = exchange_copies(slot_ref, back_ref, *ride_sems)
    per = span // (2 * rows)

    @pl.when(turn == -blocks)
    def _():
        greet([mate] + riders)
        gm_ref[...] = jnp.zeros_like(gm_ref)

    counts = [1] * blocks + [RIDE_PER_TURN] * len(ride)
    first = 0
    for at, many in enumerate(counts):
        if first < len(ride):

            @pl.when(turn == at - blocks)
            def _():
                for copy in ride[first : first + many]:
                    copy.start()

        first += many

    @pl.when(turn < 0)
    def _():
        slots = din_ref.shape[0]
        here = pl.ds(pl.multiple_of((turn + blocks) * span, span), span)
        col = col_ref[...]
        hot0, hot1 = hot_rows(col, 0, span, slots), hot_rows(col, 1, span, slots)
        gathered = dot_nn(hot0 + hot1, din_ref[...])
        table = pull_ref[:, 0, :]
        d_log, d_state, d_att, term = state_rows(
            col, gate_ref[...], h_ref[...], og_ref[...], gain_ref[...], wr_ref[...], gathered,
            pull_rows(col, 0, table, slots), pull_rows(col, 1, table, slots),
        )
        dstate_ref[...] = d_state
        dlog_ref[here, :] = d_log
        datt_ref[here, :] = d_att
        dmix_ref[here, :] = dot_nt(d_att, w_out_ref[...]).astype(bf16)
        gm_ref[...] += term

    @pl.when(turn == 0)
    def _():
        norm_t[...] = jnp.transpose(norm_ref[...])
        mix_t[...] = jnp.transpose(mix_ref[...])
        for row in range(0, width, span):
            extra = dot_tn(moe_ref[:, row : row + span], dlog_ref[...])
            gain = jnp.transpose(jnp.sum(gm_ref[:, row : row + span], axis=0, keepdims=True))
            extra = extra + jnp.where(iota(extra.shape, 1) == 64, gain, 0.0)
            at = row // (2 * rows)
            terms[place(pairs), at : at + per, :, :, 0:LANES] = extra.astype(bf16).reshape(per, 2, rows, LANES)
        swap(pairs).start()

    for s in range(levels + 1, 0, -1):
        c = turn - LAG * s

        @pl.when((c >= 0) & (c < pairs))
        def _():
            stage(c, s)

        @pl.when(c == 0)
        def _():
            stage(pairs, s)

    @pl.when((turn >= 0) & (turn < pairs))
    def _():
        lanes = pl.ds(pl.multiple_of(turn * LANES, LANES), LANES)
        attend_back_kernel(
            q_ref, k_ref, v_ref, o_ref, dmix_ref.at[:, lanes], lse_ref, out_ref, dk_sc, dv_sc
        )
        for i in range(3):
            right[:, i * LANES : (i + 1) * LANES] = out_ref[i]
        for row in range(0, width, span):
            qkv_rows = dot_nn(norm_t[row : row + span, :], right[...])
            out_rows = dot_nn(mix_t[row : row + span, :], datt_ref[:, lanes])
            at = row // (2 * rows)
            terms[place(turn), at : at + per, :, :, 0 : 3 * LANES] = (
                qkv_rows.astype(bf16).reshape(per, 2, rows, 3 * LANES)
            )
            terms[place(turn), at : at + per, :, :, 3 * LANES :] = (
                out_rows.astype(bf16).reshape(per, 2, rows, LANES)
            )
        swap(turn).start()

    @pl.when(pl.program_id(0) == pl.num_programs(0) - 1)
    def _():
        for copy in ride:
            copy.wait()


def attend_back_reduce(
    qkv, mixed, lse, normed, moe_low, col, gates, d_in, hidden, out_grad, gain, wr, pulls, w_out, slot_rows, n_dev
):
    count, width = mixed.shape
    pairs = width // LANES
    chips = n_dev // 2
    levels = chips.bit_length() - 1
    rows = width // n_dev
    wide = 4 * LANES
    span = 256
    blocks = count // span
    vmem, dma = pltpu.VMEM, pltpu.SemaphoreType.DMA
    anywhere = pl.BlockSpec(memory_space=pl.ANY)

    def pair_at(i):
        return jnp.clip(i - blocks, 0, pairs - 1)

    def block(lanes):
        return pl.BlockSpec((span, lanes), lambda i: (jnp.minimum(i, blocks - 1), 0))

    def third(which):
        return pl.BlockSpec((None, count, LANES), lambda i: (which, 0, pair_at(i)))

    def whole(array):
        return pl.BlockSpec(array.shape, lambda i: (0,) * array.ndim, pipeline_mode=pl.Buffered(1))

    gain = gain.reshape(1, width)
    d_state, d_qkv, sums, extra, back = pl.pallas_call(
        functools.partial(back_reduce_kernel, chips),
        out_shape=(
            jax.ShapeDtypeStruct((count, width), f32),
            jax.ShapeDtypeStruct((3, count, width), bf16),
            jax.ShapeDtypeStruct((pairs, rows, wide), f32),
            jax.ShapeDtypeStruct((rows, LANES), f32),
            jax.ShapeDtypeStruct(slot_rows.shape, bf16),
        ),
        grid=(blocks + pairs + LAG * (levels + 1),),
        in_specs=[
            third(0),
            third(1),
            third(2),
            pl.BlockSpec((count, LANES), lambda i: (0, pair_at(i))),
            pl.BlockSpec((1, 8, count), lambda i: (pair_at(i), 0, 0)),
            whole(normed),
            whole(mixed),
            whole(moe_low),
            block(LANES),
            block(LANES),
            whole(d_in),
            block(width),
            block(width),
            whole(gain),
            whole(wr),
            whole(pulls),
            whole(w_out),
            anywhere,
        ],
        out_specs=(
            block(width),
            pl.BlockSpec((3, count, LANES), lambda i: (0, 0, pair_at(i))),
            pl.BlockSpec((pairs, rows, wide), lambda i: (0, 0, 0)),
            pl.BlockSpec((rows, LANES), lambda i: (0, 0)),
            anywhere,
        ),
        scratch_shapes=[
            vmem((count, width), bf16),
            vmem((count, width), bf16),
            vmem((count, LANES), bf16),
            vmem((8, width), f32),
            vmem((count, LANES), f32),
            vmem((count, LANES), f32),
            vmem((width, count), bf16),
            vmem((width, count), bf16),
            vmem((count, 3 * LANES), bf16),
            vmem((LAG + 2, chips, 2, rows, wide), bf16),
            vmem((pairs + 1, chips, rows, wide), bf16),
            vmem((pairs + 1, chips, rows, wide), bf16),
        ]
        + [vmem((pairs + 1, chips >> (level + 1), rows, wide), bf16) for level in range(levels)]
        + [dma((pairs + 1, levels + 1)), dma((pairs + 1, levels + 1))]
        + exchange_sems(chips),
        compiler_params=params(62, collective_id=1, has_side_effects=True),
        cost_estimate=cost(5 * 4 * count * count * width, 40 * count * width, 8 * count * count),
        name="back_reduce",
    )(
        qkv, qkv, qkv, mixed, lse, normed, mixed, moe_low,
        col, gates, d_in, hidden, out_grad, gain, wr, pulls, w_out, slot_rows,
    )
    parts = sums.reshape(pairs, rows, 4, LANES)
    parts = jnp.transpose(parts, (1, 2, 0, 3)).reshape(rows, 4 * width)
    return d_state, d_qkv, parts[:, 0 : 3 * width], parts[:, 3 * width :], extra, back


def middle_rows(mixed, w_out, tokens, gain, wr, col):
    first, second, valid = col[:, 2:3], col[:, 3:4], col[:, 4:5].astype(f32)
    hidden = tokens.astype(f32) + valid * dot_nn(mixed, w_out)
    inverse = lax.rsqrt(jnp.mean(hidden * hidden, axis=1, keepdims=True) + epsilon)
    low = (hidden * inverse * gain).astype(bf16)
    logits = dot_nn(low, wr)
    lane = iota(logits.shape, 1)
    own = jnp.sum(jnp.where(lane == first, logits, 0.0), axis=1, keepdims=True)
    alt = jnp.sum(jnp.where(lane == second, logits, 0.0), axis=1, keepdims=True)
    gate0 = 1.0 / (1.0 + jnp.exp(alt - own))
    gate1 = 1.0 / (1.0 + jnp.exp(own - alt))
    return hidden, low, jnp.where(lane == 0, gate0, 0.0) + jnp.where(lane == 1, gate1, 0.0)


def middle_kernel(mixed_ref, w_out_ref, tok_ref, gain_ref, wr_ref, col_ref, h_ref, low_ref, gate_ref):
    h_ref[...], low_ref[...], gate_ref[...] = middle_rows(
        mixed_ref[...], w_out_ref[...], tok_ref[...], gain_ref[...], wr_ref[...], col_ref[...]
    )


def middle(mixed, w_out, tokens, gain, wr, col):
    count, width = mixed.shape
    rows = 256
    whole = lambda i: (0, 0)
    part = lambda i: (i, 0)
    return pl.pallas_call(
        middle_kernel,
        out_shape=(
            jax.ShapeDtypeStruct((count, width), f32),
            jax.ShapeDtypeStruct((count, width), bf16),
            jax.ShapeDtypeStruct((count, LANES), f32),
        ),
        grid=(count // rows,),
        in_specs=[
            pl.BlockSpec((rows, width), part),
            pl.BlockSpec((width, width), whole),
            pl.BlockSpec((rows, width), part),
            pl.BlockSpec((1, width), whole),
            pl.BlockSpec((width, LANES), whole),
            pl.BlockSpec((rows, LANES), part),
        ],
        out_specs=(
            pl.BlockSpec((rows, width), part),
            pl.BlockSpec((rows, width), part),
            pl.BlockSpec((rows, LANES), part),
        ),
        compiler_params=params(40),
        cost_estimate=cost(2 * count * width * width, 12 * count * width),
        name="middle",
    )(mixed, w_out, tokens, gain.reshape(1, width), wr, col)


GELU_C = math.sqrt(2.0 / math.pi)


def expert_kernel(
    split, x_ref, g_ref, wg_ref, wu_ref, wd_ref, wr_ref, act_ref, dgp_ref, dup_ref, de_ref, part_ref, din_ref
):
    rows, width = x_ref.shape
    me = lax.axis_index("dp")
    expert, part = me // split, lax.rem(me, split)
    x = x_ref[...]
    lane = iota((rows, LANES), 1)
    logits = dot_nn(x, wr_ref[...])
    own = jnp.sum(jnp.where(lane == expert, logits, 0.0), axis=1, keepdims=True)
    other = g_ref[:, width:].astype(f32).astype(jnp.int32)
    alt = jnp.sum(jnp.where(lane == other, logits, 0.0), axis=1, keepdims=True)
    gate = 1.0 / (1.0 + jnp.exp(alt - own))
    d_rows = (g_ref[:, 0:width].astype(f32) * gate).astype(bf16)
    de_ref[...] = d_rows
    pre = dot_nn(x, wg_ref[...])
    up = dot_nn(x, wu_ref[...])
    d_hidden = dot_nt(d_rows, wd_ref[...])
    square = pre * pre
    bent = jnp.tanh(GELU_C * pre * (1.0 + 0.044715 * square))
    half = 0.5 * (1.0 + bent)
    gelu = pre * half
    slope = half + 0.5 * pre * (1.0 - bent * bent) * (GELU_C * (1.0 + 3 * 0.044715 * square))
    act = (gelu * up).astype(bf16)
    act_ref[...] = act
    dgp = (d_hidden * up * slope).astype(bf16)
    dup = (d_hidden * gelu).astype(bf16)
    dgp_ref[...] = dgp
    dup_ref[...] = dup
    pull = jnp.sum(act.astype(f32) * d_hidden, axis=1, keepdims=True)
    pull_high = pull.astype(bf16)
    pull_low = (pull - pull_high.astype(f32)).astype(bf16)
    part_ref[...] = dot_nn(act, wd_ref[...]).astype(bf16)
    din_ref[:, 0:width] = (dot_nt(dgp, wg_ref[...]) + dot_nt(dup, wu_ref[...])).astype(bf16)
    extra = jnp.where(lane == 2 * part, pull_high.astype(f32), 0.0)
    extra = extra + jnp.where(lane == 2 * part + 1, pull_low.astype(f32), 0.0)
    din_ref[:, width:] = extra.astype(bf16)


def expert_pass(x, g, wg, wu, wd, wr, split):
    count, width = x.shape
    ff = wg.shape[1]
    rows = 256
    whole = lambda i: (0, 0)
    part = lambda i: (i, 0)
    once = dict(pipeline_mode=pl.Buffered(1))
    return pl.pallas_call(
        functools.partial(expert_kernel, split),
        out_shape=(
            jax.ShapeDtypeStruct((count, ff), bf16),
            jax.ShapeDtypeStruct((count, ff), bf16),
            jax.ShapeDtypeStruct((count, ff), bf16),
            jax.ShapeDtypeStruct((count, width), bf16),
            jax.ShapeDtypeStruct((count, width), bf16),
            jax.ShapeDtypeStruct((count, width + LANES), bf16),
        ),
        grid=(count // rows,),
        in_specs=[
            pl.BlockSpec((rows, width), part),
            pl.BlockSpec((rows, width + LANES), part),
            pl.BlockSpec((width, ff), whole, **once),
            pl.BlockSpec((width, ff), whole, **once),
            pl.BlockSpec((ff, width), whole, **once),
            pl.BlockSpec((width, LANES), whole),
        ],
        out_specs=(
            pl.BlockSpec((rows, ff), part),
            pl.BlockSpec((rows, ff), part),
            pl.BlockSpec((rows, ff), part),
            pl.BlockSpec((rows, width), part),
            pl.BlockSpec((rows, width), part),
            pl.BlockSpec((rows, width + LANES), part),
        ),
        compiler_params=params(56),
        cost_estimate=cost(12 * count * width * ff, 2 * count * (3 * ff + 5 * width), count * ff),
        name="experts",
    )(x, g, wg, wu, wd, wr)


def expert_exchange_kernel(
    group, x_ref, g_ref, oth_ref, wg_hbm, wu_hbm, wd_hbm, wr_ref,
    gg_ref, ug_ref, dg_ref, slot_ref, back_ref, pulls_ref, gm_ref,
    xb, gb, oth, oth_mate, ds, rd, pd, sp, rp, pp, pt, pq, rq, act, dgp, dup, de, xt, acc_g, acc_u, acc_d,
    wg_ref, wu_ref, wd_ref,
    w_sem, x_send, x_recv, f_send, f_recv, g_load, g_send, g_recv,
    d_send, d_recv, p_send, p_recv, q_send, q_recv, b_send, b_recv, t_send, t_recv, s_sem, l_sem, o_sem,
):
    experts, capacity, width = x_ref.shape
    ff = wg_ref.shape[1]
    steps = experts // group
    pair = 2 * capacity
    rows = group * pair
    half = experts // 2
    me = lax.axis_index("dp")
    chip, core = lax.div(me, 2), lax.rem(me, 2)
    mate = 2 * chip + 1 - core

    def bits(place):
        if isinstance(place, int):
            return half + place // 2 if place % 2 else place // 2
        return lax.rem(place, 2) * half + lax.div(place, 2)

    def chip_at(place):
        return flip(chip, bits(place), experts)

    def remote(src, dst, send, recv, device):
        return pltpu.make_async_remote_copy(
            src_ref=src, dst_ref=dst, send_sem=send, recv_sem=recv, device_id=(device,), device_id_type=MESH
        )

    def block(q, g, second):
        start = q * rows + g * pair + second * capacity
        return xb.at[pl.ds(start if isinstance(start, int) else pl.multiple_of(start, 16), capacity)]

    def x_copy(place):
        peer = chip_at(place)
        own = block(place // group, place % group, 0)
        return remote(x_ref.at[peer], own, x_send.at[place], x_recv.at[place], 2 * peer + core)

    def x_arrival(q, g):
        place = q * group + g
        return remote(x_ref.at[chip], block(q, g, 0), x_send.at[place], x_recv.at[place], mate)

    def forward(q, g):
        place = q * group + g
        return remote(block(q, g, 0), block(q, g, 1), f_send.at[place], f_recv.at[place], mate)

    def g_mate(q, g):
        place = q * group + g
        at = chip_at(place)
        return remote(g_ref.at[at], gm_ref.at[at], g_send.at[place], g_recv.at[place], mate)

    def g_loads(q, g):
        slot, at = lax.rem(q, 2), chip_at(q * group + g)
        first, second = g * pair, g * pair + capacity
        return (
            pltpu.make_async_copy(g_ref.at[at], gb.at[slot, first:second], g_load.at[slot, 2 * g]),
            pltpu.make_async_copy(gm_ref.at[at], gb.at[slot, second : second + capacity], g_load.at[slot, 2 * g + 1]),
        )

    def load_g(q):
        for g in range(group):
            g_mate(q, g).wait_recv()
            for copy in g_loads(q, g):
                copy.start()

    def d_copy(q, g):
        place, slot = q * group + g, lax.rem(q, 2)
        return remote(pd.at[slot, g], rd.at[slot, g], d_send.at[place], d_recv.at[place], mate)

    def p_copy(q, g):
        place, slot = q * group + g, lax.rem(q, 2)
        return remote(pp.at[slot, g], rp.at[slot, g], p_send.at[place], p_recv.at[place], mate)

    def q_copy(q, g):
        place, slot = q * group + g, lax.rem(q, 2)
        return remote(pq.at[slot, g], rq.at[slot, g], q_send.at[place], q_recv.at[place], mate)

    def back_copies(q, g):
        place = q * group + g
        device = 2 * chip_at(place) + core
        return (
            remote(pt.at[place], pulls_ref.at[chip], t_send.at[place], t_recv.at[place], device),
            remote(ds.at[place], back_ref.at[chip], b_send.at[place], b_recv.at[place], device),
        )

    def slot_copy(q, g):
        place = q * group + g
        return pltpu.make_async_copy(sp.at[place], slot_ref.at[chip_at(place)], s_sem.at[place])

    weights = [
        pltpu.make_async_copy(src, dst, w_sem.at[i])
        for i, (src, dst) in enumerate(((wg_hbm, wg_ref), (wu_hbm, wu_ref), (wd_hbm, wd_ref)))
    ]
    grads = [
        pltpu.make_async_copy(src, dst, o_sem.at[i])
        for i, (src, dst) in enumerate(((acc_g, gg_ref), (acc_u, ug_ref), (acc_d, dg_ref)))
    ]
    self_x = pltpu.make_async_copy(x_ref.at[chip], block(0, 0, 0), l_sem.at[0])
    self_pull = pltpu.make_async_copy(pt.at[0], pulls_ref.at[chip], l_sem.at[1])
    self_back = pltpu.make_async_copy(ds.at[0], back_ref.at[chip], l_sem.at[2])
    oth_own = pltpu.make_async_copy(oth_ref, oth, l_sem.at[3])
    oth_copy = remote(oth_ref, oth_mate, l_sem.at[4], l_sem.at[5], mate)

    for copy in weights:
        copy.start()
    self_x.start()
    oth_own.start()
    greet([2 * chip_at(place) + core for place in range(1, experts)] + [mate])
    oth_copy.start()
    for place in range(1, group):
        x_copy(place).start()
    for q in range(steps):
        for g in range(group):
            g_mate(q, g).start()
        for g in range(group):
            if (q + 1) * group + g < experts:
                x_copy((q + 1) * group + g).start()
    for acc in (acc_g, acc_u, acc_d):
        acc[...] = jnp.zeros_like(acc)
    pt[...] = jnp.zeros_like(pt)
    pq[...] = jnp.zeros_like(pq)
    self_x.wait()
    forward(0, 0).start()
    oth_own.wait()
    oth_copy.wait()
    load_g(jnp.int32(0))
    for g in range(1, group):
        x_arrival(0, g).wait_recv()
        forward(0, g).start()
    for copy in weights:
        copy.wait()

    def finish(q):
        slot = lax.rem(q, 2)
        for g in range(group):
            place = q * group + g
            q_copy(q, g).wait_recv()
            d_copy(q, g).wait_recv()
            pt[place] = pt[place] + rq[slot, g]
            ds[place] = (ds[place].astype(f32) + rd[slot, g].astype(f32)).astype(bf16)
            if g == 0:

                @pl.when(q == 0)
                def _():
                    self_pull.start()
                    self_back.start()

                @pl.when(q > 0)
                def _():
                    for copy in back_copies(q, g):
                        copy.start()

            else:
                for copy in back_copies(q, g):
                    copy.start()
        for g in range(group):
            place = q * group + g
            p_copy(q, g).wait_recv()
            sp[place] = (sp[place].astype(f32) + rp[slot, g].astype(f32)).astype(bf16)
            slot_copy(q, g).start()

    def weight_grads(q):
        xt[...] = jnp.transpose(xb[pl.ds(pl.multiple_of((q - 2) * rows, 16), 2 * rows), :])
        span = 256
        for row in range(0, width, span):
            acc_g[row : row + span, :] += dot_nn(xt[row : row + span, :], dgp[...])
            acc_u[row : row + span, :] += dot_nn(xt[row : row + span, :], dup[...])
        for row in range(0, ff, LANES):
            acc_d[row : row + LANES, :] += dot_tn(act[:, row : row + LANES], de[...])

    def main(q):
        slot = lax.rem(q, 2)
        here = pl.ds(pl.multiple_of(slot * rows, 16), rows)
        for g in range(group):
            for copy in g_loads(q, g):
                copy.wait()
            forward(q, g).wait_recv()

        @pl.when(q + 1 < steps)
        def _():
            load_g(q + 1)

        x = xb[pl.ds(pl.multiple_of(q * rows, 16), rows), :]
        lane = iota((rows, LANES), 1)
        logits = dot_nn(x, wr_ref[...])
        mine = jnp.sum(jnp.where(lane == chip, logits, 0.0), axis=1, keepdims=True)
        ids = []
        for g in range(group):
            at = chip_at(q * group + g)
            for table in (oth, oth_mate):
                ids.append(jnp.transpose(table[at])[0:capacity, 0:1])
        other = jnp.concatenate(ids, axis=0).astype(jnp.int32)
        alt = jnp.sum(jnp.where(lane == other, logits, 0.0), axis=1, keepdims=True)
        gate = 1.0 / (1.0 + jnp.exp(alt - mine))
        d_rows = (gb[slot].astype(f32) * gate).astype(bf16)
        de[here, :] = d_rows
        pre = dot_nn(x, wg_ref[...])
        up = dot_nn(x, wu_ref[...])
        d_hidden = dot_nt(d_rows, wd_ref[...])
        square = pre * pre
        bent = jnp.tanh(GELU_C * pre * (1.0 + 0.044715 * square))
        hill = 0.5 * (1.0 + bent)
        gelu = pre * hill
        slope = hill + 0.5 * pre * (1.0 - bent * bent) * (GELU_C * (1.0 + 3 * 0.044715 * square))
        now = (gelu * up).astype(bf16)
        act[here, :] = now
        dgp[here, :] = (d_hidden * up * slope).astype(bf16)
        dup[here, :] = (d_hidden * gelu).astype(bf16)
        pull = jnp.sum(now.astype(f32) * d_hidden, axis=1, keepdims=True)

        @pl.when(q + 1 < steps)
        def _():
            for g in range(group):
                x_arrival(q + 1, g).wait_recv()
                forward(q + 1, g).start()

        @pl.when(q >= 1)
        def _():
            finish(q - 1)

        @pl.when(q >= 2)
        def _():
            for g in range(group):
                q_copy(q - 2, g).wait_send()
                d_copy(q - 2, g).wait_send()
                p_copy(q - 2, g).wait_send()

        d_in = (dot_nt(dgp[here, :], wg_ref[...]) + dot_nt(dup[here, :], wu_ref[...])).astype(bf16)
        pull = jnp.broadcast_to(pull, (rows, LANES))
        for g in range(group):
            place = q * group + g
            low, mid, high = g * pair, g * pair + capacity, (g + 1) * pair
            pt[place, :, 0:capacity] = jnp.transpose(pull[low:mid])[0:8, :]
            pq[slot, g, :, 0:capacity] = jnp.transpose(pull[mid:high])[0:8, :]
            ds[place] = d_in[low:mid]
            pd[slot, g] = d_in[mid:high]
            q_copy(q, g).start()
            d_copy(q, g).start()
        partial = dot_nn(act[here, :], wd_ref[...]).astype(bf16)
        for g in range(group):
            place = q * group + g
            low, mid, high = g * pair, g * pair + capacity, (g + 1) * pair
            sp[place] = partial[low:mid]
            pp[slot, g] = partial[mid:high]
            p_copy(q, g).start()

    def step(q, carry):
        @pl.when(q == steps)
        def _():
            finish(q - 1)

        @pl.when((q >= 2) & (lax.rem(q, 2) == 0))
        def _():
            weight_grads(q)

        @pl.when(q < steps)
        def _():
            main(q)

        return carry

    lax.fori_loop(0, steps + 1, step, 0)
    for copy in grads:
        copy.start()
    for q in (steps - 2, steps - 1):
        for g in range(group):
            q_copy(q, g).wait_send()
            d_copy(q, g).wait_send()
            p_copy(q, g).wait_send()
    self_pull.wait()
    self_back.wait()
    for q in range(steps):
        for g in range(group):
            place = q * group + g
            slot_copy(q, g).wait()
            forward(q, g).wait_send()
            g_mate(q, g).wait_send()
            if place:
                x_copy(place).wait_send()
                for copy in back_copies(q, g):
                    copy.wait()
    for copy in grads:
        copy.wait()


def expert_exchange(x, g, others, wg, wu, wd, wr, group=2):
    experts, capacity, width = x.shape
    ff = wg.shape[1]
    steps = experts // group
    rows = 2 * capacity * group
    anywhere = pl.BlockSpec(memory_space=pl.ANY)
    vmem, dma = pltpu.VMEM, pltpu.SemaphoreType.DMA
    each = dma((experts,))
    count = rows * steps
    outs = pl.pallas_call(
        functools.partial(expert_exchange_kernel, group),
        out_shape=(
            jax.ShapeDtypeStruct((width, ff), f32),
            jax.ShapeDtypeStruct((width, ff), f32),
            jax.ShapeDtypeStruct((ff, width), f32),
            jax.ShapeDtypeStruct((experts, capacity, width), bf16),
            jax.ShapeDtypeStruct((experts, capacity, width), bf16),
            jax.ShapeDtypeStruct((experts, 8, LANES), f32),
            jax.ShapeDtypeStruct((experts, capacity, width), bf16),
        ),
        in_specs=[anywhere] * 6 + [pl.BlockSpec(memory_space=vmem)],
        out_specs=(anywhere,) * 7,
        scratch_shapes=[
            vmem((steps * rows, width), bf16),
            vmem((2, rows, width), bf16),
            vmem((experts, 8, LANES), f32),
            vmem((experts, 8, LANES), f32),
            vmem((experts, capacity, width), bf16),
            vmem((2, group, capacity, width), bf16),
            vmem((2, group, capacity, width), bf16),
            vmem((experts, capacity, width), bf16),
            vmem((2, group, capacity, width), bf16),
            vmem((2, group, capacity, width), bf16),
            vmem((experts, 8, LANES), f32),
            vmem((2, group, 8, LANES), f32),
            vmem((2, group, 8, LANES), f32),
            vmem((2 * rows, ff), bf16),
            vmem((2 * rows, ff), bf16),
            vmem((2 * rows, ff), bf16),
            vmem((2 * rows, width), bf16),
            vmem((width, 2 * rows), bf16),
            vmem((width, ff), f32),
            vmem((width, ff), f32),
            vmem((ff, width), f32),
            vmem((width, ff), bf16),
            vmem((width, ff), bf16),
            vmem((ff, width), bf16),
            dma((3,)),
            each, each, each, each,
            dma((2, 2 * group)),
            each, each,
            each, each, each, each, each, each, each, each, each, each, each,
            dma((6,)),
            dma((3,)),
        ],
        compiler_params=params(62, collective_id=2, has_side_effects=True),
        cost_estimate=cost(18 * count * width * ff, 2 * count * 4 * width + 18 * width * ff, count * ff),
        name="experts",
    )(x, g, others, wg, wu, wd, wr)
    return outs[:6]


def hot_rows(col, k, rows, slots):
    return jnp.where(iota((rows, slots), 1) == col[:, k : k + 1], 1.0, 0.0).astype(bf16)


def state_rows(col, gates, hidden, out_grad, gain, wr, gathered, pull0, pull1):
    valid = col[:, 4:5].astype(f32)
    total = pull0 + pull1
    lane = iota((col.shape[0], LANES), 1)
    d_log = jnp.where(lane == col[:, 2:3], pull0 - gates[:, 0:1] * total, 0.0)
    d_log = d_log + jnp.where(lane == col[:, 3:4], pull1 - gates[:, 1:2] * total, 0.0)
    d_log = d_log.astype(bf16)
    d_moe = gathered + dot_nt(d_log, wr)
    inverse = lax.rsqrt(jnp.mean(hidden * hidden, axis=1, keepdims=True) + epsilon)
    normal = hidden * inverse
    scaled = gain * d_moe
    share = jnp.mean(normal * scaled, axis=1, keepdims=True)
    d_state = out_grad.astype(f32) + inverse * (scaled - normal * share)
    term = jnp.sum((normal * d_moe).reshape(hidden.shape[0] // 8, 8, hidden.shape[1]), axis=0)
    return d_log, d_state, (valid * d_state).astype(bf16), term


def pull_rows(col, k, table, slots):
    experts, rows = table.shape[0], col.shape[0]
    chosen = jnp.where(iota((rows, experts), 1) == col[:, 2 + k : 3 + k], 1.0, 0.0)
    values = dot_nn(chosen, table, precision=lax.Precision.HIGHEST)
    slot = col[:, k : k + 1] - slots // experts * col[:, 2 + k : 3 + k]
    here = (iota((rows, LANES), 1) == slot) & (col[:, k : k + 1] < slots)
    return jnp.sum(jnp.where(here, values, 0.0), axis=1, keepdims=True)


def state_kernel(
    col_ref, gate_ref, din_ref, h_ref, og_ref, gain_ref, wr_ref, dstate_ref, dattn_ref, dlog_ref, gterm_ref
):
    rows, width = h_ref.shape
    slots = din_ref.shape[0]
    col = col_ref[...]
    hot0, hot1 = hot_rows(col, 0, rows, slots), hot_rows(col, 1, rows, slots)
    pulls = din_ref[:, width:]
    pull0 = jnp.sum(dot_nn(hot0, pulls), axis=1, keepdims=True)
    pull1 = jnp.sum(dot_nn(hot1, pulls), axis=1, keepdims=True)
    gathered = dot_nn(hot0 + hot1, din_ref[:, 0:width])
    dlog_ref[...], dstate_ref[...], dattn_ref[...], term = state_rows(
        col, gate_ref[...], h_ref[...], og_ref[...], gain_ref[...], wr_ref[...], gathered, pull0, pull1
    )

    @pl.when(pl.program_id(0) == 0)
    def _():
        gterm_ref[...] = jnp.zeros_like(gterm_ref)

    gterm_ref[...] += term


def state_back(col, gates, din, hidden, out_grad, gain, wr):
    count, width = hidden.shape
    slots = din.shape[0]
    rows = 256
    whole = lambda i: (0, 0)
    part = lambda i: (i, 0)
    return pl.pallas_call(
        state_kernel,
        out_shape=(
            jax.ShapeDtypeStruct((count, width), f32),
            jax.ShapeDtypeStruct((count, width), bf16),
            jax.ShapeDtypeStruct((count, LANES), bf16),
            jax.ShapeDtypeStruct((8, width), f32),
        ),
        grid=(count // rows,),
        in_specs=[
            pl.BlockSpec((rows, LANES), part),
            pl.BlockSpec((rows, LANES), part),
            pl.BlockSpec(din.shape, whole),
            pl.BlockSpec((rows, width), part),
            pl.BlockSpec((rows, width), part),
            pl.BlockSpec((1, width), whole),
            pl.BlockSpec((width, LANES), whole),
        ],
        out_specs=(
            pl.BlockSpec((rows, width), part),
            pl.BlockSpec((rows, width), part),
            pl.BlockSpec((rows, LANES), part),
            pl.BlockSpec((8, width), whole),
        ),
        compiler_params=params(48),
        cost_estimate=cost(2 * slots * count * width, 14 * count * width),
        name="state_back",
    )(col, gates, din, hidden, out_grad, gain.reshape(1, width), wr)


def block_out_kernel(n_ride, col_ref, gate_ref, rows_ref, h_ref, *refs):
    srcs, out_ref, dsts = refs[:n_ride], refs[n_ride], refs[n_ride + 1 :]
    for src, dst in zip(srcs, dsts):
        dst[...] = src[...]
    rows, width = h_ref.shape
    slots = rows_ref.shape[0]
    col = col_ref[...]
    pick0 = dot_nn(hot_rows(col, 0, rows, slots), rows_ref[...])
    pick1 = dot_nn(hot_rows(col, 1, rows, slots), rows_ref[...])
    out_ref[...] = (h_ref[...] + gate_ref[:, 0:1] * pick0 + gate_ref[:, 1:2] * pick1).astype(bf16)


def make_block_out(col, gates, slot_rows, hidden, riders=()):
    count, width = hidden.shape
    slots = slot_rows.shape[0]
    rows = 256
    steps = count // rows
    whole = lambda i: (0, 0)
    part = lambda i: (i, 0)
    passed = [pl.BlockSpec((array.shape[0] // steps, array.shape[1]), part) for array in riders]
    return pl.pallas_call(
        functools.partial(block_out_kernel, len(riders)),
        out_shape=[jax.ShapeDtypeStruct((count, width), bf16)]
        + [jax.ShapeDtypeStruct(array.shape, array.dtype) for array in riders],
        grid=(steps,),
        in_specs=[
            pl.BlockSpec((rows, LANES), part),
            pl.BlockSpec((rows, LANES), part),
            pl.BlockSpec((slots, width), whole),
            pl.BlockSpec((rows, width), part),
        ]
        + passed,
        out_specs=[pl.BlockSpec((rows, width), part)] + passed,
        compiler_params=params(48),
        cost_estimate=cost(4 * slots * count * width, 9 * count * width),
        name="block_out",
    )(col, gates, slot_rows, hidden, *riders)


def input_kernel(n_ride, d_ref, w_ref, tok_ref, gain_ref, dstate_ref, *refs):
    srcs, grad_ref, dsts = refs[:n_ride], refs[n_ride], refs[n_ride + 1 :]
    for src, dst in zip(srcs, dsts):
        dst[...] = src[...]
    rows, width = tok_ref.shape
    d_normed = dot_nt(d_ref[0], w_ref[:, 0:width])
    for i in range(1, 3):
        d_normed = d_normed + dot_nt(d_ref[i], w_ref[:, i * width : (i + 1) * width])
    values = tok_ref[...].astype(f32)
    inverse = lax.rsqrt(jnp.mean(values * values, axis=1, keepdims=True) + epsilon)
    normal = values * inverse
    scaled = gain_ref[...] * d_normed
    share = jnp.mean(normal * scaled, axis=1, keepdims=True)
    grad_ref[...] = dstate_ref[...] + inverse * (scaled - normal * share)


def input_back(d_qkv, w_qkv, tokens, gain, d_state, riders=()):
    count, width = tokens.shape
    rows = 256
    steps = count // rows
    whole = lambda i: (0, 0)
    part = lambda i: (i, 0)
    passed = [pl.BlockSpec((array.shape[0] // steps, array.shape[1]), part) for array in riders]
    return pl.pallas_call(
        functools.partial(input_kernel, len(riders)),
        out_shape=[jax.ShapeDtypeStruct((count, width), f32)]
        + [jax.ShapeDtypeStruct(array.shape, array.dtype) for array in riders],
        grid=(steps,),
        in_specs=[
            pl.BlockSpec((3, rows, width), lambda i: (0, i, 0)),
            pl.BlockSpec((width, 3 * width), whole),
            pl.BlockSpec((rows, width), part),
            pl.BlockSpec((1, width), whole),
            pl.BlockSpec((rows, width), part),
        ]
        + passed,
        out_specs=[pl.BlockSpec((rows, width), part)] + passed,
        compiler_params=params(56),
        cost_estimate=cost(6 * count * width * width, 22 * count * width),
        name="input_back",
    )(d_qkv, w_qkv, tokens, gain.reshape(1, width), d_state, *riders)


def shards(
    tokens,
    lengths,
    expert_ids,
    slot_order,
    gain_attn,
    w_qkv,
    w_out,
    gain_moe,
    w_router,
    w_gate,
    w_up,
    w_down,
    out_grad,
):
    tok_dev, width = tokens.shape
    n_dev = lax.axis_size("dp")
    experts = w_router.shape[1]
    split = n_dev // experts
    capacity = split * (5 * tok_dev // (4 * n_dev))
    slots = experts * capacity
    me = lax.axis_index("dp")
    part = lax.rem(me, split)
    same_part = [[e * split + p for e in range(experts)] for p in range(split)]
    same_expert = [[e * split + p for p in range(split)] for e in range(experts)]
    swap = [(d, d ^ 1) for d in range(n_dev)]

    def across(blocks):
        return lax.all_to_all(blocks, "dp", 0, 0, axis_index_groups=same_part, tiled=True)

    def share(rows):
        if split == 2:
            return jnp.concatenate([rows, lax.ppermute(rows, "dp", swap)], axis=0)
        return lax.all_gather(rows, "dp", axis_index_groups=same_expert, tiled=True)

    def settle(pieces):
        if split == 2:
            theirs = lax.ppermute(pieces[1], "dp", swap)
            return (pieces[0].astype(f32) + theirs.astype(f32)).astype(bf16)
        got = lax.all_to_all(pieces, "dp", 0, 0, axis_index_groups=same_expert, tiled=True)
        return jnp.sum(got.astype(f32), axis=0).astype(bf16)

    def send_in(rows):
        return share(across(rows.reshape(experts, capacity, -1)).reshape(slots, -1))

    def send_back(rows):
        summed = settle(rows.reshape(split, slots, -1))
        return across(summed.reshape(experts, capacity, -1)).reshape(slots, -1)

    def reduce_rows(term):
        pieces = term.reshape(experts, split, -1, term.shape[-1])
        if split == 2:
            mine = lax.dynamic_index_in_dim(pieces, part, 1, keepdims=False)
            theirs = lax.dynamic_index_in_dim(pieces, 1 - part, 1, keepdims=False)
            theirs = lax.ppermute(theirs.astype(bf16), "dp", swap)
            summed = (mine + theirs.astype(f32)).astype(bf16)
        else:
            pieces = jnp.moveaxis(pieces, 1, 0).astype(bf16)
            got = lax.all_to_all(pieces, "dp", 0, 0, axis_index_groups=same_expert, tiled=True)
            summed = jnp.sum(got.astype(f32), axis=0).astype(bf16)
        return jnp.sum(across(summed).astype(f32), axis=0)

    wr = jnp.pad(w_router, ((0, 0), (0, LANES - experts)))
    col, row = make_slots(lengths, expert_ids, slot_order, experts, capacity)
    direct = split == 2 and experts == 16

    if direct:
        grad_out, others = dispatch_pair(row, out_grad, experts, capacity)
        normed_low, qkv, mixed, lse, hidden, moe_low, gates, rows_out, grad_in, others = front(
            tokens, gain_attn, w_qkv, w_out, gain_moe, wr, col, row, slots,
            (grad_out.reshape(experts, capacity, -1), others),
        )
    else:
        token_vals = tokens.astype(f32)
        inverse_attn = lax.rsqrt(jnp.mean(token_vals * token_vals, axis=-1, keepdims=True) + epsilon)
        normed_low = (token_vals * inverse_attn * gain_attn).astype(bf16)
        qkv = jnp.dot(normed_low, w_qkv, preferred_element_type=f32).astype(bf16)
        mixed, lse = attend(qkv)
        grad_in = send_in(dispatch_grad(row, out_grad, slots))
        hidden, moe_low, gates = middle(mixed, w_out, tokens, gain_moe, wr, col)
        rows_out = dispatch(row, moe_low, slots)
    if direct:
        gate_grad, up_grad, down_grad, slot_part, d_in_back, pulls = expert_exchange(
            rows_out.reshape(experts, capacity, -1), grad_in, others, w_gate[0], w_up[0], w_down[0], wr
        )
        d_in_back = d_in_back.reshape(slots, -1)
    else:
        rows_in = send_in(rows_out)
        act, d_pre, d_up, d_rows, partial_out, d_in = expert_pass(
            rows_in, grad_in, w_gate[0], w_up[0], w_down[0], wr, split
        )
        d_in_back = send_back(d_in)
        slot_out = send_back(partial_out)
        down_grad = dot_tn(act, d_rows)
        gate_grad = dot_tn(rows_in, d_pre)
        up_grad = dot_tn(rows_in, d_up)

    if direct:
        d_state, d_qkv, qkv_sum, out_rows, extra, slot_out = attend_back_reduce(
            qkv, mixed, lse, normed_low, moe_low, col, gates, d_in_back, hidden, out_grad,
            gain_moe, wr, pulls, w_out, slot_part, n_dev,
        )
        slot_out = slot_out.reshape(slots, -1)
        router_sum, gain_moe_sum = extra[:, 0:experts], extra[:, 64]
    else:
        d_state, d_attn, d_log, gain_moe_rows = state_back(
            col, gates, d_in_back, hidden, out_grad, gain_moe, wr
        )
        d_mixed = dot_nt(d_attn, w_out).astype(bf16)
        d_qkv = attend_back(qkv, mixed, d_mixed, lse)
        lane = jnp.arange(LANES, dtype=jnp.int32)[None, :]
        gain_moe_term = jnp.sum(gain_moe_rows, axis=0)
        extra = jnp.where(lane == experts, gain_moe_term[:, None], dot_tn(moe_low, d_log))
        early = reduce_rows(jnp.concatenate([dot_tn(mixed, d_attn), extra], axis=1))
        out_rows, router_sum, gain_moe_sum = (
            early[:, 0:width], early[:, width : width + experts], early[:, width + experts]
        )
        qkv_sum = reduce_rows(jnp.concatenate([dot_tn(normed_low, d_qkv[i]) for i in range(3)], axis=1))
    if direct:
        tokens_grad, gate_grad, up_grad = input_back(
            d_qkv, w_qkv, tokens, gain_attn, d_state, (gate_grad, up_grad)
        )
        block_out, down_grad = make_block_out(col, gates, slot_out, hidden, (down_grad,))
    else:
        (tokens_grad,) = input_back(d_qkv, w_qkv, tokens, gain_attn, d_state)
        (block_out,) = make_block_out(col, gates, slot_out, hidden)
    my_rows = width // n_dev
    weight_rows = lax.dynamic_slice_in_dim(w_qkv, me * my_rows, my_rows, 0).astype(f32)
    gain_attn_sum = jnp.sum(weight_rows * qkv_sum, axis=1) / lax.dynamic_slice_in_dim(gain_attn, me * my_rows, my_rows, 0)

    return (
        block_out,
        tokens_grad,
        gain_attn_sum,
        qkv_sum,
        out_rows,
        gain_moe_sum,
        router_sum,
        gate_grad[None],
        up_grad[None],
        down_grad[None],
    )


def solution(mesh):
    rows, one = P("dp", None), P("dp")
    cube = P("dp", None, None)
    return jax.shard_map(
        shards,
        mesh=mesh,
        in_specs=(rows, one, rows, rows, P(), P(), P(), P(), P(), cube, cube, cube, rows),
        out_specs=(rows, rows, one, rows, rows, one, rows, cube, cube, cube),
        check_vma=False,
    )
```

```python
import functools
import math

import jax
import jax.numpy as jnp
from jax import lax
from jax.experimental import pallas as pl
from jax.experimental.pallas import tpu as pltpu
from jax.sharding import PartitionSpec as P

HEADS = 16
HEAD_DIM = 64
LEN = 1024
LANES = 128
MIB = 1 << 20

epsilon = 1e-06
mask_fill = -1e30
f32 = jnp.float32
bf16 = jnp.bfloat16


def dot_nn(left, right, **kw):
    return lax.dot_general(left, right, (((1,), (0,)), ((), ())), preferred_element_type=f32, **kw)


def dot_nt(left, right, **kw):
    return lax.dot_general(left, right, (((1,), (1,)), ((), ())), preferred_element_type=f32, **kw)


def dot_tn(left, right, **kw):
    return lax.dot_general(left, right, (((0,), (0,)), ((), ())), preferred_element_type=f32, **kw)


def iota(shape, dim):
    return lax.broadcasted_iota(jnp.int32, shape, dim)


def params(mib, **kw):
    return pltpu.CompilerParams(vmem_limit_bytes=mib * MIB, **kw)


def cost(flops, nbytes, trans=0):
    return pl.CostEstimate(flops=int(flops), bytes_accessed=int(nbytes), transcendentals=int(trans))


def slot_kernel(capacity, experts, len_ref, ids_ref, rank_col_ref, rank_row_ref, col_ref, row_ref):
    count = ids_ref.shape[0]
    length = len_ref[0]
    ids = ids_ref[...]
    first, second = ids[:, 0:1], ids[:, 1:2]
    lane = iota((count, LANES), 1)
    place = iota((count, LANES), 0)
    hot0 = (lane == first) & (lane < experts)
    hot1 = (lane == second + experts) & (lane >= experts) & (lane < 2 * experts)
    valid = place < length
    hot = jnp.where((hot0 | hot1) & valid, 1.0, 0.0).astype(bf16)
    before = (rank_row_ref[...] < rank_col_ref[...]).astype(f32).astype(bf16)
    counts = dot_nn(before, hot)
    shifted = (lane == first + experts) & (lane >= experts) & (lane < 2 * experts) & valid
    totals = jnp.sum(jnp.where(shifted, 1.0, 0.0), axis=0, keepdims=True)
    slot0 = jnp.sum(jnp.where(hot0, counts, 0.0), axis=1, keepdims=True).astype(jnp.int32)
    slot1 = jnp.sum(jnp.where(hot1, counts + totals, 0.0), axis=1, keepdims=True).astype(jnp.int32)
    sentinel = experts * capacity
    ok = valid[:, 0:1]
    flat0 = jnp.where(ok & (slot0 < capacity), first * capacity + slot0, sentinel)
    flat1 = jnp.where(ok & (slot1 < capacity), second * capacity + slot1, sentinel)
    col = jnp.where(lane == 0, flat0, 0) + jnp.where(lane == 1, flat1, 0)
    col = col + jnp.where(lane == 2, first, 0) + jnp.where(lane == 3, second, 0)
    col = col + jnp.where(lane == 4, ok.astype(jnp.int32), 0)
    col_ref[...] = col
    row_ref[...] = jnp.transpose(col.astype(f32))[0:8, :].astype(jnp.int32)


def make_slots(lengths, expert_ids, slot_order, experts, capacity):
    count = expert_ids.shape[0]
    return pl.pallas_call(
        functools.partial(slot_kernel, capacity, experts),
        out_shape=(
            jax.ShapeDtypeStruct((count, LANES), jnp.int32),
            jax.ShapeDtypeStruct((8, count), jnp.int32),
        ),
        in_specs=[
            pl.BlockSpec(memory_space=pltpu.SMEM),
            pl.BlockSpec(memory_space=pltpu.VMEM),
            pl.BlockSpec(memory_space=pltpu.VMEM),
            pl.BlockSpec(memory_space=pltpu.VMEM),
        ],
        out_specs=(pl.BlockSpec(memory_space=pltpu.VMEM), pl.BlockSpec(memory_space=pltpu.VMEM)),
        compiler_params=params(40),
        cost_estimate=cost(2 * count * count * LANES, 4 * count * LANES),
        name="slots",
    )(lengths, expert_ids, slot_order.reshape(count, 1), slot_order)


def dispatch_kernel(rows, row_ref, data_ref, out_ref):
    count = data_ref.shape[0]
    slot = pl.program_id(0) * rows + iota((rows, count), 0)
    hot = (slot == row_ref[0:1, :]) | (slot == row_ref[1:2, :])
    out_ref[...] = dot_nn(jnp.where(hot, 1.0, 0.0).astype(bf16), data_ref[...]).astype(bf16)


def dispatch(row, data, slots):
    count, width = data.shape
    rows = 256
    return pl.pallas_call(
        functools.partial(dispatch_kernel, rows),
        out_shape=jax.ShapeDtypeStruct((slots, width), bf16),
        grid=(slots // rows,),
        in_specs=[
            pl.BlockSpec((8, count), lambda i: (0, 0)),
            pl.BlockSpec((count, width), lambda i: (0, 0)),
        ],
        out_specs=pl.BlockSpec((rows, width), lambda i: (i, 0)),
        compiler_params=params(40),
        cost_estimate=cost(2 * slots * count * width, 2 * (slots + count) * width),
        name="dispatch",
    )(row, data)


def dispatch_grad_kernel(rows, row_ref, data_ref, out_ref):
    count, width = data_ref.shape
    slot = pl.program_id(0) * rows + iota((rows, count), 0)
    hot0 = slot == row_ref[0:1, :]
    hot1 = slot == row_ref[1:2, :]
    both = jnp.where(hot0 | hot1, 1.0, 0.0).astype(bf16)
    out_ref[:, 0:width] = dot_nn(both, data_ref[...]).astype(bf16)
    other = jnp.where(hot0, row_ref[3:4, :], 0) + jnp.where(hot1, row_ref[2:3, :], 0)
    other = jnp.sum(other.astype(f32), axis=1, keepdims=True)
    out_ref[:, width:] = jnp.broadcast_to(other, (rows, LANES)).astype(bf16)


def dispatch_grad(row, data, slots):
    count, width = data.shape
    rows = 256
    return pl.pallas_call(
        functools.partial(dispatch_grad_kernel, rows),
        out_shape=jax.ShapeDtypeStruct((slots, width + LANES), bf16),
        grid=(slots // rows,),
        in_specs=[
            pl.BlockSpec((8, count), lambda i: (0, 0)),
            pl.BlockSpec((count, width), lambda i: (0, 0)),
        ],
        out_specs=pl.BlockSpec((rows, width + LANES), lambda i: (i, 0)),
        compiler_params=params(40),
        cost_estimate=cost(2 * slots * count * width, 2 * (slots + count) * width),
        name="dispatch_grad",
    )(row, data)


MESH = pl.DeviceIdType.MESH


def flip(chip, bits, experts):
    out, b = chip, 1
    while b < experts:
        if isinstance(bits, int):
            out = out + (bits // b % 2) * (b - 2 * b * lax.rem(lax.div(chip, b), 2))
        else:
            mine, theirs = lax.rem(lax.div(chip, b), 2), lax.rem(lax.div(bits, b), 2)
            out = out + b * theirs * (1 - 2 * mine)
        b *= 2
    return out


def greet(peers):
    barrier = pltpu.get_barrier_semaphore()
    for peer in peers:
        pl.semaphore_signal(barrier, inc=1, device_id=(peer,), device_id_type=MESH)
    pl.semaphore_wait(barrier, len(peers))


def exchange_copies(src, dst, send_sem, recv_sem, local_sem):
    experts = src.shape[0]
    me = lax.axis_index("dp")
    chip, core = lax.div(me, 2), lax.rem(me, 2)
    copies = [pltpu.make_async_copy(src.at[chip], dst.at[chip], local_sem)]
    peers = []
    half = experts // 2
    for place in range(1, experts):
        step = half + place // 2 if place % 2 else place // 2
        peer = flip(chip, step, experts)
        peers.append(2 * peer + core)
        copies.append(
            pltpu.make_async_remote_copy(
                src_ref=src.at[peer],
                dst_ref=dst.at[chip],
                send_sem=send_sem.at[step],
                recv_sem=recv_sem.at[step],
                device_id=(2 * peer + core,),
                device_id_type=MESH,
            )
        )
    return peers, copies


def exchange_sems(experts):
    return [
        pltpu.SemaphoreType.DMA((experts,)),
        pltpu.SemaphoreType.DMA((experts,)),
        pltpu.SemaphoreType.DMA,
    ]


SCALE2 = math.log2(math.e) / math.sqrt(HEAD_DIM)
QB = 256


def attend_kernel(q_ref, k_ref, v_ref, mixed_ref, lse_ref):
    lane = iota((QB, LANES), 1)
    wide = jnp.concatenate([v_ref[...], jnp.ones(v_ref.shape, bf16)], axis=1)
    causal = iota((QB, QB), 1) <= iota((QB, QB), 0)
    for block in range(LEN // QB):
        start, stop = block * QB, (block + 1) * QB
        query = q_ref[start:stop, :]
        halves, norms = [], []
        for head in range(2):
            mine = (lane // HEAD_DIM) == head
            scores = dot_nt(jnp.where(mine, query, jnp.zeros_like(query)), k_ref[0:stop, :])
            tail = jnp.where(causal, scores[:, start:stop], mask_fill)
            scores = tail if block == 0 else jnp.concatenate([scores[:, 0:start], tail], axis=1)
            highest = jnp.max(scores, axis=1, keepdims=True) * SCALE2
            raised = jnp.exp2(scores * SCALE2 - highest)
            out = dot_nn(raised.astype(bf16), wide[0:stop, :])
            summed = out[:, LANES:]
            halves.append(out[:, 0:LANES] / summed)
            norms.append(highest + jnp.log2(summed))
        mixed_ref[start:stop, :] = jnp.where(lane < HEAD_DIM, halves[0], halves[1]).astype(bf16)
        norm = jnp.where(lane == 0, norms[0], norms[1])
        lse_ref[0, :, start:stop] = jnp.transpose(norm)[0:8, :]


def attend(qkv):
    count, width3 = qkv.shape
    width = width3 // 3
    pairs = width // LANES
    return pl.pallas_call(
        attend_kernel,
        out_shape=(
            jax.ShapeDtypeStruct((count, width), bf16),
            jax.ShapeDtypeStruct((pairs, 8, count), f32),
        ),
        grid=(pairs,),
        in_specs=[
            pl.BlockSpec((count, LANES), lambda i: (0, i)),
            pl.BlockSpec((count, LANES), lambda i: (0, i + pairs)),
            pl.BlockSpec((count, LANES), lambda i: (0, i + 2 * pairs)),
        ],
        out_specs=(
            pl.BlockSpec((count, LANES), lambda i: (0, i)),
            pl.BlockSpec((1, 8, count), lambda i: (i, 0, 0)),
        ),
        compiler_params=params(40),
        cost_estimate=cost(2 * 4 * count * count * width, 8 * count * width, 8 * count * count),
        name="attend",
    )(qkv, qkv, qkv)


def front_kernel(
    pairs, blocks,
    tok_ref, gain_ref, wq_ref, wk_ref, wv_ref, w_out_ref, gain_moe_ref, wr_ref, col_ref, row_ref, og_ref,
    norm_t_ref, qkv_ref, mixed_ref, mixed_t_ref, lse_ref, h_ref, low_t_ref, gate_ref, rows_ref, og_out, oth_out,
    norm_ref, mixed_sc, low_ref, og_sc, oth_sc, og_send, og_recv, oth_send, oth_recv, self_sem,
):
    experts, capacity, width = og_sc.shape
    half = experts // 2
    turn = pl.program_id(0) - half
    me = lax.axis_index("dp")
    chip, core = lax.div(me, 2), lax.rem(me, 2)

    def chip_at(place):
        if isinstance(place, int):
            return flip(chip, half + place // 2 if place % 2 else place // 2, experts)
        return flip(chip, lax.rem(place, 2) * half + lax.div(place, 2), experts)

    def copies(place):
        return [
            pltpu.make_async_remote_copy(
                src_ref=src.at[place], dst_ref=dst.at[chip], send_sem=send.at[place], recv_sem=recv.at[place],
                device_id=(2 * chip_at(place) + core,), device_id_type=MESH,
            )
            for src, dst, send, recv in (
                (og_sc, og_out, og_send, og_recv), (oth_sc, oth_out, oth_send, oth_recv),
            )
        ]

    selves = [
        pltpu.make_async_copy(src.at[0], dst.at[chip], self_sem.at[i])
        for i, (src, dst) in enumerate(((og_sc, og_out), (oth_sc, oth_out)))
    ]

    @pl.when(turn == -half)
    def _():
        greet([2 * chip_at(place) + core for place in range(1, experts)])
        oth_sc[...] = jnp.zeros_like(oth_sc)

    @pl.when(turn < 0)
    def _():
        count = og_ref.shape[0]
        place = 2 * (turn + half)
        bases = [capacity * chip_at(place), capacity * chip_at(place + 1)]
        slot = iota((2 * capacity, count), 0)
        slot = jnp.where(slot < capacity, slot + bases[0], slot - capacity + bases[1])
        hot0 = jnp.where(slot == row_ref[0:1, :], 1.0, 0.0).astype(bf16)
        hot1 = jnp.where(slot == row_ref[1:2, :], 1.0, 0.0).astype(bf16)
        ids = row_ref[...].astype(f32).astype(bf16)
        other = dot_nt(ids, hot0)[3:4] + dot_nt(ids, hot1)[2:3]
        picked = dot_nn(hot0 + hot1, og_ref[...]).astype(bf16)
        for k in range(2):
            og_sc[place + k] = picked[k * capacity : (k + 1) * capacity]
            mine = other[:, k * capacity : (k + 1) * capacity]
            oth_sc[place + k, :, 0:capacity] = jnp.broadcast_to(mine, (8, capacity))
        for copy in copies(place + 1):
            copy.start()

        @pl.when(turn == -half)
        def _():
            for copy in selves:
                copy.start()

        @pl.when(turn > -half)
        def _():
            for copy in copies(place):
                copy.start()

    @pl.when(pl.program_id(0) == pl.num_programs(0) - 1)
    def _():
        for copy in selves:
            copy.wait()
        for place in range(1, experts):
            for copy in copies(place):
                copy.wait()

    @pl.when(turn == 0)
    def _():
        values = tok_ref[...].astype(f32)
        inverse = lax.rsqrt(jnp.mean(values * values, axis=1, keepdims=True) + epsilon)
        norm_ref[...] = (values * inverse * gain_ref[...]).astype(bf16)
        norm_t_ref[...] = jnp.transpose(norm_ref[...])

    @pl.when((turn >= 0) & (turn < pairs))
    def _():
        weights = jnp.concatenate([wq_ref[...], wk_ref[...], wv_ref[...]], axis=1)

        @pl.loop(0, LEN // QB)
        def _(block):
            here = pl.ds(pl.multiple_of(block * QB, QB), QB)
            part = dot_nn(norm_ref[here, :], weights).astype(bf16)
            for i in range(3):
                qkv_ref[i, here, :] = part[:, i * LANES : (i + 1) * LANES]

        attend_kernel(qkv_ref.at[0], qkv_ref.at[1], qkv_ref.at[2], mixed_ref, lse_ref)
        mixed_t_ref[...] = jnp.transpose(mixed_ref[...])
        mixed_sc[:, pl.ds(pl.multiple_of(turn * LANES, LANES), LANES)] = mixed_ref[...]

    span = h_ref.shape[0]

    @pl.when((turn >= pairs) & (turn < pairs + blocks))
    def _():
        here = pl.ds(pl.multiple_of((turn - pairs) * span, span), span)
        h_ref[...], low, gate_ref[...] = middle_rows(
            mixed_sc[here, :], w_out_ref[...], tok_ref[here, :], gain_moe_ref[...], wr_ref[...], col_ref[...]
        )
        low_ref[here, :] = low
        low_t_ref[...] = jnp.transpose(low)

    @pl.when(turn >= pairs + blocks)
    def _():
        rows, count = rows_ref.shape[0], low_ref.shape[0]
        slot = (turn - pairs - blocks) * rows + iota((rows, count), 0)
        hot = (slot == row_ref[0:1, :]) | (slot == row_ref[1:2, :])
        rows_ref[...] = dot_nn(jnp.where(hot, 1.0, 0.0).astype(bf16), low_ref[...]).astype(bf16)


def front(tokens, gain, w_qkv, w_out, gain_moe, wr, col, row, out_grad, experts, capacity):
    count, width = tokens.shape
    slots = experts * capacity
    half = experts // 2
    pairs = width // LANES
    span = 256
    blocks, turns = count // span, slots // span
    anywhere = pl.BlockSpec(memory_space=pl.ANY)

    def pair_at(i):
        return jnp.clip(i - half, 0, pairs - 1)

    def block_at(i):
        return jnp.clip(i - half - pairs, 0, blocks - 1)

    def fixed(array):
        return pl.BlockSpec(array.shape, lambda i: (0, 0), pipeline_mode=pl.Buffered(1))

    gain, gain_moe = gain.reshape(1, width), gain_moe.reshape(1, width)
    in_specs = [
        fixed(tokens),
        fixed(gain),
        pl.BlockSpec((width, LANES), lambda i: (0, pair_at(i))),
        pl.BlockSpec((width, LANES), lambda i: (0, pair_at(i) + pairs)),
        pl.BlockSpec((width, LANES), lambda i: (0, pair_at(i) + 2 * pairs)),
        fixed(w_out),
        fixed(gain_moe),
        fixed(wr),
        pl.BlockSpec((span, LANES), lambda i: (block_at(i), 0)),
        fixed(row),
        fixed(out_grad),
    ]
    out_specs = [
        pl.BlockSpec((width, count), lambda i: (0, 0)),
        pl.BlockSpec((3, count, LANES), lambda i: (0, 0, pair_at(i))),
        pl.BlockSpec((count, LANES), lambda i: (0, pair_at(i))),
        pl.BlockSpec((LANES, count), lambda i: (pair_at(i), 0)),
        pl.BlockSpec((1, 8, count), lambda i: (pair_at(i), 0, 0)),
        pl.BlockSpec((span, width), lambda i: (block_at(i), 0)),
        pl.BlockSpec((width, span), lambda i: (0, block_at(i))),
        pl.BlockSpec((span, LANES), lambda i: (block_at(i), 0)),
        pl.BlockSpec((span, width), lambda i: (jnp.clip(i - half - pairs - blocks, 0, turns - 1), 0)),
        anywhere,
        anywhere,
    ]
    out_shape = [
        jax.ShapeDtypeStruct((width, count), bf16),
        jax.ShapeDtypeStruct((3, count, width), bf16),
        jax.ShapeDtypeStruct((count, width), bf16),
        jax.ShapeDtypeStruct((width, count), bf16),
        jax.ShapeDtypeStruct((pairs, 8, count), f32),
        jax.ShapeDtypeStruct((count, width), f32),
        jax.ShapeDtypeStruct((width, count), bf16),
        jax.ShapeDtypeStruct((count, LANES), f32),
        jax.ShapeDtypeStruct((slots, width), bf16),
        jax.ShapeDtypeStruct((experts, capacity, width), bf16),
        jax.ShapeDtypeStruct((experts, 8, LANES), f32),
    ]
    each = pltpu.SemaphoreType.DMA((experts,))
    scratch = [pltpu.VMEM((count, width), bf16)] * 3
    scratch += [pltpu.VMEM((experts, capacity, width), bf16), pltpu.VMEM((experts, 8, LANES), f32)]
    scratch += [each, each, each, each, pltpu.SemaphoreType.DMA((2,))]
    return pl.pallas_call(
        functools.partial(front_kernel, pairs, blocks),
        out_shape=out_shape,
        grid=(half + pairs + blocks + turns,),
        in_specs=in_specs,
        out_specs=out_specs,
        scratch_shapes=scratch,
        compiler_params=params(52, collective_id=0, has_side_effects=True),
        cost_estimate=cost(18 * count * count * width, 24 * count * width, 8 * count * count),
        name="front",
    )(tokens, gain, w_qkv, w_qkv, w_qkv, w_out, gain_moe, wr, col, row, out_grad)


def attend_back_kernel(q_ref, k_ref, v_ref, o_ref, do_ref, lse_ref, out_ref, dk_sc, dv_sc):
    lane = iota((QB, LANES), 1)
    keep = iota((QB, QB), 0) <= iota((QB, QB), 1)
    dk_sc[...] = jnp.zeros_like(dk_sc)
    dv_sc[...] = jnp.zeros_like(dv_sc)
    sub = iota((8, LANES), 0)
    picks = jnp.where(iota((8, LANES), 1) // HEAD_DIM == sub, 1.0, 0.0)
    low = (iota((LEN, LANES), 1) // HEAD_DIM) == 0
    key = k_ref[...]
    none = jnp.zeros_like(key)
    keys = (jnp.where(low, key, none), jnp.where(low, none, key))
    for block in range(LEN // QB):
        start, stop = block * QB, (block + 1) * QB
        query = q_ref[start:stop, :]
        d_out = do_ref[start:stop, :]
        product = d_out.astype(f32) * o_ref[start:stop, :].astype(f32)
        delta = dot_nt(picks, product, precision=lax.Precision.HIGHEST)
        d_query = jnp.zeros((QB, LANES), f32)
        for head in range(2):
            mine = (lane // HEAD_DIM) == head
            query_one = jnp.where(mine, query, jnp.zeros_like(query))
            d_one = jnp.where(mine, d_out, jnp.zeros_like(d_out))
            scores = dot_nt(k_ref[0:stop, :], query_one)
            tail = jnp.where(keep, scores[start:stop, :], mask_fill)
            scores = tail if block == 0 else jnp.concatenate([scores[0:start, :], tail], axis=0)
            probs = jnp.exp2(scores * SCALE2 - lse_ref[0, head : head + 1, start:stop])
            d_probs = dot_nt(v_ref[0:stop, :], d_one)
            d_scores = (probs * (d_probs - delta[head : head + 1, :])).astype(bf16)
            dv_sc[0:stop, :] += dot_nn(probs.astype(bf16), d_one)
            dk_sc[0:stop, :] += dot_nn(d_scores, query_one)
            d_query = d_query + dot_tn(d_scores, keys[head][0:stop, :])
        out_ref[0, start:stop, :] = (d_query * (1.0 / math.sqrt(HEAD_DIM))).astype(bf16)
    out_ref[1, :, :] = (dk_sc[...] * (1.0 / math.sqrt(HEAD_DIM))).astype(bf16)
    out_ref[2, :, :] = dv_sc[...].astype(bf16)


def attend_back(qkv, mixed, d_mixed, lse):
    count, width = mixed.shape
    pairs = width // LANES
    return pl.pallas_call(
        attend_back_kernel,
        out_shape=jax.ShapeDtypeStruct((3, count, width), bf16),
        grid=(pairs,),
        in_specs=[
            pl.BlockSpec((count, LANES), lambda i: (0, i)),
            pl.BlockSpec((count, LANES), lambda i: (0, i + pairs)),
            pl.BlockSpec((count, LANES), lambda i: (0, i + 2 * pairs)),
            pl.BlockSpec((count, LANES), lambda i: (0, i)),
            pl.BlockSpec((count, LANES), lambda i: (0, i)),
            pl.BlockSpec((1, 8, count), lambda i: (i, 0, 0)),
        ],
        out_specs=pl.BlockSpec((3, count, LANES), lambda i: (0, 0, i)),
        scratch_shapes=[pltpu.VMEM((count, LANES), f32), pltpu.VMEM((count, LANES), f32)],
        compiler_params=params(40),
        cost_estimate=cost(5 * 4 * count * count * width, 16 * count * width, 8 * count * count),
        name="attend_back",
    )(qkv, qkv, qkv, mixed, d_mixed, lse)


RIDE_PER_TURN = 2
LAG = 2


def back_reduce_kernel(
    chips,
    q_ref, k_ref, v_ref, o_ref, lse_ref, norm_t, mix_t, moe_t,
    col_ref, gate_ref, din_ref, h_ref, og_ref, gain_ref, wr_ref, pull_ref, w_out_ref, slot_ref,
    dstate_ref, out_ref, sum_ref, extra_ref, back_ref,
    datt_ref, dmix_ref, dlog_ref, gm_ref,
    dk_sc, dv_sc, right, terms, firsts, sums, half0, half1, half2, half3, s_send, s_recv,
    *ride_sems,
):
    halves = (half0, half1, half2, half3)
    levels = chips.bit_length() - 1
    count = k_ref.shape[0]
    width = norm_t.shape[0]
    rows = terms.shape[3]
    span = 256
    blocks = count // span
    turn = pl.program_id(0) - blocks
    pairs = sum_ref.shape[0]
    me = lax.axis_index("dp")
    chip, core = lax.div(me, 2), lax.rem(me, 2)
    mate = 2 * chip + 1 - core
    order0 = [1 << b for b in range(levels)]
    order1 = list(order0)
    order1[0], order1[1] = order0[1], order0[0]
    order0[2:] = order0[2:][::-1]

    def bit(mask):
        return lax.rem(lax.div(chip, mask), 2)

    own, peers = [], []
    for level in range(levels):
        b0, b1 = bit(order0[level]), bit(order1[level])
        own.append(b0 + core * (b1 - b0))
        p0 = order0[level] * (1 - 2 * b0)
        p1 = order1[level] * (1 - 2 * b1)
        peers.append(2 * (chip + p0 + core * (p1 - p0)) + core)
    bases = [0]
    for level in range(levels):
        bases.append(bases[-1] + own[level] * (chips >> (level + 1)))

    def remote(src, dst, c, level, device):
        return pltpu.make_async_remote_copy(
            src_ref=src, dst_ref=dst, send_sem=s_send.at[c, level], recv_sem=s_recv.at[c, level],
            device_id=(device,), device_id_type=MESH,
        )

    def cols(c):
        return pl.ds(0, LANES) if isinstance(c, int) else slice(None)

    def place(c):
        return LAG + 1 if isinstance(c, int) else lax.rem(c, LAG + 1)

    def swap(c):
        return remote(
            terms.at[place(c), :, 1 - core, :, cols(c)], firsts.at[c, :, :, cols(c)], c, levels, mate
        )

    def send(c, level):
        span = chips >> (level + 1)
        start = bases[level] + (1 - own[level]) * span
        return remote(
            sums.at[c, pl.ds(start, span), :, cols(c)], halves[level].at[c, :, :, cols(c)], c, level, peers[level]
        )

    def fold_swap(c):
        swap(c).wait()
        for b in range(chips):
            places = []
            for order in (order0, order1):
                spot = 0
                for level in range(levels):
                    spot += (b // order[level] % 2) * (chips >> (level + 1))
                places.append(spot)
            at = places[0] + core * (places[1] - places[0])
            total = terms[place(c), b, core, :, cols(c)].astype(f32) + firsts[c, b, :, cols(c)].astype(f32)
            sums[c, at, :, cols(c)] = total.astype(bf16)

    def fold(c, level):
        send(c, level).wait()
        for t in range(chips >> (level + 1)):
            at = bases[level + 1] + t
            total = sums[c, at, :, cols(c)].astype(f32) + halves[level][c, t, :, cols(c)].astype(f32)
            if level < levels - 1:
                sums[c, at, :, cols(c)] = total.astype(bf16)
            elif isinstance(c, int):
                extra_ref[...] = total
            else:
                sum_ref[c] = total

    def stage(c, s):
        if s == 1:
            fold_swap(c)
        else:
            fold(c, s - 2)
        if s - 1 < levels:
            send(c, s - 1).start()

    riders, ride = exchange_copies(slot_ref, back_ref, *ride_sems)
    per = span // (2 * rows)

    @pl.when(turn == -blocks)
    def _():
        greet([mate] + riders)
        gm_ref[...] = jnp.zeros_like(gm_ref)

    counts = [1] * blocks + [RIDE_PER_TURN] * len(ride)
    first = 0
    for at, many in enumerate(counts):
        if first < len(ride):

            @pl.when(turn == at - blocks)
            def _():
                for copy in ride[first : first + many]:
                    copy.start()

        first += many

    @pl.when(turn < 0)
    def _():
        slots = din_ref.shape[0]
        here = pl.ds(pl.multiple_of((turn + blocks) * span, span), span)
        col = col_ref[...]
        hot0, hot1 = hot_rows(col, 0, span, slots), hot_rows(col, 1, span, slots)
        gathered = dot_nn(hot0 + hot1, din_ref[...])
        table = pull_ref[:, 0, :]
        d_log, d_state, d_att, term = state_rows(
            col, gate_ref[...], h_ref[...], og_ref[...], gain_ref[...], wr_ref[...], gathered,
            pull_rows(col, 0, table, slots), pull_rows(col, 1, table, slots),
        )
        dstate_ref[...] = d_state
        dlog_ref[here, :] = d_log
        datt_ref[here, :] = d_att
        dmix_ref[here, :] = dot_nt(d_att, w_out_ref[...]).astype(bf16)
        gm_ref[...] += term

    @pl.when(turn == 0)
    def _():
        for row in range(0, width, span):
            extra = dot_nn(moe_t[row : row + span, :], dlog_ref[...])
            gain = jnp.transpose(jnp.sum(gm_ref[:, row : row + span], axis=0, keepdims=True))
            extra = extra + jnp.where(iota(extra.shape, 1) == 64, gain, 0.0)
            at = row // (2 * rows)
            terms[place(pairs), at : at + per, :, :, 0:LANES] = extra.astype(bf16).reshape(per, 2, rows, LANES)
        swap(pairs).start()

    for s in range(levels + 1, 0, -1):
        c = turn - LAG * s

        @pl.when((c >= 0) & (c < pairs))
        def _():
            stage(c, s)

        @pl.when(c == 0)
        def _():
            stage(pairs, s)

    @pl.when((turn >= 0) & (turn < pairs))
    def _():
        lanes = pl.ds(pl.multiple_of(turn * LANES, LANES), LANES)
        attend_back_kernel(
            q_ref, k_ref, v_ref, o_ref, dmix_ref.at[:, lanes], lse_ref, out_ref, dk_sc, dv_sc
        )
        for i in range(3):
            right[:, i * LANES : (i + 1) * LANES] = out_ref[i]

        @pl.loop(0, width // span)
        def _(part):
            here = pl.ds(pl.multiple_of(part * span, span), span)
            qkv_rows = dot_nn(norm_t[here, :], right[...])
            out_rows = dot_nn(mix_t[here, :], datt_ref[:, lanes])
            at = pl.ds(part * per, per)
            terms[place(turn), at, :, :, 0 : 3 * LANES] = (
                qkv_rows.astype(bf16).reshape(per, 2, rows, 3 * LANES)
            )
            terms[place(turn), at, :, :, 3 * LANES :] = out_rows.astype(bf16).reshape(per, 2, rows, LANES)

        swap(turn).start()

    @pl.when(pl.program_id(0) == pl.num_programs(0) - 1)
    def _():
        for copy in ride:
            copy.wait()


def attend_back_reduce(
    qkv, mixed, lse, norm_t, mixed_t, moe_t, col, gates, d_in, hidden, out_grad, gain, wr, pulls, w_out, slot_rows,
    n_dev,
):
    count, width = mixed.shape
    pairs = width // LANES
    chips = n_dev // 2
    levels = chips.bit_length() - 1
    rows = width // n_dev
    wide = 4 * LANES
    span = 256
    blocks = count // span
    vmem, dma = pltpu.VMEM, pltpu.SemaphoreType.DMA
    anywhere = pl.BlockSpec(memory_space=pl.ANY)

    def pair_at(i):
        return jnp.clip(i - blocks, 0, pairs - 1)

    def block(lanes):
        return pl.BlockSpec((span, lanes), lambda i: (jnp.minimum(i, blocks - 1), 0))

    def third(which):
        return pl.BlockSpec((None, count, LANES), lambda i: (which, 0, pair_at(i)))

    def whole(array):
        return pl.BlockSpec(array.shape, lambda i: (0,) * array.ndim, pipeline_mode=pl.Buffered(1))

    gain = gain.reshape(1, width)
    d_state, d_qkv, sums, extra, back = pl.pallas_call(
        functools.partial(back_reduce_kernel, chips),
        out_shape=(
            jax.ShapeDtypeStruct((count, width), f32),
            jax.ShapeDtypeStruct((3, count, width), bf16),
            jax.ShapeDtypeStruct((pairs, rows, wide), f32),
            jax.ShapeDtypeStruct((rows, LANES), f32),
            jax.ShapeDtypeStruct(slot_rows.shape, bf16),
        ),
        grid=(blocks + pairs + LAG * (levels + 1),),
        in_specs=[
            third(0),
            third(1),
            third(2),
            pl.BlockSpec((count, LANES), lambda i: (0, pair_at(i))),
            pl.BlockSpec((1, 8, count), lambda i: (pair_at(i), 0, 0)),
            whole(norm_t),
            whole(mixed_t),
            whole(moe_t),
            block(LANES),
            block(LANES),
            whole(d_in),
            block(width),
            block(width),
            whole(gain),
            whole(wr),
            whole(pulls),
            whole(w_out),
            anywhere,
        ],
        out_specs=(
            block(width),
            pl.BlockSpec((3, count, LANES), lambda i: (0, 0, pair_at(i))),
            pl.BlockSpec((pairs, rows, wide), lambda i: (0, 0, 0)),
            pl.BlockSpec((rows, LANES), lambda i: (0, 0)),
            anywhere,
        ),
        scratch_shapes=[
            vmem((count, width), bf16),
            vmem((count, width), bf16),
            vmem((count, LANES), bf16),
            vmem((8, width), f32),
            vmem((count, LANES), f32),
            vmem((count, LANES), f32),
            vmem((count, 3 * LANES), bf16),
            vmem((LAG + 2, chips, 2, rows, wide), bf16),
            vmem((pairs + 1, chips, rows, wide), bf16),
            vmem((pairs + 1, chips, rows, wide), bf16),
        ]
        + [vmem((pairs + 1, chips >> (level + 1), rows, wide), bf16) for level in range(levels)]
        + [dma((pairs + 1, levels + 1)), dma((pairs + 1, levels + 1))]
        + exchange_sems(chips),
        compiler_params=params(62, collective_id=1, has_side_effects=True),
        cost_estimate=cost(5 * 4 * count * count * width, 40 * count * width, 8 * count * count),
        name="back_reduce",
    )(
        qkv, qkv, qkv, mixed, lse, norm_t, mixed_t, moe_t,
        col, gates, d_in, hidden, out_grad, gain, wr, pulls, w_out, slot_rows,
    )
    parts = sums.reshape(pairs, rows, 4, LANES)
    parts = jnp.transpose(parts, (1, 2, 0, 3)).reshape(rows, 4 * width)
    return d_state, d_qkv, parts[:, 0 : 3 * width], parts[:, 3 * width :], extra, back


def middle_rows(mixed, w_out, tokens, gain, wr, col):
    first, second, valid = col[:, 2:3], col[:, 3:4], col[:, 4:5].astype(f32)
    hidden = tokens.astype(f32) + valid * dot_nn(mixed, w_out)
    inverse = lax.rsqrt(jnp.mean(hidden * hidden, axis=1, keepdims=True) + epsilon)
    low = (hidden * inverse * gain).astype(bf16)
    logits = dot_nn(low, wr)
    lane = iota(logits.shape, 1)
    own = jnp.sum(jnp.where(lane == first, logits, 0.0), axis=1, keepdims=True)
    alt = jnp.sum(jnp.where(lane == second, logits, 0.0), axis=1, keepdims=True)
    gate0 = 1.0 / (1.0 + jnp.exp(alt - own))
    gate1 = 1.0 / (1.0 + jnp.exp(own - alt))
    return hidden, low, jnp.where(lane == 0, gate0, 0.0) + jnp.where(lane == 1, gate1, 0.0)


def middle_kernel(mixed_ref, w_out_ref, tok_ref, gain_ref, wr_ref, col_ref, h_ref, low_ref, gate_ref):
    h_ref[...], low_ref[...], gate_ref[...] = middle_rows(
        mixed_ref[...], w_out_ref[...], tok_ref[...], gain_ref[...], wr_ref[...], col_ref[...]
    )


def middle(mixed, w_out, tokens, gain, wr, col):
    count, width = mixed.shape
    rows = 256
    whole = lambda i: (0, 0)
    part = lambda i: (i, 0)
    return pl.pallas_call(
        middle_kernel,
        out_shape=(
            jax.ShapeDtypeStruct((count, width), f32),
            jax.ShapeDtypeStruct((count, width), bf16),
            jax.ShapeDtypeStruct((count, LANES), f32),
        ),
        grid=(count // rows,),
        in_specs=[
            pl.BlockSpec((rows, width), part),
            pl.BlockSpec((width, width), whole),
            pl.BlockSpec((rows, width), part),
            pl.BlockSpec((1, width), whole),
            pl.BlockSpec((width, LANES), whole),
            pl.BlockSpec((rows, LANES), part),
        ],
        out_specs=(
            pl.BlockSpec((rows, width), part),
            pl.BlockSpec((rows, width), part),
            pl.BlockSpec((rows, LANES), part),
        ),
        compiler_params=params(40),
        cost_estimate=cost(2 * count * width * width, 12 * count * width),
        name="middle",
    )(mixed, w_out, tokens, gain.reshape(1, width), wr, col)


GELU_C = math.sqrt(2.0 / math.pi)


def expert_kernel(
    split, x_ref, g_ref, wg_ref, wu_ref, wd_ref, wr_ref, act_ref, dgp_ref, dup_ref, de_ref, part_ref, din_ref
):
    rows, width = x_ref.shape
    me = lax.axis_index("dp")
    expert, part = me // split, lax.rem(me, split)
    x = x_ref[...]
    lane = iota((rows, LANES), 1)
    logits = dot_nn(x, wr_ref[...])
    own = jnp.sum(jnp.where(lane == expert, logits, 0.0), axis=1, keepdims=True)
    other = g_ref[:, width:].astype(f32).astype(jnp.int32)
    alt = jnp.sum(jnp.where(lane == other, logits, 0.0), axis=1, keepdims=True)
    gate = 1.0 / (1.0 + jnp.exp(alt - own))
    d_rows = (g_ref[:, 0:width].astype(f32) * gate).astype(bf16)
    de_ref[...] = d_rows
    pre = dot_nn(x, wg_ref[...])
    up = dot_nn(x, wu_ref[...])
    d_hidden = dot_nt(d_rows, wd_ref[...])
    square = pre * pre
    bent = jnp.tanh(GELU_C * pre * (1.0 + 0.044715 * square))
    half = 0.5 * (1.0 + bent)
    gelu = pre * half
    slope = half + 0.5 * pre * (1.0 - bent * bent) * (GELU_C * (1.0 + 3 * 0.044715 * square))
    act = (gelu * up).astype(bf16)
    act_ref[...] = act
    dgp = (d_hidden * up * slope).astype(bf16)
    dup = (d_hidden * gelu).astype(bf16)
    dgp_ref[...] = dgp
    dup_ref[...] = dup
    pull = jnp.sum(act.astype(f32) * d_hidden, axis=1, keepdims=True)
    pull_high = pull.astype(bf16)
    pull_low = (pull - pull_high.astype(f32)).astype(bf16)
    part_ref[...] = dot_nn(act, wd_ref[...]).astype(bf16)
    din_ref[:, 0:width] = (dot_nt(dgp, wg_ref[...]) + dot_nt(dup, wu_ref[...])).astype(bf16)
    extra = jnp.where(lane == 2 * part, pull_high.astype(f32), 0.0)
    extra = extra + jnp.where(lane == 2 * part + 1, pull_low.astype(f32), 0.0)
    din_ref[:, width:] = extra.astype(bf16)


def expert_pass(x, g, wg, wu, wd, wr, split):
    count, width = x.shape
    ff = wg.shape[1]
    rows = 256
    whole = lambda i: (0, 0)
    part = lambda i: (i, 0)
    once = dict(pipeline_mode=pl.Buffered(1))
    return pl.pallas_call(
        functools.partial(expert_kernel, split),
        out_shape=(
            jax.ShapeDtypeStruct((count, ff), bf16),
            jax.ShapeDtypeStruct((count, ff), bf16),
            jax.ShapeDtypeStruct((count, ff), bf16),
            jax.ShapeDtypeStruct((count, width), bf16),
            jax.ShapeDtypeStruct((count, width), bf16),
            jax.ShapeDtypeStruct((count, width + LANES), bf16),
        ),
        grid=(count // rows,),
        in_specs=[
            pl.BlockSpec((rows, width), part),
            pl.BlockSpec((rows, width + LANES), part),
            pl.BlockSpec((width, ff), whole, **once),
            pl.BlockSpec((width, ff), whole, **once),
            pl.BlockSpec((ff, width), whole, **once),
            pl.BlockSpec((width, LANES), whole),
        ],
        out_specs=(
            pl.BlockSpec((rows, ff), part),
            pl.BlockSpec((rows, ff), part),
            pl.BlockSpec((rows, ff), part),
            pl.BlockSpec((rows, width), part),
            pl.BlockSpec((rows, width), part),
            pl.BlockSpec((rows, width + LANES), part),
        ),
        compiler_params=params(56),
        cost_estimate=cost(12 * count * width * ff, 2 * count * (3 * ff + 5 * width), count * ff),
        name="experts",
    )(x, g, wg, wu, wd, wr)


def expert_exchange_kernel(
    group, x_ref, g_ref, oth_ref, wg_hbm, wu_hbm, wd_hbm, wr_ref,
    gg_ref, ug_ref, dg_ref, slot_ref, back_ref, pulls_ref, gm_ref,
    xb, gb, oth, oth_mate, ds, rd, pd, sp, rp, pp, pt, pq, rq, act, dgp, dup, de, xt, acc_g, acc_u, acc_d,
    wg_ref, wu_ref, wd_ref,
    w_sem, x_send, x_recv, f_send, f_recv, g_load, g_send, g_recv,
    d_send, d_recv, p_send, p_recv, q_send, q_recv, b_send, b_recv, t_send, t_recv, s_sem, l_sem, o_sem,
):
    experts, capacity, width = x_ref.shape
    ff = wg_ref.shape[1]
    steps = experts // group
    pair = 2 * capacity
    rows = group * pair
    half = experts // 2
    me = lax.axis_index("dp")
    chip, core = lax.div(me, 2), lax.rem(me, 2)
    mate = 2 * chip + 1 - core

    def bits(place):
        if isinstance(place, int):
            return half + place // 2 if place % 2 else place // 2
        return lax.rem(place, 2) * half + lax.div(place, 2)

    def chip_at(place):
        return flip(chip, bits(place), experts)

    def remote(src, dst, send, recv, device):
        return pltpu.make_async_remote_copy(
            src_ref=src, dst_ref=dst, send_sem=send, recv_sem=recv, device_id=(device,), device_id_type=MESH
        )

    def block(q, g, second):
        start = q * rows + g * pair + second * capacity
        return xb.at[pl.ds(start if isinstance(start, int) else pl.multiple_of(start, 16), capacity)]

    def x_copy(place):
        peer = chip_at(place)
        own = block(place // group, place % group, 0)
        return remote(x_ref.at[peer], own, x_send.at[place], x_recv.at[place], 2 * peer + core)

    def x_arrival(q, g):
        place = q * group + g
        return remote(x_ref.at[chip], block(q, g, 0), x_send.at[place], x_recv.at[place], mate)

    def forward(q, g):
        place = q * group + g
        return remote(block(q, g, 0), block(q, g, 1), f_send.at[place], f_recv.at[place], mate)

    def g_mate(q, g):
        place = q * group + g
        at = chip_at(place)
        return remote(g_ref.at[at], gm_ref.at[at], g_send.at[place], g_recv.at[place], mate)

    def g_loads(q, g):
        slot, at = lax.rem(q, 2), chip_at(q * group + g)
        first, second = g * pair, g * pair + capacity
        return (
            pltpu.make_async_copy(g_ref.at[at], gb.at[slot, first:second], g_load.at[slot, 2 * g]),
            pltpu.make_async_copy(gm_ref.at[at], gb.at[slot, second : second + capacity], g_load.at[slot, 2 * g + 1]),
        )

    def load_g(q):
        for g in range(group):
            g_mate(q, g).wait_recv()
            for copy in g_loads(q, g):
                copy.start()

    def d_copy(q, g):
        place, slot = q * group + g, lax.rem(q, 2)
        return remote(pd.at[slot, g], rd.at[slot, g], d_send.at[place], d_recv.at[place], mate)

    def p_copy(q, g):
        place, slot = q * group + g, lax.rem(q, 2)
        return remote(pp.at[slot, g], rp.at[slot, g], p_send.at[place], p_recv.at[place], mate)

    def q_copy(q, g):
        place, slot = q * group + g, lax.rem(q, 2)
        return remote(pq.at[slot, g], rq.at[slot, g], q_send.at[place], q_recv.at[place], mate)

    def back_copies(q, g):
        place = q * group + g
        device = 2 * chip_at(place) + core
        return (
            remote(pt.at[place], pulls_ref.at[chip], t_send.at[place], t_recv.at[place], device),
            remote(ds.at[place], back_ref.at[chip], b_send.at[place], b_recv.at[place], device),
        )

    def slot_copy(q, g):
        place = q * group + g
        return pltpu.make_async_copy(sp.at[place], slot_ref.at[chip_at(place)], s_sem.at[place])

    weights = [
        pltpu.make_async_copy(src, dst, w_sem.at[i])
        for i, (src, dst) in enumerate(((wg_hbm, wg_ref), (wu_hbm, wu_ref), (wd_hbm, wd_ref)))
    ]
    grads = [
        pltpu.make_async_copy(src, dst, o_sem.at[i])
        for i, (src, dst) in enumerate(((acc_g, gg_ref), (acc_u, ug_ref), (acc_d, dg_ref)))
    ]
    self_x = pltpu.make_async_copy(x_ref.at[chip], block(0, 0, 0), l_sem.at[0])
    self_pull = pltpu.make_async_copy(pt.at[0], pulls_ref.at[chip], l_sem.at[1])
    self_back = pltpu.make_async_copy(ds.at[0], back_ref.at[chip], l_sem.at[2])
    oth_own = pltpu.make_async_copy(oth_ref, oth, l_sem.at[3])
    oth_copy = remote(oth_ref, oth_mate, l_sem.at[4], l_sem.at[5], mate)

    for copy in weights:
        copy.start()
    self_x.start()
    oth_own.start()
    greet([2 * chip_at(place) + core for place in range(1, experts)] + [mate])
    oth_copy.start()
    for place in range(1, group):
        x_copy(place).start()
    for q in range(steps):
        for g in range(group):
            g_mate(q, g).start()
        for g in range(group):
            if (q + 1) * group + g < experts:
                x_copy((q + 1) * group + g).start()
    for acc in (acc_g, acc_u, acc_d):
        acc[...] = jnp.zeros_like(acc)
    pt[...] = jnp.zeros_like(pt)
    pq[...] = jnp.zeros_like(pq)
    self_x.wait()
    forward(0, 0).start()
    oth_own.wait()
    oth_copy.wait()
    load_g(jnp.int32(0))
    for g in range(1, group):
        x_arrival(0, g).wait_recv()
        forward(0, g).start()
    for copy in weights:
        copy.wait()

    def finish(q):
        slot = lax.rem(q, 2)
        for g in range(group):
            place = q * group + g
            q_copy(q, g).wait_recv()
            d_copy(q, g).wait_recv()
            pt[place] = pt[place] + rq[slot, g]
            ds[place] = (ds[place].astype(f32) + rd[slot, g].astype(f32)).astype(bf16)
            if g == 0:

                @pl.when(q == 0)
                def _():
                    self_pull.start()
                    self_back.start()

                @pl.when(q > 0)
                def _():
                    for copy in back_copies(q, g):
                        copy.start()

            else:
                for copy in back_copies(q, g):
                    copy.start()
        for g in range(group):
            place = q * group + g
            p_copy(q, g).wait_recv()
            sp[place] = (sp[place].astype(f32) + rp[slot, g].astype(f32)).astype(bf16)
            slot_copy(q, g).start()

    def weight_grads(q):
        xt[...] = jnp.transpose(xb[pl.ds(pl.multiple_of((q - 2) * rows, 16), 2 * rows), :])
        span = 256
        for row in range(0, width, span):
            acc_g[row : row + span, :] += dot_nn(xt[row : row + span, :], dgp[...])
            acc_u[row : row + span, :] += dot_nn(xt[row : row + span, :], dup[...])
        for row in range(0, ff, LANES):
            acc_d[row : row + LANES, :] += dot_tn(act[:, row : row + LANES], de[...])

    def main(q):
        slot = lax.rem(q, 2)
        here = pl.ds(pl.multiple_of(slot * rows, 16), rows)
        for g in range(group):
            for copy in g_loads(q, g):
                copy.wait()
            forward(q, g).wait_recv()

        @pl.when(q + 1 < steps)
        def _():
            load_g(q + 1)

        x = xb[pl.ds(pl.multiple_of(q * rows, 16), rows), :]
        lane = iota((rows, LANES), 1)
        logits = dot_nn(x, wr_ref[...])
        mine = jnp.sum(jnp.where(lane == chip, logits, 0.0), axis=1, keepdims=True)
        ids = []
        for g in range(group):
            at = chip_at(q * group + g)
            for table in (oth, oth_mate):
                ids.append(jnp.transpose(table[at])[0:capacity, 0:1])
        other = jnp.concatenate(ids, axis=0).astype(jnp.int32)
        alt = jnp.sum(jnp.where(lane == other, logits, 0.0), axis=1, keepdims=True)
        gate = 1.0 / (1.0 + jnp.exp(alt - mine))
        d_rows = (gb[slot].astype(f32) * gate).astype(bf16)
        de[here, :] = d_rows
        pre = dot_nn(x, wg_ref[...])
        up = dot_nn(x, wu_ref[...])
        d_hidden = dot_nt(d_rows, wd_ref[...])
        square = pre * pre
        bent = jnp.tanh(GELU_C * pre * (1.0 + 0.044715 * square))
        hill = 0.5 * (1.0 + bent)
        gelu = pre * hill
        slope = hill + 0.5 * pre * (1.0 - bent * bent) * (GELU_C * (1.0 + 3 * 0.044715 * square))
        now = (gelu * up).astype(bf16)
        act[here, :] = now
        dgp[here, :] = (d_hidden * up * slope).astype(bf16)
        dup[here, :] = (d_hidden * gelu).astype(bf16)
        pull = jnp.sum(now.astype(f32) * d_hidden, axis=1, keepdims=True)

        @pl.when(q + 1 < steps)
        def _():
            for g in range(group):
                x_arrival(q + 1, g).wait_recv()
                forward(q + 1, g).start()

        @pl.when(q >= 1)
        def _():
            finish(q - 1)

        @pl.when(q >= 2)
        def _():
            for g in range(group):
                q_copy(q - 2, g).wait_send()
                d_copy(q - 2, g).wait_send()
                p_copy(q - 2, g).wait_send()

        d_in = (dot_nt(dgp[here, :], wg_ref[...]) + dot_nt(dup[here, :], wu_ref[...])).astype(bf16)
        pull = jnp.broadcast_to(pull, (rows, LANES))
        for g in range(group):
            place = q * group + g
            low, mid, high = g * pair, g * pair + capacity, (g + 1) * pair
            pt[place, :, 0:capacity] = jnp.transpose(pull[low:mid])[0:8, :]
            pq[slot, g, :, 0:capacity] = jnp.transpose(pull[mid:high])[0:8, :]
            ds[place] = d_in[low:mid]
            pd[slot, g] = d_in[mid:high]
            q_copy(q, g).start()
            d_copy(q, g).start()
        partial = dot_nn(act[here, :], wd_ref[...]).astype(bf16)
        for g in range(group):
            place = q * group + g
            low, mid, high = g * pair, g * pair + capacity, (g + 1) * pair
            sp[place] = partial[low:mid]
            pp[slot, g] = partial[mid:high]
            p_copy(q, g).start()

    def step(q, carry):
        @pl.when(q == steps)
        def _():
            finish(q - 1)

        @pl.when((q >= 2) & (lax.rem(q, 2) == 0))
        def _():
            weight_grads(q)

        @pl.when(q < steps)
        def _():
            main(q)

        return carry

    lax.fori_loop(0, steps + 1, step, 0)
    for copy in grads:
        copy.start()
    for q in (steps - 2, steps - 1):
        for g in range(group):
            q_copy(q, g).wait_send()
            d_copy(q, g).wait_send()
            p_copy(q, g).wait_send()
    self_pull.wait()
    self_back.wait()
    for q in range(steps):
        for g in range(group):
            place = q * group + g
            slot_copy(q, g).wait()
            forward(q, g).wait_send()
            g_mate(q, g).wait_send()
            if place:
                x_copy(place).wait_send()
                for copy in back_copies(q, g):
                    copy.wait()
    for copy in grads:
        copy.wait()


def expert_exchange(x, g, others, wg, wu, wd, wr, group=2):
    experts, capacity, width = x.shape
    ff = wg.shape[1]
    steps = experts // group
    rows = 2 * capacity * group
    anywhere = pl.BlockSpec(memory_space=pl.ANY)
    vmem, dma = pltpu.VMEM, pltpu.SemaphoreType.DMA
    each = dma((experts,))
    count = rows * steps
    outs = pl.pallas_call(
        functools.partial(expert_exchange_kernel, group),
        out_shape=(
            jax.ShapeDtypeStruct((width, ff), f32),
            jax.ShapeDtypeStruct((width, ff), f32),
            jax.ShapeDtypeStruct((ff, width), f32),
            jax.ShapeDtypeStruct((experts, capacity, width), bf16),
            jax.ShapeDtypeStruct((experts, capacity, width), bf16),
            jax.ShapeDtypeStruct((experts, 8, LANES), f32),
            jax.ShapeDtypeStruct((experts, capacity, width), bf16),
        ),
        in_specs=[anywhere] * 6 + [pl.BlockSpec(memory_space=vmem)],
        out_specs=(anywhere,) * 7,
        scratch_shapes=[
            vmem((steps * rows, width), bf16),
            vmem((2, rows, width), bf16),
            vmem((experts, 8, LANES), f32),
            vmem((experts, 8, LANES), f32),
            vmem((experts, capacity, width), bf16),
            vmem((2, group, capacity, width), bf16),
            vmem((2, group, capacity, width), bf16),
            vmem((experts, capacity, width), bf16),
            vmem((2, group, capacity, width), bf16),
            vmem((2, group, capacity, width), bf16),
            vmem((experts, 8, LANES), f32),
            vmem((2, group, 8, LANES), f32),
            vmem((2, group, 8, LANES), f32),
            vmem((2 * rows, ff), bf16),
            vmem((2 * rows, ff), bf16),
            vmem((2 * rows, ff), bf16),
            vmem((2 * rows, width), bf16),
            vmem((width, 2 * rows), bf16),
            vmem((width, ff), f32),
            vmem((width, ff), f32),
            vmem((ff, width), f32),
            vmem((width, ff), bf16),
            vmem((width, ff), bf16),
            vmem((ff, width), bf16),
            dma((3,)),
            each, each, each, each,
            dma((2, 2 * group)),
            each, each,
            each, each, each, each, each, each, each, each, each, each, each,
            dma((6,)),
            dma((3,)),
        ],
        compiler_params=params(62, collective_id=2, has_side_effects=True),
        cost_estimate=cost(18 * count * width * ff, 2 * count * 4 * width + 18 * width * ff, count * ff),
        name="experts",
    )(x, g, others, wg, wu, wd, wr)
    return outs[:6]


def hot_rows(col, k, rows, slots):
    return jnp.where(iota((rows, slots), 1) == col[:, k : k + 1], 1.0, 0.0).astype(bf16)


def state_rows(col, gates, hidden, out_grad, gain, wr, gathered, pull0, pull1):
    valid = col[:, 4:5].astype(f32)
    total = pull0 + pull1
    lane = iota((col.shape[0], LANES), 1)
    d_log = jnp.where(lane == col[:, 2:3], pull0 - gates[:, 0:1] * total, 0.0)
    d_log = d_log + jnp.where(lane == col[:, 3:4], pull1 - gates[:, 1:2] * total, 0.0)
    d_log = d_log.astype(bf16)
    d_moe = gathered + dot_nt(d_log, wr)
    inverse = lax.rsqrt(jnp.mean(hidden * hidden, axis=1, keepdims=True) + epsilon)
    normal = hidden * inverse
    scaled = gain * d_moe
    share = jnp.mean(normal * scaled, axis=1, keepdims=True)
    d_state = out_grad.astype(f32) + inverse * (scaled - normal * share)
    term = jnp.sum((normal * d_moe).reshape(hidden.shape[0] // 8, 8, hidden.shape[1]), axis=0)
    return d_log, d_state, (valid * d_state).astype(bf16), term


def pull_rows(col, k, table, slots):
    experts, rows = table.shape[0], col.shape[0]
    chosen = jnp.where(iota((rows, experts), 1) == col[:, 2 + k : 3 + k], 1.0, 0.0)
    values = dot_nn(chosen, table, precision=lax.Precision.HIGHEST)
    slot = col[:, k : k + 1] - slots // experts * col[:, 2 + k : 3 + k]
    here = (iota((rows, LANES), 1) == slot) & (col[:, k : k + 1] < slots)
    return jnp.sum(jnp.where(here, values, 0.0), axis=1, keepdims=True)


def state_kernel(
    col_ref, gate_ref, din_ref, h_ref, og_ref, gain_ref, wr_ref, dstate_ref, dattn_ref, dlog_ref, gterm_ref
):
    rows, width = h_ref.shape
    slots = din_ref.shape[0]
    col = col_ref[...]
    hot0, hot1 = hot_rows(col, 0, rows, slots), hot_rows(col, 1, rows, slots)
    pulls = din_ref[:, width:]
    pull0 = jnp.sum(dot_nn(hot0, pulls), axis=1, keepdims=True)
    pull1 = jnp.sum(dot_nn(hot1, pulls), axis=1, keepdims=True)
    gathered = dot_nn(hot0 + hot1, din_ref[:, 0:width])
    dlog_ref[...], dstate_ref[...], dattn_ref[...], term = state_rows(
        col, gate_ref[...], h_ref[...], og_ref[...], gain_ref[...], wr_ref[...], gathered, pull0, pull1
    )

    @pl.when(pl.program_id(0) == 0)
    def _():
        gterm_ref[...] = jnp.zeros_like(gterm_ref)

    gterm_ref[...] += term


def state_back(col, gates, din, hidden, out_grad, gain, wr):
    count, width = hidden.shape
    slots = din.shape[0]
    rows = 256
    whole = lambda i: (0, 0)
    part = lambda i: (i, 0)
    return pl.pallas_call(
        state_kernel,
        out_shape=(
            jax.ShapeDtypeStruct((count, width), f32),
            jax.ShapeDtypeStruct((count, width), bf16),
            jax.ShapeDtypeStruct((count, LANES), bf16),
            jax.ShapeDtypeStruct((8, width), f32),
        ),
        grid=(count // rows,),
        in_specs=[
            pl.BlockSpec((rows, LANES), part),
            pl.BlockSpec((rows, LANES), part),
            pl.BlockSpec(din.shape, whole),
            pl.BlockSpec((rows, width), part),
            pl.BlockSpec((rows, width), part),
            pl.BlockSpec((1, width), whole),
            pl.BlockSpec((width, LANES), whole),
        ],
        out_specs=(
            pl.BlockSpec((rows, width), part),
            pl.BlockSpec((rows, width), part),
            pl.BlockSpec((rows, LANES), part),
            pl.BlockSpec((8, width), whole),
        ),
        compiler_params=params(48),
        cost_estimate=cost(2 * slots * count * width, 14 * count * width),
        name="state_back",
    )(col, gates, din, hidden, out_grad, gain.reshape(1, width), wr)


def tail_kernel(
    n_ride, d_ref, w_ref, tok_ref, gain_ref, dstate_ref, col_ref, gate_ref, rows_ref, h_ref, *refs
):
    srcs, (grad_ref, out_ref), dsts = refs[:n_ride], refs[n_ride : n_ride + 2], refs[n_ride + 2 :]
    for src, dst in zip(srcs, dsts):
        dst[...] = src[...]
    rows, width = tok_ref.shape
    d_normed = dot_nt(d_ref[0], w_ref[:, 0:width])
    for i in range(1, 3):
        d_normed = d_normed + dot_nt(d_ref[i], w_ref[:, i * width : (i + 1) * width])
    values = tok_ref[...].astype(f32)
    inverse = lax.rsqrt(jnp.mean(values * values, axis=1, keepdims=True) + epsilon)
    normal = values * inverse
    scaled = gain_ref[...] * d_normed
    share = jnp.mean(normal * scaled, axis=1, keepdims=True)
    grad_ref[...] = dstate_ref[...] + inverse * (scaled - normal * share)
    slots = rows_ref.shape[0]
    col = col_ref[...]
    pick0 = dot_nn(hot_rows(col, 0, rows, slots), rows_ref[...])
    pick1 = dot_nn(hot_rows(col, 1, rows, slots), rows_ref[...])
    out_ref[...] = (h_ref[...] + gate_ref[:, 0:1] * pick0 + gate_ref[:, 1:2] * pick1).astype(bf16)


def tail(d_qkv, w_qkv, tokens, gain, d_state, col, gates, slot_rows, hidden, riders=()):
    count, width = tokens.shape
    rows = 256
    steps = count // rows
    part = lambda i: (i, 0)
    passed = [pl.BlockSpec((array.shape[0] // steps, array.shape[1]), part) for array in riders]

    def whole(array):
        return pl.BlockSpec(array.shape, lambda i: (0, 0), pipeline_mode=pl.Buffered(1))

    gain = gain.reshape(1, width)
    return pl.pallas_call(
        functools.partial(tail_kernel, len(riders)),
        out_shape=[jax.ShapeDtypeStruct((count, width), f32), jax.ShapeDtypeStruct((count, width), bf16)]
        + [jax.ShapeDtypeStruct(array.shape, array.dtype) for array in riders],
        grid=(steps,),
        in_specs=[
            pl.BlockSpec((3, rows, width), lambda i: (0, i, 0)),
            whole(w_qkv),
            pl.BlockSpec((rows, width), part),
            whole(gain),
            pl.BlockSpec((rows, width), part),
            pl.BlockSpec((rows, LANES), part),
            pl.BlockSpec((rows, LANES), part),
            whole(slot_rows),
            pl.BlockSpec((rows, width), part),
        ]
        + passed,
        out_specs=[pl.BlockSpec((rows, width), part)] * 2 + passed,
        compiler_params=params(56),
        cost_estimate=cost(12 * count * width * width, 60 * count * width),
        name="tail",
    )(d_qkv, w_qkv, tokens, gain, d_state, col, gates, slot_rows, hidden, *riders)


def shards(
    tokens,
    lengths,
    expert_ids,
    slot_order,
    gain_attn,
    w_qkv,
    w_out,
    gain_moe,
    w_router,
    w_gate,
    w_up,
    w_down,
    out_grad,
):
    tok_dev, width = tokens.shape
    n_dev = lax.axis_size("dp")
    experts = w_router.shape[1]
    split = n_dev // experts
    capacity = split * (5 * tok_dev // (4 * n_dev))
    slots = experts * capacity
    me = lax.axis_index("dp")
    part = lax.rem(me, split)
    same_part = [[e * split + p for e in range(experts)] for p in range(split)]
    same_expert = [[e * split + p for p in range(split)] for e in range(experts)]
    swap = [(d, d ^ 1) for d in range(n_dev)]

    def across(blocks):
        return lax.all_to_all(blocks, "dp", 0, 0, axis_index_groups=same_part, tiled=True)

    def share(rows):
        if split == 2:
            return jnp.concatenate([rows, lax.ppermute(rows, "dp", swap)], axis=0)
        return lax.all_gather(rows, "dp", axis_index_groups=same_expert, tiled=True)

    def settle(pieces):
        if split == 2:
            theirs = lax.ppermute(pieces[1], "dp", swap)
            return (pieces[0].astype(f32) + theirs.astype(f32)).astype(bf16)
        got = lax.all_to_all(pieces, "dp", 0, 0, axis_index_groups=same_expert, tiled=True)
        return jnp.sum(got.astype(f32), axis=0).astype(bf16)

    def send_in(rows):
        return share(across(rows.reshape(experts, capacity, -1)).reshape(slots, -1))

    def send_back(rows):
        summed = settle(rows.reshape(split, slots, -1))
        return across(summed.reshape(experts, capacity, -1)).reshape(slots, -1)

    def reduce_rows(term):
        pieces = term.reshape(experts, split, -1, term.shape[-1])
        if split == 2:
            mine = lax.dynamic_index_in_dim(pieces, part, 1, keepdims=False)
            theirs = lax.dynamic_index_in_dim(pieces, 1 - part, 1, keepdims=False)
            theirs = lax.ppermute(theirs.astype(bf16), "dp", swap)
            summed = (mine + theirs.astype(f32)).astype(bf16)
        else:
            pieces = jnp.moveaxis(pieces, 1, 0).astype(bf16)
            got = lax.all_to_all(pieces, "dp", 0, 0, axis_index_groups=same_expert, tiled=True)
            summed = jnp.sum(got.astype(f32), axis=0).astype(bf16)
        return jnp.sum(across(summed).astype(f32), axis=0)

    wr = jnp.pad(w_router, ((0, 0), (0, LANES - experts)))
    col, row = make_slots(lengths, expert_ids, slot_order, experts, capacity)
    direct = split == 2 and experts == 16

    if direct:
        norm_t, qkv, mixed, mixed_t, lse, hidden, moe_t, gates, rows_out, grad_in, others = front(
            tokens, gain_attn, w_qkv, w_out, gain_moe, wr, col, row, out_grad, experts, capacity
        )
    else:
        token_vals = tokens.astype(f32)
        inverse_attn = lax.rsqrt(jnp.mean(token_vals * token_vals, axis=-1, keepdims=True) + epsilon)
        normed_low = (token_vals * inverse_attn * gain_attn).astype(bf16)
        qkv = jnp.dot(normed_low, w_qkv, preferred_element_type=f32).astype(bf16)
        mixed, lse = attend(qkv)
        grad_in = send_in(dispatch_grad(row, out_grad, slots))
        hidden, moe_low, gates = middle(mixed, w_out, tokens, gain_moe, wr, col)
        rows_out = dispatch(row, moe_low, slots)
    if direct:
        gate_grad, up_grad, down_grad, slot_part, d_in_back, pulls = expert_exchange(
            rows_out.reshape(experts, capacity, -1), grad_in, others, w_gate[0], w_up[0], w_down[0], wr
        )
        d_in_back = d_in_back.reshape(slots, -1)
    else:
        rows_in = send_in(rows_out)
        act, d_pre, d_up, d_rows, partial_out, d_in = expert_pass(
            rows_in, grad_in, w_gate[0], w_up[0], w_down[0], wr, split
        )
        d_in_back = send_back(d_in)
        slot_out = send_back(partial_out)
        down_grad = dot_tn(act, d_rows)
        gate_grad = dot_tn(rows_in, d_pre)
        up_grad = dot_tn(rows_in, d_up)

    if direct:
        d_state, d_qkv, qkv_sum, out_rows, extra, slot_out = attend_back_reduce(
            qkv, mixed, lse, norm_t, mixed_t, moe_t, col, gates, d_in_back, hidden, out_grad,
            gain_moe, wr, pulls, w_out, slot_part, n_dev,
        )
        slot_out = slot_out.reshape(slots, -1)
        router_sum, gain_moe_sum = extra[:, 0:experts], extra[:, 64]
    else:
        d_state, d_attn, d_log, gain_moe_rows = state_back(
            col, gates, d_in_back, hidden, out_grad, gain_moe, wr
        )
        d_mixed = dot_nt(d_attn, w_out).astype(bf16)
        d_qkv = attend_back(qkv, mixed, d_mixed, lse)
        lane = jnp.arange(LANES, dtype=jnp.int32)[None, :]
        gain_moe_term = jnp.sum(gain_moe_rows, axis=0)
        extra = jnp.where(lane == experts, gain_moe_term[:, None], dot_tn(moe_low, d_log))
        early = reduce_rows(jnp.concatenate([dot_tn(mixed, d_attn), extra], axis=1))
        out_rows, router_sum, gain_moe_sum = (
            early[:, 0:width], early[:, width : width + experts], early[:, width + experts]
        )
        qkv_sum = reduce_rows(jnp.concatenate([dot_tn(normed_low, d_qkv[i]) for i in range(3)], axis=1))
    riders = (gate_grad, up_grad, down_grad) if direct else ()
    tokens_grad, block_out, *passed = tail(
        d_qkv, w_qkv, tokens, gain_attn, d_state, col, gates, slot_out, hidden, riders
    )
    if direct:
        gate_grad, up_grad, down_grad = passed
    my_rows = width // n_dev
    weight_rows = lax.dynamic_slice_in_dim(w_qkv, me * my_rows, my_rows, 0).astype(f32)
    gain_attn_sum = jnp.sum(weight_rows * qkv_sum, axis=1) / lax.dynamic_slice_in_dim(gain_attn, me * my_rows, my_rows, 0)

    return (
        block_out,
        tokens_grad,
        gain_attn_sum,
        qkv_sum,
        out_rows,
        gain_moe_sum,
        router_sum,
        gate_grad[None],
        up_grad[None],
        down_grad[None],
    )


def solution(mesh):
    rows, one = P("dp", None), P("dp")
    cube = P("dp", None, None)
    return jax.shard_map(
        shards,
        mesh=mesh,
        in_specs=(rows, one, rows, rows, P(), P(), P(), P(), P(), cube, cube, cube, rows),
        out_specs=(rows, rows, one, rows, rows, one, rows, cube, cube, cube),
        check_vma=False,
    )
```

```python
import functools
import math

import jax
import jax.numpy as jnp
from jax import lax
from jax.experimental import pallas as pl
from jax.experimental.pallas import tpu as pltpu
from jax.sharding import PartitionSpec as P

HEADS = 16
HEAD_DIM = 64
LEN = 1024
LANES = 128
MIB = 1 << 20

epsilon = 1e-06
mask_fill = -1e30
f32 = jnp.float32
bf16 = jnp.bfloat16


def dot_nn(left, right, **kw):
    return lax.dot_general(left, right, (((1,), (0,)), ((), ())), preferred_element_type=f32, **kw)


def dot_nt(left, right, **kw):
    return lax.dot_general(left, right, (((1,), (1,)), ((), ())), preferred_element_type=f32, **kw)


def dot_tn(left, right, **kw):
    return lax.dot_general(left, right, (((0,), (0,)), ((), ())), preferred_element_type=f32, **kw)


def iota(shape, dim):
    return lax.broadcasted_iota(jnp.int32, shape, dim)


def params(mib, **kw):
    return pltpu.CompilerParams(vmem_limit_bytes=mib * MIB, **kw)


def cost(flops, nbytes, trans=0):
    return pl.CostEstimate(flops=int(flops), bytes_accessed=int(nbytes), transcendentals=int(trans))


def slot_kernel(capacity, experts, len_ref, ids_ref, rank_col_ref, rank_row_ref, col_ref, row_ref):
    count = ids_ref.shape[0]
    length = len_ref[0]
    ids = ids_ref[...]
    first, second = ids[:, 0:1], ids[:, 1:2]
    lane = iota((count, LANES), 1)
    place = iota((count, LANES), 0)
    hot0 = (lane == first) & (lane < experts)
    hot1 = (lane == second + experts) & (lane >= experts) & (lane < 2 * experts)
    valid = place < length
    hot = jnp.where((hot0 | hot1) & valid, 1.0, 0.0).astype(bf16)
    before = (rank_row_ref[...] < rank_col_ref[...]).astype(f32).astype(bf16)
    counts = dot_nn(before, hot)
    shifted = (lane == first + experts) & (lane >= experts) & (lane < 2 * experts) & valid
    totals = jnp.sum(jnp.where(shifted, 1.0, 0.0), axis=0, keepdims=True)
    slot0 = jnp.sum(jnp.where(hot0, counts, 0.0), axis=1, keepdims=True).astype(jnp.int32)
    slot1 = jnp.sum(jnp.where(hot1, counts + totals, 0.0), axis=1, keepdims=True).astype(jnp.int32)
    sentinel = experts * capacity
    ok = valid[:, 0:1]
    flat0 = jnp.where(ok & (slot0 < capacity), first * capacity + slot0, sentinel)
    flat1 = jnp.where(ok & (slot1 < capacity), second * capacity + slot1, sentinel)
    col = jnp.where(lane == 0, flat0, 0) + jnp.where(lane == 1, flat1, 0)
    col = col + jnp.where(lane == 2, first, 0) + jnp.where(lane == 3, second, 0)
    col = col + jnp.where(lane == 4, ok.astype(jnp.int32), 0)
    col_ref[...] = col
    row_ref[...] = jnp.transpose(col.astype(f32))[0:8, :].astype(jnp.int32)


def make_slots(lengths, expert_ids, slot_order, experts, capacity):
    count = expert_ids.shape[0]
    return pl.pallas_call(
        functools.partial(slot_kernel, capacity, experts),
        out_shape=(
            jax.ShapeDtypeStruct((count, LANES), jnp.int32),
            jax.ShapeDtypeStruct((8, count), jnp.int32),
        ),
        in_specs=[
            pl.BlockSpec(memory_space=pltpu.SMEM),
            pl.BlockSpec(memory_space=pltpu.VMEM),
            pl.BlockSpec(memory_space=pltpu.VMEM),
            pl.BlockSpec(memory_space=pltpu.VMEM),
        ],
        out_specs=(pl.BlockSpec(memory_space=pltpu.VMEM), pl.BlockSpec(memory_space=pltpu.VMEM)),
        compiler_params=params(40),
        cost_estimate=cost(2 * count * count * LANES, 4 * count * LANES),
        name="slots",
    )(lengths, expert_ids, slot_order.reshape(count, 1), slot_order)


def dispatch_kernel(rows, row_ref, data_ref, out_ref):
    count = data_ref.shape[0]
    slot = pl.program_id(0) * rows + iota((rows, count), 0)
    hot = (slot == row_ref[0:1, :]) | (slot == row_ref[1:2, :])
    out_ref[...] = dot_nn(jnp.where(hot, 1.0, 0.0).astype(bf16), data_ref[...]).astype(bf16)


def dispatch(row, data, slots):
    count, width = data.shape
    rows = 256
    return pl.pallas_call(
        functools.partial(dispatch_kernel, rows),
        out_shape=jax.ShapeDtypeStruct((slots, width), bf16),
        grid=(slots // rows,),
        in_specs=[
            pl.BlockSpec((8, count), lambda i: (0, 0)),
            pl.BlockSpec((count, width), lambda i: (0, 0)),
        ],
        out_specs=pl.BlockSpec((rows, width), lambda i: (i, 0)),
        compiler_params=params(40),
        cost_estimate=cost(2 * slots * count * width, 2 * (slots + count) * width),
        name="dispatch",
    )(row, data)


def dispatch_grad_kernel(rows, row_ref, data_ref, out_ref):
    count, width = data_ref.shape
    slot = pl.program_id(0) * rows + iota((rows, count), 0)
    hot0 = slot == row_ref[0:1, :]
    hot1 = slot == row_ref[1:2, :]
    both = jnp.where(hot0 | hot1, 1.0, 0.0).astype(bf16)
    out_ref[:, 0:width] = dot_nn(both, data_ref[...]).astype(bf16)
    other = jnp.where(hot0, row_ref[3:4, :], 0) + jnp.where(hot1, row_ref[2:3, :], 0)
    other = jnp.sum(other.astype(f32), axis=1, keepdims=True)
    out_ref[:, width:] = jnp.broadcast_to(other, (rows, LANES)).astype(bf16)


def dispatch_grad(row, data, slots):
    count, width = data.shape
    rows = 256
    return pl.pallas_call(
        functools.partial(dispatch_grad_kernel, rows),
        out_shape=jax.ShapeDtypeStruct((slots, width + LANES), bf16),
        grid=(slots // rows,),
        in_specs=[
            pl.BlockSpec((8, count), lambda i: (0, 0)),
            pl.BlockSpec((count, width), lambda i: (0, 0)),
        ],
        out_specs=pl.BlockSpec((rows, width + LANES), lambda i: (i, 0)),
        compiler_params=params(40),
        cost_estimate=cost(2 * slots * count * width, 2 * (slots + count) * width),
        name="dispatch_grad",
    )(row, data)


MESH = pl.DeviceIdType.MESH


def flip(chip, bits, experts):
    out, b = chip, 1
    while b < experts:
        if isinstance(bits, int):
            out = out + (bits // b % 2) * (b - 2 * b * lax.rem(lax.div(chip, b), 2))
        else:
            mine, theirs = lax.rem(lax.div(chip, b), 2), lax.rem(lax.div(bits, b), 2)
            out = out + b * theirs * (1 - 2 * mine)
        b *= 2
    return out


def greet(peers):
    barrier = pltpu.get_barrier_semaphore()
    for peer in peers:
        pl.semaphore_signal(barrier, inc=1, device_id=(peer,), device_id_type=MESH)
    pl.semaphore_wait(barrier, len(peers))


def exchange_copies(src, dst, send_sem, recv_sem, local_sem):
    experts = src.shape[0]
    me = lax.axis_index("dp")
    chip, core = lax.div(me, 2), lax.rem(me, 2)
    copies = [pltpu.make_async_copy(src.at[chip], dst.at[chip], local_sem)]
    peers = []
    half = experts // 2
    for place in range(1, experts):
        step = half + place // 2 if place % 2 else place // 2
        peer = flip(chip, step, experts)
        peers.append(2 * peer + core)
        copies.append(
            pltpu.make_async_remote_copy(
                src_ref=src.at[peer],
                dst_ref=dst.at[chip],
                send_sem=send_sem.at[step],
                recv_sem=recv_sem.at[step],
                device_id=(2 * peer + core,),
                device_id_type=MESH,
            )
        )
    return peers, copies


def exchange_sems(experts):
    return [
        pltpu.SemaphoreType.DMA((experts,)),
        pltpu.SemaphoreType.DMA((experts,)),
        pltpu.SemaphoreType.DMA,
    ]


SCALE2 = math.log2(math.e) / math.sqrt(HEAD_DIM)
QB = 256


def attend_kernel(q_ref, k_ref, v_ref, mixed_ref, lse_ref):
    lane = iota((QB, LANES), 1)
    wide = jnp.concatenate([v_ref[...], jnp.ones(v_ref.shape, bf16)], axis=1)
    causal = iota((QB, QB), 1) <= iota((QB, QB), 0)
    for block in range(LEN // QB):
        start, stop = block * QB, (block + 1) * QB
        query = q_ref[start:stop, :]
        halves, norms = [], []
        for head in range(2):
            mine = (lane // HEAD_DIM) == head
            scores = dot_nt(jnp.where(mine, query, jnp.zeros_like(query)), k_ref[0:stop, :])
            tail = jnp.where(causal, scores[:, start:stop], mask_fill)
            scores = tail if block == 0 else jnp.concatenate([scores[:, 0:start], tail], axis=1)
            highest = jnp.max(scores, axis=1, keepdims=True) * SCALE2
            raised = jnp.exp2(scores * SCALE2 - highest)
            out = dot_nn(raised.astype(bf16), wide[0:stop, :])
            summed = out[:, LANES:]
            halves.append(out[:, 0:LANES] / summed)
            norms.append(highest + jnp.log2(summed))
        mixed_ref[start:stop, :] = jnp.where(lane < HEAD_DIM, halves[0], halves[1]).astype(bf16)
        norm = jnp.where(lane == 0, norms[0], norms[1])
        lse_ref[0, :, start:stop] = jnp.transpose(norm)[0:8, :]


def attend(qkv):
    count, width3 = qkv.shape
    width = width3 // 3
    pairs = width // LANES
    return pl.pallas_call(
        attend_kernel,
        out_shape=(
            jax.ShapeDtypeStruct((count, width), bf16),
            jax.ShapeDtypeStruct((pairs, 8, count), f32),
        ),
        grid=(pairs,),
        in_specs=[
            pl.BlockSpec((count, LANES), lambda i: (0, i)),
            pl.BlockSpec((count, LANES), lambda i: (0, i + pairs)),
            pl.BlockSpec((count, LANES), lambda i: (0, i + 2 * pairs)),
        ],
        out_specs=(
            pl.BlockSpec((count, LANES), lambda i: (0, i)),
            pl.BlockSpec((1, 8, count), lambda i: (i, 0, 0)),
        ),
        compiler_params=params(40),
        cost_estimate=cost(2 * 4 * count * count * width, 8 * count * width, 8 * count * count),
        name="attend",
    )(qkv, qkv, qkv)


def front_kernel(
    pairs, blocks,
    tok_ref, gain_ref, wq_ref, wk_ref, wv_ref, w_out_ref, gain_moe_ref, wr_ref, col_ref, row_ref, og_ref,
    norm_t_ref, qkv_ref, mixed_ref, mixed_t_ref, lse_ref, h_ref, low_t_ref, gate_ref, rows_ref, og_out, oth_out,
    norm_ref, mixed_sc, low_ref, og_sc, oth_sc, og_send, og_recv, oth_send, oth_recv, self_sem,
):
    experts, capacity, width = og_sc.shape
    half = experts // 2
    turn = pl.program_id(0) - half
    me = lax.axis_index("dp")
    chip, core = lax.div(me, 2), lax.rem(me, 2)

    def chip_at(place):
        if isinstance(place, int):
            return flip(chip, half + place // 2 if place % 2 else place // 2, experts)
        return flip(chip, lax.rem(place, 2) * half + lax.div(place, 2), experts)

    def copies(place):
        return [
            pltpu.make_async_remote_copy(
                src_ref=src.at[place], dst_ref=dst.at[chip], send_sem=send.at[place], recv_sem=recv.at[place],
                device_id=(2 * chip_at(place) + core,), device_id_type=MESH,
            )
            for src, dst, send, recv in (
                (og_sc, og_out, og_send, og_recv), (oth_sc, oth_out, oth_send, oth_recv),
            )
        ]

    selves = [
        pltpu.make_async_copy(src.at[0], dst.at[chip], self_sem.at[i])
        for i, (src, dst) in enumerate(((og_sc, og_out), (oth_sc, oth_out)))
    ]

    @pl.when(turn == -half)
    def _():
        greet([2 * chip_at(place) + core for place in range(1, experts)])
        oth_sc[...] = jnp.zeros_like(oth_sc)

    @pl.when(turn < 0)
    def _():
        count = og_ref.shape[0]
        place = 2 * (turn + half)
        bases = [capacity * chip_at(place), capacity * chip_at(place + 1)]
        slot = iota((2 * capacity, count), 0)
        slot = jnp.where(slot < capacity, slot + bases[0], slot - capacity + bases[1])
        hot0 = jnp.where(slot == row_ref[0:1, :], 1.0, 0.0).astype(bf16)
        hot1 = jnp.where(slot == row_ref[1:2, :], 1.0, 0.0).astype(bf16)
        ids = row_ref[...].astype(f32).astype(bf16)
        other = dot_nt(ids, hot0)[3:4] + dot_nt(ids, hot1)[2:3]
        picked = dot_nn(hot0 + hot1, og_ref[...]).astype(bf16)
        for k in range(2):
            og_sc[place + k] = picked[k * capacity : (k + 1) * capacity]
            mine = other[:, k * capacity : (k + 1) * capacity]
            oth_sc[place + k, :, 0:capacity] = jnp.broadcast_to(mine, (8, capacity))
        for copy in copies(place + 1):
            copy.start()

        @pl.when(turn == -half)
        def _():
            for copy in selves:
                copy.start()

        @pl.when(turn > -half)
        def _():
            for copy in copies(place):
                copy.start()

    @pl.when(pl.program_id(0) == pl.num_programs(0) - 1)
    def _():
        for copy in selves:
            copy.wait()
        for place in range(1, experts):
            for copy in copies(place):
                copy.wait()

    @pl.when(turn == 0)
    def _():
        values = tok_ref[...].astype(f32)
        inverse = lax.rsqrt(jnp.mean(values * values, axis=1, keepdims=True) + epsilon)
        norm_ref[...] = (values * inverse * gain_ref[...]).astype(bf16)
        norm_t_ref[...] = jnp.transpose(norm_ref[...])

    @pl.when((turn >= 0) & (turn < pairs))
    def _():
        weights = jnp.concatenate([wq_ref[...], wk_ref[...], wv_ref[...]], axis=1)

        @pl.loop(0, LEN // QB)
        def _(block):
            here = pl.ds(pl.multiple_of(block * QB, QB), QB)
            part = dot_nn(norm_ref[here, :], weights).astype(bf16)
            for i in range(3):
                qkv_ref[i, here, :] = part[:, i * LANES : (i + 1) * LANES]

        attend_kernel(qkv_ref.at[0], qkv_ref.at[1], qkv_ref.at[2], mixed_ref, lse_ref)
        mixed_t_ref[...] = jnp.transpose(mixed_ref[...])
        mixed_sc[:, pl.ds(pl.multiple_of(turn * LANES, LANES), LANES)] = mixed_ref[...]

    span = h_ref.shape[0]

    @pl.when((turn >= pairs) & (turn < pairs + blocks))
    def _():
        here = pl.ds(pl.multiple_of((turn - pairs) * span, span), span)
        h_ref[...], low, gate_ref[...] = middle_rows(
            mixed_sc[here, :], w_out_ref[...], tok_ref[here, :], gain_moe_ref[...], wr_ref[...], col_ref[...]
        )
        low_ref[here, :] = low
        low_t_ref[...] = jnp.transpose(low)

    @pl.when(turn >= pairs + blocks)
    def _():
        rows, count = rows_ref.shape[0], low_ref.shape[0]
        slot = (turn - pairs - blocks) * rows + iota((rows, count), 0)
        hot = (slot == row_ref[0:1, :]) | (slot == row_ref[1:2, :])
        rows_ref[...] = dot_nn(jnp.where(hot, 1.0, 0.0).astype(bf16), low_ref[...]).astype(bf16)


def front(tokens, gain, w_qkv, w_out, gain_moe, wr, col, row, out_grad, experts, capacity):
    count, width = tokens.shape
    slots = experts * capacity
    half = experts // 2
    pairs = width // LANES
    span = 256
    blocks, turns = count // span, slots // span
    anywhere = pl.BlockSpec(memory_space=pl.ANY)

    def pair_at(i):
        return jnp.clip(i - half, 0, pairs - 1)

    def block_at(i):
        return jnp.clip(i - half - pairs, 0, blocks - 1)

    def fixed(array):
        return pl.BlockSpec(array.shape, lambda i: (0, 0), pipeline_mode=pl.Buffered(1))

    gain, gain_moe = gain.reshape(1, width), gain_moe.reshape(1, width)
    in_specs = [
        fixed(tokens),
        fixed(gain),
        pl.BlockSpec((width, LANES), lambda i: (0, pair_at(i))),
        pl.BlockSpec((width, LANES), lambda i: (0, pair_at(i) + pairs)),
        pl.BlockSpec((width, LANES), lambda i: (0, pair_at(i) + 2 * pairs)),
        fixed(w_out),
        fixed(gain_moe),
        fixed(wr),
        pl.BlockSpec((span, LANES), lambda i: (block_at(i), 0)),
        fixed(row),
        fixed(out_grad),
    ]
    out_specs = [
        pl.BlockSpec((width, count), lambda i: (0, 0)),
        pl.BlockSpec((3, count, LANES), lambda i: (0, 0, pair_at(i))),
        pl.BlockSpec((count, LANES), lambda i: (0, pair_at(i))),
        pl.BlockSpec((LANES, count), lambda i: (pair_at(i), 0)),
        pl.BlockSpec((1, 8, count), lambda i: (pair_at(i), 0, 0)),
        pl.BlockSpec((span, width), lambda i: (block_at(i), 0)),
        pl.BlockSpec((width, span), lambda i: (0, block_at(i))),
        pl.BlockSpec((span, LANES), lambda i: (block_at(i), 0)),
        pl.BlockSpec((span, width), lambda i: (jnp.clip(i - half - pairs - blocks, 0, turns - 1), 0)),
        anywhere,
        anywhere,
    ]
    out_shape = [
        jax.ShapeDtypeStruct((width, count), bf16),
        jax.ShapeDtypeStruct((3, count, width), bf16),
        jax.ShapeDtypeStruct((count, width), bf16),
        jax.ShapeDtypeStruct((width, count), bf16),
        jax.ShapeDtypeStruct((pairs, 8, count), f32),
        jax.ShapeDtypeStruct((count, width), f32),
        jax.ShapeDtypeStruct((width, count), bf16),
        jax.ShapeDtypeStruct((count, LANES), f32),
        jax.ShapeDtypeStruct((slots, width), bf16),
        jax.ShapeDtypeStruct((experts, capacity, width), bf16),
        jax.ShapeDtypeStruct((experts, 8, LANES), f32),
    ]
    each = pltpu.SemaphoreType.DMA((experts,))
    scratch = [pltpu.VMEM((count, width), bf16)] * 3
    scratch += [pltpu.VMEM((experts, capacity, width), bf16), pltpu.VMEM((experts, 8, LANES), f32)]
    scratch += [each, each, each, each, pltpu.SemaphoreType.DMA((2,))]
    return pl.pallas_call(
        functools.partial(front_kernel, pairs, blocks),
        out_shape=out_shape,
        grid=(half + pairs + blocks + turns,),
        in_specs=in_specs,
        out_specs=out_specs,
        scratch_shapes=scratch,
        compiler_params=params(52, collective_id=0, has_side_effects=True),
        cost_estimate=cost(18 * count * count * width, 24 * count * width, 8 * count * count),
        name="front",
    )(tokens, gain, w_qkv, w_qkv, w_qkv, w_out, gain_moe, wr, col, row, out_grad)


def attend_back_kernel(q_ref, k_ref, v_ref, o_ref, do_ref, lse_ref, out_ref, dk_sc, dv_sc):
    lane = iota((QB, LANES), 1)
    keep = iota((QB, QB), 0) <= iota((QB, QB), 1)
    dk_sc[...] = jnp.zeros_like(dk_sc)
    dv_sc[...] = jnp.zeros_like(dv_sc)
    sub = iota((8, LANES), 0)
    picks = jnp.where(iota((8, LANES), 1) // HEAD_DIM == sub, 1.0, 0.0)
    low = (iota((LEN, LANES), 1) // HEAD_DIM) == 0
    key = k_ref[...]
    none = jnp.zeros_like(key)
    keys = (jnp.where(low, key, none), jnp.where(low, none, key))
    for block in range(LEN // QB):
        start, stop = block * QB, (block + 1) * QB
        query = q_ref[start:stop, :]
        d_out = do_ref[start:stop, :]
        product = d_out.astype(f32) * o_ref[start:stop, :].astype(f32)
        delta = dot_nt(picks, product, precision=lax.Precision.HIGHEST)
        d_query = jnp.zeros((QB, LANES), f32)
        for head in range(2):
            mine = (lane // HEAD_DIM) == head
            query_one = jnp.where(mine, query, jnp.zeros_like(query))
            d_one = jnp.where(mine, d_out, jnp.zeros_like(d_out))
            scores = dot_nt(k_ref[0:stop, :], query_one)
            tail = jnp.where(keep, scores[start:stop, :], mask_fill)
            scores = tail if block == 0 else jnp.concatenate([scores[0:start, :], tail], axis=0)
            probs = jnp.exp2(scores * SCALE2 - lse_ref[0, head : head + 1, start:stop])
            d_probs = dot_nt(v_ref[0:stop, :], d_one)
            d_scores = (probs * (d_probs - delta[head : head + 1, :])).astype(bf16)
            dv_sc[0:stop, :] += dot_nn(probs.astype(bf16), d_one)
            dk_sc[0:stop, :] += dot_nn(d_scores, query_one)
            d_query = d_query + dot_tn(d_scores, keys[head][0:stop, :])
        out_ref[0, start:stop, :] = (d_query * (1.0 / math.sqrt(HEAD_DIM))).astype(bf16)
    out_ref[1, :, :] = (dk_sc[...] * (1.0 / math.sqrt(HEAD_DIM))).astype(bf16)
    out_ref[2, :, :] = dv_sc[...].astype(bf16)


def attend_back(qkv, mixed, d_mixed, lse):
    count, width = mixed.shape
    pairs = width // LANES
    return pl.pallas_call(
        attend_back_kernel,
        out_shape=jax.ShapeDtypeStruct((3, count, width), bf16),
        grid=(pairs,),
        in_specs=[
            pl.BlockSpec((count, LANES), lambda i: (0, i)),
            pl.BlockSpec((count, LANES), lambda i: (0, i + pairs)),
            pl.BlockSpec((count, LANES), lambda i: (0, i + 2 * pairs)),
            pl.BlockSpec((count, LANES), lambda i: (0, i)),
            pl.BlockSpec((count, LANES), lambda i: (0, i)),
            pl.BlockSpec((1, 8, count), lambda i: (i, 0, 0)),
        ],
        out_specs=pl.BlockSpec((3, count, LANES), lambda i: (0, 0, i)),
        scratch_shapes=[pltpu.VMEM((count, LANES), f32), pltpu.VMEM((count, LANES), f32)],
        compiler_params=params(40),
        cost_estimate=cost(5 * 4 * count * count * width, 16 * count * width, 8 * count * count),
        name="attend_back",
    )(qkv, qkv, qkv, mixed, d_mixed, lse)


RIDE_PER_TURN = 2
LAG = 2


def back_reduce_kernel(
    chips,
    q_ref, k_ref, v_ref, o_ref, lse_ref, norm_t, mix_t, moe_t,
    col_ref, gate_ref, din_ref, h_ref, og_ref, gain_ref, wr_ref, pull_ref, w_out_ref, slot_ref,
    dstate_ref, out_ref, sum_ref, extra_ref, back_ref,
    datt_ref, dmix_ref, dlog_ref, gm_ref,
    dk_sc, dv_sc, right, terms, firsts, sums, half0, half1, half2, half3, s_send, s_recv,
    *ride_sems,
):
    halves = (half0, half1, half2, half3)
    levels = chips.bit_length() - 1
    count = k_ref.shape[0]
    width = norm_t.shape[0]
    rows = terms.shape[3]
    span = 256
    blocks = count // span
    turn = pl.program_id(0) - blocks
    pairs = sum_ref.shape[0]
    me = lax.axis_index("dp")
    chip, core = lax.div(me, 2), lax.rem(me, 2)
    mate = 2 * chip + 1 - core
    order0 = [1 << b for b in range(levels)]
    order1 = list(order0)
    order1[0], order1[1] = order0[1], order0[0]
    order0[2:] = order0[2:][::-1]

    def bit(mask):
        return lax.rem(lax.div(chip, mask), 2)

    own, peers = [], []
    for level in range(levels):
        b0, b1 = bit(order0[level]), bit(order1[level])
        own.append(b0 + core * (b1 - b0))
        p0 = order0[level] * (1 - 2 * b0)
        p1 = order1[level] * (1 - 2 * b1)
        peers.append(2 * (chip + p0 + core * (p1 - p0)) + core)
    bases = [0]
    for level in range(levels):
        bases.append(bases[-1] + own[level] * (chips >> (level + 1)))

    def remote(src, dst, c, level, device):
        return pltpu.make_async_remote_copy(
            src_ref=src, dst_ref=dst, send_sem=s_send.at[c, level], recv_sem=s_recv.at[c, level],
            device_id=(device,), device_id_type=MESH,
        )

    def cols(c):
        return pl.ds(0, LANES) if isinstance(c, int) else slice(None)

    def place(c):
        return LAG + 1 if isinstance(c, int) else lax.rem(c, LAG + 1)

    def swap(c):
        return remote(
            terms.at[place(c), :, 1 - core, :, cols(c)], firsts.at[c, :, :, cols(c)], c, levels, mate
        )

    def send(c, level):
        span = chips >> (level + 1)
        start = bases[level] + (1 - own[level]) * span
        return remote(
            sums.at[c, pl.ds(start, span), :, cols(c)], halves[level].at[c, :, :, cols(c)], c, level, peers[level]
        )

    def fold_swap(c):
        swap(c).wait()
        for b in range(chips):
            places = []
            for order in (order0, order1):
                spot = 0
                for level in range(levels):
                    spot += (b // order[level] % 2) * (chips >> (level + 1))
                places.append(spot)
            at = places[0] + core * (places[1] - places[0])
            total = terms[place(c), b, core, :, cols(c)].astype(f32) + firsts[c, b, :, cols(c)].astype(f32)
            sums[c, at, :, cols(c)] = total.astype(bf16)

    def fold(c, level):
        send(c, level).wait()
        for t in range(chips >> (level + 1)):
            at = bases[level + 1] + t
            total = sums[c, at, :, cols(c)].astype(f32) + halves[level][c, t, :, cols(c)].astype(f32)
            if level < levels - 1:
                sums[c, at, :, cols(c)] = total.astype(bf16)
            elif isinstance(c, int):
                extra_ref[...] = total
            else:
                sum_ref[c] = total

    def stage(c, s):
        if s == 1:
            fold_swap(c)
        else:
            fold(c, s - 2)
        if s - 1 < levels:
            send(c, s - 1).start()

    riders, ride = exchange_copies(slot_ref, back_ref, *ride_sems)
    per = span // (2 * rows)

    @pl.when(turn == -blocks)
    def _():
        greet([mate] + riders)
        gm_ref[...] = jnp.zeros_like(gm_ref)

    counts = [1] * blocks + [RIDE_PER_TURN] * len(ride)
    first = 0
    for at, many in enumerate(counts):
        if first < len(ride):

            @pl.when(turn == at - blocks)
            def _():
                for copy in ride[first : first + many]:
                    copy.start()

        first += many

    @pl.when(turn < 0)
    def _():
        slots = din_ref.shape[0]
        here = pl.ds(pl.multiple_of((turn + blocks) * span, span), span)
        col = col_ref[...]
        hot0, hot1 = hot_rows(col, 0, span, slots), hot_rows(col, 1, span, slots)
        gathered = dot_nn(hot0 + hot1, din_ref[...])
        table = pull_ref[:, 0, :]
        d_log, d_state, d_att, term = state_rows(
            col, gate_ref[...], h_ref[...], og_ref[...], gain_ref[...], wr_ref[...], gathered,
            pull_rows(col, 0, table, slots), pull_rows(col, 1, table, slots),
        )
        dstate_ref[...] = d_state
        dlog_ref[here, :] = d_log
        datt_ref[here, :] = d_att
        dmix_ref[here, :] = dot_nt(d_att, w_out_ref[...]).astype(bf16)
        gm_ref[...] += term

    @pl.when(turn == 0)
    def _():
        for row in range(0, width, span):
            extra = dot_nn(moe_t[row : row + span, :], dlog_ref[...])
            gain = jnp.transpose(jnp.sum(gm_ref[:, row : row + span], axis=0, keepdims=True))
            extra = extra + jnp.where(iota(extra.shape, 1) == 64, gain, 0.0)
            at = row // (2 * rows)
            terms[place(pairs), at : at + per, :, :, 0:LANES] = extra.astype(bf16).reshape(per, 2, rows, LANES)
        swap(pairs).start()

    for s in range(levels + 1, 0, -1):
        c = turn - LAG * s

        @pl.when((c >= 0) & (c < pairs))
        def _():
            stage(c, s)

        @pl.when(c == 0)
        def _():
            stage(pairs, s)

    @pl.when((turn >= 0) & (turn < pairs))
    def _():
        lanes = pl.ds(pl.multiple_of(turn * LANES, LANES), LANES)
        attend_back_kernel(
            q_ref, k_ref, v_ref, o_ref, dmix_ref.at[:, lanes], lse_ref, out_ref, dk_sc, dv_sc
        )
        for i in range(3):
            right[:, i * LANES : (i + 1) * LANES] = out_ref[i]

        @pl.loop(0, width // span)
        def _(part):
            here = pl.ds(pl.multiple_of(part * span, span), span)
            qkv_rows = dot_nn(norm_t[here, :], right[...])
            out_rows = dot_nn(mix_t[here, :], datt_ref[:, lanes])
            at = pl.ds(part * per, per)
            terms[place(turn), at, :, :, 0 : 3 * LANES] = (
                qkv_rows.astype(bf16).reshape(per, 2, rows, 3 * LANES)
            )
            terms[place(turn), at, :, :, 3 * LANES :] = out_rows.astype(bf16).reshape(per, 2, rows, LANES)

        swap(turn).start()

    @pl.when(pl.program_id(0) == pl.num_programs(0) - 1)
    def _():
        for copy in ride:
            copy.wait()


def attend_back_reduce(
    qkv, mixed, lse, norm_t, mixed_t, moe_t, col, gates, d_in, hidden, out_grad, gain, wr, pulls, w_out, slot_rows,
    n_dev,
):
    count, width = mixed.shape
    pairs = width // LANES
    chips = n_dev // 2
    levels = chips.bit_length() - 1
    rows = width // n_dev
    wide = 4 * LANES
    span = 256
    blocks = count // span
    vmem, dma = pltpu.VMEM, pltpu.SemaphoreType.DMA
    anywhere = pl.BlockSpec(memory_space=pl.ANY)

    def pair_at(i):
        return jnp.clip(i - blocks, 0, pairs - 1)

    def block(lanes):
        return pl.BlockSpec((span, lanes), lambda i: (jnp.minimum(i, blocks - 1), 0))

    def third(which):
        return pl.BlockSpec((None, count, LANES), lambda i: (which, 0, pair_at(i)))

    def whole(array):
        return pl.BlockSpec(array.shape, lambda i: (0,) * array.ndim, pipeline_mode=pl.Buffered(1))

    gain = gain.reshape(1, width)
    d_state, d_qkv, sums, extra, back = pl.pallas_call(
        functools.partial(back_reduce_kernel, chips),
        out_shape=(
            jax.ShapeDtypeStruct((count, width), f32),
            jax.ShapeDtypeStruct((3, count, width), bf16),
            jax.ShapeDtypeStruct((pairs, rows, wide), f32),
            jax.ShapeDtypeStruct((rows, LANES), f32),
            jax.ShapeDtypeStruct(slot_rows.shape, bf16),
        ),
        grid=(blocks + pairs + LAG * (levels + 1),),
        in_specs=[
            third(0),
            third(1),
            third(2),
            pl.BlockSpec((count, LANES), lambda i: (0, pair_at(i))),
            pl.BlockSpec((1, 8, count), lambda i: (pair_at(i), 0, 0)),
            whole(norm_t),
            whole(mixed_t),
            whole(moe_t),
            block(LANES),
            block(LANES),
            whole(d_in),
            block(width),
            block(width),
            whole(gain),
            whole(wr),
            whole(pulls),
            whole(w_out),
            anywhere,
        ],
        out_specs=(
            block(width),
            pl.BlockSpec((3, count, LANES), lambda i: (0, 0, pair_at(i))),
            pl.BlockSpec((pairs, rows, wide), lambda i: (0, 0, 0)),
            pl.BlockSpec((rows, LANES), lambda i: (0, 0)),
            anywhere,
        ),
        scratch_shapes=[
            vmem((count, width), bf16),
            vmem((count, width), bf16),
            vmem((count, LANES), bf16),
            vmem((8, width), f32),
            vmem((count, LANES), f32),
            vmem((count, LANES), f32),
            vmem((count, 3 * LANES), bf16),
            vmem((LAG + 2, chips, 2, rows, wide), bf16),
            vmem((pairs + 1, chips, rows, wide), bf16),
            vmem((pairs + 1, chips, rows, wide), bf16),
        ]
        + [vmem((pairs + 1, chips >> (level + 1), rows, wide), bf16) for level in range(levels)]
        + [dma((pairs + 1, levels + 1)), dma((pairs + 1, levels + 1))]
        + exchange_sems(chips),
        compiler_params=params(62, collective_id=1, has_side_effects=True),
        cost_estimate=cost(5 * 4 * count * count * width, 40 * count * width, 8 * count * count),
        name="back_reduce",
    )(
        qkv, qkv, qkv, mixed, lse, norm_t, mixed_t, moe_t,
        col, gates, d_in, hidden, out_grad, gain, wr, pulls, w_out, slot_rows,
    )
    return d_state, d_qkv, sums, extra, back


def middle_rows(mixed, w_out, tokens, gain, wr, col):
    first, second, valid = col[:, 2:3], col[:, 3:4], col[:, 4:5].astype(f32)
    hidden = tokens.astype(f32) + valid * dot_nn(mixed, w_out)
    inverse = lax.rsqrt(jnp.mean(hidden * hidden, axis=1, keepdims=True) + epsilon)
    low = (hidden * inverse * gain).astype(bf16)
    logits = dot_nn(low, wr)
    lane = iota(logits.shape, 1)
    own = jnp.sum(jnp.where(lane == first, logits, 0.0), axis=1, keepdims=True)
    alt = jnp.sum(jnp.where(lane == second, logits, 0.0), axis=1, keepdims=True)
    gate0 = 1.0 / (1.0 + jnp.exp(alt - own))
    gate1 = 1.0 / (1.0 + jnp.exp(own - alt))
    return hidden, low, jnp.where(lane == 0, gate0, 0.0) + jnp.where(lane == 1, gate1, 0.0)


def middle_kernel(mixed_ref, w_out_ref, tok_ref, gain_ref, wr_ref, col_ref, h_ref, low_ref, gate_ref):
    h_ref[...], low_ref[...], gate_ref[...] = middle_rows(
        mixed_ref[...], w_out_ref[...], tok_ref[...], gain_ref[...], wr_ref[...], col_ref[...]
    )


def middle(mixed, w_out, tokens, gain, wr, col):
    count, width = mixed.shape
    rows = 256
    whole = lambda i: (0, 0)
    part = lambda i: (i, 0)
    return pl.pallas_call(
        middle_kernel,
        out_shape=(
            jax.ShapeDtypeStruct((count, width), f32),
            jax.ShapeDtypeStruct((count, width), bf16),
            jax.ShapeDtypeStruct((count, LANES), f32),
        ),
        grid=(count // rows,),
        in_specs=[
            pl.BlockSpec((rows, width), part),
            pl.BlockSpec((width, width), whole),
            pl.BlockSpec((rows, width), part),
            pl.BlockSpec((1, width), whole),
            pl.BlockSpec((width, LANES), whole),
            pl.BlockSpec((rows, LANES), part),
        ],
        out_specs=(
            pl.BlockSpec((rows, width), part),
            pl.BlockSpec((rows, width), part),
            pl.BlockSpec((rows, LANES), part),
        ),
        compiler_params=params(40),
        cost_estimate=cost(2 * count * width * width, 12 * count * width),
        name="middle",
    )(mixed, w_out, tokens, gain.reshape(1, width), wr, col)


GELU_C = math.sqrt(2.0 / math.pi)


def expert_kernel(
    split, x_ref, g_ref, wg_ref, wu_ref, wd_ref, wr_ref, act_ref, dgp_ref, dup_ref, de_ref, part_ref, din_ref
):
    rows, width = x_ref.shape
    me = lax.axis_index("dp")
    expert, part = me // split, lax.rem(me, split)
    x = x_ref[...]
    lane = iota((rows, LANES), 1)
    logits = dot_nn(x, wr_ref[...])
    own = jnp.sum(jnp.where(lane == expert, logits, 0.0), axis=1, keepdims=True)
    other = g_ref[:, width:].astype(f32).astype(jnp.int32)
    alt = jnp.sum(jnp.where(lane == other, logits, 0.0), axis=1, keepdims=True)
    gate = 1.0 / (1.0 + jnp.exp(alt - own))
    d_rows = (g_ref[:, 0:width].astype(f32) * gate).astype(bf16)
    de_ref[...] = d_rows
    pre = dot_nn(x, wg_ref[...])
    up = dot_nn(x, wu_ref[...])
    d_hidden = dot_nt(d_rows, wd_ref[...])
    square = pre * pre
    bent = jnp.tanh(GELU_C * pre * (1.0 + 0.044715 * square))
    half = 0.5 * (1.0 + bent)
    gelu = pre * half
    slope = half + 0.5 * pre * (1.0 - bent * bent) * (GELU_C * (1.0 + 3 * 0.044715 * square))
    act = (gelu * up).astype(bf16)
    act_ref[...] = act
    dgp = (d_hidden * up * slope).astype(bf16)
    dup = (d_hidden * gelu).astype(bf16)
    dgp_ref[...] = dgp
    dup_ref[...] = dup
    pull = jnp.sum(act.astype(f32) * d_hidden, axis=1, keepdims=True)
    pull_high = pull.astype(bf16)
    pull_low = (pull - pull_high.astype(f32)).astype(bf16)
    part_ref[...] = dot_nn(act, wd_ref[...]).astype(bf16)
    din_ref[:, 0:width] = (dot_nt(dgp, wg_ref[...]) + dot_nt(dup, wu_ref[...])).astype(bf16)
    extra = jnp.where(lane == 2 * part, pull_high.astype(f32), 0.0)
    extra = extra + jnp.where(lane == 2 * part + 1, pull_low.astype(f32), 0.0)
    din_ref[:, width:] = extra.astype(bf16)


def expert_pass(x, g, wg, wu, wd, wr, split):
    count, width = x.shape
    ff = wg.shape[1]
    rows = 256
    whole = lambda i: (0, 0)
    part = lambda i: (i, 0)
    once = dict(pipeline_mode=pl.Buffered(1))
    return pl.pallas_call(
        functools.partial(expert_kernel, split),
        out_shape=(
            jax.ShapeDtypeStruct((count, ff), bf16),
            jax.ShapeDtypeStruct((count, ff), bf16),
            jax.ShapeDtypeStruct((count, ff), bf16),
            jax.ShapeDtypeStruct((count, width), bf16),
            jax.ShapeDtypeStruct((count, width), bf16),
            jax.ShapeDtypeStruct((count, width + LANES), bf16),
        ),
        grid=(count // rows,),
        in_specs=[
            pl.BlockSpec((rows, width), part),
            pl.BlockSpec((rows, width + LANES), part),
            pl.BlockSpec((width, ff), whole, **once),
            pl.BlockSpec((width, ff), whole, **once),
            pl.BlockSpec((ff, width), whole, **once),
            pl.BlockSpec((width, LANES), whole),
        ],
        out_specs=(
            pl.BlockSpec((rows, ff), part),
            pl.BlockSpec((rows, ff), part),
            pl.BlockSpec((rows, ff), part),
            pl.BlockSpec((rows, width), part),
            pl.BlockSpec((rows, width), part),
            pl.BlockSpec((rows, width + LANES), part),
        ),
        compiler_params=params(56),
        cost_estimate=cost(12 * count * width * ff, 2 * count * (3 * ff + 5 * width), count * ff),
        name="experts",
    )(x, g, wg, wu, wd, wr)


def expert_exchange_kernel(
    group, x_ref, g_ref, oth_ref, wg_hbm, wu_hbm, wd_hbm, wr_ref,
    gg_ref, ug_ref, dg_ref, slot_ref, back_ref, pulls_ref, gm_ref,
    xb, gb, oth, oth_mate, ds, rd, pd, sp, rp, pp, pt, pq, rq, act, dgp, dup, de, xt, acc_g, acc_u, acc_d,
    wg_ref, wu_ref, wd_ref,
    w_sem, x_send, x_recv, f_send, f_recv, g_load, g_send, g_recv,
    d_send, d_recv, p_send, p_recv, q_send, q_recv, b_send, b_recv, t_send, t_recv, s_sem, l_sem, o_sem,
):
    experts, capacity, width = x_ref.shape
    ff = wg_ref.shape[1]
    steps = experts // group
    pair = 2 * capacity
    rows = group * pair
    half = experts // 2
    me = lax.axis_index("dp")
    chip, core = lax.div(me, 2), lax.rem(me, 2)
    mate = 2 * chip + 1 - core

    def bits(place):
        if isinstance(place, int):
            return half + place // 2 if place % 2 else place // 2
        return lax.rem(place, 2) * half + lax.div(place, 2)

    def chip_at(place):
        return flip(chip, bits(place), experts)

    def remote(src, dst, send, recv, device):
        return pltpu.make_async_remote_copy(
            src_ref=src, dst_ref=dst, send_sem=send, recv_sem=recv, device_id=(device,), device_id_type=MESH
        )

    def block(q, g, second):
        start = q * rows + g * pair + second * capacity
        return xb.at[pl.ds(start if isinstance(start, int) else pl.multiple_of(start, 16), capacity)]

    def x_copy(place):
        peer = chip_at(place)
        own = block(place // group, place % group, 0)
        return remote(x_ref.at[peer], own, x_send.at[place], x_recv.at[place], 2 * peer + core)

    def x_arrival(q, g):
        place = q * group + g
        return remote(x_ref.at[chip], block(q, g, 0), x_send.at[place], x_recv.at[place], mate)

    def forward(q, g):
        place = q * group + g
        return remote(block(q, g, 0), block(q, g, 1), f_send.at[place], f_recv.at[place], mate)

    def g_mate(q, g):
        place = q * group + g
        at = chip_at(place)
        return remote(g_ref.at[at], gm_ref.at[at], g_send.at[place], g_recv.at[place], mate)

    def g_loads(q, g):
        slot, at = lax.rem(q, 2), chip_at(q * group + g)
        first, second = g * pair, g * pair + capacity
        return (
            pltpu.make_async_copy(g_ref.at[at], gb.at[slot, first:second], g_load.at[slot, 2 * g]),
            pltpu.make_async_copy(gm_ref.at[at], gb.at[slot, second : second + capacity], g_load.at[slot, 2 * g + 1]),
        )

    def load_g(q):
        for g in range(group):
            g_mate(q, g).wait_recv()
            for copy in g_loads(q, g):
                copy.start()

    def d_copy(q, g):
        place, slot = q * group + g, lax.rem(q, 2)
        return remote(pd.at[slot, g], rd.at[slot, g], d_send.at[place], d_recv.at[place], mate)

    def p_copy(q, g):
        place, slot = q * group + g, lax.rem(q, 2)
        return remote(pp.at[slot, g], rp.at[slot, g], p_send.at[place], p_recv.at[place], mate)

    def q_copy(q, g):
        place, slot = q * group + g, lax.rem(q, 2)
        return remote(pq.at[slot, g], rq.at[slot, g], q_send.at[place], q_recv.at[place], mate)

    def back_copies(q, g):
        place = q * group + g
        device = 2 * chip_at(place) + core
        return (
            remote(pt.at[place], pulls_ref.at[chip], t_send.at[place], t_recv.at[place], device),
            remote(ds.at[place], back_ref.at[chip], b_send.at[place], b_recv.at[place], device),
        )

    def slot_copy(q, g):
        place = q * group + g
        return pltpu.make_async_copy(sp.at[place], slot_ref.at[chip_at(place)], s_sem.at[place])

    weights = [
        pltpu.make_async_copy(src, dst, w_sem.at[i])
        for i, (src, dst) in enumerate(((wg_hbm, wg_ref), (wu_hbm, wu_ref), (wd_hbm, wd_ref)))
    ]
    grads = [
        pltpu.make_async_copy(src, dst, o_sem.at[i])
        for i, (src, dst) in enumerate(((wg_ref, gg_ref), (wu_ref, ug_ref), (wd_ref, dg_ref)))
    ]
    self_x = pltpu.make_async_copy(x_ref.at[chip], block(0, 0, 0), l_sem.at[0])
    self_pull = pltpu.make_async_copy(pt.at[0], pulls_ref.at[chip], l_sem.at[1])
    self_back = pltpu.make_async_copy(ds.at[0], back_ref.at[chip], l_sem.at[2])
    oth_own = pltpu.make_async_copy(oth_ref, oth, l_sem.at[3])
    oth_copy = remote(oth_ref, oth_mate, l_sem.at[4], l_sem.at[5], mate)

    for copy in weights:
        copy.start()
    self_x.start()
    oth_own.start()
    greet([2 * chip_at(place) + core for place in range(1, experts)] + [mate])
    oth_copy.start()
    for place in range(1, group):
        x_copy(place).start()
    for q in range(steps):
        for g in range(group):
            g_mate(q, g).start()
        for g in range(group):
            if (q + 1) * group + g < experts:
                x_copy((q + 1) * group + g).start()
    for acc in (acc_g, acc_u, acc_d):
        acc[...] = jnp.zeros_like(acc)
    pt[...] = jnp.zeros_like(pt)
    pq[...] = jnp.zeros_like(pq)
    self_x.wait()
    forward(0, 0).start()
    oth_own.wait()
    oth_copy.wait()
    load_g(jnp.int32(0))
    for g in range(1, group):
        x_arrival(0, g).wait_recv()
        forward(0, g).start()
    for copy in weights:
        copy.wait()

    def finish(q):
        slot = lax.rem(q, 2)
        for g in range(group):
            place = q * group + g
            q_copy(q, g).wait_recv()
            d_copy(q, g).wait_recv()
            pt[place] = pt[place] + rq[slot, g]
            ds[place] = (ds[place].astype(f32) + rd[slot, g].astype(f32)).astype(bf16)
            if g == 0:

                @pl.when(q == 0)
                def _():
                    self_pull.start()
                    self_back.start()

                @pl.when(q > 0)
                def _():
                    for copy in back_copies(q, g):
                        copy.start()

            else:
                for copy in back_copies(q, g):
                    copy.start()
        for g in range(group):
            place = q * group + g
            p_copy(q, g).wait_recv()
            sp[place] = (sp[place].astype(f32) + rp[slot, g].astype(f32)).astype(bf16)
            slot_copy(q, g).start()

    def weight_grads(q):
        xt[...] = jnp.transpose(xb[pl.ds(pl.multiple_of((q - 2) * rows, 16), 2 * rows), :])
        span = 256
        for row in range(0, width, span):
            acc_g[row : row + span, :] += dot_nn(xt[row : row + span, :], dgp[...])
            acc_u[row : row + span, :] += dot_nn(xt[row : row + span, :], dup[...])
        for row in range(0, ff, LANES):
            acc_d[row : row + LANES, :] += dot_tn(act[:, row : row + LANES], de[...])

    def main(q):
        slot = lax.rem(q, 2)
        here = pl.ds(pl.multiple_of(slot * rows, 16), rows)
        for g in range(group):
            for copy in g_loads(q, g):
                copy.wait()
            forward(q, g).wait_recv()

        @pl.when(q + 1 < steps)
        def _():
            load_g(q + 1)

        x = xb[pl.ds(pl.multiple_of(q * rows, 16), rows), :]
        lane = iota((rows, LANES), 1)
        logits = dot_nn(x, wr_ref[...])
        mine = jnp.sum(jnp.where(lane == chip, logits, 0.0), axis=1, keepdims=True)
        ids = []
        for g in range(group):
            at = chip_at(q * group + g)
            for table in (oth, oth_mate):
                ids.append(jnp.transpose(table[at])[0:capacity, 0:1])
        other = jnp.concatenate(ids, axis=0).astype(jnp.int32)
        alt = jnp.sum(jnp.where(lane == other, logits, 0.0), axis=1, keepdims=True)
        gate = 1.0 / (1.0 + jnp.exp(alt - mine))
        d_rows = (gb[slot].astype(f32) * gate).astype(bf16)
        de[here, :] = d_rows
        pre = dot_nn(x, wg_ref[...])
        up = dot_nn(x, wu_ref[...])
        d_hidden = dot_nt(d_rows, wd_ref[...])
        square = pre * pre
        bent = jnp.tanh(GELU_C * pre * (1.0 + 0.044715 * square))
        hill = 0.5 * (1.0 + bent)
        gelu = pre * hill
        slope = hill + 0.5 * pre * (1.0 - bent * bent) * (GELU_C * (1.0 + 3 * 0.044715 * square))
        now = (gelu * up).astype(bf16)
        act[here, :] = now
        dgp[here, :] = (d_hidden * up * slope).astype(bf16)
        dup[here, :] = (d_hidden * gelu).astype(bf16)
        pull = jnp.sum(now.astype(f32) * d_hidden, axis=1, keepdims=True)

        @pl.when(q + 1 < steps)
        def _():
            for g in range(group):
                x_arrival(q + 1, g).wait_recv()
                forward(q + 1, g).start()

        @pl.when(q >= 1)
        def _():
            finish(q - 1)

        @pl.when(q >= 2)
        def _():
            for g in range(group):
                q_copy(q - 2, g).wait_send()
                d_copy(q - 2, g).wait_send()
                p_copy(q - 2, g).wait_send()

        d_in = (dot_nt(dgp[here, :], wg_ref[...]) + dot_nt(dup[here, :], wu_ref[...])).astype(bf16)
        pull = jnp.broadcast_to(pull, (rows, LANES))
        for g in range(group):
            place = q * group + g
            low, mid, high = g * pair, g * pair + capacity, (g + 1) * pair
            pt[place, :, 0:capacity] = jnp.transpose(pull[low:mid])[0:8, :]
            pq[slot, g, :, 0:capacity] = jnp.transpose(pull[mid:high])[0:8, :]
            ds[place] = d_in[low:mid]
            pd[slot, g] = d_in[mid:high]
            q_copy(q, g).start()
            d_copy(q, g).start()
        partial = dot_nn(act[here, :], wd_ref[...]).astype(bf16)
        for g in range(group):
            place = q * group + g
            low, mid, high = g * pair, g * pair + capacity, (g + 1) * pair
            sp[place] = partial[low:mid]
            pp[slot, g] = partial[mid:high]
            p_copy(q, g).start()

    def step(q, carry):
        @pl.when(q == steps)
        def _():
            finish(q - 1)

        @pl.when((q >= 2) & (lax.rem(q, 2) == 0))
        def _():
            weight_grads(q)

        @pl.when(q < steps)
        def _():
            main(q)

        return carry

    lax.fori_loop(0, steps + 1, step, 0)
    for copy, buf, acc in zip(grads, (wg_ref, wu_ref, wd_ref), (acc_g, acc_u, acc_d)):
        buf[...] = acc[...].astype(bf16)
        copy.start()
    for q in (steps - 2, steps - 1):
        for g in range(group):
            q_copy(q, g).wait_send()
            d_copy(q, g).wait_send()
            p_copy(q, g).wait_send()
    self_pull.wait()
    self_back.wait()
    for q in range(steps):
        for g in range(group):
            place = q * group + g
            slot_copy(q, g).wait()
            forward(q, g).wait_send()
            g_mate(q, g).wait_send()
            if place:
                x_copy(place).wait_send()
                for copy in back_copies(q, g):
                    copy.wait()
    for copy in grads:
        copy.wait()


def expert_exchange(x, g, others, wg, wu, wd, wr, group=2):
    experts, capacity, width = x.shape
    ff = wg.shape[1]
    steps = experts // group
    rows = 2 * capacity * group
    anywhere = pl.BlockSpec(memory_space=pl.ANY)
    vmem, dma = pltpu.VMEM, pltpu.SemaphoreType.DMA
    each = dma((experts,))
    count = rows * steps
    outs = pl.pallas_call(
        functools.partial(expert_exchange_kernel, group),
        out_shape=(
            jax.ShapeDtypeStruct((width, ff), bf16),
            jax.ShapeDtypeStruct((width, ff), bf16),
            jax.ShapeDtypeStruct((ff, width), bf16),
            jax.ShapeDtypeStruct((experts, capacity, width), bf16),
            jax.ShapeDtypeStruct((experts, capacity, width), bf16),
            jax.ShapeDtypeStruct((experts, 8, LANES), f32),
            jax.ShapeDtypeStruct((experts, capacity, width), bf16),
        ),
        in_specs=[anywhere] * 6 + [pl.BlockSpec(memory_space=vmem)],
        out_specs=(anywhere,) * 7,
        scratch_shapes=[
            vmem((steps * rows, width), bf16),
            vmem((2, rows, width), bf16),
            vmem((experts, 8, LANES), f32),
            vmem((experts, 8, LANES), f32),
            vmem((experts, capacity, width), bf16),
            vmem((2, group, capacity, width), bf16),
            vmem((2, group, capacity, width), bf16),
            vmem((experts, capacity, width), bf16),
            vmem((2, group, capacity, width), bf16),
            vmem((2, group, capacity, width), bf16),
            vmem((experts, 8, LANES), f32),
            vmem((2, group, 8, LANES), f32),
            vmem((2, group, 8, LANES), f32),
            vmem((2 * rows, ff), bf16),
            vmem((2 * rows, ff), bf16),
            vmem((2 * rows, ff), bf16),
            vmem((2 * rows, width), bf16),
            vmem((width, 2 * rows), bf16),
            vmem((width, ff), f32),
            vmem((width, ff), f32),
            vmem((ff, width), f32),
            vmem((width, ff), bf16),
            vmem((width, ff), bf16),
            vmem((ff, width), bf16),
            dma((3,)),
            each, each, each, each,
            dma((2, 2 * group)),
            each, each,
            each, each, each, each, each, each, each, each, each, each, each,
            dma((6,)),
            dma((3,)),
        ],
        compiler_params=params(62, collective_id=2, has_side_effects=True),
        cost_estimate=cost(18 * count * width * ff, 2 * count * 4 * width + 18 * width * ff, count * ff),
        name="experts",
    )(x, g, others, wg, wu, wd, wr)
    return outs[:6]


def hot_rows(col, k, rows, slots):
    return jnp.where(iota((rows, slots), 1) == col[:, k : k + 1], 1.0, 0.0).astype(bf16)


def state_rows(col, gates, hidden, out_grad, gain, wr, gathered, pull0, pull1):
    valid = col[:, 4:5].astype(f32)
    total = pull0 + pull1
    lane = iota((col.shape[0], LANES), 1)
    d_log = jnp.where(lane == col[:, 2:3], pull0 - gates[:, 0:1] * total, 0.0)
    d_log = d_log + jnp.where(lane == col[:, 3:4], pull1 - gates[:, 1:2] * total, 0.0)
    d_log = d_log.astype(bf16)
    d_moe = gathered + dot_nt(d_log, wr)
    inverse = lax.rsqrt(jnp.mean(hidden * hidden, axis=1, keepdims=True) + epsilon)
    normal = hidden * inverse
    scaled = gain * d_moe
    share = jnp.mean(normal * scaled, axis=1, keepdims=True)
    d_state = out_grad.astype(f32) + inverse * (scaled - normal * share)
    term = jnp.sum((normal * d_moe).reshape(hidden.shape[0] // 8, 8, hidden.shape[1]), axis=0)
    return d_log, d_state, (valid * d_state).astype(bf16), term


def pull_rows(col, k, table, slots):
    experts, rows = table.shape[0], col.shape[0]
    chosen = jnp.where(iota((rows, experts), 1) == col[:, 2 + k : 3 + k], 1.0, 0.0)
    values = dot_nn(chosen, table, precision=lax.Precision.HIGHEST)
    slot = col[:, k : k + 1] - slots // experts * col[:, 2 + k : 3 + k]
    here = (iota((rows, LANES), 1) == slot) & (col[:, k : k + 1] < slots)
    return jnp.sum(jnp.where(here, values, 0.0), axis=1, keepdims=True)


def state_kernel(
    col_ref, gate_ref, din_ref, h_ref, og_ref, gain_ref, wr_ref, dstate_ref, dattn_ref, dlog_ref, gterm_ref
):
    rows, width = h_ref.shape
    slots = din_ref.shape[0]
    col = col_ref[...]
    hot0, hot1 = hot_rows(col, 0, rows, slots), hot_rows(col, 1, rows, slots)
    pulls = din_ref[:, width:]
    pull0 = jnp.sum(dot_nn(hot0, pulls), axis=1, keepdims=True)
    pull1 = jnp.sum(dot_nn(hot1, pulls), axis=1, keepdims=True)
    gathered = dot_nn(hot0 + hot1, din_ref[:, 0:width])
    dlog_ref[...], dstate_ref[...], dattn_ref[...], term = state_rows(
        col, gate_ref[...], h_ref[...], og_ref[...], gain_ref[...], wr_ref[...], gathered, pull0, pull1
    )

    @pl.when(pl.program_id(0) == 0)
    def _():
        gterm_ref[...] = jnp.zeros_like(gterm_ref)

    gterm_ref[...] += term


def state_back(col, gates, din, hidden, out_grad, gain, wr):
    count, width = hidden.shape
    slots = din.shape[0]
    rows = 256
    whole = lambda i: (0, 0)
    part = lambda i: (i, 0)
    return pl.pallas_call(
        state_kernel,
        out_shape=(
            jax.ShapeDtypeStruct((count, width), f32),
            jax.ShapeDtypeStruct((count, width), bf16),
            jax.ShapeDtypeStruct((count, LANES), bf16),
            jax.ShapeDtypeStruct((8, width), f32),
        ),
        grid=(count // rows,),
        in_specs=[
            pl.BlockSpec((rows, LANES), part),
            pl.BlockSpec((rows, LANES), part),
            pl.BlockSpec(din.shape, whole),
            pl.BlockSpec((rows, width), part),
            pl.BlockSpec((rows, width), part),
            pl.BlockSpec((1, width), whole),
            pl.BlockSpec((width, LANES), whole),
        ],
        out_specs=(
            pl.BlockSpec((rows, width), part),
            pl.BlockSpec((rows, width), part),
            pl.BlockSpec((rows, LANES), part),
            pl.BlockSpec((8, width), whole),
        ),
        compiler_params=params(48),
        cost_estimate=cost(2 * slots * count * width, 14 * count * width),
        name="state_back",
    )(col, gates, din, hidden, out_grad, gain.reshape(1, width), wr)


def finish_sums(w_ref, gain_ref, sum_ref, extra_ref, qkv_ref, out_ref, small_ref):
    pairs, rows = sum_ref.shape[0:2]
    width = w_ref.shape[0]
    me = lax.axis_index("dp")
    for pair in range(pairs):
        at = pair * LANES
        for i in range(3):
            qkv_ref[:, i * width + at : i * width + at + LANES] = sum_ref[pair, :, i * LANES : (i + 1) * LANES]
        out_ref[:, at : at + LANES] = sum_ref[pair, :, 3 * LANES :]
    mine = w_ref[pl.ds(pl.multiple_of(me * rows, rows), rows), :].astype(f32)
    total = jnp.sum(mine * qkv_ref[...], axis=1, keepdims=True)
    here = iota((rows, width), 1) == iota((rows, width), 0) + me * rows
    gain = jnp.sum(jnp.where(here, gain_ref[...], 0.0), axis=1, keepdims=True)
    small_ref[...] = jnp.where(iota(small_ref.shape, 1) == 65, total / gain, extra_ref[...])


def tail_kernel(
    n_ride, n_sum, d_ref, w_ref, tok_ref, gain_ref, dstate_ref, col_ref, gate_ref, rows_ref, h_ref, *refs
):
    srcs, sums, refs = refs[:n_ride], refs[n_ride : n_ride + n_sum], refs[n_ride + n_sum :]
    (grad_ref, out_ref), dsts, finals = refs[0:2], refs[2 : 2 + n_ride], refs[2 + n_ride :]
    for src, dst in zip(srcs, dsts):
        dst[...] = src[...].astype(f32)
    if n_sum:

        @pl.when(pl.program_id(0) == 0)
        def _():
            finish_sums(w_ref, gain_ref, *sums, *finals)

    rows, width = tok_ref.shape
    d_normed = dot_nt(d_ref[0], w_ref[:, 0:width])
    for i in range(1, 3):
        d_normed = d_normed + dot_nt(d_ref[i], w_ref[:, i * width : (i + 1) * width])
    values = tok_ref[...].astype(f32)
    inverse = lax.rsqrt(jnp.mean(values * values, axis=1, keepdims=True) + epsilon)
    normal = values * inverse
    scaled = gain_ref[...] * d_normed
    share = jnp.mean(normal * scaled, axis=1, keepdims=True)
    grad_ref[...] = dstate_ref[...] + inverse * (scaled - normal * share)
    slots = rows_ref.shape[0]
    col = col_ref[...]
    pick0 = dot_nn(hot_rows(col, 0, rows, slots), rows_ref[...])
    pick1 = dot_nn(hot_rows(col, 1, rows, slots), rows_ref[...])
    out_ref[...] = (h_ref[...] + gate_ref[:, 0:1] * pick0 + gate_ref[:, 1:2] * pick1).astype(bf16)


def tail(d_qkv, w_qkv, tokens, gain, d_state, col, gates, slot_rows, hidden, riders=(), sums=()):
    count, width = tokens.shape
    rows = 256
    steps = count // rows
    part = lambda i: (i, 0)
    passed = [pl.BlockSpec((array.shape[0] // steps, array.shape[1]), part) for array in riders]

    def whole(array):
        return pl.BlockSpec(array.shape, lambda i: (0,) * len(array.shape), pipeline_mode=pl.Buffered(1))

    finals = []
    if sums:
        mine = sums[1].shape[0]
        finals = [jax.ShapeDtypeStruct((mine, lanes), f32) for lanes in (3 * width, width, LANES)]
    gain = gain.reshape(1, width)
    return pl.pallas_call(
        functools.partial(tail_kernel, len(riders), len(sums)),
        out_shape=[jax.ShapeDtypeStruct((count, width), f32), jax.ShapeDtypeStruct((count, width), bf16)]
        + [jax.ShapeDtypeStruct(array.shape, f32) for array in riders]
        + finals,
        grid=(steps,),
        in_specs=[
            pl.BlockSpec((3, rows, width), lambda i: (0, i, 0)),
            whole(w_qkv),
            pl.BlockSpec((rows, width), part),
            whole(gain),
            pl.BlockSpec((rows, width), part),
            pl.BlockSpec((rows, LANES), part),
            pl.BlockSpec((rows, LANES), part),
            whole(slot_rows),
            pl.BlockSpec((rows, width), part),
        ]
        + passed
        + [whole(array) for array in sums],
        out_specs=[pl.BlockSpec((rows, width), part)] * 2
        + passed
        + [pl.BlockSpec(final.shape, lambda i: (0, 0)) for final in finals],
        compiler_params=params(56),
        cost_estimate=cost(12 * count * width * width, 60 * count * width),
        name="tail",
    )(d_qkv, w_qkv, tokens, gain, d_state, col, gates, slot_rows, hidden, *riders, *sums)


def shards(
    tokens,
    lengths,
    expert_ids,
    slot_order,
    gain_attn,
    w_qkv,
    w_out,
    gain_moe,
    w_router,
    w_gate,
    w_up,
    w_down,
    out_grad,
):
    tok_dev, width = tokens.shape
    n_dev = lax.axis_size("dp")
    experts = w_router.shape[1]
    split = n_dev // experts
    capacity = split * (5 * tok_dev // (4 * n_dev))
    slots = experts * capacity
    me = lax.axis_index("dp")
    part = lax.rem(me, split)
    same_part = [[e * split + p for e in range(experts)] for p in range(split)]
    same_expert = [[e * split + p for p in range(split)] for e in range(experts)]
    swap = [(d, d ^ 1) for d in range(n_dev)]

    def across(blocks):
        return lax.all_to_all(blocks, "dp", 0, 0, axis_index_groups=same_part, tiled=True)

    def share(rows):
        if split == 2:
            return jnp.concatenate([rows, lax.ppermute(rows, "dp", swap)], axis=0)
        return lax.all_gather(rows, "dp", axis_index_groups=same_expert, tiled=True)

    def settle(pieces):
        if split == 2:
            theirs = lax.ppermute(pieces[1], "dp", swap)
            return (pieces[0].astype(f32) + theirs.astype(f32)).astype(bf16)
        got = lax.all_to_all(pieces, "dp", 0, 0, axis_index_groups=same_expert, tiled=True)
        return jnp.sum(got.astype(f32), axis=0).astype(bf16)

    def send_in(rows):
        return share(across(rows.reshape(experts, capacity, -1)).reshape(slots, -1))

    def send_back(rows):
        summed = settle(rows.reshape(split, slots, -1))
        return across(summed.reshape(experts, capacity, -1)).reshape(slots, -1)

    def reduce_rows(term):
        pieces = term.reshape(experts, split, -1, term.shape[-1])
        if split == 2:
            mine = lax.dynamic_index_in_dim(pieces, part, 1, keepdims=False)
            theirs = lax.dynamic_index_in_dim(pieces, 1 - part, 1, keepdims=False)
            theirs = lax.ppermute(theirs.astype(bf16), "dp", swap)
            summed = (mine + theirs.astype(f32)).astype(bf16)
        else:
            pieces = jnp.moveaxis(pieces, 1, 0).astype(bf16)
            got = lax.all_to_all(pieces, "dp", 0, 0, axis_index_groups=same_expert, tiled=True)
            summed = jnp.sum(got.astype(f32), axis=0).astype(bf16)
        return jnp.sum(across(summed).astype(f32), axis=0)

    wr = jnp.pad(w_router, ((0, 0), (0, LANES - experts)))
    col, row = make_slots(lengths, expert_ids, slot_order, experts, capacity)
    direct = split == 2 and experts == 16

    if direct:
        norm_t, qkv, mixed, mixed_t, lse, hidden, moe_t, gates, rows_out, grad_in, others = front(
            tokens, gain_attn, w_qkv, w_out, gain_moe, wr, col, row, out_grad, experts, capacity
        )
    else:
        token_vals = tokens.astype(f32)
        inverse_attn = lax.rsqrt(jnp.mean(token_vals * token_vals, axis=-1, keepdims=True) + epsilon)
        normed_low = (token_vals * inverse_attn * gain_attn).astype(bf16)
        qkv = jnp.dot(normed_low, w_qkv, preferred_element_type=f32).astype(bf16)
        mixed, lse = attend(qkv)
        grad_in = send_in(dispatch_grad(row, out_grad, slots))
        hidden, moe_low, gates = middle(mixed, w_out, tokens, gain_moe, wr, col)
        rows_out = dispatch(row, moe_low, slots)
    if direct:
        gate_grad, up_grad, down_grad, slot_part, d_in_back, pulls = expert_exchange(
            rows_out.reshape(experts, capacity, -1), grad_in, others, w_gate[0], w_up[0], w_down[0], wr
        )
        d_in_back = d_in_back.reshape(slots, -1)
    else:
        rows_in = send_in(rows_out)
        act, d_pre, d_up, d_rows, partial_out, d_in = expert_pass(
            rows_in, grad_in, w_gate[0], w_up[0], w_down[0], wr, split
        )
        d_in_back = send_back(d_in)
        slot_out = send_back(partial_out)
        down_grad = dot_tn(act, d_rows)
        gate_grad = dot_tn(rows_in, d_pre)
        up_grad = dot_tn(rows_in, d_up)

    if direct:
        d_state, d_qkv, sums, extra, slot_out = attend_back_reduce(
            qkv, mixed, lse, norm_t, mixed_t, moe_t, col, gates, d_in_back, hidden, out_grad,
            gain_moe, wr, pulls, w_out, slot_part, n_dev,
        )
        tokens_grad, block_out, gate_grad, up_grad, down_grad, qkv_sum, out_rows, extra = tail(
            d_qkv, w_qkv, tokens, gain_attn, d_state, col, gates, slot_out.reshape(slots, -1), hidden,
            (gate_grad, up_grad, down_grad), (sums, extra),
        )
        router_sum, gain_moe_sum, gain_attn_sum = extra[:, 0:experts], extra[:, 64], extra[:, 65]
    else:
        d_state, d_attn, d_log, gain_moe_rows = state_back(
            col, gates, d_in_back, hidden, out_grad, gain_moe, wr
        )
        d_mixed = dot_nt(d_attn, w_out).astype(bf16)
        d_qkv = attend_back(qkv, mixed, d_mixed, lse)
        lane = jnp.arange(LANES, dtype=jnp.int32)[None, :]
        gain_moe_term = jnp.sum(gain_moe_rows, axis=0)
        extra = jnp.where(lane == experts, gain_moe_term[:, None], dot_tn(moe_low, d_log))
        early = reduce_rows(jnp.concatenate([dot_tn(mixed, d_attn), extra], axis=1))
        out_rows, router_sum, gain_moe_sum = (
            early[:, 0:width], early[:, width : width + experts], early[:, width + experts]
        )
        qkv_sum = reduce_rows(jnp.concatenate([dot_tn(normed_low, d_qkv[i]) for i in range(3)], axis=1))
        tokens_grad, block_out = tail(d_qkv, w_qkv, tokens, gain_attn, d_state, col, gates, slot_out, hidden)
        my_rows = width // n_dev
        weight_rows = lax.dynamic_slice_in_dim(w_qkv, me * my_rows, my_rows, 0).astype(f32)
        my_gain = lax.dynamic_slice_in_dim(gain_attn, me * my_rows, my_rows, 0)
        gain_attn_sum = jnp.sum(weight_rows * qkv_sum, axis=1) / my_gain
    return (
        block_out,
        tokens_grad,
        gain_attn_sum,
        qkv_sum,
        out_rows,
        gain_moe_sum,
        router_sum,
        gate_grad[None],
        up_grad[None],
        down_grad[None],
    )


def solution(mesh):
    rows, one = P("dp", None), P("dp")
    cube = P("dp", None, None)
    return jax.shard_map(
        shards,
        mesh=mesh,
        in_specs=(rows, one, rows, rows, P(), P(), P(), P(), P(), cube, cube, cube, rows),
        out_specs=(rows, rows, one, rows, rows, one, rows, cube, cube, cube),
        check_vma=False,
    )
```

```python
import functools
import math

import jax
import jax.numpy as jnp
from jax import lax
from jax.experimental import pallas as pl
from jax.experimental.pallas import tpu as pltpu
from jax.sharding import PartitionSpec as P

HEADS = 16
HEAD_DIM = 64
LEN = 1024
LANES = 128
MIB = 1 << 20

epsilon = 1e-06
mask_fill = -1e30
f32 = jnp.float32
bf16 = jnp.bfloat16


def dot_nn(left, right, **kw):
    return lax.dot_general(left, right, (((1,), (0,)), ((), ())), preferred_element_type=f32, **kw)


def dot_nt(left, right, **kw):
    return lax.dot_general(left, right, (((1,), (1,)), ((), ())), preferred_element_type=f32, **kw)


def dot_tn(left, right, **kw):
    return lax.dot_general(left, right, (((0,), (0,)), ((), ())), preferred_element_type=f32, **kw)


def iota(shape, dim):
    return lax.broadcasted_iota(jnp.int32, shape, dim)


def params(mib, **kw):
    return pltpu.CompilerParams(vmem_limit_bytes=mib * MIB, **kw)


def cost(flops, nbytes, trans=0):
    return pl.CostEstimate(flops=int(flops), bytes_accessed=int(nbytes), transcendentals=int(trans))


def slot_kernel(capacity, experts, len_ref, ids_ref, rank_col_ref, rank_row_ref, col_ref, row_ref):
    count = ids_ref.shape[0]
    length = len_ref[0]
    ids = ids_ref[...]
    first, second = ids[:, 0:1], ids[:, 1:2]
    lane = iota((count, LANES), 1)
    place = iota((count, LANES), 0)
    hot0 = (lane == first) & (lane < experts)
    hot1 = (lane == second + experts) & (lane >= experts) & (lane < 2 * experts)
    valid = place < length
    hot = jnp.where((hot0 | hot1) & valid, 1.0, 0.0).astype(bf16)
    before = (rank_row_ref[...] < rank_col_ref[...]).astype(f32).astype(bf16)
    counts = dot_nn(before, hot)
    shifted = (lane == first + experts) & (lane >= experts) & (lane < 2 * experts) & valid
    totals = jnp.sum(jnp.where(shifted, 1.0, 0.0), axis=0, keepdims=True)
    slot0 = jnp.sum(jnp.where(hot0, counts, 0.0), axis=1, keepdims=True).astype(jnp.int32)
    slot1 = jnp.sum(jnp.where(hot1, counts + totals, 0.0), axis=1, keepdims=True).astype(jnp.int32)
    sentinel = experts * capacity
    ok = valid[:, 0:1]
    flat0 = jnp.where(ok & (slot0 < capacity), first * capacity + slot0, sentinel)
    flat1 = jnp.where(ok & (slot1 < capacity), second * capacity + slot1, sentinel)
    col = jnp.where(lane == 0, flat0, 0) + jnp.where(lane == 1, flat1, 0)
    col = col + jnp.where(lane == 2, first, 0) + jnp.where(lane == 3, second, 0)
    col = col + jnp.where(lane == 4, ok.astype(jnp.int32), 0)
    col_ref[...] = col
    row_ref[...] = jnp.transpose(col.astype(f32))[0:8, :].astype(jnp.int32)


def make_slots(lengths, expert_ids, slot_order, experts, capacity):
    count = expert_ids.shape[0]
    return pl.pallas_call(
        functools.partial(slot_kernel, capacity, experts),
        out_shape=(
            jax.ShapeDtypeStruct((count, LANES), jnp.int32),
            jax.ShapeDtypeStruct((8, count), jnp.int32),
        ),
        in_specs=[
            pl.BlockSpec(memory_space=pltpu.SMEM),
            pl.BlockSpec(memory_space=pltpu.VMEM),
            pl.BlockSpec(memory_space=pltpu.VMEM),
            pl.BlockSpec(memory_space=pltpu.VMEM),
        ],
        out_specs=(pl.BlockSpec(memory_space=pltpu.VMEM), pl.BlockSpec(memory_space=pltpu.VMEM)),
        compiler_params=params(40),
        cost_estimate=cost(2 * count * count * LANES, 4 * count * LANES),
        name="slots",
    )(lengths, expert_ids, slot_order.reshape(count, 1), slot_order)


def dispatch_kernel(rows, row_ref, data_ref, out_ref):
    count = data_ref.shape[0]
    slot = pl.program_id(0) * rows + iota((rows, count), 0)
    hot = (slot == row_ref[0:1, :]) | (slot == row_ref[1:2, :])
    out_ref[...] = dot_nn(jnp.where(hot, 1.0, 0.0).astype(bf16), data_ref[...]).astype(bf16)


def dispatch(row, data, slots):
    count, width = data.shape
    rows = 256
    return pl.pallas_call(
        functools.partial(dispatch_kernel, rows),
        out_shape=jax.ShapeDtypeStruct((slots, width), bf16),
        grid=(slots // rows,),
        in_specs=[
            pl.BlockSpec((8, count), lambda i: (0, 0)),
            pl.BlockSpec((count, width), lambda i: (0, 0)),
        ],
        out_specs=pl.BlockSpec((rows, width), lambda i: (i, 0)),
        compiler_params=params(40),
        cost_estimate=cost(2 * slots * count * width, 2 * (slots + count) * width),
        name="dispatch",
    )(row, data)


def dispatch_grad_kernel(rows, row_ref, data_ref, out_ref):
    count, width = data_ref.shape
    slot = pl.program_id(0) * rows + iota((rows, count), 0)
    hot0 = slot == row_ref[0:1, :]
    hot1 = slot == row_ref[1:2, :]
    both = jnp.where(hot0 | hot1, 1.0, 0.0).astype(bf16)
    out_ref[:, 0:width] = dot_nn(both, data_ref[...]).astype(bf16)
    other = jnp.where(hot0, row_ref[3:4, :], 0) + jnp.where(hot1, row_ref[2:3, :], 0)
    other = jnp.sum(other.astype(f32), axis=1, keepdims=True)
    out_ref[:, width:] = jnp.broadcast_to(other, (rows, LANES)).astype(bf16)


def dispatch_grad(row, data, slots):
    count, width = data.shape
    rows = 256
    return pl.pallas_call(
        functools.partial(dispatch_grad_kernel, rows),
        out_shape=jax.ShapeDtypeStruct((slots, width + LANES), bf16),
        grid=(slots // rows,),
        in_specs=[
            pl.BlockSpec((8, count), lambda i: (0, 0)),
            pl.BlockSpec((count, width), lambda i: (0, 0)),
        ],
        out_specs=pl.BlockSpec((rows, width + LANES), lambda i: (i, 0)),
        compiler_params=params(40),
        cost_estimate=cost(2 * slots * count * width, 2 * (slots + count) * width),
        name="dispatch_grad",
    )(row, data)


MESH = pl.DeviceIdType.MESH


def flip(chip, bits, experts):
    out, b = chip, 1
    while b < experts:
        if isinstance(bits, int):
            out = out + (bits // b % 2) * (b - 2 * b * lax.rem(lax.div(chip, b), 2))
        else:
            mine, theirs = lax.rem(lax.div(chip, b), 2), lax.rem(lax.div(bits, b), 2)
            out = out + b * theirs * (1 - 2 * mine)
        b *= 2
    return out


def greet(peers):
    barrier = pltpu.get_barrier_semaphore()
    for peer in peers:
        pl.semaphore_signal(barrier, inc=1, device_id=(peer,), device_id_type=MESH)
    pl.semaphore_wait(barrier, len(peers))


def exchange_copies(src, dst, send_sem, recv_sem, local_sem):
    experts = src.shape[0]
    me = lax.axis_index("dp")
    chip, core = lax.div(me, 2), lax.rem(me, 2)
    copies = [pltpu.make_async_copy(src.at[chip], dst.at[chip], local_sem)]
    peers = []
    half = experts // 2
    for place in range(1, experts):
        step = half + place // 2 if place % 2 else place // 2
        peer = flip(chip, step, experts)
        peers.append(2 * peer + core)
        copies.append(
            pltpu.make_async_remote_copy(
                src_ref=src.at[peer],
                dst_ref=dst.at[chip],
                send_sem=send_sem.at[step],
                recv_sem=recv_sem.at[step],
                device_id=(2 * peer + core,),
                device_id_type=MESH,
            )
        )
    return peers, copies


def exchange_sems(experts):
    return [
        pltpu.SemaphoreType.DMA((experts,)),
        pltpu.SemaphoreType.DMA((experts,)),
        pltpu.SemaphoreType.DMA,
    ]


SCALE2 = math.log2(math.e) / math.sqrt(HEAD_DIM)
QB = 256


def attend_kernel(q_ref, k_ref, v_ref, mixed_ref, lse_ref):
    lane = iota((QB, LANES), 1)
    wide = jnp.concatenate([v_ref[...], jnp.ones(v_ref.shape, bf16)], axis=1)
    causal = iota((QB, QB), 1) <= iota((QB, QB), 0)
    for block in range(LEN // QB):
        start, stop = block * QB, (block + 1) * QB
        query = q_ref[start:stop, :]
        halves, norms = [], []
        for head in range(2):
            mine = (lane // HEAD_DIM) == head
            scores = dot_nt(jnp.where(mine, query, jnp.zeros_like(query)), k_ref[0:stop, :])
            tail = jnp.where(causal, scores[:, start:stop], mask_fill)
            scores = tail if block == 0 else jnp.concatenate([scores[:, 0:start], tail], axis=1)
            highest = jnp.max(scores, axis=1, keepdims=True) * SCALE2
            raised = jnp.exp2(scores * SCALE2 - highest)
            out = dot_nn(raised.astype(bf16), wide[0:stop, :])
            summed = out[:, LANES:]
            halves.append(out[:, 0:LANES] / summed)
            norms.append(highest + jnp.log2(summed))
        mixed_ref[start:stop, :] = jnp.where(lane < HEAD_DIM, halves[0], halves[1]).astype(bf16)
        norm = jnp.where(lane == 0, norms[0], norms[1])
        lse_ref[0, :, start:stop] = jnp.transpose(norm)[0:8, :]


def attend(qkv):
    count, width3 = qkv.shape
    width = width3 // 3
    pairs = width // LANES
    return pl.pallas_call(
        attend_kernel,
        out_shape=(
            jax.ShapeDtypeStruct((count, width), bf16),
            jax.ShapeDtypeStruct((pairs, 8, count), f32),
        ),
        grid=(pairs,),
        in_specs=[
            pl.BlockSpec((count, LANES), lambda i: (0, i)),
            pl.BlockSpec((count, LANES), lambda i: (0, i + pairs)),
            pl.BlockSpec((count, LANES), lambda i: (0, i + 2 * pairs)),
        ],
        out_specs=(
            pl.BlockSpec((count, LANES), lambda i: (0, i)),
            pl.BlockSpec((1, 8, count), lambda i: (i, 0, 0)),
        ),
        compiler_params=params(40),
        cost_estimate=cost(2 * 4 * count * count * width, 8 * count * width, 8 * count * count),
        name="attend",
    )(qkv, qkv, qkv)


def front_kernel(
    pairs, blocks,
    tok_ref, gain_ref, wq_ref, wk_ref, wv_ref, w_out_ref, gain_moe_ref, wr_ref, col_ref, row_ref, og_ref,
    norm_t_ref, qkv_ref, mixed_ref, mixed_t_ref, lse_ref, h_ref, low_t_ref, gate_ref, rows_ref, og_out, oth_out,
    norm_ref, mixed_sc, low_ref, og_sc, oth_sc, og_send, og_recv, oth_send, oth_recv, self_sem,
):
    experts, capacity, width = og_sc.shape
    half = experts // 2
    turn = pl.program_id(0) - half
    me = lax.axis_index("dp")
    chip, core = lax.div(me, 2), lax.rem(me, 2)

    def chip_at(place):
        if isinstance(place, int):
            return flip(chip, half + place // 2 if place % 2 else place // 2, experts)
        return flip(chip, lax.rem(place, 2) * half + lax.div(place, 2), experts)

    def copies(place):
        return [
            pltpu.make_async_remote_copy(
                src_ref=src.at[place], dst_ref=dst.at[chip], send_sem=send.at[place], recv_sem=recv.at[place],
                device_id=(2 * chip_at(place) + core,), device_id_type=MESH,
            )
            for src, dst, send, recv in (
                (og_sc, og_out, og_send, og_recv), (oth_sc, oth_out, oth_send, oth_recv),
            )
        ]

    selves = [
        pltpu.make_async_copy(src.at[0], dst.at[chip], self_sem.at[i])
        for i, (src, dst) in enumerate(((og_sc, og_out), (oth_sc, oth_out)))
    ]

    @pl.when(turn == -half)
    def _():
        greet([2 * chip_at(place) + core for place in range(1, experts)])
        oth_sc[...] = jnp.zeros_like(oth_sc)

    @pl.when(turn < 0)
    def _():
        count = og_ref.shape[0]
        place = 2 * (turn + half)
        bases = [capacity * chip_at(place), capacity * chip_at(place + 1)]
        slot = iota((2 * capacity, count), 0)
        slot = jnp.where(slot < capacity, slot + bases[0], slot - capacity + bases[1])
        hot0 = jnp.where(slot == row_ref[0:1, :], 1.0, 0.0).astype(bf16)
        hot1 = jnp.where(slot == row_ref[1:2, :], 1.0, 0.0).astype(bf16)
        ids = row_ref[...].astype(f32).astype(bf16)
        other = dot_nt(ids, hot0)[3:4] + dot_nt(ids, hot1)[2:3]
        picked = dot_nn(hot0 + hot1, og_ref[...]).astype(bf16)
        for k in range(2):
            og_sc[place + k] = picked[k * capacity : (k + 1) * capacity]
            mine = other[:, k * capacity : (k + 1) * capacity]
            oth_sc[place + k, :, 0:capacity] = jnp.broadcast_to(mine, (8, capacity))
        for copy in copies(place + 1):
            copy.start()

        @pl.when(turn == -half)
        def _():
            for copy in selves:
                copy.start()

        @pl.when(turn > -half)
        def _():
            for copy in copies(place):
                copy.start()

    @pl.when(pl.program_id(0) == pl.num_programs(0) - 1)
    def _():
        for copy in selves:
            copy.wait()
        for place in range(1, experts):
            for copy in copies(place):
                copy.wait()

    @pl.when(turn == 0)
    def _():
        values = tok_ref[...].astype(f32)
        inverse = lax.rsqrt(jnp.mean(values * values, axis=1, keepdims=True) + epsilon)
        norm_ref[...] = (values * inverse * gain_ref[...]).astype(bf16)
        norm_t_ref[...] = jnp.transpose(norm_ref[...])

    @pl.when((turn >= 0) & (turn < pairs))
    def _():
        weights = jnp.concatenate([wq_ref[...], wk_ref[...], wv_ref[...]], axis=1)

        @pl.loop(0, LEN // QB)
        def _(block):
            here = pl.ds(pl.multiple_of(block * QB, QB), QB)
            part = dot_nn(norm_ref[here, :], weights).astype(bf16)
            for i in range(3):
                qkv_ref[i, here, :] = part[:, i * LANES : (i + 1) * LANES]

        attend_kernel(qkv_ref.at[0], qkv_ref.at[1], qkv_ref.at[2], mixed_ref, lse_ref)
        mixed_t_ref[...] = jnp.transpose(mixed_ref[...])
        mixed_sc[:, pl.ds(pl.multiple_of(turn * LANES, LANES), LANES)] = mixed_ref[...]

    span = h_ref.shape[0]

    @pl.when((turn >= pairs) & (turn < pairs + blocks))
    def _():
        here = pl.ds(pl.multiple_of((turn - pairs) * span, span), span)
        h_ref[...], low, gate_ref[...] = middle_rows(
            mixed_sc[here, :], w_out_ref[...], tok_ref[here, :], gain_moe_ref[...], wr_ref[...], col_ref[...]
        )
        low_ref[here, :] = low
        low_t_ref[...] = jnp.transpose(low)

    @pl.when(turn >= pairs + blocks)
    def _():
        rows, count = rows_ref.shape[0], low_ref.shape[0]
        slot = (turn - pairs - blocks) * rows + iota((rows, count), 0)
        hot = (slot == row_ref[0:1, :]) | (slot == row_ref[1:2, :])
        rows_ref[...] = dot_nn(jnp.where(hot, 1.0, 0.0).astype(bf16), low_ref[...]).astype(bf16)


def front(tokens, gain, w_qkv, w_out, gain_moe, wr, col, row, out_grad, experts, capacity):
    count, width = tokens.shape
    slots = experts * capacity
    half = experts // 2
    pairs = width // LANES
    span = 256
    blocks, turns = count // span, slots // span
    anywhere = pl.BlockSpec(memory_space=pl.ANY)

    def pair_at(i):
        return jnp.clip(i - half, 0, pairs - 1)

    def block_at(i):
        return jnp.clip(i - half - pairs, 0, blocks - 1)

    def fixed(array):
        return pl.BlockSpec(array.shape, lambda i: (0, 0), pipeline_mode=pl.Buffered(1))

    gain, gain_moe = gain.reshape(1, width), gain_moe.reshape(1, width)
    in_specs = [
        fixed(tokens),
        fixed(gain),
        pl.BlockSpec((width, LANES), lambda i: (0, pair_at(i))),
        pl.BlockSpec((width, LANES), lambda i: (0, pair_at(i) + pairs)),
        pl.BlockSpec((width, LANES), lambda i: (0, pair_at(i) + 2 * pairs)),
        fixed(w_out),
        fixed(gain_moe),
        fixed(wr),
        pl.BlockSpec((span, LANES), lambda i: (block_at(i), 0)),
        fixed(row),
        fixed(out_grad),
    ]
    out_specs = [
        pl.BlockSpec((width, count), lambda i: (0, 0)),
        pl.BlockSpec((3, count, LANES), lambda i: (0, 0, pair_at(i))),
        pl.BlockSpec((count, LANES), lambda i: (0, pair_at(i))),
        pl.BlockSpec((LANES, count), lambda i: (pair_at(i), 0)),
        pl.BlockSpec((1, 8, count), lambda i: (pair_at(i), 0, 0)),
        pl.BlockSpec((span, width), lambda i: (block_at(i), 0)),
        pl.BlockSpec((width, span), lambda i: (0, block_at(i))),
        pl.BlockSpec((span, LANES), lambda i: (block_at(i), 0)),
        pl.BlockSpec((span, width), lambda i: (jnp.clip(i - half - pairs - blocks, 0, turns - 1), 0)),
        anywhere,
        anywhere,
    ]
    out_shape = [
        jax.ShapeDtypeStruct((width, count), bf16),
        jax.ShapeDtypeStruct((3, count, width), bf16),
        jax.ShapeDtypeStruct((count, width), bf16),
        jax.ShapeDtypeStruct((width, count), bf16),
        jax.ShapeDtypeStruct((pairs, 8, count), f32),
        jax.ShapeDtypeStruct((count, width), f32),
        jax.ShapeDtypeStruct((width, count), bf16),
        jax.ShapeDtypeStruct((count, LANES), f32),
        jax.ShapeDtypeStruct((slots, width), bf16),
        jax.ShapeDtypeStruct((experts, capacity, width), bf16),
        jax.ShapeDtypeStruct((experts, 8, LANES), f32),
    ]
    each = pltpu.SemaphoreType.DMA((experts,))
    scratch = [pltpu.VMEM((count, width), bf16)] * 3
    scratch += [pltpu.VMEM((experts, capacity, width), bf16), pltpu.VMEM((experts, 8, LANES), f32)]
    scratch += [each, each, each, each, pltpu.SemaphoreType.DMA((2,))]
    return pl.pallas_call(
        functools.partial(front_kernel, pairs, blocks),
        out_shape=out_shape,
        grid=(half + pairs + blocks + turns,),
        in_specs=in_specs,
        out_specs=out_specs,
        scratch_shapes=scratch,
        compiler_params=params(52, collective_id=0, has_side_effects=True),
        cost_estimate=cost(18 * count * count * width, 24 * count * width, 8 * count * count),
        name="front",
    )(tokens, gain, w_qkv, w_qkv, w_qkv, w_out, gain_moe, wr, col, row, out_grad)


def attend_back_kernel(q_ref, k_ref, v_ref, o_ref, do_ref, lse_ref, out_ref, dk_sc, dv_sc):
    lane = iota((QB, LANES), 1)
    keep = iota((QB, QB), 0) <= iota((QB, QB), 1)
    dk_sc[...] = jnp.zeros_like(dk_sc)
    dv_sc[...] = jnp.zeros_like(dv_sc)
    sub = iota((8, LANES), 0)
    picks = jnp.where(iota((8, LANES), 1) // HEAD_DIM == sub, 1.0, 0.0)
    low = (iota((LEN, LANES), 1) // HEAD_DIM) == 0
    key = k_ref[...]
    none = jnp.zeros_like(key)
    keys = (jnp.where(low, key, none), jnp.where(low, none, key))
    for block in range(LEN // QB):
        start, stop = block * QB, (block + 1) * QB
        query = q_ref[start:stop, :]
        d_out = do_ref[start:stop, :]
        product = d_out.astype(f32) * o_ref[start:stop, :].astype(f32)
        delta = dot_nt(picks, product, precision=lax.Precision.HIGHEST)
        d_query = jnp.zeros((QB, LANES), f32)
        for head in range(2):
            mine = (lane // HEAD_DIM) == head
            query_one = jnp.where(mine, query, jnp.zeros_like(query))
            d_one = jnp.where(mine, d_out, jnp.zeros_like(d_out))
            scores = dot_nt(k_ref[0:stop, :], query_one)
            tail = jnp.where(keep, scores[start:stop, :], mask_fill)
            scores = tail if block == 0 else jnp.concatenate([scores[0:start, :], tail], axis=0)
            probs = jnp.exp2(scores * SCALE2 - lse_ref[0, head : head + 1, start:stop])
            d_probs = dot_nt(v_ref[0:stop, :], d_one)
            d_scores = (probs * (d_probs - delta[head : head + 1, :])).astype(bf16)
            dv_sc[0:stop, :] += dot_nn(probs.astype(bf16), d_one)
            dk_sc[0:stop, :] += dot_nn(d_scores, query_one)
            d_query = d_query + dot_tn(d_scores, keys[head][0:stop, :])
        out_ref[0, start:stop, :] = (d_query * (1.0 / math.sqrt(HEAD_DIM))).astype(bf16)
    out_ref[1, :, :] = (dk_sc[...] * (1.0 / math.sqrt(HEAD_DIM))).astype(bf16)
    out_ref[2, :, :] = dv_sc[...].astype(bf16)


def attend_back(qkv, mixed, d_mixed, lse):
    count, width = mixed.shape
    pairs = width // LANES
    return pl.pallas_call(
        attend_back_kernel,
        out_shape=jax.ShapeDtypeStruct((3, count, width), bf16),
        grid=(pairs,),
        in_specs=[
            pl.BlockSpec((count, LANES), lambda i: (0, i)),
            pl.BlockSpec((count, LANES), lambda i: (0, i + pairs)),
            pl.BlockSpec((count, LANES), lambda i: (0, i + 2 * pairs)),
            pl.BlockSpec((count, LANES), lambda i: (0, i)),
            pl.BlockSpec((count, LANES), lambda i: (0, i)),
            pl.BlockSpec((1, 8, count), lambda i: (i, 0, 0)),
        ],
        out_specs=pl.BlockSpec((3, count, LANES), lambda i: (0, 0, i)),
        scratch_shapes=[pltpu.VMEM((count, LANES), f32), pltpu.VMEM((count, LANES), f32)],
        compiler_params=params(40),
        cost_estimate=cost(5 * 4 * count * count * width, 16 * count * width, 8 * count * count),
        name="attend_back",
    )(qkv, qkv, qkv, mixed, d_mixed, lse)


RIDE_PER_TURN = 15
LAG = 2


def back_reduce_kernel(
    chips,
    q_ref, k_ref, v_ref, o_ref, lse_ref, norm_t, mix_t, moe_t,
    col_ref, gate_ref, din_ref, h_ref, og_ref, gain_ref, wr_ref, pull_ref, w_out_ref, slot_ref,
    dstate_ref, out_ref, sum_ref, extra_ref, back_ref,
    datt_ref, dmix_ref, dlog_ref, gm_ref,
    dk_sc, dv_sc, right, terms, firsts, sums, half0, half1, half2, half3, s_send, s_recv,
    *ride_sems,
):
    halves = (half0, half1, half2, half3)
    levels = chips.bit_length() - 1
    count = k_ref.shape[0]
    width = norm_t.shape[0]
    rows = terms.shape[3]
    span = 256
    blocks = count // span
    turn = pl.program_id(0) - blocks
    pairs = sum_ref.shape[0]
    me = lax.axis_index("dp")
    chip, core = lax.div(me, 2), lax.rem(me, 2)
    mate = 2 * chip + 1 - core
    order0 = [1 << b for b in range(levels)]
    order1 = list(order0)
    order1[0], order1[1] = order0[1], order0[0]
    order0[2:] = order0[2:][::-1]

    def bit(mask):
        return lax.rem(lax.div(chip, mask), 2)

    own, peers = [], []
    for level in range(levels):
        b0, b1 = bit(order0[level]), bit(order1[level])
        own.append(b0 + core * (b1 - b0))
        p0 = order0[level] * (1 - 2 * b0)
        p1 = order1[level] * (1 - 2 * b1)
        peers.append(2 * (chip + p0 + core * (p1 - p0)) + core)
    bases = [0]
    for level in range(levels):
        bases.append(bases[-1] + own[level] * (chips >> (level + 1)))

    def remote(src, dst, c, level, device):
        return pltpu.make_async_remote_copy(
            src_ref=src, dst_ref=dst, send_sem=s_send.at[c, level], recv_sem=s_recv.at[c, level],
            device_id=(device,), device_id_type=MESH,
        )

    def cols(c):
        return pl.ds(0, LANES) if isinstance(c, int) else slice(None)

    def place(c):
        return LAG + 1 if isinstance(c, int) else lax.rem(c, LAG + 1)

    def swap(c):
        return remote(
            terms.at[place(c), :, 1 - core, :, cols(c)], firsts.at[c, :, :, cols(c)], c, levels, mate
        )

    def send(c, level):
        span = chips >> (level + 1)
        start = bases[level] + (1 - own[level]) * span
        return remote(
            sums.at[c, pl.ds(start, span), :, cols(c)], halves[level].at[c, :, :, cols(c)], c, level, peers[level]
        )

    def fold_swap(c):
        swap(c).wait()
        for b in range(chips):
            places = []
            for order in (order0, order1):
                spot = 0
                for level in range(levels):
                    spot += (b // order[level] % 2) * (chips >> (level + 1))
                places.append(spot)
            at = places[0] + core * (places[1] - places[0])
            total = terms[place(c), b, core, :, cols(c)].astype(f32) + firsts[c, b, :, cols(c)].astype(f32)
            sums[c, at, :, cols(c)] = total.astype(bf16)

    def fold(c, level):
        send(c, level).wait()
        for t in range(chips >> (level + 1)):
            at = bases[level + 1] + t
            total = sums[c, at, :, cols(c)].astype(f32) + halves[level][c, t, :, cols(c)].astype(f32)
            if level < levels - 1:
                sums[c, at, :, cols(c)] = total.astype(bf16)
            elif isinstance(c, int):
                extra_ref[...] = total
            else:
                sum_ref[c] = total

    def stage(c, s):
        if s == 1:
            fold_swap(c)
        else:
            fold(c, s - 2)
        if s - 1 < levels:
            send(c, s - 1).start()

    riders, ride = exchange_copies(slot_ref, back_ref, *ride_sems)
    per = span // (2 * rows)

    @pl.when(turn == -blocks)
    def _():
        greet([mate] + riders)
        gm_ref[...] = jnp.zeros_like(gm_ref)

    counts = [1] * blocks + [RIDE_PER_TURN] * len(ride)
    first = 0
    for at, many in enumerate(counts):
        if first < len(ride):

            @pl.when(turn == at - blocks)
            def _():
                for copy in ride[first : first + many]:
                    copy.start()

        first += many

    @pl.when(turn < 0)
    def _():
        slots = din_ref.shape[0]
        here = pl.ds(pl.multiple_of((turn + blocks) * span, span), span)
        col = col_ref[...]
        hot0, hot1 = hot_rows(col, 0, span, slots), hot_rows(col, 1, span, slots)
        gathered = dot_nn(hot0 + hot1, din_ref[...])
        table = pull_ref[:, 0, :]
        d_log, d_state, d_att, term = state_rows(
            col, gate_ref[...], h_ref[...], og_ref[...], gain_ref[...], wr_ref[...], gathered,
            pull_rows(col, 0, table, slots), pull_rows(col, 1, table, slots),
        )
        dstate_ref[...] = d_state
        dlog_ref[here, :] = d_log
        datt_ref[here, :] = d_att
        dmix_ref[here, :] = dot_nt(d_att, w_out_ref[...]).astype(bf16)
        gm_ref[...] += term

    @pl.when(turn == 0)
    def _():
        for row in range(0, width, span):
            extra = dot_nn(moe_t[row : row + span, :], dlog_ref[...])
            gain = jnp.transpose(jnp.sum(gm_ref[:, row : row + span], axis=0, keepdims=True))
            extra = extra + jnp.where(iota(extra.shape, 1) == 64, gain, 0.0)
            at = row // (2 * rows)
            terms[place(pairs), at : at + per, :, :, 0:LANES] = extra.astype(bf16).reshape(per, 2, rows, LANES)
        swap(pairs).start()

    for s in range(levels + 1, 0, -1):
        c = turn - LAG * s

        @pl.when((c >= 0) & (c < pairs))
        def _():
            stage(c, s)

        @pl.when(c == 0)
        def _():
            stage(pairs, s)

    @pl.when((turn >= 0) & (turn < pairs))
    def _():
        lanes = pl.ds(pl.multiple_of(turn * LANES, LANES), LANES)
        attend_back_kernel(
            q_ref, k_ref, v_ref, o_ref, dmix_ref.at[:, lanes], lse_ref, out_ref, dk_sc, dv_sc
        )
        for i in range(3):
            right[:, i * LANES : (i + 1) * LANES] = out_ref[i]

        @pl.loop(0, width // span)
        def _(part):
            here = pl.ds(pl.multiple_of(part * span, span), span)
            qkv_rows = dot_nn(norm_t[here, :], right[...])
            out_rows = dot_nn(mix_t[here, :], datt_ref[:, lanes])
            at = pl.ds(part * per, per)
            terms[place(turn), at, :, :, 0 : 3 * LANES] = (
                qkv_rows.astype(bf16).reshape(per, 2, rows, 3 * LANES)
            )
            terms[place(turn), at, :, :, 3 * LANES :] = out_rows.astype(bf16).reshape(per, 2, rows, LANES)

        swap(turn).start()

    @pl.when(pl.program_id(0) == pl.num_programs(0) - 1)
    def _():
        for copy in ride:
            copy.wait()


def attend_back_reduce(
    qkv, mixed, lse, norm_t, mixed_t, moe_t, col, gates, d_in, hidden, out_grad, gain, wr, pulls, w_out, slot_rows,
    n_dev,
):
    count, width = mixed.shape
    pairs = width // LANES
    chips = n_dev // 2
    levels = chips.bit_length() - 1
    rows = width // n_dev
    wide = 4 * LANES
    span = 256
    blocks = count // span
    vmem, dma = pltpu.VMEM, pltpu.SemaphoreType.DMA
    anywhere = pl.BlockSpec(memory_space=pl.ANY)

    def pair_at(i):
        return jnp.clip(i - blocks, 0, pairs - 1)

    def block(lanes):
        return pl.BlockSpec((span, lanes), lambda i: (jnp.minimum(i, blocks - 1), 0))

    def third(which):
        return pl.BlockSpec((None, count, LANES), lambda i: (which, 0, pair_at(i)))

    def whole(array):
        return pl.BlockSpec(array.shape, lambda i: (0,) * array.ndim, pipeline_mode=pl.Buffered(1))

    gain = gain.reshape(1, width)
    d_state, d_qkv, sums, extra, back = pl.pallas_call(
        functools.partial(back_reduce_kernel, chips),
        out_shape=(
            jax.ShapeDtypeStruct((count, width), f32),
            jax.ShapeDtypeStruct((3, count, width), bf16),
            jax.ShapeDtypeStruct((pairs, rows, wide), f32),
            jax.ShapeDtypeStruct((rows, LANES), f32),
            jax.ShapeDtypeStruct(slot_rows.shape, bf16),
        ),
        grid=(blocks + pairs + LAG * (levels + 1),),
        in_specs=[
            third(0),
            third(1),
            third(2),
            pl.BlockSpec((count, LANES), lambda i: (0, pair_at(i))),
            pl.BlockSpec((1, 8, count), lambda i: (pair_at(i), 0, 0)),
            whole(norm_t),
            whole(mixed_t),
            whole(moe_t),
            block(LANES),
            block(LANES),
            whole(d_in),
            block(width),
            block(width),
            whole(gain),
            whole(wr),
            whole(pulls),
            whole(w_out),
            anywhere,
        ],
        out_specs=(
            block(width),
            pl.BlockSpec((3, count, LANES), lambda i: (0, 0, pair_at(i))),
            pl.BlockSpec((pairs, rows, wide), lambda i: (0, 0, 0)),
            pl.BlockSpec((rows, LANES), lambda i: (0, 0)),
            anywhere,
        ),
        scratch_shapes=[
            vmem((count, width), bf16),
            vmem((count, width), bf16),
            vmem((count, LANES), bf16),
            vmem((8, width), f32),
            vmem((count, LANES), f32),
            vmem((count, LANES), f32),
            vmem((count, 3 * LANES), bf16),
            vmem((LAG + 2, chips, 2, rows, wide), bf16),
            vmem((pairs + 1, chips, rows, wide), bf16),
            vmem((pairs + 1, chips, rows, wide), bf16),
        ]
        + [vmem((pairs + 1, chips >> (level + 1), rows, wide), bf16) for level in range(levels)]
        + [dma((pairs + 1, levels + 1)), dma((pairs + 1, levels + 1))]
        + exchange_sems(chips),
        compiler_params=params(62, collective_id=1, has_side_effects=True),
        cost_estimate=cost(5 * 4 * count * count * width, 40 * count * width, 8 * count * count),
        name="back_reduce",
    )(
        qkv, qkv, qkv, mixed, lse, norm_t, mixed_t, moe_t,
        col, gates, d_in, hidden, out_grad, gain, wr, pulls, w_out, slot_rows,
    )
    return d_state, d_qkv, sums, extra, back


def middle_rows(mixed, w_out, tokens, gain, wr, col):
    first, second, valid = col[:, 2:3], col[:, 3:4], col[:, 4:5].astype(f32)
    hidden = tokens.astype(f32) + valid * dot_nn(mixed, w_out)
    inverse = lax.rsqrt(jnp.mean(hidden * hidden, axis=1, keepdims=True) + epsilon)
    low = (hidden * inverse * gain).astype(bf16)
    logits = dot_nn(low, wr)
    lane = iota(logits.shape, 1)
    own = jnp.sum(jnp.where(lane == first, logits, 0.0), axis=1, keepdims=True)
    alt = jnp.sum(jnp.where(lane == second, logits, 0.0), axis=1, keepdims=True)
    gate0 = 1.0 / (1.0 + jnp.exp(alt - own))
    gate1 = 1.0 / (1.0 + jnp.exp(own - alt))
    return hidden, low, jnp.where(lane == 0, gate0, 0.0) + jnp.where(lane == 1, gate1, 0.0)


def middle_kernel(mixed_ref, w_out_ref, tok_ref, gain_ref, wr_ref, col_ref, h_ref, low_ref, gate_ref):
    h_ref[...], low_ref[...], gate_ref[...] = middle_rows(
        mixed_ref[...], w_out_ref[...], tok_ref[...], gain_ref[...], wr_ref[...], col_ref[...]
    )


def middle(mixed, w_out, tokens, gain, wr, col):
    count, width = mixed.shape
    rows = 256
    whole = lambda i: (0, 0)
    part = lambda i: (i, 0)
    return pl.pallas_call(
        middle_kernel,
        out_shape=(
            jax.ShapeDtypeStruct((count, width), f32),
            jax.ShapeDtypeStruct((count, width), bf16),
            jax.ShapeDtypeStruct((count, LANES), f32),
        ),
        grid=(count // rows,),
        in_specs=[
            pl.BlockSpec((rows, width), part),
            pl.BlockSpec((width, width), whole),
            pl.BlockSpec((rows, width), part),
            pl.BlockSpec((1, width), whole),
            pl.BlockSpec((width, LANES), whole),
            pl.BlockSpec((rows, LANES), part),
        ],
        out_specs=(
            pl.BlockSpec((rows, width), part),
            pl.BlockSpec((rows, width), part),
            pl.BlockSpec((rows, LANES), part),
        ),
        compiler_params=params(40),
        cost_estimate=cost(2 * count * width * width, 12 * count * width),
        name="middle",
    )(mixed, w_out, tokens, gain.reshape(1, width), wr, col)


GELU_C = math.sqrt(2.0 / math.pi)


def expert_kernel(
    split, x_ref, g_ref, wg_ref, wu_ref, wd_ref, wr_ref, act_ref, dgp_ref, dup_ref, de_ref, part_ref, din_ref
):
    rows, width = x_ref.shape
    me = lax.axis_index("dp")
    expert, part = me // split, lax.rem(me, split)
    x = x_ref[...]
    lane = iota((rows, LANES), 1)
    logits = dot_nn(x, wr_ref[...])
    own = jnp.sum(jnp.where(lane == expert, logits, 0.0), axis=1, keepdims=True)
    other = g_ref[:, width:].astype(f32).astype(jnp.int32)
    alt = jnp.sum(jnp.where(lane == other, logits, 0.0), axis=1, keepdims=True)
    gate = 1.0 / (1.0 + jnp.exp(alt - own))
    d_rows = (g_ref[:, 0:width].astype(f32) * gate).astype(bf16)
    de_ref[...] = d_rows
    pre = dot_nn(x, wg_ref[...])
    up = dot_nn(x, wu_ref[...])
    d_hidden = dot_nt(d_rows, wd_ref[...])
    square = pre * pre
    bent = jnp.tanh(GELU_C * pre * (1.0 + 0.044715 * square))
    half = 0.5 * (1.0 + bent)
    gelu = pre * half
    slope = half + 0.5 * pre * (1.0 - bent * bent) * (GELU_C * (1.0 + 3 * 0.044715 * square))
    act = (gelu * up).astype(bf16)
    act_ref[...] = act
    dgp = (d_hidden * up * slope).astype(bf16)
    dup = (d_hidden * gelu).astype(bf16)
    dgp_ref[...] = dgp
    dup_ref[...] = dup
    pull = jnp.sum(act.astype(f32) * d_hidden, axis=1, keepdims=True)
    pull_high = pull.astype(bf16)
    pull_low = (pull - pull_high.astype(f32)).astype(bf16)
    part_ref[...] = dot_nn(act, wd_ref[...]).astype(bf16)
    din_ref[:, 0:width] = (dot_nt(dgp, wg_ref[...]) + dot_nt(dup, wu_ref[...])).astype(bf16)
    extra = jnp.where(lane == 2 * part, pull_high.astype(f32), 0.0)
    extra = extra + jnp.where(lane == 2 * part + 1, pull_low.astype(f32), 0.0)
    din_ref[:, width:] = extra.astype(bf16)


def expert_pass(x, g, wg, wu, wd, wr, split):
    count, width = x.shape
    ff = wg.shape[1]
    rows = 256
    whole = lambda i: (0, 0)
    part = lambda i: (i, 0)
    once = dict(pipeline_mode=pl.Buffered(1))
    return pl.pallas_call(
        functools.partial(expert_kernel, split),
        out_shape=(
            jax.ShapeDtypeStruct((count, ff), bf16),
            jax.ShapeDtypeStruct((count, ff), bf16),
            jax.ShapeDtypeStruct((count, ff), bf16),
            jax.ShapeDtypeStruct((count, width), bf16),
            jax.ShapeDtypeStruct((count, width), bf16),
            jax.ShapeDtypeStruct((count, width + LANES), bf16),
        ),
        grid=(count // rows,),
        in_specs=[
            pl.BlockSpec((rows, width), part),
            pl.BlockSpec((rows, width + LANES), part),
            pl.BlockSpec((width, ff), whole, **once),
            pl.BlockSpec((width, ff), whole, **once),
            pl.BlockSpec((ff, width), whole, **once),
            pl.BlockSpec((width, LANES), whole),
        ],
        out_specs=(
            pl.BlockSpec((rows, ff), part),
            pl.BlockSpec((rows, ff), part),
            pl.BlockSpec((rows, ff), part),
            pl.BlockSpec((rows, width), part),
            pl.BlockSpec((rows, width), part),
            pl.BlockSpec((rows, width + LANES), part),
        ),
        compiler_params=params(56),
        cost_estimate=cost(12 * count * width * ff, 2 * count * (3 * ff + 5 * width), count * ff),
        name="experts",
    )(x, g, wg, wu, wd, wr)


def expert_exchange_kernel(
    group, x_ref, g_ref, oth_ref, wg_hbm, wu_hbm, wd_hbm, wr_ref,
    gg_ref, ug_ref, dg_ref, slot_ref, back_ref, pulls_ref, gm_ref,
    xb, gb, oth, oth_mate, ds, rd, pd, sp, rp, pp, pt, pq, rq, act, dgp, dup, de, xt, acc_g, acc_u, acc_d,
    wg_ref, wu_ref, wd_ref,
    w_sem, x_send, x_recv, f_send, f_recv, g_load, g_send, g_recv,
    d_send, d_recv, p_send, p_recv, q_send, q_recv, b_send, b_recv, t_send, t_recv, s_sem, l_sem, o_sem,
):
    experts, capacity, width = x_ref.shape
    ff = wg_ref.shape[1]
    steps = experts // group
    pair = 2 * capacity
    rows = group * pair
    half = experts // 2
    me = lax.axis_index("dp")
    chip, core = lax.div(me, 2), lax.rem(me, 2)
    mate = 2 * chip + 1 - core

    def bits(place):
        if isinstance(place, int):
            return half + place // 2 if place % 2 else place // 2
        return lax.rem(place, 2) * half + lax.div(place, 2)

    def chip_at(place):
        return flip(chip, bits(place), experts)

    def remote(src, dst, send, recv, device):
        return pltpu.make_async_remote_copy(
            src_ref=src, dst_ref=dst, send_sem=send, recv_sem=recv, device_id=(device,), device_id_type=MESH
        )

    def block(q, g, second):
        start = q * rows + g * pair + second * capacity
        return xb.at[pl.ds(start if isinstance(start, int) else pl.multiple_of(start, 16), capacity)]

    def x_copy(place):
        peer = chip_at(place)
        own = block(place // group, place % group, 0)
        return remote(x_ref.at[peer], own, x_send.at[place], x_recv.at[place], 2 * peer + core)

    def x_arrival(q, g):
        place = q * group + g
        return remote(x_ref.at[chip], block(q, g, 0), x_send.at[place], x_recv.at[place], mate)

    def forward(q, g):
        place = q * group + g
        return remote(block(q, g, 0), block(q, g, 1), f_send.at[place], f_recv.at[place], mate)

    def g_mate(q, g):
        place = q * group + g
        at = chip_at(place)
        return remote(g_ref.at[at], gm_ref.at[at], g_send.at[place], g_recv.at[place], mate)

    def g_loads(q, g):
        slot, at = lax.rem(q, 2), chip_at(q * group + g)
        first, second = g * pair, g * pair + capacity
        return (
            pltpu.make_async_copy(g_ref.at[at], gb.at[slot, first:second], g_load.at[slot, 2 * g]),
            pltpu.make_async_copy(gm_ref.at[at], gb.at[slot, second : second + capacity], g_load.at[slot, 2 * g + 1]),
        )

    def load_g(q):
        for g in range(group):
            g_mate(q, g).wait_recv()
            for copy in g_loads(q, g):
                copy.start()

    def d_copy(q, g):
        place, slot = q * group + g, lax.rem(q, 2)
        return remote(pd.at[slot, g], rd.at[slot, g], d_send.at[place], d_recv.at[place], mate)

    def p_copy(q, g):
        place, slot = q * group + g, lax.rem(q, 2)
        return remote(pp.at[slot, g], rp.at[slot, g], p_send.at[place], p_recv.at[place], mate)

    def q_copy(q, g):
        place, slot = q * group + g, lax.rem(q, 2)
        return remote(pq.at[slot, g], rq.at[slot, g], q_send.at[place], q_recv.at[place], mate)

    def back_copies(q, g):
        place = q * group + g
        device = 2 * chip_at(place) + core
        return (
            remote(pt.at[place], pulls_ref.at[chip], t_send.at[place], t_recv.at[place], device),
            remote(ds.at[place], back_ref.at[chip], b_send.at[place], b_recv.at[place], device),
        )

    def slot_copy(q, g):
        place = q * group + g
        return pltpu.make_async_copy(sp.at[place], slot_ref.at[chip_at(place)], s_sem.at[place])

    weights = [
        pltpu.make_async_copy(src, dst, w_sem.at[i])
        for i, (src, dst) in enumerate(((wg_hbm, wg_ref), (wu_hbm, wu_ref), (wd_hbm, wd_ref)))
    ]
    grads = [
        pltpu.make_async_copy(src, dst, o_sem.at[i])
        for i, (src, dst) in enumerate(((wg_ref, gg_ref), (wu_ref, ug_ref), (wd_ref, dg_ref)))
    ]
    self_x = pltpu.make_async_copy(x_ref.at[chip], block(0, 0, 0), l_sem.at[0])
    self_pull = pltpu.make_async_copy(pt.at[0], pulls_ref.at[chip], l_sem.at[1])
    self_back = pltpu.make_async_copy(ds.at[0], back_ref.at[chip], l_sem.at[2])
    oth_own = pltpu.make_async_copy(oth_ref, oth, l_sem.at[3])
    oth_copy = remote(oth_ref, oth_mate, l_sem.at[4], l_sem.at[5], mate)

    for copy in weights:
        copy.start()
    self_x.start()
    oth_own.start()
    greet([2 * chip_at(place) + core for place in range(1, experts)] + [mate])
    oth_copy.start()
    for place in range(1, group):
        x_copy(place).start()
    for q in range(steps):
        for g in range(group):
            g_mate(q, g).start()
        for g in range(group):
            if (q + 1) * group + g < experts:
                x_copy((q + 1) * group + g).start()
    for acc in (acc_g, acc_u, acc_d):
        acc[...] = jnp.zeros_like(acc)
    pt[...] = jnp.zeros_like(pt)
    pq[...] = jnp.zeros_like(pq)
    self_x.wait()
    forward(0, 0).start()
    oth_own.wait()
    oth_copy.wait()
    load_g(jnp.int32(0))
    for g in range(1, group):
        x_arrival(0, g).wait_recv()
        forward(0, g).start()
    for copy in weights:
        copy.wait()

    def finish(q):
        slot = lax.rem(q, 2)
        for g in range(group):
            place = q * group + g
            q_copy(q, g).wait_recv()
            d_copy(q, g).wait_recv()
            pt[place] = pt[place] + rq[slot, g]
            ds[place] = (ds[place].astype(f32) + rd[slot, g].astype(f32)).astype(bf16)
            if g == 0:

                @pl.when(q == 0)
                def _():
                    self_pull.start()
                    self_back.start()

                @pl.when(q > 0)
                def _():
                    for copy in back_copies(q, g):
                        copy.start()

            else:
                for copy in back_copies(q, g):
                    copy.start()
        for g in range(group):
            place = q * group + g
            p_copy(q, g).wait_recv()
            sp[place] = (sp[place].astype(f32) + rp[slot, g].astype(f32)).astype(bf16)
            slot_copy(q, g).start()

    def weight_grads(q):
        xt[...] = jnp.transpose(xb[pl.ds(pl.multiple_of((q - 2) * rows, 16), 2 * rows), :])
        span = 256
        for row in range(0, width, span):
            acc_g[row : row + span, :] += dot_nn(xt[row : row + span, :], dgp[...])
            acc_u[row : row + span, :] += dot_nn(xt[row : row + span, :], dup[...])
        for row in range(0, ff, LANES):
            acc_d[row : row + LANES, :] += dot_tn(act[:, row : row + LANES], de[...])

    def main(q):
        slot = lax.rem(q, 2)
        here = pl.ds(pl.multiple_of(slot * rows, 16), rows)
        for g in range(group):
            for copy in g_loads(q, g):
                copy.wait()
            forward(q, g).wait_recv()

        @pl.when(q + 1 < steps)
        def _():
            load_g(q + 1)

        x = xb[pl.ds(pl.multiple_of(q * rows, 16), rows), :]
        lane = iota((rows, LANES), 1)
        logits = dot_nn(x, wr_ref[...])
        mine = jnp.sum(jnp.where(lane == chip, logits, 0.0), axis=1, keepdims=True)
        ids = []
        for g in range(group):
            at = chip_at(q * group + g)
            for table in (oth, oth_mate):
                ids.append(jnp.transpose(table[at])[0:capacity, 0:1])
        other = jnp.concatenate(ids, axis=0).astype(jnp.int32)
        alt = jnp.sum(jnp.where(lane == other, logits, 0.0), axis=1, keepdims=True)
        gate = 1.0 / (1.0 + jnp.exp(alt - mine))
        d_rows = (gb[slot].astype(f32) * gate).astype(bf16)
        de[here, :] = d_rows
        pre = dot_nn(x, wg_ref[...])
        up = dot_nn(x, wu_ref[...])
        d_hidden = dot_nt(d_rows, wd_ref[...])
        square = pre * pre
        bent = jnp.tanh(GELU_C * pre * (1.0 + 0.044715 * square))
        hill = 0.5 * (1.0 + bent)
        gelu = pre * hill
        slope = hill + 0.5 * pre * (1.0 - bent * bent) * (GELU_C * (1.0 + 3 * 0.044715 * square))
        now = (gelu * up).astype(bf16)
        act[here, :] = now
        dgp[here, :] = (d_hidden * up * slope).astype(bf16)
        dup[here, :] = (d_hidden * gelu).astype(bf16)
        pull = jnp.sum(now.astype(f32) * d_hidden, axis=1, keepdims=True)

        @pl.when(q + 1 < steps)
        def _():
            for g in range(group):
                x_arrival(q + 1, g).wait_recv()
                forward(q + 1, g).start()

        @pl.when(q >= 1)
        def _():
            finish(q - 1)

        @pl.when(q >= 2)
        def _():
            for g in range(group):
                q_copy(q - 2, g).wait_send()
                d_copy(q - 2, g).wait_send()
                p_copy(q - 2, g).wait_send()

        d_in = (dot_nt(dgp[here, :], wg_ref[...]) + dot_nt(dup[here, :], wu_ref[...])).astype(bf16)
        pull = jnp.broadcast_to(pull, (rows, LANES))
        for g in range(group):
            place = q * group + g
            low, mid, high = g * pair, g * pair + capacity, (g + 1) * pair
            pt[place, :, 0:capacity] = jnp.transpose(pull[low:mid])[0:8, :]
            pq[slot, g, :, 0:capacity] = jnp.transpose(pull[mid:high])[0:8, :]
            ds[place] = d_in[low:mid]
            pd[slot, g] = d_in[mid:high]
            q_copy(q, g).start()
            d_copy(q, g).start()
        partial = dot_nn(act[here, :], wd_ref[...]).astype(bf16)
        for g in range(group):
            place = q * group + g
            low, mid, high = g * pair, g * pair + capacity, (g + 1) * pair
            sp[place] = partial[low:mid]
            pp[slot, g] = partial[mid:high]
            p_copy(q, g).start()

    def step(q, carry):
        @pl.when(q == steps)
        def _():
            finish(q - 1)

        @pl.when((q >= 2) & (lax.rem(q, 2) == 0))
        def _():
            weight_grads(q)

        @pl.when(q < steps)
        def _():
            main(q)

        return carry

    lax.fori_loop(0, steps + 1, step, 0)
    for copy, buf, acc in zip(grads, (wg_ref, wu_ref, wd_ref), (acc_g, acc_u, acc_d)):
        buf[...] = acc[...].astype(bf16)
        copy.start()
    for q in (steps - 2, steps - 1):
        for g in range(group):
            q_copy(q, g).wait_send()
            d_copy(q, g).wait_send()
            p_copy(q, g).wait_send()
    self_pull.wait()
    self_back.wait()
    for q in range(steps):
        for g in range(group):
            place = q * group + g
            slot_copy(q, g).wait()
            forward(q, g).wait_send()
            g_mate(q, g).wait_send()
            if place:
                x_copy(place).wait_send()
                for copy in back_copies(q, g):
                    copy.wait()
    for copy in grads:
        copy.wait()


def expert_exchange(x, g, others, wg, wu, wd, wr, group=2):
    experts, capacity, width = x.shape
    ff = wg.shape[1]
    steps = experts // group
    rows = 2 * capacity * group
    anywhere = pl.BlockSpec(memory_space=pl.ANY)
    vmem, dma = pltpu.VMEM, pltpu.SemaphoreType.DMA
    each = dma((experts,))
    count = rows * steps
    outs = pl.pallas_call(
        functools.partial(expert_exchange_kernel, group),
        out_shape=(
            jax.ShapeDtypeStruct((width, ff), bf16),
            jax.ShapeDtypeStruct((width, ff), bf16),
            jax.ShapeDtypeStruct((ff, width), bf16),
            jax.ShapeDtypeStruct((experts, capacity, width), bf16),
            jax.ShapeDtypeStruct((experts, capacity, width), bf16),
            jax.ShapeDtypeStruct((experts, 8, LANES), f32),
            jax.ShapeDtypeStruct((experts, capacity, width), bf16),
        ),
        in_specs=[anywhere] * 6 + [pl.BlockSpec(memory_space=vmem)],
        out_specs=(anywhere,) * 7,
        scratch_shapes=[
            vmem((steps * rows, width), bf16),
            vmem((2, rows, width), bf16),
            vmem((experts, 8, LANES), f32),
            vmem((experts, 8, LANES), f32),
            vmem((experts, capacity, width), bf16),
            vmem((2, group, capacity, width), bf16),
            vmem((2, group, capacity, width), bf16),
            vmem((experts, capacity, width), bf16),
            vmem((2, group, capacity, width), bf16),
            vmem((2, group, capacity, width), bf16),
            vmem((experts, 8, LANES), f32),
            vmem((2, group, 8, LANES), f32),
            vmem((2, group, 8, LANES), f32),
            vmem((2 * rows, ff), bf16),
            vmem((2 * rows, ff), bf16),
            vmem((2 * rows, ff), bf16),
            vmem((2 * rows, width), bf16),
            vmem((width, 2 * rows), bf16),
            vmem((width, ff), f32),
            vmem((width, ff), f32),
            vmem((ff, width), f32),
            vmem((width, ff), bf16),
            vmem((width, ff), bf16),
            vmem((ff, width), bf16),
            dma((3,)),
            each, each, each, each,
            dma((2, 2 * group)),
            each, each,
            each, each, each, each, each, each, each, each, each, each, each,
            dma((6,)),
            dma((3,)),
        ],
        compiler_params=params(62, collective_id=2, has_side_effects=True),
        cost_estimate=cost(18 * count * width * ff, 2 * count * 4 * width + 18 * width * ff, count * ff),
        name="experts",
    )(x, g, others, wg, wu, wd, wr)
    return outs[:6]


def hot_rows(col, k, rows, slots):
    return jnp.where(iota((rows, slots), 1) == col[:, k : k + 1], 1.0, 0.0).astype(bf16)


def state_rows(col, gates, hidden, out_grad, gain, wr, gathered, pull0, pull1):
    valid = col[:, 4:5].astype(f32)
    total = pull0 + pull1
    lane = iota((col.shape[0], LANES), 1)
    d_log = jnp.where(lane == col[:, 2:3], pull0 - gates[:, 0:1] * total, 0.0)
    d_log = d_log + jnp.where(lane == col[:, 3:4], pull1 - gates[:, 1:2] * total, 0.0)
    d_log = d_log.astype(bf16)
    d_moe = gathered + dot_nt(d_log, wr)
    inverse = lax.rsqrt(jnp.mean(hidden * hidden, axis=1, keepdims=True) + epsilon)
    normal = hidden * inverse
    scaled = gain * d_moe
    share = jnp.mean(normal * scaled, axis=1, keepdims=True)
    d_state = out_grad.astype(f32) + inverse * (scaled - normal * share)
    term = jnp.sum((normal * d_moe).reshape(hidden.shape[0] // 8, 8, hidden.shape[1]), axis=0)
    return d_log, d_state, (valid * d_state).astype(bf16), term


def pull_rows(col, k, table, slots):
    experts, rows = table.shape[0], col.shape[0]
    chosen = jnp.where(iota((rows, experts), 1) == col[:, 2 + k : 3 + k], 1.0, 0.0)
    values = dot_nn(chosen, table, precision=lax.Precision.HIGHEST)
    slot = col[:, k : k + 1] - slots // experts * col[:, 2 + k : 3 + k]
    here = (iota((rows, LANES), 1) == slot) & (col[:, k : k + 1] < slots)
    return jnp.sum(jnp.where(here, values, 0.0), axis=1, keepdims=True)


def state_kernel(
    col_ref, gate_ref, din_ref, h_ref, og_ref, gain_ref, wr_ref, dstate_ref, dattn_ref, dlog_ref, gterm_ref
):
    rows, width = h_ref.shape
    slots = din_ref.shape[0]
    col = col_ref[...]
    hot0, hot1 = hot_rows(col, 0, rows, slots), hot_rows(col, 1, rows, slots)
    pulls = din_ref[:, width:]
    pull0 = jnp.sum(dot_nn(hot0, pulls), axis=1, keepdims=True)
    pull1 = jnp.sum(dot_nn(hot1, pulls), axis=1, keepdims=True)
    gathered = dot_nn(hot0 + hot1, din_ref[:, 0:width])
    dlog_ref[...], dstate_ref[...], dattn_ref[...], term = state_rows(
        col, gate_ref[...], h_ref[...], og_ref[...], gain_ref[...], wr_ref[...], gathered, pull0, pull1
    )

    @pl.when(pl.program_id(0) == 0)
    def _():
        gterm_ref[...] = jnp.zeros_like(gterm_ref)

    gterm_ref[...] += term


def state_back(col, gates, din, hidden, out_grad, gain, wr):
    count, width = hidden.shape
    slots = din.shape[0]
    rows = 256
    whole = lambda i: (0, 0)
    part = lambda i: (i, 0)
    return pl.pallas_call(
        state_kernel,
        out_shape=(
            jax.ShapeDtypeStruct((count, width), f32),
            jax.ShapeDtypeStruct((count, width), bf16),
            jax.ShapeDtypeStruct((count, LANES), bf16),
            jax.ShapeDtypeStruct((8, width), f32),
        ),
        grid=(count // rows,),
        in_specs=[
            pl.BlockSpec((rows, LANES), part),
            pl.BlockSpec((rows, LANES), part),
            pl.BlockSpec(din.shape, whole),
            pl.BlockSpec((rows, width), part),
            pl.BlockSpec((rows, width), part),
            pl.BlockSpec((1, width), whole),
            pl.BlockSpec((width, LANES), whole),
        ],
        out_specs=(
            pl.BlockSpec((rows, width), part),
            pl.BlockSpec((rows, width), part),
            pl.BlockSpec((rows, LANES), part),
            pl.BlockSpec((8, width), whole),
        ),
        compiler_params=params(48),
        cost_estimate=cost(2 * slots * count * width, 14 * count * width),
        name="state_back",
    )(col, gates, din, hidden, out_grad, gain.reshape(1, width), wr)


def finish_sums(w_ref, gain_ref, sum_ref, extra_ref, qkv_ref, out_ref, small_ref):
    pairs, rows = sum_ref.shape[0:2]
    width = w_ref.shape[0]
    me = lax.axis_index("dp")
    for pair in range(pairs):
        at = pair * LANES
        for i in range(3):
            qkv_ref[:, i * width + at : i * width + at + LANES] = sum_ref[pair, :, i * LANES : (i + 1) * LANES]
        out_ref[:, at : at + LANES] = sum_ref[pair, :, 3 * LANES :]
    mine = w_ref[pl.ds(pl.multiple_of(me * rows, rows), rows), :].astype(f32)
    total = jnp.sum(mine * qkv_ref[...], axis=1, keepdims=True)
    here = iota((rows, width), 1) == iota((rows, width), 0) + me * rows
    gain = jnp.sum(jnp.where(here, gain_ref[...], 0.0), axis=1, keepdims=True)
    small_ref[...] = jnp.where(iota(small_ref.shape, 1) == 65, total / gain, extra_ref[...])


def tail_kernel(
    n_ride, n_sum, d_ref, w_ref, tok_ref, gain_ref, dstate_ref, col_ref, gate_ref, rows_ref, h_ref, *refs
):
    srcs, sums, refs = refs[:n_ride], refs[n_ride : n_ride + n_sum], refs[n_ride + n_sum :]
    (grad_ref, out_ref), dsts, finals = refs[0:2], refs[2 : 2 + n_ride], refs[2 + n_ride :]
    for src, dst in zip(srcs, dsts):
        dst[...] = src[...].astype(f32)
    if n_sum:

        @pl.when(pl.program_id(0) == 0)
        def _():
            finish_sums(w_ref, gain_ref, *sums, *finals)

    rows, width = tok_ref.shape
    d_normed = dot_nt(d_ref[0], w_ref[:, 0:width])
    for i in range(1, 3):
        d_normed = d_normed + dot_nt(d_ref[i], w_ref[:, i * width : (i + 1) * width])
    values = tok_ref[...].astype(f32)
    inverse = lax.rsqrt(jnp.mean(values * values, axis=1, keepdims=True) + epsilon)
    normal = values * inverse
    scaled = gain_ref[...] * d_normed
    share = jnp.mean(normal * scaled, axis=1, keepdims=True)
    grad_ref[...] = dstate_ref[...] + inverse * (scaled - normal * share)
    slots = rows_ref.shape[0]
    col = col_ref[...]
    pick0 = dot_nn(hot_rows(col, 0, rows, slots), rows_ref[...])
    pick1 = dot_nn(hot_rows(col, 1, rows, slots), rows_ref[...])
    out_ref[...] = (h_ref[...] + gate_ref[:, 0:1] * pick0 + gate_ref[:, 1:2] * pick1).astype(bf16)


def tail(d_qkv, w_qkv, tokens, gain, d_state, col, gates, slot_rows, hidden, riders=(), sums=()):
    count, width = tokens.shape
    rows = 256
    steps = count // rows
    part = lambda i: (i, 0)
    passed = [pl.BlockSpec((array.shape[0] // steps, array.shape[1]), part) for array in riders]

    def whole(array):
        return pl.BlockSpec(array.shape, lambda i: (0,) * len(array.shape), pipeline_mode=pl.Buffered(1))

    finals = []
    if sums:
        mine = sums[1].shape[0]
        finals = [jax.ShapeDtypeStruct((mine, lanes), f32) for lanes in (3 * width, width, LANES)]
    gain = gain.reshape(1, width)
    return pl.pallas_call(
        functools.partial(tail_kernel, len(riders), len(sums)),
        out_shape=[jax.ShapeDtypeStruct((count, width), f32), jax.ShapeDtypeStruct((count, width), bf16)]
        + [jax.ShapeDtypeStruct(array.shape, f32) for array in riders]
        + finals,
        grid=(steps,),
        in_specs=[
            pl.BlockSpec((3, rows, width), lambda i: (0, i, 0)),
            whole(w_qkv),
            pl.BlockSpec((rows, width), part),
            whole(gain),
            pl.BlockSpec((rows, width), part),
            pl.BlockSpec((rows, LANES), part),
            pl.BlockSpec((rows, LANES), part),
            whole(slot_rows),
            pl.BlockSpec((rows, width), part),
        ]
        + passed
        + [whole(array) for array in sums],
        out_specs=[pl.BlockSpec((rows, width), part)] * 2
        + passed
        + [pl.BlockSpec(final.shape, lambda i: (0, 0)) for final in finals],
        compiler_params=params(56),
        cost_estimate=cost(12 * count * width * width, 60 * count * width),
        name="tail",
    )(d_qkv, w_qkv, tokens, gain, d_state, col, gates, slot_rows, hidden, *riders, *sums)


def shards(
    tokens,
    lengths,
    expert_ids,
    slot_order,
    gain_attn,
    w_qkv,
    w_out,
    gain_moe,
    w_router,
    w_gate,
    w_up,
    w_down,
    out_grad,
):
    tok_dev, width = tokens.shape
    n_dev = lax.axis_size("dp")
    experts = w_router.shape[1]
    split = n_dev // experts
    capacity = split * (5 * tok_dev // (4 * n_dev))
    slots = experts * capacity
    me = lax.axis_index("dp")
    part = lax.rem(me, split)
    same_part = [[e * split + p for e in range(experts)] for p in range(split)]
    same_expert = [[e * split + p for p in range(split)] for e in range(experts)]
    swap = [(d, d ^ 1) for d in range(n_dev)]

    def across(blocks):
        return lax.all_to_all(blocks, "dp", 0, 0, axis_index_groups=same_part, tiled=True)

    def share(rows):
        if split == 2:
            return jnp.concatenate([rows, lax.ppermute(rows, "dp", swap)], axis=0)
        return lax.all_gather(rows, "dp", axis_index_groups=same_expert, tiled=True)

    def settle(pieces):
        if split == 2:
            theirs = lax.ppermute(pieces[1], "dp", swap)
            return (pieces[0].astype(f32) + theirs.astype(f32)).astype(bf16)
        got = lax.all_to_all(pieces, "dp", 0, 0, axis_index_groups=same_expert, tiled=True)
        return jnp.sum(got.astype(f32), axis=0).astype(bf16)

    def send_in(rows):
        return share(across(rows.reshape(experts, capacity, -1)).reshape(slots, -1))

    def send_back(rows):
        summed = settle(rows.reshape(split, slots, -1))
        return across(summed.reshape(experts, capacity, -1)).reshape(slots, -1)

    def reduce_rows(term):
        pieces = term.reshape(experts, split, -1, term.shape[-1])
        if split == 2:
            mine = lax.dynamic_index_in_dim(pieces, part, 1, keepdims=False)
            theirs = lax.dynamic_index_in_dim(pieces, 1 - part, 1, keepdims=False)
            theirs = lax.ppermute(theirs.astype(bf16), "dp", swap)
            summed = (mine + theirs.astype(f32)).astype(bf16)
        else:
            pieces = jnp.moveaxis(pieces, 1, 0).astype(bf16)
            got = lax.all_to_all(pieces, "dp", 0, 0, axis_index_groups=same_expert, tiled=True)
            summed = jnp.sum(got.astype(f32), axis=0).astype(bf16)
        return jnp.sum(across(summed).astype(f32), axis=0)

    wr = jnp.pad(w_router, ((0, 0), (0, LANES - experts)))
    col, row = make_slots(lengths, expert_ids, slot_order, experts, capacity)
    direct = split == 2 and experts == 16

    if direct:
        norm_t, qkv, mixed, mixed_t, lse, hidden, moe_t, gates, rows_out, grad_in, others = front(
            tokens, gain_attn, w_qkv, w_out, gain_moe, wr, col, row, out_grad, experts, capacity
        )
    else:
        token_vals = tokens.astype(f32)
        inverse_attn = lax.rsqrt(jnp.mean(token_vals * token_vals, axis=-1, keepdims=True) + epsilon)
        normed_low = (token_vals * inverse_attn * gain_attn).astype(bf16)
        qkv = jnp.dot(normed_low, w_qkv, preferred_element_type=f32).astype(bf16)
        mixed, lse = attend(qkv)
        grad_in = send_in(dispatch_grad(row, out_grad, slots))
        hidden, moe_low, gates = middle(mixed, w_out, tokens, gain_moe, wr, col)
        rows_out = dispatch(row, moe_low, slots)
    if direct:
        gate_grad, up_grad, down_grad, slot_part, d_in_back, pulls = expert_exchange(
            rows_out.reshape(experts, capacity, -1), grad_in, others, w_gate[0], w_up[0], w_down[0], wr
        )
        d_in_back = d_in_back.reshape(slots, -1)
    else:
        rows_in = send_in(rows_out)
        act, d_pre, d_up, d_rows, partial_out, d_in = expert_pass(
            rows_in, grad_in, w_gate[0], w_up[0], w_down[0], wr, split
        )
        d_in_back = send_back(d_in)
        slot_out = send_back(partial_out)
        down_grad = dot_tn(act, d_rows)
        gate_grad = dot_tn(rows_in, d_pre)
        up_grad = dot_tn(rows_in, d_up)

    if direct:
        d_state, d_qkv, sums, extra, slot_out = attend_back_reduce(
            qkv, mixed, lse, norm_t, mixed_t, moe_t, col, gates, d_in_back, hidden, out_grad,
            gain_moe, wr, pulls, w_out, slot_part, n_dev,
        )
        tokens_grad, block_out, gate_grad, up_grad, down_grad, qkv_sum, out_rows, extra = tail(
            d_qkv, w_qkv, tokens, gain_attn, d_state, col, gates, slot_out.reshape(slots, -1), hidden,
            (gate_grad, up_grad, down_grad), (sums, extra),
        )
        router_sum, gain_moe_sum, gain_attn_sum = extra[:, 0:experts], extra[:, 64], extra[:, 65]
    else:
        d_state, d_attn, d_log, gain_moe_rows = state_back(
            col, gates, d_in_back, hidden, out_grad, gain_moe, wr
        )
        d_mixed = dot_nt(d_attn, w_out).astype(bf16)
        d_qkv = attend_back(qkv, mixed, d_mixed, lse)
        lane = jnp.arange(LANES, dtype=jnp.int32)[None, :]
        gain_moe_term = jnp.sum(gain_moe_rows, axis=0)
        extra = jnp.where(lane == experts, gain_moe_term[:, None], dot_tn(moe_low, d_log))
        early = reduce_rows(jnp.concatenate([dot_tn(mixed, d_attn), extra], axis=1))
        out_rows, router_sum, gain_moe_sum = (
            early[:, 0:width], early[:, width : width + experts], early[:, width + experts]
        )
        qkv_sum = reduce_rows(jnp.concatenate([dot_tn(normed_low, d_qkv[i]) for i in range(3)], axis=1))
        tokens_grad, block_out = tail(d_qkv, w_qkv, tokens, gain_attn, d_state, col, gates, slot_out, hidden)
        my_rows = width // n_dev
        weight_rows = lax.dynamic_slice_in_dim(w_qkv, me * my_rows, my_rows, 0).astype(f32)
        my_gain = lax.dynamic_slice_in_dim(gain_attn, me * my_rows, my_rows, 0)
        gain_attn_sum = jnp.sum(weight_rows * qkv_sum, axis=1) / my_gain
    return (
        block_out,
        tokens_grad,
        gain_attn_sum,
        qkv_sum,
        out_rows,
        gain_moe_sum,
        router_sum,
        gate_grad[None],
        up_grad[None],
        down_grad[None],
    )


def solution(mesh):
    rows, one = P("dp", None), P("dp")
    cube = P("dp", None, None)
    return jax.shard_map(
        shards,
        mesh=mesh,
        in_specs=(rows, one, rows, rows, P(), P(), P(), P(), P(), cube, cube, cube, rows),
        out_specs=(rows, rows, one, rows, rows, one, rows, cube, cube, cube),
        check_vma=False,
    )
```
